32 devices in a mesh: batch: 8 (over z, x), chan: 4 (over y, core).
Axes of the slice: x: 2, y: 2, z: 4, core: 2. Of those that a mesh axis runs over, the one named last changes fastest.
Arguments:
- features: bfloat16 [16, 8, 32, 2048], P('batch', None, None, 'chan'), may hold values from -6 to 6
- image_ids: int32 [16, 8, 32], P('batch'), may hold values from 0 to 3, as said below
- reduce_weight: bfloat16 [2048, 512], P('chan', 'batch'), may hold values from -0.125 to 0.125
- spatial_weight: bfloat16 [9, 512, 512], P(None, 'batch', 'chan'), may hold values from -0.09375 to 0.09375
- expand_weight: bfloat16 [512, 2048], P('batch', 'chan'), may hold values from -0.25 to 0.25
- head_weights: bfloat16 [9, 2048, 4, 512], P(None, 'chan', None, 'batch'), may hold values from -0.046875 to 0.046875
- distil_weights: bfloat16 [2, 9, 4, 512, 512], P(None, None, None, 'batch', 'chan'), may hold values from -0.09375 to 0.09375
- block_scale: float32 [2, 512], P(None, 'chan'), may hold values from 0.5 to 1.5
- block_shift: float32 [2, 512], P(None, 'chan'), may hold values from -0.5 to 0.5
- head_scale: float32 [4, 512], P(None, 'chan'), may hold values from 0.5 to 1.5
- head_shift: float32 [4, 512], P(None, 'chan'), may hold values from -0.5 to 0.5
- gate_bias: float32 [2, 512], P(None, 'chan'), may hold values from -3 to 3
- output_scale: float32 [2048], P('chan'), may hold values from 0.5 to 1.5
- output_shift: float32 [2048], P('chan'), may hold values from -0.5 to 0.5
- depth_cotangent: bfloat16 [16, 8, 32, 512], P('batch', None, None, 'chan'), may hold values from -6 to 6
- segment_cotangent: bfloat16 [16, 8, 32, 512], P('batch', None, None, 'chan'), may hold values from -6 to 6
Outputs:
- depth_stream: bfloat16 [16, 8, 32, 512], P('batch', None, None, 'chan')
- segment_stream: bfloat16 [16, 8, 32, 512], P('batch', None, None, 'chan')
- features_grad: float32 [16, 8, 32, 2048], P('batch', None, None, 'chan')
- reduce_grad: float32 [2048, 512], P('chan', 'batch')
- spatial_grad: float32 [9, 512, 512], P(None, 'batch', 'chan')
- expand_grad: float32 [512, 2048], P('batch', 'chan')
- heads_grad: float32 [9, 2048, 4, 512], P(None, 'chan', None, 'batch')
- distil_grad: float32 [2, 9, 4, 512, 512], P(None, None, None, 'batch', 'chan')
- block_scale_grad: float32 [2, 512], P(None, 'chan')
- block_shift_grad: float32 [2, 512], P(None, 'chan')
- head_scale_grad: float32 [4, 512], P(None, 'chan')
- head_shift_grad: float32 [4, 512], P(None, 'chan')
- gate_bias_grad: float32 [2, 512], P(None, 'chan')
- output_scale_grad: float32 [2048], P('chan')
- output_shift_grad: float32 [2048], P('chan')
The draws below stay inside these ranges and needn't reach their ends.
Inputs may be any that keep to these rules, and one draw needn't show every extreme that they name: `image_ids`: in each canvas the ids 0, 1, 2 and 3 each mark one rectangle of pixels, and the four rectangles cover the canvas.
All inputs are finite; a program needn't handle non-finite values.
Results may differ from the reference program's by a relative error of at most 0.033.
Values may be sent and summed in bfloat16 or wider, within the bound.
A program may use at most 256 MiB of HBM per device.

```python
import jax
import jax.numpy as jnp
from jax import lax

WIDE = 2048
MID = 512
HEAD = 512
ROWS = 8
COLS = 32
MICRO = 2
CANVASES = 16
N_BATCH = 8


def draw_features(key, part):
    first_key = jax.random.fold_in(key, 0)
    canvas = jnp.arange(CANVASES, dtype=jnp.float32)
    rising = 0.6 + 1.2 * canvas / max(CANVASES - 1, 1)
    values = jax.random.normal(first_key, (CANVASES, ROWS, COLS, WIDE), jnp.float32)
    return jnp.clip(values * rising[:, None, None, None], -6.0, 6.0).astype(jnp.bfloat16)


def draw_image_ids(key, part):
    column_key, upper_key, lower_key = jax.random.split(key, 3)
    column_cut = jax.random.randint(column_key, (CANVASES, 1, 1), COLS // 4, 3 * COLS // 4 + 1)
    left_cut = jax.random.randint(upper_key, (CANVASES, 1, 1), ROWS // 4, 3 * ROWS // 4 + 1)
    right_cut = jax.random.randint(lower_key, (CANVASES, 1, 1), ROWS // 4, 3 * ROWS // 4 + 1)
    row_index = jnp.arange(ROWS, dtype=jnp.int32)[None, :, None]
    column_index = jnp.arange(COLS, dtype=jnp.int32)[None, None, :]
    right_side = (column_index >= column_cut).astype(jnp.int32)
    row_cut = jnp.where(right_side == 1, right_cut, left_cut)
    return 2 * right_side + (row_index >= row_cut).astype(jnp.int32)


def steps_of(key, dims, cuts, smallest, high):
    loudness, own = 1.0, jax.random.fold_in(key, 6)
    for dim, blocks in cuts:
        steps = jnp.exp(jax.random.uniform(jax.random.fold_in(own, dim), (blocks,), jnp.float32, smallest / len(cuts), high / len(cuts)))
        loudness = loudness * jnp.repeat(steps, dims[dim] // blocks).reshape([-1 if axis == dim else 1 for axis in range(len(dims))])
    return loudness


def bell_draw(stream_key, extent, scale, bound, shards=(), kind=jnp.bfloat16):
    loudness = steps_of(stream_key, extent, shards, -0.22, 0.18) if shards else 1.0
    entries = jax.random.normal(stream_key, extent, jnp.float32) * scale * loudness
    return jnp.minimum(jnp.maximum(entries, -bound), bound).astype(kind)


def setup_inputs(seed: int = 0) -> dict:
    splits = jax.random.split(jax.random.key(seed), 17)
    return {
        "features": draw_features(jax.random.fold_in(splits[16], 71), 0),
        "image_ids": draw_image_ids(jax.random.fold_in(splits[16], 71), 0),
        "reduce_weight": bell_draw(splits[2], (WIDE, MID), WIDE ** -0.5, 0.125, ((0, 4), (1, 8))),
        "spatial_weight": bell_draw(splits[3], (9, MID, MID), (9 * MID) ** -0.5, 0.09375, ((1, 8), (2, 4))),
        "expand_weight": bell_draw(splits[4], (MID, WIDE), MID ** -0.5, 0.25, ((0, 8), (1, 4))),
        "head_weights": bell_draw(splits[5], (9, WIDE, 4, HEAD), (9 * WIDE) ** -0.5, 0.046875, ((1, 4), (3, 8))),
        "distil_weights": bell_draw(splits[6], (2, 9, 4, HEAD, HEAD), (9 * HEAD) ** -0.5, 0.09375, ((3, 8), (4, 4))),
        "block_scale": jnp.clip(0.5 + 1.0 * jax.random.uniform(splits[7], (2, MID), jnp.float32) ** steps_of(splits[7], (2, MID), ((1, 4),), -0.2, 0.2), 0.5, 1.5),
        "block_shift": jnp.clip(jax.random.uniform(splits[8], (2, MID), jnp.float32, -0.5, 0.5) * steps_of(splits[8], (2, MID), ((1, 4),), -0.4, 0.0), -0.5, 0.5),
        "head_scale": jnp.clip(0.5 + 1.0 * jax.random.uniform(splits[9], (4, HEAD), jnp.float32) ** steps_of(splits[9], (4, HEAD), ((1, 4),), -0.2, 0.2), 0.5, 1.5),
        "head_shift": jnp.clip(jax.random.uniform(splits[10], (4, HEAD), jnp.float32, -0.5, 0.5) * steps_of(splits[10], (4, HEAD), ((1, 4),), -0.4, 0.0), -0.5, 0.5),
        "gate_bias": bell_draw(splits[11], (2, HEAD), 1.0, 3.0, ((1, 4),), jnp.float32),
        "output_scale": jnp.clip(0.5 + 1.0 * jax.random.uniform(splits[12], (WIDE,), jnp.float32) ** steps_of(splits[12], (WIDE,), ((0, 4),), -0.2, 0.2), 0.5, 1.5),
        "output_shift": jnp.clip(jax.random.uniform(splits[13], (WIDE,), jnp.float32, -0.5, 0.5) * steps_of(splits[13], (WIDE,), ((0, 4),), -0.4, 0.0), -0.5, 0.5),
        "depth_cotangent": bell_draw(splits[14], (CANVASES, ROWS, COLS, HEAD), 1.0, 6.0, ((0, 8), (3, 4))),
        "segment_cotangent": bell_draw(splits[15], (CANVASES, ROWS, COLS, HEAD), 1.0, 6.0, ((0, 8), (3, 4))),
    }


EPSILON = 1e-05
HIGHEST = lax.Precision.HIGHEST
OFFSETS = ((-1, -1), (-1, 0), (-1, 1), (0, -1), (0, 0), (0, 1), (1, -1), (1, 0), (1, 1))
OWN_HEAD = (0, 3)
SOURCE_START = (1, 0)

@jax.custom_vjp
def low(v):
    return lax.optimization_barrier(v.astype(jnp.bfloat16)).astype(jnp.float32)

@jax.custom_vjp
def low_back(v):
    return v

def low_keep(v):
    return (low(v), None)

def low_pass(kept, grad):
    return (grad,)

def back_keep(v):
    return (v, None)

def back_low(kept, grad):
    return (low(grad),)
low.defvjp(low_keep, low_pass)
low_back.defvjp(back_keep, back_low)

def tap_masks(image_ids):
    row_count, column_count = (image_ids.shape[1], image_ids.shape[2])
    padded = jnp.pad(image_ids, ((0, 0), (1, 1), (1, 1)), constant_values=-1)
    masks = []
    for vertical, lateral in OFFSETS:
        beside = padded[:, 1 + vertical:1 + vertical + row_count, 1 + lateral:1 + lateral + column_count]
        masks.append((beside == image_ids).astype(jnp.float32))
    return jnp.stack(masks)

def conv(values, weight, masks):
    row_count, column_count = (values.shape[1], values.shape[2])
    padded = jnp.pad(values, ((0, 0), (1, 1), (1, 1), (0, 0)))
    total = jnp.zeros(values.shape[:3] + (weight.shape[2],), jnp.float32)
    for number, (vertical, lateral) in enumerate(OFFSETS):
        moved = padded[:, 1 + vertical:1 + vertical + row_count, 1 + lateral:1 + lateral + column_count] * masks[number][..., None]
        total = total + jnp.einsum('nhwc,co->nhwo', moved, weight[number], precision=HIGHEST)
    return total

def batch_norm(values, scale, shift):
    center = lax.optimization_barrier(jnp.mean(values, axis=(0, 1, 2)))
    spread = lax.optimization_barrier(jnp.mean(values * values, axis=(0, 1, 2))) - center * center
    return (values - center) * lax.rsqrt(spread + EPSILON) * scale + shift

def forward(inputs, reduce_weight, spatial_weight, expand_weight, head_weights, distil_weights, block_scale, block_shift, head_scale, head_shift, gate_bias, output_scale, output_shift, masks):
    first = low_back(jnp.einsum('nhwc,co->nhwo', inputs, reduce_weight, precision=HIGHEST))
    first_act = low(jax.nn.silu(batch_norm(first, block_scale[0], block_shift[0])))
    second = low_back(conv(first_act, spatial_weight, masks))
    second_act = low(jax.nn.silu(batch_norm(second, block_scale[1], block_shift[1])))
    third = low_back(jnp.einsum('nhwc,co->nhwo', second_act, expand_weight, precision=HIGHEST))
    block_out = low(jax.nn.silu(batch_norm(third, output_scale, output_shift) + inputs))
    heads = conv(block_out, head_weights.reshape(9, WIDE, 4 * HEAD), masks)
    heads = low_back(heads.reshape(block_out.shape[:3] + (4, HEAD)))
    head_act = low(jax.nn.silu(batch_norm(heads, head_scale, head_shift)))
    streams = []
    for stream in range(2):
        own_index = OWN_HEAD[stream]
        first_source = SOURCE_START[stream]
        gate_input = low_back(conv(head_act[:, :, :, own_index], distil_weights[stream, :, 0], masks) + gate_bias[stream])
        sources = head_act[:, :, :, first_source:first_source + 3].reshape(head_act.shape[:3] + (3 * HEAD,))
        message = low_back(conv(sources, distil_weights[stream, :, 1:].reshape(9, 3 * HEAD, HEAD), masks))
        streams.append(head_act[:, :, :, own_index] + jax.nn.sigmoid(gate_input) * message)
    return (streams[0], streams[1])

def micro_view(array):
    return array.reshape((N_BATCH, MICRO) + array.shape[1:])

def joined(pieces):
    return jnp.stack(pieces, axis=1).reshape((CANVASES,) + pieces[0].shape[1:])

def reference(features, image_ids, reduce_weight, spatial_weight, expand_weight, head_weights, distil_weights, block_scale, block_shift, head_scale, head_shift, gate_bias, output_scale, output_shift, depth_cotangent, segment_cotangent):
    weights = [argument_value.astype(jnp.float32) for argument_value in (reduce_weight, spatial_weight, expand_weight, head_weights, distil_weights, block_scale, block_shift, head_scale, head_shift, gate_bias, output_scale, output_shift)]
    depth_parts, segment_parts, input_parts = ([], [], [])
    grads_total = None
    for micro_index in range(MICRO):
        inputs = micro_view(features)[:, micro_index].astype(jnp.float32)
        masks = tap_masks(micro_view(image_ids)[:, micro_index])
        cotangents = (micro_view(depth_cotangent)[:, micro_index].astype(jnp.float32), micro_view(segment_cotangent)[:, micro_index].astype(jnp.float32))

        def micro_forward(*arrays):
            return forward(*arrays, masks)
        outputs, pullback = jax.vjp(micro_forward, inputs, *weights)
        grads = pullback(cotangents)
        depth_parts.append(outputs[0].astype(jnp.bfloat16))
        segment_parts.append(outputs[1].astype(jnp.bfloat16))
        input_parts.append(grads[0])
        if grads_total is None:
            grads_total = tuple(grads[1:])
        else:
            grads_total = tuple((earlier + later for earlier, later in zip(grads_total, grads[1:])))
    reduce_grad, spatial_grad, expand_grad, heads_grad, distil_grad, block_scale_grad, block_shift_grad, head_scale_grad, head_shift_grad, gate_bias_grad, output_scale_grad, output_shift_grad = grads_total
    return (joined(depth_parts), joined(segment_parts), joined(input_parts), reduce_grad, spatial_grad, expand_grad, heads_grad, distil_grad, block_scale_grad, block_shift_grad, head_scale_grad, head_shift_grad, gate_bias_grad, output_scale_grad, output_shift_grad)
```

```python
import jax
import jax.numpy as jnp
from jax import lax
from jax.sharding import PartitionSpec as P

EPSILON = 1e-05
OFFSETS = ((-1, -1), (-1, 0), (-1, 1), (0, -1), (0, 0), (0, 1), (1, -1), (1, 0), (1, 1))
OWN_HEAD = (0, 3)
SOURCE_START = (1, 0)


def silu_slope(values):
    sig = jax.nn.sigmoid(values)
    return sig * (1.0 + values * (1.0 - sig))


def shifted(values, vertical, lateral):
    row_count, column_count = (values.shape[1], values.shape[2])
    widths = [(0, 0)] * values.ndim
    widths[1] = (1, 1)
    widths[2] = (1, 1)
    padded = jnp.pad(values, widths)
    return padded[
        :, 1 + vertical : 1 + vertical + row_count, 1 + lateral : 1 + lateral + column_count
    ]


def tap_masks(image_ids):
    row_count, column_count = (image_ids.shape[1], image_ids.shape[2])
    padded = jnp.pad(image_ids, ((0, 0), (1, 1), (1, 1)), constant_values=-1)
    masks = []
    for vertical, lateral in OFFSETS:
        beside = padded[
            :, 1 + vertical : 1 + vertical + row_count, 1 + lateral : 1 + lateral + column_count
        ]
        masks.append((beside == image_ids).astype(jnp.float32))
    return jnp.stack(masks)


def conv_forward(inputs, weight, masks):
    total = 0.0
    for number, (vertical, lateral) in enumerate(OFFSETS):
        moved = shifted(inputs, vertical, lateral) * masks[number][..., None].astype(inputs.dtype)
        total = total + jnp.einsum(
            "nhwc,co->nhwo", moved, weight[number], preferred_element_type=jnp.float32
        )
    return total


def conv_input_grad(grads, weight, masks):
    total = 0.0
    for number, (vertical, lateral) in enumerate(OFFSETS):
        term = jnp.einsum(
            "nhwo,co->nhwc", grads, weight[number], preferred_element_type=jnp.float32
        )
        total = total + shifted(term * masks[number][..., None], -vertical, -lateral)
    return total


def conv_weight_grad(inputs, grads, masks):
    pieces = []
    for number, (vertical, lateral) in enumerate(OFFSETS):
        moved = shifted(inputs, vertical, lateral) * masks[number][..., None].astype(inputs.dtype)
        pieces.append(jnp.einsum("nhwc,nhwo->co", moved, grads, preferred_element_type=jnp.float32))
    return jnp.stack(pieces)


def pixel_sum(values):
    return jnp.sum(values, axis=(0, 1, 2))


def normalize(values, scale, shift, count):
    total, squares = lax.psum((pixel_sum(values), pixel_sum(values * values)), "batch")
    center = total / count
    inverse = lax.rsqrt(squares / count - center * center + EPSILON)
    normed = (values - center) * inverse
    return (normed, inverse, normed * scale + shift)


def grad_sums(first_sum, second_sum):
    return lax.psum((first_sum, second_sum), "batch")


def normalize_back(grads, normed, inverse, scale, shift_sum, scale_sum, count):
    return scale * inverse * (grads - (shift_sum + normed * scale_sum) / count)


def channel_gather(values):
    return lax.all_gather(values, "chan", axis=4, tiled=True)


def channel_sum(values):
    return lax.psum_scatter(
        values.astype(jnp.bfloat16), "chan", scatter_dimension=4, tiled=True
    ).astype(jnp.float32)


def fetch_weights(reduce_weight, spatial_weight, expand_weight, head_weights, distil_weights):
    return (
        lax.all_gather(reduce_weight, "batch", axis=1, tiled=True),
        lax.all_gather(spatial_weight, "batch", axis=1, tiled=True),
        lax.all_gather(expand_weight, "batch", axis=0, tiled=True),
        lax.all_gather(head_weights, "batch", axis=3, tiled=True),
        lax.all_gather(distil_weights, "batch", axis=3, tiled=True),
    )


def scatter_weights(grads):
    reduce_grad, spatial_grad, expand_grad, heads_grad, distil_grad = grads
    return (
        lax.psum_scatter(reduce_grad, "batch", scatter_dimension=1, tiled=True),
        lax.psum_scatter(spatial_grad, "batch", scatter_dimension=1, tiled=True),
        lax.psum_scatter(expand_grad, "batch", scatter_dimension=0, tiled=True),
        lax.psum_scatter(heads_grad, "batch", scatter_dimension=3, tiled=True),
        lax.psum_scatter(distil_grad, "batch", scatter_dimension=3, tiled=True),
    )


def micro_step(inputs, image_ids, depth_cot, segment_cot, gathered, small, batch_count):
    reduce_full, spatial_full, expand_full, heads_full, distil_full = gathered
    block_scale, block_shift, head_scale, head_shift, gate_bias, output_scale, output_shift = small
    masks = tap_masks(image_ids)
    canvases, row_count, column_count = image_ids.shape
    count = float(batch_count * canvases * row_count * column_count)
    first_partial = jnp.einsum(
        "nhwc,co->nhwo", inputs, reduce_full, preferred_element_type=jnp.float32
    )
    first = channel_sum(first_partial[:, :, :, None, :])
    first_norm, first_inv, first_out = normalize(first, block_scale[0:1], block_shift[0:1], count)
    first_act = jax.nn.silu(first_out).astype(jnp.bfloat16)
    first_full = channel_gather(first_act)[:, :, :, 0, :]
    second = conv_forward(first_full, spatial_full, masks)[:, :, :, None, :]
    second_norm, second_inv, second_out = normalize(
        second, block_scale[1:2], block_shift[1:2], count
    )
    second_act = jax.nn.silu(second_out).astype(jnp.bfloat16)
    second_full = channel_gather(second_act)[:, :, :, 0, :]
    third = jnp.einsum(
        "nhwc,co->nhwo", second_full, expand_full, preferred_element_type=jnp.float32
    )[:, :, :, None, :]
    third_norm, third_inv, third_out = normalize(
        third, output_scale[None], output_shift[None], count
    )
    summed = third_out[:, :, :, 0, :] + inputs.astype(jnp.float32)
    block_out = jax.nn.silu(summed).astype(jnp.bfloat16)
    heads_flat = heads_full.reshape(heads_full.shape[0], heads_full.shape[1], -1)
    head_partial = conv_forward(block_out, heads_flat, masks)
    head_pre = channel_sum(
        head_partial.reshape(head_partial.shape[:3] + (heads_full.shape[2], heads_full.shape[3]))
    )
    head_norm, head_inv, head_out = normalize(head_pre, head_scale, head_shift, count)
    head_act = jax.nn.silu(head_out).astype(jnp.bfloat16)
    head_full = channel_gather(head_act)
    head_width = head_full.shape[4]
    gate_pre = [0.0, 0.0]
    message = [0.0, 0.0]
    for number, (vertical, lateral) in enumerate(OFFSETS):
        moved = shifted(head_full, vertical, lateral) * masks[number][:, :, :, None, None].astype(
            jnp.bfloat16
        )
        for stream in range(2):
            weights_here = distil_full[stream, number]
            first_source = SOURCE_START[stream]
            sources = moved[:, :, :, first_source : first_source + 3].reshape(
                moved.shape[:3] + (3 * head_width,)
            )
            gate_pre[stream] = gate_pre[stream] + jnp.einsum(
                "nhwc,co->nhwo",
                moved[:, :, :, OWN_HEAD[stream]],
                weights_here[0],
                preferred_element_type=jnp.float32,
            )
            message[stream] = message[stream] + jnp.einsum(
                "nhwc,co->nhwo",
                sources,
                weights_here[1:].reshape(3 * head_width, -1),
                preferred_element_type=jnp.float32,
            )
    cotangents = (depth_cot.astype(jnp.float32), segment_cot.astype(jnp.float32))
    outputs, message_grads, gate_grads = ([], [], [])
    for stream in range(2):
        gate_value = jax.nn.sigmoid(gate_pre[stream] + gate_bias[stream])
        own_feature = head_act[:, :, :, OWN_HEAD[stream]].astype(jnp.float32)
        outputs.append((own_feature + gate_value * message[stream]).astype(jnp.bfloat16))
        message_grads.append((cotangents[stream] * gate_value).astype(jnp.bfloat16))
        gate_grads.append(
            (cotangents[stream] * message[stream] * gate_value * (1.0 - gate_value)).astype(
                jnp.bfloat16
            )
        )
    spread_grad = 0.0
    distil_parts = [[], []]
    for number, (vertical, lateral) in enumerate(OFFSETS):
        tap_mask = masks[number][:, :, :, None, None]
        moved = shifted(head_full, vertical, lateral) * tap_mask.astype(jnp.bfloat16)
        tap_grad = jnp.zeros(head_full.shape, jnp.float32)
        for stream in range(2):
            weights_here = distil_full[stream, number]
            first_source = SOURCE_START[stream]
            sources = moved[:, :, :, first_source : first_source + 3].reshape(
                moved.shape[:3] + (3 * head_width,)
            )
            own_grad = jnp.einsum(
                "nhwo,co->nhwc",
                gate_grads[stream],
                weights_here[0],
                preferred_element_type=jnp.float32,
            )
            source_grad = jnp.einsum(
                "nhwo,co->nhwc",
                message_grads[stream],
                weights_here[1:].reshape(3 * head_width, -1),
                preferred_element_type=jnp.float32,
            )
            tap_grad = tap_grad.at[:, :, :, OWN_HEAD[stream]].add(own_grad)
            tap_grad = tap_grad.at[:, :, :, first_source : first_source + 3].add(
                source_grad.reshape(source_grad.shape[:3] + (3, head_width))
            )
            gate_weight_grad = jnp.einsum(
                "nhwc,nhwo->co",
                moved[:, :, :, OWN_HEAD[stream]],
                gate_grads[stream],
                preferred_element_type=jnp.float32,
            )
            source_weight_grad = jnp.einsum(
                "nhwc,nhwo->co", sources, message_grads[stream], preferred_element_type=jnp.float32
            )
            distil_parts[stream].append(
                jnp.concatenate(
                    [gate_weight_grad[None], source_weight_grad.reshape(3, head_width, -1)], axis=0
                )
            )
        spread_grad = spread_grad + shifted(tap_grad * tap_mask, -vertical, -lateral)
    distil_grad = jnp.stack([jnp.stack(distil_parts[0]), jnp.stack(distil_parts[1])])
    head_grad = channel_sum(spread_grad)
    head_grad = (
        head_grad.at[:, :, :, OWN_HEAD[0]]
        .add(cotangents[0])
        .at[:, :, :, OWN_HEAD[1]]
        .add(cotangents[1])
    )
    head_grad = head_grad * silu_slope(head_out)
    gate_sums = jnp.stack(
        [pixel_sum(gate_grads[0].astype(jnp.float32)), pixel_sum(gate_grads[1].astype(jnp.float32))]
    )
    shift_sums, scale_sums = grad_sums(
        jnp.concatenate([pixel_sum(head_grad), gate_sums], axis=0), pixel_sum(head_grad * head_norm)
    )
    head_pre_grad = normalize_back(
        head_grad, head_norm, head_inv, head_scale, shift_sums[:4], scale_sums, count
    ).astype(jnp.bfloat16)
    head_pre_full = channel_gather(head_pre_grad)
    head_flat_grad = head_pre_full.reshape(head_pre_full.shape[:3] + (-1,))
    block_grad = conv_input_grad(head_flat_grad, heads_flat, masks)
    heads_grad = conv_weight_grad(block_out, head_flat_grad, masks).reshape(heads_full.shape)
    summed_grad = block_grad * silu_slope(summed)
    third_grad = summed_grad[:, :, :, None, :]
    third_shift, third_scale = grad_sums(pixel_sum(third_grad), pixel_sum(third_grad * third_norm))
    third_pre = normalize_back(
        third_grad, third_norm, third_inv, output_scale[None], third_shift, third_scale, count
    ).astype(jnp.bfloat16)[:, :, :, 0, :]
    expand_grad = jnp.einsum(
        "nhwc,nhwo->co", second_full, third_pre, preferred_element_type=jnp.float32
    )
    second_grad = channel_sum(
        jnp.einsum("nhwo,co->nhwc", third_pre, expand_full, preferred_element_type=jnp.float32)[
            :, :, :, None, :
        ]
    )
    second_grad = second_grad * silu_slope(second_out)
    second_shift, second_scale = grad_sums(
        pixel_sum(second_grad), pixel_sum(second_grad * second_norm)
    )
    second_pre = normalize_back(
        second_grad, second_norm, second_inv, block_scale[1:2], second_shift, second_scale, count
    ).astype(jnp.bfloat16)[:, :, :, 0, :]
    spatial_grad = conv_weight_grad(first_full, second_pre, masks)
    first_grad = channel_sum(conv_input_grad(second_pre, spatial_full, masks)[:, :, :, None, :])
    first_grad = first_grad * silu_slope(first_out)
    first_shift, first_scale = grad_sums(pixel_sum(first_grad), pixel_sum(first_grad * first_norm))
    first_pre = normalize_back(
        first_grad, first_norm, first_inv, block_scale[0:1], first_shift, first_scale, count
    ).astype(jnp.bfloat16)
    first_pre_full = channel_gather(first_pre)[:, :, :, 0, :]
    reduce_grad = jnp.einsum(
        "nhwc,nhwo->co", inputs, first_pre_full, preferred_element_type=jnp.float32
    )
    input_grad = summed_grad + jnp.einsum(
        "nhwo,co->nhwc", first_pre_full, reduce_full, preferred_element_type=jnp.float32
    )
    weight_grads = (reduce_grad, spatial_grad, expand_grad, heads_grad, distil_grad)
    small_grads = (
        jnp.concatenate([first_scale, second_scale], axis=0),
        jnp.concatenate([first_shift, second_shift], axis=0),
        scale_sums,
        shift_sums[:4],
        shift_sums[4:],
        third_scale[0],
        third_shift[0],
    )
    return (outputs[0], outputs[1], input_grad, weight_grads, small_grads)


def gathered_local(
    features,
    image_ids,
    reduce_weight,
    spatial_weight,
    expand_weight,
    head_weights,
    distil_weights,
    block_scale,
    block_shift,
    head_scale,
    head_shift,
    gate_bias,
    output_scale,
    output_shift,
    depth_cotangent,
    segment_cotangent,
):
    batch_count = lax.axis_size("batch")
    small = (
        block_scale,
        block_shift,
        head_scale,
        head_shift,
        gate_bias,
        output_scale,
        output_shift,
    )
    depth_list, segment_list, input_list = ([], [], [])
    weight_total = None
    small_total = None
    for micro_index in range(features.shape[0]):
        gathered = fetch_weights(
            reduce_weight, spatial_weight, expand_weight, head_weights, distil_weights
        )
        canvas_pick = slice(micro_index, micro_index + 1)
        depth_out, segment_out, input_grad, weight_grads, small_grads = micro_step(
            features[canvas_pick],
            image_ids[canvas_pick],
            depth_cotangent[canvas_pick],
            segment_cotangent[canvas_pick],
            gathered,
            small,
            batch_count,
        )
        weight_grads = scatter_weights(weight_grads)
        weight_total = (
            weight_grads
            if weight_total is None
            else jax.tree.map(jnp.add, weight_total, weight_grads)
        )
        small_total = (
            small_grads if small_total is None else jax.tree.map(jnp.add, small_total, small_grads)
        )
        depth_list.append(depth_out)
        segment_list.append(segment_out)
        input_list.append(input_grad)
    reduce_grad, spatial_grad, expand_grad, heads_grad, distil_grad = weight_total
    scale_mid, shift_mid, scale_heads, shift_heads, bias_gates, scale_out, shift_out = small_total
    return (
        jnp.concatenate(depth_list, axis=0),
        jnp.concatenate(segment_list, axis=0),
        jnp.concatenate(input_list, axis=0),
        reduce_grad,
        spatial_grad,
        expand_grad,
        heads_grad,
        distil_grad,
        scale_mid,
        shift_mid,
        scale_heads,
        shift_heads,
        bias_gates,
        scale_out,
        shift_out,
    )


def canvas_sum(values):
    return jnp.sum(values, axis=(1, 2))


def spread(values):
    return values[:, None, None, :]


def normalize_each(values, scale, shift, count):
    total, squares = lax.psum((canvas_sum(values), canvas_sum(values * values)), "batch")
    center = total / count
    inverse = lax.rsqrt(squares / count - center * center + EPSILON)
    normed = (values - spread(center)) * spread(inverse)
    return (normed, inverse, normed * scale + shift)


def normalize_each_back(grads, normed, inverse, scale, count):
    shift_sum, scale_sum = lax.psum((canvas_sum(grads), canvas_sum(grads * normed)), "batch")
    back = scale * spread(inverse) * (grads - (spread(shift_sum) + normed * spread(scale_sum)) / count)
    return (back.astype(jnp.bfloat16), shift_sum, scale_sum)


def sum_chan(values):
    return lax.psum_scatter(
        values.astype(jnp.bfloat16), "chan", scatter_dimension=3, tiled=True
    ).astype(jnp.float32)


def gather_chan(values):
    return lax.all_gather(values, "chan", axis=3, tiled=True)


def sum_batch(values, axis):
    return lax.psum_scatter(
        values.astype(jnp.bfloat16), "batch", scatter_dimension=axis, tiled=True
    ).astype(jnp.float32)


def distil_matrix(weights):
    taps = weights.shape[1]
    width = weights.shape[3]
    columns = []
    for stream in range(2):
        for part in range(2):
            rows = []
            for head in range(4):
                source = head - SOURCE_START[stream]
                if part == 0 and head == OWN_HEAD[stream]:
                    rows.append(weights[stream, :, 0])
                elif part == 1 and 0 <= source < 3:
                    rows.append(weights[stream, :, 1 + source])
                else:
                    rows.append(jnp.zeros((taps, width, weights.shape[4]), weights.dtype))
            columns.append(jnp.concatenate(rows, axis=1))
    return jnp.concatenate(columns, axis=2)


def distil_blocks(grads, width):
    outs = []
    for stream in range(2):
        gate = grads[:, :, (2 * stream) * 128 : (2 * stream + 1) * 128]
        message = grads[:, :, (2 * stream + 1) * 128 : (2 * stream + 2) * 128]
        own = OWN_HEAD[stream]
        first = SOURCE_START[stream]
        pieces = [gate[:, own * width : (own + 1) * width]]
        for source in range(3):
            pieces.append(message[:, (first + source) * width : (first + source + 1) * width])
        outs.append(jnp.stack(pieces, axis=1))
    return jnp.stack(outs)


def stationary_local(
    features,
    image_ids,
    reduce_weight,
    spatial_weight,
    expand_weight,
    head_weights,
    distil_weights,
    block_scale,
    block_shift,
    head_scale,
    head_shift,
    gate_bias,
    output_scale,
    output_shift,
    depth_cotangent,
    segment_cotangent,
):
    groups = lax.axis_size("batch")
    place = lax.axis_index("batch")
    lane = lax.axis_index("chan")
    canvases, row_count, column_count = image_ids.shape
    count = float(groups * row_count * column_count)
    pixels = row_count * column_count
    width = head_weights.shape[3]
    reduce_full = lax.all_gather(reduce_weight, "batch", axis=1, tiled=True)
    spatial_full = lax.all_gather(spatial_weight, "batch", axis=1, tiled=True)
    expand_full = lax.all_gather(expand_weight, "batch", axis=0, tiled=True)
    ids_full = lax.all_gather(image_ids, "batch", axis=0, tiled=True)
    masks = tap_masks(image_ids)
    masks_full = tap_masks(ids_full)
    first = sum_chan(
        jnp.einsum("nhwc,co->nhwo", features, reduce_full, preferred_element_type=jnp.float32)
    )
    first_norm, first_inv, first_out = normalize_each(first, block_scale[0], block_shift[0], count)
    first_full = gather_chan(jax.nn.silu(first_out).astype(jnp.bfloat16))
    second = conv_forward(first_full, spatial_full, masks)
    second_norm, second_inv, second_out = normalize_each(
        second, block_scale[1], block_shift[1], count
    )
    second_full = gather_chan(jax.nn.silu(second_out).astype(jnp.bfloat16))
    third = jnp.einsum(
        "nhwc,co->nhwo", second_full, expand_full, preferred_element_type=jnp.float32
    )
    third_norm, third_inv, third_out = normalize_each(third, output_scale, output_shift, count)
    summed = third_out + features.astype(jnp.float32)
    block_out = jax.nn.silu(summed).astype(jnp.bfloat16)

    block_all = lax.all_gather(block_out, "batch", axis=0, tiled=True)
    heads_flat = head_weights.reshape(9, head_weights.shape[1], -1)
    head_partial = conv_forward(block_all, heads_flat, masks_full).astype(jnp.bfloat16)
    head_parts = head_partial.reshape(groups, canvases, pixels, 2, 2 * width).transpose(3, 1, 0, 2, 4)
    head_parts = head_parts.reshape((2 * canvases,) + head_parts.shape[2:])
    head_pre = lax.psum_scatter(head_parts, "chan", scatter_dimension=0, tiled=True)[0].astype(
        jnp.float32
    )
    half = lane // 2

    def mine(values):
        whole = lax.all_gather(values, "chan", axis=1, tiled=True)
        part = lax.dynamic_slice_in_dim(whole, place * width, width, axis=1)
        return lax.dynamic_slice_in_dim(part.reshape(2, 2 * width), half, 1, axis=0)[0]

    my_scale, my_shift = mine(head_scale), mine(head_shift)
    center = jnp.sum(head_pre, axis=(0, 1)) / count
    spreads = jnp.sum(head_pre * head_pre, axis=(0, 1)) / count
    head_inv = lax.rsqrt(spreads - center * center + EPSILON)
    head_norm = (head_pre - center) * head_inv
    head_out = head_norm * my_scale + my_shift
    head_act = jax.nn.silu(head_out).astype(jnp.bfloat16)
    head_all = lax.all_gather(head_act, "chan", axis=0).reshape(
        2, canvases, groups, pixels, 2 * width
    )
    head_full = head_all.transpose(2, 1, 3, 0, 4).reshape(
        groups * canvases, row_count, column_count, 4 * width
    )
    mixed = distil_matrix(distil_weights)
    pre = sum_batch(conv_forward(head_full, mixed, masks_full), 0)
    own_part = jnp.concatenate(
        [head_full[..., :width], head_full[..., 3 * width :]], axis=-1
    )
    own_all = lax.all_to_all(own_part, "batch", split_axis=0, concat_axis=0, tiled=True).reshape(
        groups, canvases, row_count, column_count, 2, width
    )
    per = groups // 4
    own_all = lax.dynamic_slice_in_dim(own_all, lane * per, per, axis=0)
    own_all = own_all.transpose(4, 1, 2, 3, 0, 5).reshape(
        2, canvases, row_count, column_count, per * width
    )
    cots = (depth_cotangent.astype(jnp.float32), segment_cotangent.astype(jnp.float32))
    outputs, pre_grads, gate_sums = ([], [], [])
    for stream in range(2):
        gate_pre = pre[..., (2 * stream) * 128 : (2 * stream + 1) * 128]
        message = pre[..., (2 * stream + 1) * 128 : (2 * stream + 2) * 128]
        gate = jax.nn.sigmoid(gate_pre + gate_bias[stream])
        outputs.append(
            (own_all[stream].astype(jnp.float32) + gate * message).astype(jnp.bfloat16)
        )
        gate_grad = (cots[stream] * message * gate * (1.0 - gate)).astype(jnp.bfloat16)
        gate_sums.append(pixel_sum(gate_grad.astype(jnp.float32)))
        pre_grads.append(gate_grad)
        pre_grads.append((cots[stream] * gate).astype(jnp.bfloat16))
    pre_grad_all = lax.all_gather(
        jnp.concatenate(pre_grads, axis=-1), "batch", axis=0, tiled=True
    )
    distil_grad = distil_blocks(conv_weight_grad(head_full, pre_grad_all, masks_full), width)
    spread_grad = conv_input_grad(pre_grad_all, mixed, masks_full).astype(jnp.bfloat16)
    spread_parts = spread_grad.reshape(groups, canvases, pixels, 2, 2 * width).transpose(3, 1, 0, 2, 4)
    spread_parts = spread_parts.reshape((2 * canvases,) + spread_parts.shape[2:])
    head_grad = lax.psum_scatter(spread_parts, "chan", scatter_dimension=0, tiled=True)[0].astype(
        jnp.float32
    )
    cot_pair = jnp.stack([depth_cotangent, segment_cotangent]).reshape(
        2, canvases, pixels, 4 // 2 * width
    )
    cot_all = lax.all_gather(cot_pair, ("batch", "chan"), axis=0)
    cot_all = cot_all.reshape(groups, 4, 2, canvases, pixels, 2, width)
    cot_mine = lax.dynamic_index_in_dim(cot_all, place // 2, axis=1, keepdims=False)
    cot_mine = lax.dynamic_index_in_dim(cot_mine, half, axis=1, keepdims=False)
    cot_mine = lax.dynamic_index_in_dim(cot_mine, lane % 2, axis=1, keepdims=False)
    cot_mine = lax.dynamic_index_in_dim(cot_mine, place % 2, axis=2, keepdims=False)
    zeros = jnp.zeros_like(cot_mine)
    cot_wide = jnp.where(
        half == 0,
        jnp.concatenate([cot_mine, zeros], axis=-1),
        jnp.concatenate([zeros, cot_mine], axis=-1),
    )
    head_grad = (head_grad + cot_wide.astype(jnp.float32)) * silu_slope(head_out)
    head_shift_sum = jnp.sum(head_grad, axis=(0, 1))
    head_scale_sum = jnp.sum(head_grad * head_norm, axis=(0, 1))
    head_pre_grad = (
        my_scale * head_inv * (head_grad - (head_shift_sum + head_norm * head_scale_sum) / count)
    ).astype(jnp.bfloat16)
    head_grad_all = lax.all_gather(head_pre_grad, "chan", axis=0).reshape(
        2, canvases, groups, pixels, 2 * width
    )
    head_grad_all = head_grad_all.transpose(2, 1, 3, 0, 4).reshape(
        groups * canvases, row_count, column_count, 4 * width
    )
    heads_grad = conv_weight_grad(block_all, head_grad_all, masks_full).reshape(head_weights.shape)
    block_grad = sum_batch(conv_input_grad(head_grad_all, heads_flat, masks_full), 0)
    summed_grad = block_grad * silu_slope(summed)
    third_pre, third_shift, third_scale = normalize_each_back(
        summed_grad, third_norm, third_inv, output_scale, count
    )
    expand_grad = sum_batch(
        jnp.einsum("nhwc,nhwo->co", second_full, third_pre, preferred_element_type=jnp.float32), 0
    )
    second_grad = sum_chan(
        jnp.einsum("nhwo,co->nhwc", third_pre, expand_full, preferred_element_type=jnp.float32)
    ) * silu_slope(second_out)
    second_pre, second_shift, second_scale = normalize_each_back(
        second_grad, second_norm, second_inv, block_scale[1], count
    )
    spatial_grad = sum_batch(conv_weight_grad(first_full, second_pre, masks), 1)
    first_grad = sum_chan(conv_input_grad(second_pre, spatial_full, masks)) * silu_slope(first_out)
    first_pre, first_shift, first_scale = normalize_each_back(
        first_grad, first_norm, first_inv, block_scale[0], count
    )
    first_pre_full = gather_chan(first_pre)
    reduce_grad = sum_batch(
        jnp.einsum("nhwc,nhwo->co", features, first_pre_full, preferred_element_type=jnp.float32), 1
    )
    features_grad = summed_grad + jnp.einsum(
        "nhwo,co->nhwc", first_pre_full, reduce_full, preferred_element_type=jnp.float32
    )
    sums = jnp.stack([head_scale_sum, head_shift_sum]).reshape(2, 1, 2, width)
    wide = jnp.zeros((2, 2, 2, groups * width), jnp.float32)
    sums = lax.dynamic_update_slice(wide, sums, (0, half, 0, place * width)).reshape(2, 4, -1)
    sums = lax.psum(sums, ("batch", "chan"))
    sums = lax.dynamic_slice_in_dim(sums, lane * 128, 128, axis=2)
    gate_total = lax.psum(jnp.stack(gate_sums), "batch")
    return (
        outputs[0],
        outputs[1],
        features_grad,
        reduce_grad,
        spatial_grad,
        expand_grad,
        heads_grad,
        distil_grad,
        jnp.stack([jnp.sum(first_scale, 0), jnp.sum(second_scale, 0)]),
        jnp.stack([jnp.sum(first_shift, 0), jnp.sum(second_shift, 0)]),
        sums[0],
        sums[1],
        gate_total,
        jnp.sum(third_scale, 0),
        jnp.sum(third_shift, 0),
    )


def solution(mesh):
    local = stationary_local if mesh.shape["batch"] <= 8 else gathered_local
    placed = (
        P("batch", None, None, "chan"),
        P("batch", None, None),
        P("chan", "batch"),
        P(None, "batch", "chan"),
        P("batch", "chan"),
        P(None, "chan", None, "batch"),
        P(None, None, None, "batch", "chan"),
        P(None, "chan"),
        P(None, "chan"),
        P(None, "chan"),
        P(None, "chan"),
        P(None, "chan"),
        P("chan"),
        P("chan"),
        P("batch", None, None, "chan"),
        P("batch", None, None, "chan"),
    )
    return jax.shard_map(
        local,
        mesh=mesh,
        in_specs=placed,
        out_specs=(
            P("batch", None, None, "chan"),
            P("batch", None, None, "chan"),
            P("batch", None, None, "chan"),
            P("chan", "batch"),
            P(None, "batch", "chan"),
            P("batch", "chan"),
            P(None, "chan", None, "batch"),
            P(None, None, None, "batch", "chan"),
            P(None, "chan"),
            P(None, "chan"),
            P(None, "chan"),
            P(None, "chan"),
            P(None, "chan"),
            P("chan"),
            P("chan"),
        ),
        check_vma=False,
    )
```

```python
import functools

import jax
import jax.numpy as jnp
from jax import lax
from jax.experimental import pallas as pl
from jax.experimental.pallas import tpu as pltpu
from jax.sharding import PartitionSpec as P

EPSILON = 1e-05
OFFSETS = ((-1, -1), (-1, 0), (-1, 1), (0, -1), (0, 0), (0, 1), (1, -1), (1, 0), (1, 1))
OWN_HEAD = (0, 3)
SOURCE_START = (1, 0)


def silu_slope(values):
    sig = jax.nn.sigmoid(values)
    return sig * (1.0 + values * (1.0 - sig))


def shifted(values, vertical, lateral):
    row_count, column_count = (values.shape[1], values.shape[2])
    widths = [(0, 0)] * values.ndim
    widths[1] = (1, 1)
    widths[2] = (1, 1)
    padded = jnp.pad(values, widths)
    return padded[
        :, 1 + vertical : 1 + vertical + row_count, 1 + lateral : 1 + lateral + column_count
    ]


def tap_masks(image_ids):
    row_count, column_count = (image_ids.shape[1], image_ids.shape[2])
    padded = jnp.pad(image_ids, ((0, 0), (1, 1), (1, 1)), constant_values=-1)
    masks = []
    for vertical, lateral in OFFSETS:
        beside = padded[
            :, 1 + vertical : 1 + vertical + row_count, 1 + lateral : 1 + lateral + column_count
        ]
        masks.append((beside == image_ids).astype(jnp.float32))
    return jnp.stack(masks)


def conv_forward(inputs, weight, masks):
    total = 0.0
    for number, (vertical, lateral) in enumerate(OFFSETS):
        moved = shifted(inputs, vertical, lateral) * masks[number][..., None].astype(inputs.dtype)
        total = total + jnp.einsum(
            "nhwc,co->nhwo", moved, weight[number], preferred_element_type=jnp.float32
        )
    return total


def conv_input_grad(grads, weight, masks):
    total = 0.0
    for number, (vertical, lateral) in enumerate(OFFSETS):
        term = jnp.einsum(
            "nhwo,co->nhwc", grads, weight[number], preferred_element_type=jnp.float32
        )
        total = total + shifted(term * masks[number][..., None], -vertical, -lateral)
    return total


def conv_weight_grad(inputs, grads, masks):
    pieces = []
    for number, (vertical, lateral) in enumerate(OFFSETS):
        moved = shifted(inputs, vertical, lateral) * masks[number][..., None].astype(inputs.dtype)
        pieces.append(jnp.einsum("nhwc,nhwo->co", moved, grads, preferred_element_type=jnp.float32))
    return jnp.stack(pieces)


def pixel_sum(values):
    return jnp.sum(values, axis=(0, 1, 2))


def normalize(values, scale, shift, count):
    total, squares = lax.psum((pixel_sum(values), pixel_sum(values * values)), "batch")
    center = total / count
    inverse = lax.rsqrt(squares / count - center * center + EPSILON)
    normed = (values - center) * inverse
    return (normed, inverse, normed * scale + shift)


def grad_sums(first_sum, second_sum):
    return lax.psum((first_sum, second_sum), "batch")


def normalize_back(grads, normed, inverse, scale, shift_sum, scale_sum, count):
    return scale * inverse * (grads - (shift_sum + normed * scale_sum) / count)


def channel_gather(values):
    return lax.all_gather(values, "chan", axis=4, tiled=True)


def channel_sum(values):
    return lax.psum_scatter(
        values.astype(jnp.bfloat16), "chan", scatter_dimension=4, tiled=True
    ).astype(jnp.float32)


def fetch_weights(reduce_weight, spatial_weight, expand_weight, head_weights, distil_weights):
    return (
        lax.all_gather(reduce_weight, "batch", axis=1, tiled=True),
        lax.all_gather(spatial_weight, "batch", axis=1, tiled=True),
        lax.all_gather(expand_weight, "batch", axis=0, tiled=True),
        lax.all_gather(head_weights, "batch", axis=3, tiled=True),
        lax.all_gather(distil_weights, "batch", axis=3, tiled=True),
    )


def scatter_weights(grads):
    reduce_grad, spatial_grad, expand_grad, heads_grad, distil_grad = grads
    return (
        lax.psum_scatter(reduce_grad, "batch", scatter_dimension=1, tiled=True),
        lax.psum_scatter(spatial_grad, "batch", scatter_dimension=1, tiled=True),
        lax.psum_scatter(expand_grad, "batch", scatter_dimension=0, tiled=True),
        lax.psum_scatter(heads_grad, "batch", scatter_dimension=3, tiled=True),
        lax.psum_scatter(distil_grad, "batch", scatter_dimension=3, tiled=True),
    )


def micro_step(inputs, image_ids, depth_cot, segment_cot, gathered, small, batch_count):
    reduce_full, spatial_full, expand_full, heads_full, distil_full = gathered
    block_scale, block_shift, head_scale, head_shift, gate_bias, output_scale, output_shift = small
    masks = tap_masks(image_ids)
    canvases, row_count, column_count = image_ids.shape
    count = float(batch_count * canvases * row_count * column_count)
    first_partial = jnp.einsum(
        "nhwc,co->nhwo", inputs, reduce_full, preferred_element_type=jnp.float32
    )
    first = channel_sum(first_partial[:, :, :, None, :])
    first_norm, first_inv, first_out = normalize(first, block_scale[0:1], block_shift[0:1], count)
    first_act = jax.nn.silu(first_out).astype(jnp.bfloat16)
    first_full = channel_gather(first_act)[:, :, :, 0, :]
    second = conv_forward(first_full, spatial_full, masks)[:, :, :, None, :]
    second_norm, second_inv, second_out = normalize(
        second, block_scale[1:2], block_shift[1:2], count
    )
    second_act = jax.nn.silu(second_out).astype(jnp.bfloat16)
    second_full = channel_gather(second_act)[:, :, :, 0, :]
    third = jnp.einsum(
        "nhwc,co->nhwo", second_full, expand_full, preferred_element_type=jnp.float32
    )[:, :, :, None, :]
    third_norm, third_inv, third_out = normalize(
        third, output_scale[None], output_shift[None], count
    )
    summed = third_out[:, :, :, 0, :] + inputs.astype(jnp.float32)
    block_out = jax.nn.silu(summed).astype(jnp.bfloat16)
    heads_flat = heads_full.reshape(heads_full.shape[0], heads_full.shape[1], -1)
    head_partial = conv_forward(block_out, heads_flat, masks)
    head_pre = channel_sum(
        head_partial.reshape(head_partial.shape[:3] + (heads_full.shape[2], heads_full.shape[3]))
    )
    head_norm, head_inv, head_out = normalize(head_pre, head_scale, head_shift, count)
    head_act = jax.nn.silu(head_out).astype(jnp.bfloat16)
    head_full = channel_gather(head_act)
    head_width = head_full.shape[4]
    gate_pre = [0.0, 0.0]
    message = [0.0, 0.0]
    for number, (vertical, lateral) in enumerate(OFFSETS):
        moved = shifted(head_full, vertical, lateral) * masks[number][:, :, :, None, None].astype(
            jnp.bfloat16
        )
        for stream in range(2):
            weights_here = distil_full[stream, number]
            first_source = SOURCE_START[stream]
            sources = moved[:, :, :, first_source : first_source + 3].reshape(
                moved.shape[:3] + (3 * head_width,)
            )
            gate_pre[stream] = gate_pre[stream] + jnp.einsum(
                "nhwc,co->nhwo",
                moved[:, :, :, OWN_HEAD[stream]],
                weights_here[0],
                preferred_element_type=jnp.float32,
            )
            message[stream] = message[stream] + jnp.einsum(
                "nhwc,co->nhwo",
                sources,
                weights_here[1:].reshape(3 * head_width, -1),
                preferred_element_type=jnp.float32,
            )
    cotangents = (depth_cot.astype(jnp.float32), segment_cot.astype(jnp.float32))
    outputs, message_grads, gate_grads = ([], [], [])
    for stream in range(2):
        gate_value = jax.nn.sigmoid(gate_pre[stream] + gate_bias[stream])
        own_feature = head_act[:, :, :, OWN_HEAD[stream]].astype(jnp.float32)
        outputs.append((own_feature + gate_value * message[stream]).astype(jnp.bfloat16))
        message_grads.append((cotangents[stream] * gate_value).astype(jnp.bfloat16))
        gate_grads.append(
            (cotangents[stream] * message[stream] * gate_value * (1.0 - gate_value)).astype(
                jnp.bfloat16
            )
        )
    spread_grad = 0.0
    distil_parts = [[], []]
    for number, (vertical, lateral) in enumerate(OFFSETS):
        tap_mask = masks[number][:, :, :, None, None]
        moved = shifted(head_full, vertical, lateral) * tap_mask.astype(jnp.bfloat16)
        tap_grad = jnp.zeros(head_full.shape, jnp.float32)
        for stream in range(2):
            weights_here = distil_full[stream, number]
            first_source = SOURCE_START[stream]
            sources = moved[:, :, :, first_source : first_source + 3].reshape(
                moved.shape[:3] + (3 * head_width,)
            )
            own_grad = jnp.einsum(
                "nhwo,co->nhwc",
                gate_grads[stream],
                weights_here[0],
                preferred_element_type=jnp.float32,
            )
            source_grad = jnp.einsum(
                "nhwo,co->nhwc",
                message_grads[stream],
                weights_here[1:].reshape(3 * head_width, -1),
                preferred_element_type=jnp.float32,
            )
            tap_grad = tap_grad.at[:, :, :, OWN_HEAD[stream]].add(own_grad)
            tap_grad = tap_grad.at[:, :, :, first_source : first_source + 3].add(
                source_grad.reshape(source_grad.shape[:3] + (3, head_width))
            )
            gate_weight_grad = jnp.einsum(
                "nhwc,nhwo->co",
                moved[:, :, :, OWN_HEAD[stream]],
                gate_grads[stream],
                preferred_element_type=jnp.float32,
            )
            source_weight_grad = jnp.einsum(
                "nhwc,nhwo->co", sources, message_grads[stream], preferred_element_type=jnp.float32
            )
            distil_parts[stream].append(
                jnp.concatenate(
                    [gate_weight_grad[None], source_weight_grad.reshape(3, head_width, -1)], axis=0
                )
            )
        spread_grad = spread_grad + shifted(tap_grad * tap_mask, -vertical, -lateral)
    distil_grad = jnp.stack([jnp.stack(distil_parts[0]), jnp.stack(distil_parts[1])])
    head_grad = channel_sum(spread_grad)
    head_grad = (
        head_grad.at[:, :, :, OWN_HEAD[0]]
        .add(cotangents[0])
        .at[:, :, :, OWN_HEAD[1]]
        .add(cotangents[1])
    )
    head_grad = head_grad * silu_slope(head_out)
    gate_sums = jnp.stack(
        [pixel_sum(gate_grads[0].astype(jnp.float32)), pixel_sum(gate_grads[1].astype(jnp.float32))]
    )
    shift_sums, scale_sums = grad_sums(
        jnp.concatenate([pixel_sum(head_grad), gate_sums], axis=0), pixel_sum(head_grad * head_norm)
    )
    head_pre_grad = normalize_back(
        head_grad, head_norm, head_inv, head_scale, shift_sums[:4], scale_sums, count
    ).astype(jnp.bfloat16)
    head_pre_full = channel_gather(head_pre_grad)
    head_flat_grad = head_pre_full.reshape(head_pre_full.shape[:3] + (-1,))
    block_grad = conv_input_grad(head_flat_grad, heads_flat, masks)
    heads_grad = conv_weight_grad(block_out, head_flat_grad, masks).reshape(heads_full.shape)
    summed_grad = block_grad * silu_slope(summed)
    third_grad = summed_grad[:, :, :, None, :]
    third_shift, third_scale = grad_sums(pixel_sum(third_grad), pixel_sum(third_grad * third_norm))
    third_pre = normalize_back(
        third_grad, third_norm, third_inv, output_scale[None], third_shift, third_scale, count
    ).astype(jnp.bfloat16)[:, :, :, 0, :]
    expand_grad = jnp.einsum(
        "nhwc,nhwo->co", second_full, third_pre, preferred_element_type=jnp.float32
    )
    second_grad = channel_sum(
        jnp.einsum("nhwo,co->nhwc", third_pre, expand_full, preferred_element_type=jnp.float32)[
            :, :, :, None, :
        ]
    )
    second_grad = second_grad * silu_slope(second_out)
    second_shift, second_scale = grad_sums(
        pixel_sum(second_grad), pixel_sum(second_grad * second_norm)
    )
    second_pre = normalize_back(
        second_grad, second_norm, second_inv, block_scale[1:2], second_shift, second_scale, count
    ).astype(jnp.bfloat16)[:, :, :, 0, :]
    spatial_grad = conv_weight_grad(first_full, second_pre, masks)
    first_grad = channel_sum(conv_input_grad(second_pre, spatial_full, masks)[:, :, :, None, :])
    first_grad = first_grad * silu_slope(first_out)
    first_shift, first_scale = grad_sums(pixel_sum(first_grad), pixel_sum(first_grad * first_norm))
    first_pre = normalize_back(
        first_grad, first_norm, first_inv, block_scale[0:1], first_shift, first_scale, count
    ).astype(jnp.bfloat16)
    first_pre_full = channel_gather(first_pre)[:, :, :, 0, :]
    reduce_grad = jnp.einsum(
        "nhwc,nhwo->co", inputs, first_pre_full, preferred_element_type=jnp.float32
    )
    input_grad = summed_grad + jnp.einsum(
        "nhwo,co->nhwc", first_pre_full, reduce_full, preferred_element_type=jnp.float32
    )
    weight_grads = (reduce_grad, spatial_grad, expand_grad, heads_grad, distil_grad)
    small_grads = (
        jnp.concatenate([first_scale, second_scale], axis=0),
        jnp.concatenate([first_shift, second_shift], axis=0),
        scale_sums,
        shift_sums[:4],
        shift_sums[4:],
        third_scale[0],
        third_shift[0],
    )
    return (outputs[0], outputs[1], input_grad, weight_grads, small_grads)


def gathered_local(
    features,
    image_ids,
    reduce_weight,
    spatial_weight,
    expand_weight,
    head_weights,
    distil_weights,
    block_scale,
    block_shift,
    head_scale,
    head_shift,
    gate_bias,
    output_scale,
    output_shift,
    depth_cotangent,
    segment_cotangent,
):
    batch_count = lax.axis_size("batch")
    small = (
        block_scale,
        block_shift,
        head_scale,
        head_shift,
        gate_bias,
        output_scale,
        output_shift,
    )
    depth_list, segment_list, input_list = ([], [], [])
    weight_total = None
    small_total = None
    for micro_index in range(features.shape[0]):
        gathered = fetch_weights(
            reduce_weight, spatial_weight, expand_weight, head_weights, distil_weights
        )
        canvas_pick = slice(micro_index, micro_index + 1)
        depth_out, segment_out, input_grad, weight_grads, small_grads = micro_step(
            features[canvas_pick],
            image_ids[canvas_pick],
            depth_cotangent[canvas_pick],
            segment_cotangent[canvas_pick],
            gathered,
            small,
            batch_count,
        )
        weight_grads = scatter_weights(weight_grads)
        weight_total = (
            weight_grads
            if weight_total is None
            else jax.tree.map(jnp.add, weight_total, weight_grads)
        )
        small_total = (
            small_grads if small_total is None else jax.tree.map(jnp.add, small_total, small_grads)
        )
        depth_list.append(depth_out)
        segment_list.append(segment_out)
        input_list.append(input_grad)
    reduce_grad, spatial_grad, expand_grad, heads_grad, distil_grad = weight_total
    scale_mid, shift_mid, scale_heads, shift_heads, bias_gates, scale_out, shift_out = small_total
    return (
        jnp.concatenate(depth_list, axis=0),
        jnp.concatenate(segment_list, axis=0),
        jnp.concatenate(input_list, axis=0),
        reduce_grad,
        spatial_grad,
        expand_grad,
        heads_grad,
        distil_grad,
        scale_mid,
        shift_mid,
        scale_heads,
        shift_heads,
        bias_gates,
        scale_out,
        shift_out,
    )


def canvas_sum(values):
    return jnp.sum(values, axis=(1, 2))


def spread(values):
    return values[:, None, None, :]


def normalize_each(values, scale, shift, count):
    total, squares = lax.psum((canvas_sum(values), canvas_sum(values * values)), "batch")
    center = total / count
    inverse = lax.rsqrt(squares / count - center * center + EPSILON)
    normed = (values - spread(center)) * spread(inverse)
    return (normed, inverse, normed * scale + shift)


def normalize_each_back(grads, normed, inverse, scale, count):
    shift_sum, scale_sum = lax.psum((canvas_sum(grads), canvas_sum(grads * normed)), "batch")
    back = scale * spread(inverse) * (grads - (spread(shift_sum) + normed * spread(scale_sum)) / count)
    return (back.astype(jnp.bfloat16), shift_sum, scale_sum)


def sum_chan(values):
    return lax.psum_scatter(
        values.astype(jnp.bfloat16), "chan", scatter_dimension=3, tiled=True
    ).astype(jnp.float32)


def gather_chan(values):
    return lax.all_gather(values, "chan", axis=3, tiled=True)


def sum_batch(values, axis):
    return lax.psum_scatter(
        values.astype(jnp.bfloat16), "batch", scatter_dimension=axis, tiled=True
    ).astype(jnp.float32)


def distil_matrix(weights):
    taps = weights.shape[1]
    width = weights.shape[3]
    columns = []
    for stream in range(2):
        for part in range(2):
            rows = []
            for head in range(4):
                source = head - SOURCE_START[stream]
                if part == 0 and head == OWN_HEAD[stream]:
                    rows.append(weights[stream, :, 0])
                elif part == 1 and 0 <= source < 3:
                    rows.append(weights[stream, :, 1 + source])
                else:
                    rows.append(jnp.zeros((taps, width, weights.shape[4]), weights.dtype))
            columns.append(jnp.concatenate(rows, axis=1))
    return jnp.concatenate(columns, axis=2)


MESH = pl.DeviceIdType.MESH
PIXELS = 256
PAD = 32
LANES = 128


def whereabouts():
    place, lane = lax.axis_index("batch"), lax.axis_index("chan")
    return place, lane, place // 2, place % 2, lane // 2, lane % 2


def along(depth, step):
    return 2 * ((depth // 2 + step // 2) % 2) + (depth % 2 + step % 2) % 2


def push(source, target, send_sem, recv_sem, place, lane):
    return pltpu.make_async_remote_copy(
        src_ref=source,
        dst_ref=target,
        send_sem=send_sem,
        recv_sem=recv_sem,
        device_id=(place, lane),
        device_id_type=MESH,
    )


def greet(peers):
    barrier = pltpu.get_barrier_semaphore()
    for place, lane in peers:
        pl.semaphore_signal(barrier, inc=1, device_id=(place, lane), device_id_type=MESH)
    pl.semaphore_wait(barrier, len(peers))


def batch_peers():
    place, lane, depth, side, _, _ = whereabouts()
    peers = [(along(depth, step) * 2 + side, lane) for step in range(1, 4)]
    return peers + [(along(depth, step) * 2 + 1 - side, lane) for step in range(4)]


def link_peers():
    place, lane, depth, side, _, _ = whereabouts()
    return [(along(depth, step) * 2 + side, lane) for step in range(1, 4)] + [
        (depth * 2 + 1 - side, lane)
    ]


def chan_peers():
    place, lane, _, _, _, _ = whereabouts()
    return [(place, (lane + step) % 4) for step in range(1, 4)]


def clear_edges(turned):
    edge = jnp.zeros((3, PAD, turned.shape[2]), turned.dtype)
    turned[:, 0:PAD] = edge
    turned[:, PAD + PIXELS :] = edge


def fill_columns(value, mask, turned, columns, row):
    width = value.shape[1]
    wide = value.astype(jnp.float32)
    inner = slice(PAD, PAD + PIXELS)
    turned[0, inner] = pltpu.roll(wide, 1, 0).astype(jnp.bfloat16)
    turned[1, inner] = value
    turned[2, inner] = pltpu.roll(wide, PIXELS - 1, 0).astype(jnp.bfloat16)
    for number, (vertical, lateral) in enumerate(OFFSETS):
        start = PAD + 32 * vertical
        columns[row : row + PIXELS, number * width : (number + 1) * width] = (
            turned[lateral + 1, start : start + PIXELS] * mask[:, number : number + 1]
        )


def own_block(source, everything, recv_sem, z_sem, x_sem):
    place, lane, depth, side, _, _ = whereabouts()
    mine = everything.at[place]
    for step in range(1, 4):
        push(
            mine, mine, z_sem.at[step - 1], recv_sem.at[place], along(depth, step) * 2 + side, lane
        ).start()
    push(mine, mine, x_sem.at[0], recv_sem.at[place], depth * 2 + 1 - side, lane).start()


def next_block(step, everything, recv_sem, z_sem, x_sem):
    place, lane, depth, side, _, _ = whereabouts()
    far = step // 2
    block = along(depth, far) * 2 + (side + step % 2) % 2
    here = everything.at[block]

    @pl.when(step > 0)
    def _():
        push(here, here, z_sem.at[0], recv_sem.at[block], place, lane).wait_recv()

    @pl.when((step > 0) & (step % 2 == 0))
    def _():
        push(here, here, x_sem.at[far], recv_sem.at[block], depth * 2 + 1 - side, lane).start()

    return block


def sent_blocks(everything, recv_sem, z_sem, x_sem):
    place, lane, depth, side, _, _ = whereabouts()
    mine = everything.at[place]
    for step in range(3):
        push(mine, mine, z_sem.at[step], recv_sem.at[place], place, lane).wait_send()
    for step in range(4):
        push(mine, mine, x_sem.at[step], recv_sem.at[place], place, lane).wait_send()


def send_pieces(part, block, stage, got, stage_sem, got_sem):
    place, lane, _, _, _, _ = whereabouts()
    for micro in range(2):
        for half in range(2):
            piece = part[micro * PIXELS : (micro + 1) * PIXELS, half * LANES : (half + 1) * LANES]
            target = half * 2 + micro

            @pl.when(target == lane)
            def _():
                got[lane, block] = piece

            @pl.when(target != lane)
            def _():
                stage[target, block] = piece
                push(
                    stage.at[target, block],
                    got.at[lane, block],
                    stage_sem.at[target, block],
                    got_sem.at[lane, block],
                    place,
                    target,
                ).start()


def await_pieces(stage, got, stage_sem, got_sem):
    place, lane, _, _, _, _ = whereabouts()

    def body(block, _):
        for step in range(1, 4):
            other = (lane + step) % 4
            push(
                stage.at[other, block],
                got.at[other, block],
                stage_sem.at[other, block],
                got_sem.at[other, block],
                place,
                lane,
            ).wait()
        return 0

    lax.fori_loop(0, 8, body, 0)


CHUNKS = 4


def spread_chunk(chunk, values, out_sem, in_sem):
    place, lane, _, _, upper, core = whereabouts()
    here = values.at[upper, core, pl.ds(2 * chunk, 2)]
    push(
        here, here, out_sem.at[0, chunk], in_sem.at[upper, core, chunk], place, upper * 2 + 1 - core
    ).start()
    push(
        here, here, out_sem.at[1, chunk], in_sem.at[upper, core, chunk], place, 2 - 2 * upper + core
    ).start()


def finish_chunks(values, out_sem, in_sem):
    place, lane, _, _, upper, core = whereabouts()

    def relay(chunk, _):
        here = values.at[1 - upper, core, pl.ds(2 * chunk, 2)]
        copy = push(
            here,
            here,
            out_sem.at[2, chunk],
            in_sem.at[1 - upper, core, chunk],
            place,
            upper * 2 + 1 - core,
        )
        copy.wait_recv()
        copy.start()
        return 0

    lax.fori_loop(0, CHUNKS, relay, 0)

    def close(chunk, _):
        for half in range(2):
            here = values.at[half, 1 - core, pl.ds(2 * chunk, 2)]
            push(
                here, here, out_sem.at[0, chunk], in_sem.at[half, 1 - core, chunk], place, lane
            ).wait_recv()
        here = values.at[upper, core, pl.ds(2 * chunk, 2)]
        for path in range(3):
            push(
                here, here, out_sem.at[path, chunk], in_sem.at[upper, core, chunk], place, lane
            ).wait_send()
        return 0

    lax.fori_loop(0, CHUNKS, close, 0)


def heads_kernel(
    count,
    block_ref,
    weight_ref,
    mask_ref,
    scale_ref,
    shift_ref,
    all_ref,
    act_ref,
    norm_ref,
    inverse_ref,
    turned,
    columns,
    stage,
    got,
    recv_sem,
    z_sem,
    x_sem,
    stage_sem,
    got_sem,
    out_sem,
    in_sem,
):
    place, lane, depth, side, upper, core = whereabouts()
    greet(link_peers() + chan_peers())
    all_ref[place] = block_ref[...]
    own_block(block_ref, all_ref, recv_sem, z_sem, x_sem)
    clear_edges(turned)

    def body(step, _):
        block = next_block(step, all_ref, recv_sem, z_sem, x_sem)
        for micro in range(2):
            fill_columns(
                all_ref[block, micro], mask_ref[block, micro], turned, columns, micro * PIXELS
            )
        part = jnp.dot(columns[...], weight_ref[...], preferred_element_type=jnp.float32)
        send_pieces(part.astype(jnp.bfloat16), block, stage, got, stage_sem, got_sem)
        return 0

    lax.fori_loop(0, 8, body, 0)
    await_pieces(stage, got, stage_sem, got_sem)

    def collect(block, sums):
        value = got[0, block].astype(jnp.float32)
        for other in range(1, 4):
            value = value + got[other, block].astype(jnp.float32)
        norm_ref[block] = value
        return (
            sums[0] + jnp.sum(value, axis=0, keepdims=True),
            sums[1] + jnp.sum(value * value, axis=0, keepdims=True),
        )

    zero = jnp.zeros((1, LANES), jnp.float32)
    total, squares = lax.fori_loop(0, 8, collect, (zero, zero))
    center = total / count
    inverse = lax.rsqrt(squares / count - center * center + EPSILON)
    inverse_ref[...] = inverse

    def activate(chunk, _):
        for item in range(2):
            block = 2 * chunk + item
            normed = (norm_ref[block] - center) * inverse
            norm_ref[block] = normed
            out = normed * scale_ref[...] + shift_ref[...]
            act_ref[upper, core, block] = (out * jax.nn.sigmoid(out)).astype(jnp.bfloat16)
        spread_chunk(chunk, act_ref, out_sem, in_sem)
        return 0

    lax.fori_loop(0, CHUNKS, activate, 0)
    finish_chunks(act_ref, out_sem, in_sem)
    sent_blocks(all_ref, recv_sem, z_sem, x_sem)


def vmem(count):
    return [pl.BlockSpec(memory_space=pltpu.VMEM)] * count


def chan_scratch():
    return [
        pltpu.VMEM((4, 8, PIXELS, LANES), jnp.bfloat16),
        pltpu.VMEM((4, 8, PIXELS, LANES), jnp.bfloat16),
    ]


def gather_sems():
    return [
        pltpu.SemaphoreType.DMA((8,)),
        pltpu.SemaphoreType.DMA((3,)),
        pltpu.SemaphoreType.DMA((4,)),
    ]


def chan_sems():
    return [
        pltpu.SemaphoreType.DMA((4, 8)),
        pltpu.SemaphoreType.DMA((4, 8)),
        pltpu.SemaphoreType.DMA((3, CHUNKS)),
        pltpu.SemaphoreType.DMA((2, 2, CHUNKS)),
    ]


def kernel_params(number):
    return pltpu.CompilerParams(
        collective_id=number, has_side_effects=True, vmem_limit_bytes=60 * 2**20
    )


def run_heads(count, block_out, weight, masks, scale, shift):
    return pl.pallas_call(
        functools.partial(heads_kernel, count),
        name="heads",
        out_shape=(
            jax.ShapeDtypeStruct((8, 2, PIXELS, 512), jnp.bfloat16),
            jax.ShapeDtypeStruct((2, 2, 8, PIXELS, LANES), jnp.bfloat16),
            jax.ShapeDtypeStruct((8, PIXELS, LANES), jnp.float32),
            jax.ShapeDtypeStruct((1, LANES), jnp.float32),
        ),
        in_specs=vmem(5),
        out_specs=tuple(vmem(4)),
        scratch_shapes=[
            pltpu.VMEM((3, 2 * PAD + PIXELS, 512), jnp.bfloat16),
            pltpu.VMEM((2 * PIXELS, 9 * 512), jnp.bfloat16),
        ]
        + chan_scratch()
        + gather_sems()
        + chan_sems(),
        compiler_params=kernel_params(1),
    )(block_out, weight, masks, scale, shift)


def reduce_far(step, part, send_buf, recv_buf, send_sem, recv_sem):
    place, lane, depth, side, _, _ = whereabouts()
    far = 3 - step
    send_buf[far] = part.astype(jnp.bfloat16)
    push(
        send_buf.at[far],
        recv_buf.at[far],
        send_sem.at[far],
        recv_sem.at[far],
        depth * 2 + 1 - side,
        lane,
    ).start()


def reduce_near(step, part, keep, side_buf, side_sem, send_buf, recv_buf, send_sem, recv_sem):
    place, lane, depth, side, _, _ = whereabouts()
    far = 3 - step
    push(
        side_buf.at[far], side_buf.at[far], side_sem.at[far], side_sem.at[far], place, lane
    ).wait_recv()
    total = part + side_buf[far].astype(jnp.float32)

    @pl.when(far == 0)
    def _():
        keep[...] = total

    @pl.when(far > 0)
    def _():
        send_buf[far] = total.astype(jnp.bfloat16)
        push(
            send_buf.at[far],
            recv_buf.at[far],
            send_sem.at[far],
            recv_sem.at[far],
            along(depth, far) * 2 + side,
            lane,
        ).start()


def reduce_close(keep, far_buf, far_sem, far_recv, send_buf, recv_buf, send_sem, recv_sem):
    place, lane, _, _, _, _ = whereabouts()
    for far in range(4):
        push(
            far_buf.at[far], far_buf.at[far], far_sem.at[far], far_recv.at[far], place, lane
        ).wait_send()
    for far in range(1, 4):
        push(
            send_buf.at[far], recv_buf.at[far], send_sem.at[far], recv_sem.at[far], place, lane
        ).wait()
        keep[...] = keep[...] + recv_buf[far].astype(jnp.float32)


def reduce_scratch():
    return [
        pltpu.VMEM((2 * PIXELS, 512), jnp.float32),
        pltpu.VMEM((4, 2 * PIXELS, 512), jnp.bfloat16),
        pltpu.VMEM((4, 2 * PIXELS, 512), jnp.bfloat16),
        pltpu.VMEM((4, 2 * PIXELS, 512), jnp.bfloat16),
        pltpu.VMEM((4, 2 * PIXELS, 512), jnp.bfloat16),
        pltpu.SemaphoreType.DMA((4,)),
        pltpu.SemaphoreType.DMA((4,)),
        pltpu.SemaphoreType.DMA((4,)),
        pltpu.SemaphoreType.DMA((4,)),
    ]


def far_block(step):
    _, _, depth, side, _, _ = whereabouts()
    return along(depth, 3 - step) * 2 + 1 - side


def near_block(step):
    _, _, depth, side, _, _ = whereabouts()
    return along(depth, 3 - step) * 2 + side


def lane_index():
    return lax.broadcasted_iota(jnp.int32, (PIXELS, LANES), 1)


def distil_kernel(
    count,
    act_ref,
    mixed_ref,
    back_ref,
    mask_ref,
    cot_ref,
    packed_ref,
    bias_ref,
    norm_ref,
    inverse_ref,
    scale_ref,
    shift_ref,
    stream_ref,
    grad_ref,
    gate_ref,
    back_act_ref,
    sums_ref,
    turned,
    columns,
    turned_wide,
    columns_wide,
    grads_all,
    own_stage,
    own_got,
    cot_all,
    keep,
    far_send,
    far_got,
    near_send,
    near_got,
    far_sem,
    far_recv,
    near_sem,
    near_recv,
    stage,
    got,
    own_sem,
    own_recv,
    cot_sem,
    cot_recv,
    recv_sem,
    z_sem,
    x_sem,
    stage_sem,
    got_sem,
    out_sem,
    in_sem,
):
    place, lane, depth, side, upper, core = whereabouts()
    half_width = LANES // 2
    greet(batch_peers() + chan_peers())
    low = lane_index() < half_width
    source = place // 2 == lane

    for parity in range(2):
        target = 2 * lane + parity

        @pl.when(target == place)
        def _():
            cot_all[place] = packed_ref[parity]

        @pl.when(target != place)
        def _():
            push(
                packed_ref.at[parity],
                cot_all.at[place],
                cot_sem.at[parity],
                cot_recv.at[place],
                target,
                lane,
            ).start()

    @pl.when(source)
    def _():
        def pack(step, _):
            block = along(depth, step // 2) * 2 + (side + step % 2) % 2
            for micro in range(2):
                own_stage[block, micro] = jnp.where(
                    low, act_ref[0, micro, block], act_ref[1, micro, block]
                )

            @pl.when(block == place)
            def _():
                own_got[place % 2] = own_stage[block]

            @pl.when(block != place)
            def _():
                push(
                    own_stage.at[block],
                    own_got.at[place % 2],
                    own_sem.at[block],
                    own_recv.at[place % 2],
                    block,
                    lane,
                ).start()

            return 0

        lax.fori_loop(0, 8, pack, 0)

    clear_edges(turned)
    clear_edges(turned_wide)
    grad_ref[...] = jnp.zeros_like(grad_ref)

    def partial(block):
        for micro in range(2):
            value = jnp.concatenate([act_ref[0, micro, block], act_ref[1, micro, block]], axis=1)
            fill_columns(value, mask_ref[block, micro], turned, columns, micro * PIXELS)
        return jnp.dot(columns[...], mixed_ref[...], preferred_element_type=jnp.float32)

    def far_step(step, _):
        reduce_far(step, partial(far_block(step)), far_send, far_got, far_sem, far_recv)
        return 0

    lax.fori_loop(0, 4, far_step, 0)

    def near_step(step, _):
        reduce_near(
            step,
            partial(near_block(step)),
            keep,
            far_got,
            far_recv,
            near_send,
            near_got,
            near_sem,
            near_recv,
        )
        return 0

    lax.fori_loop(0, 4, near_step, 0)
    for parity in range(2):
        owner = 2 * lane + parity

        @pl.when(owner != place)
        def _():
            push(
                own_got.at[parity],
                own_got.at[parity],
                own_sem.at[0],
                own_recv.at[parity],
                place,
                lane,
            ).wait_recv()

    reduce_close(
        keep, far_send, far_sem, far_recv, near_send, near_got, near_sem, near_recv
    )
    for stream in range(2):
        bias_sum = jnp.zeros((1, LANES), jnp.float32)
        for micro in range(2):
            rows = slice(micro * PIXELS, (micro + 1) * PIXELS)
            first = own_got[0, micro].astype(jnp.float32)
            second = own_got[1, micro].astype(jnp.float32)
            if stream == 0:
                second = pltpu.roll(second, half_width, 1)
            else:
                first = pltpu.roll(first, half_width, 1)
            own = jnp.where(low, first, second)
            column = 2 * stream * LANES
            gate = jax.nn.sigmoid(
                keep[rows, column : column + LANES] + bias_ref[stream : stream + 1]
            )
            message = keep[rows, column + LANES : column + 2 * LANES]
            cot = cot_ref[stream, micro].astype(jnp.float32)
            stream_ref[stream, micro] = (own + gate * message).astype(jnp.bfloat16)
            gate_grad = (cot * message * gate * (1.0 - gate)).astype(jnp.bfloat16)
            bias_sum = bias_sum + jnp.sum(gate_grad.astype(jnp.float32), axis=0, keepdims=True)
            grads_all[place, micro, :, column : column + LANES] = gate_grad
            grads_all[place, micro, :, column + LANES : column + 2 * LANES] = (cot * gate).astype(
                jnp.bfloat16
            )
        gate_ref[stream : stream + 1] = bias_sum
    own_block(None, grads_all, recv_sem, z_sem, x_sem)

    @pl.when(source)
    def _():
        for step in range(1, 8):
            other = (place + step) % 8
            push(
                cot_all.at[other],
                cot_all.at[other],
                cot_sem.at[0],
                cot_recv.at[other],
                place,
                lane,
            ).wait_recv()

    width = 2 * half_width // 2

    def body(step, _):
        block = next_block(step, grads_all, recv_sem, z_sem, x_sem)
        for micro in range(2):
            fill_columns(
                grads_all[block, micro],
                mask_ref[block, micro],
                turned_wide,
                columns_wide,
                micro * PIXELS,
            )
        part = jnp.dot(columns_wide[...], back_ref[...], preferred_element_type=jnp.float32)
        pieces = []
        for micro in range(2):
            extra = cot_all[block, micro].astype(jnp.float32)
            rows = part[micro * PIXELS : (micro + 1) * PIXELS]
            pieces.append(
                jnp.concatenate(
                    [
                        rows[:, :LANES] + jnp.where(low & source, extra, 0.0),
                        rows[:, LANES:] + jnp.where(low | ~source, 0.0, extra),
                    ],
                    axis=1,
                )
            )
        part = jnp.concatenate(pieces, axis=0).astype(jnp.bfloat16)
        send_pieces(part, block, stage, got, stage_sem, got_sem)
        value = jnp.concatenate(
            [
                jnp.concatenate([act_ref[half, micro, block] for half in range(2)], axis=1)
                for micro in range(2)
            ],
            axis=0,
        ).T
        for number in range(9):
            product = jnp.dot(
                value,
                columns_wide[:, number * 512 : (number + 1) * 512],
                preferred_element_type=jnp.float32,
            )
            for stream in range(2):
                for part_index in range(4):
                    head = (
                        OWN_HEAD[stream]
                        if part_index == 0
                        else SOURCE_START[stream] + part_index - 1
                    )
                    column = (2 * stream + (part_index > 0)) * LANES
                    grad_ref[stream, 8 - number, part_index] += product[
                        head * width : (head + 1) * width, column : column + LANES
                    ]
        return 0

    lax.fori_loop(0, 8, body, 0)
    await_pieces(stage, got, stage_sem, got_sem)
    normalize_gradient(
        count,
        got,
        norm_ref,
        inverse_ref,
        scale_ref,
        shift_ref,
        back_act_ref,
        sums_ref,
        keep,
        out_sem,
        in_sem,
    )
    sent_blocks(grads_all, recv_sem, z_sem, x_sem)
    for parity in range(2):
        target = 2 * lane + parity

        @pl.when(target != place)
        def _():
            push(
                packed_ref.at[parity],
                cot_all.at[place],
                cot_sem.at[parity],
                cot_recv.at[place],
                target,
                lane,
            ).wait_send()

    @pl.when(source)
    def _():
        for step in range(1, 8):
            block = (place + step) % 8
            push(
                own_stage.at[block],
                own_got.at[0],
                own_sem.at[block],
                own_recv.at[0],
                block,
                lane,
            ).wait_send()


def normalize_gradient(
    count,
    got,
    norm_ref,
    inverse_ref,
    scale_ref,
    shift_ref,
    back_act_ref,
    sums_ref,
    keep,
    out_sem,
    in_sem,
):
    place, lane, depth, side, upper, core = whereabouts()

    def collect(block, sums):
        value = got[0, block].astype(jnp.float32)
        for other in range(1, 4):
            value = value + got[other, block].astype(jnp.float32)
        normed = norm_ref[block]
        value = value * silu_slope(normed * scale_ref[...] + shift_ref[...])
        keep[pl.ds(block // 4 * PIXELS, PIXELS), pl.ds(block % 4 * LANES, LANES)] = value
        return (
            sums[0] + jnp.sum(value, axis=0, keepdims=True),
            sums[1] + jnp.sum(value * normed, axis=0, keepdims=True),
        )

    zero = jnp.zeros((1, LANES), jnp.float32)
    shift_sum, scale_sum = lax.fori_loop(0, 8, collect, (zero, zero))
    sums_ref[0:1] = scale_sum
    sums_ref[1:2] = shift_sum
    factor = scale_ref[...] * inverse_ref[...]

    def activate(chunk, _):
        for item in range(2):
            block = 2 * chunk + item
            value = keep[pl.ds(block // 4 * PIXELS, PIXELS), pl.ds(block % 4 * LANES, LANES)]
            back_act_ref[upper, core, block] = (
                factor * (value - (shift_sum + norm_ref[block] * scale_sum) / count)
            ).astype(jnp.bfloat16)
        spread_chunk(chunk, back_act_ref, out_sem, in_sem)
        return 0

    lax.fori_loop(0, CHUNKS, activate, 0)
    finish_chunks(back_act_ref, out_sem, in_sem)


def run_distil(
    count, acts, mixed, mixed_back, masks, cots, packed, bias, norm, inverse, scale, shift
):
    return pl.pallas_call(
        functools.partial(distil_kernel, count),
        name="distil",
        out_shape=(
            jax.ShapeDtypeStruct((2, 2, PIXELS, LANES), jnp.bfloat16),
            jax.ShapeDtypeStruct((2, 9, 4, 64, LANES), jnp.float32),
            jax.ShapeDtypeStruct((2, LANES), jnp.float32),
            jax.ShapeDtypeStruct((2, 2, 8, PIXELS, LANES), jnp.bfloat16),
            jax.ShapeDtypeStruct((2, LANES), jnp.float32),
        ),
        in_specs=vmem(11),
        out_specs=tuple(vmem(5)),
        scratch_shapes=[
            pltpu.VMEM((3, 2 * PAD + PIXELS, 256), jnp.bfloat16),
            pltpu.VMEM((2 * PIXELS, 9 * 256), jnp.bfloat16),
            pltpu.VMEM((3, 2 * PAD + PIXELS, 512), jnp.bfloat16),
            pltpu.VMEM((2 * PIXELS, 9 * 512), jnp.bfloat16),
            pltpu.VMEM((8, 2, PIXELS, 512), jnp.bfloat16),
            pltpu.VMEM((8, 2, PIXELS, LANES), jnp.bfloat16),
            pltpu.VMEM((2, 2, PIXELS, LANES), jnp.bfloat16),
            pltpu.VMEM((8, 2, PIXELS, LANES), jnp.bfloat16),
        ]
        + reduce_scratch()
        + chan_scratch()
        + [
            pltpu.SemaphoreType.DMA((8,)),
            pltpu.SemaphoreType.DMA((2,)),
            pltpu.SemaphoreType.DMA((2,)),
            pltpu.SemaphoreType.DMA((8,)),
        ]
        + gather_sems()
        + chan_sems(),
        compiler_params=kernel_params(2),
    )(acts, mixed, mixed_back, masks, cots, packed, bias, norm, inverse, scale, shift)


def back_kernel(
    grads_ref,
    all_ref,
    weight_ref,
    mask_ref,
    out_ref,
    wgrad_ref,
    turned,
    columns,
    keep,
    far_send,
    far_got,
    near_send,
    near_got,
    far_sem,
    far_recv,
    near_sem,
    near_recv,
):
    greet(link_peers())
    clear_edges(turned)
    wgrad_ref[...] = jnp.zeros_like(wgrad_ref)

    def partial(block):
        for micro in range(2):
            value = jnp.concatenate([grads_ref[0, micro, block], grads_ref[1, micro, block]], axis=1)
            fill_columns(value, mask_ref[block, micro], turned, columns, micro * PIXELS)
        return jnp.dot(columns[...], weight_ref[...], preferred_element_type=jnp.float32)

    def weigh(block):
        value = jnp.concatenate([all_ref[block, micro] for micro in range(2)], axis=0).T
        for number in range(9):
            wgrad_ref[8 - number] += jnp.dot(
                value,
                columns[:, number * 256 : (number + 1) * 256],
                preferred_element_type=jnp.float32,
            )

    def far_step(step, _):
        block = far_block(step)
        reduce_far(step, partial(block), far_send, far_got, far_sem, far_recv)
        weigh(block)
        return 0

    lax.fori_loop(0, 4, far_step, 0)

    def near_step(step, _):
        block = near_block(step)
        part = partial(block)
        weigh(block)
        reduce_near(
            step, part, keep, far_got, far_recv, near_send, near_got, near_sem, near_recv
        )
        return 0

    lax.fori_loop(0, 4, near_step, 0)
    reduce_close(keep, far_send, far_sem, far_recv, near_send, near_got, near_sem, near_recv)
    out_ref[...] = keep[...]


def run_back(grads, block_all, weight, masks):
    return pl.pallas_call(
        back_kernel,
        name="back",
        out_shape=(
            jax.ShapeDtypeStruct((2 * PIXELS, 512), jnp.float32),
            jax.ShapeDtypeStruct((9, 512, 256), jnp.float32),
        ),
        in_specs=vmem(4),
        out_specs=tuple(vmem(2)),
        scratch_shapes=[
            pltpu.VMEM((3, 2 * PAD + PIXELS, 256), jnp.bfloat16),
            pltpu.VMEM((2 * PIXELS, 9 * 256), jnp.bfloat16),
        ]
        + reduce_scratch(),
        compiler_params=kernel_params(3),
    )(grads, block_all, weight, masks)


def stationary_local(
    features,
    image_ids,
    reduce_weight,
    spatial_weight,
    expand_weight,
    head_weights,
    distil_weights,
    block_scale,
    block_shift,
    head_scale,
    head_shift,
    gate_bias,
    output_scale,
    output_shift,
    depth_cotangent,
    segment_cotangent,
):
    groups = lax.axis_size("batch")
    place = lax.axis_index("batch")
    lane = lax.axis_index("chan")
    canvases, row_count, column_count = image_ids.shape
    count = float(groups * row_count * column_count)
    pixels = row_count * column_count
    width = head_weights.shape[3]
    reduce_full = lax.all_gather(reduce_weight, "batch", axis=1, tiled=True)
    spatial_full = lax.all_gather(spatial_weight, "batch", axis=1, tiled=True)
    expand_full = lax.all_gather(expand_weight, "batch", axis=0, tiled=True)
    ids_full = lax.all_gather(image_ids, "batch", axis=0, tiled=True)
    masks = tap_masks(image_ids)
    masks_full = tap_masks(ids_full)
    first = sum_chan(
        jnp.einsum("nhwc,co->nhwo", features, reduce_full, preferred_element_type=jnp.float32)
    )
    first_norm, first_inv, first_out = normalize_each(first, block_scale[0], block_shift[0], count)
    first_full = gather_chan(jax.nn.silu(first_out).astype(jnp.bfloat16))
    second = conv_forward(first_full, spatial_full, masks)
    second_norm, second_inv, second_out = normalize_each(
        second, block_scale[1], block_shift[1], count
    )
    second_full = gather_chan(jax.nn.silu(second_out).astype(jnp.bfloat16))
    third = jnp.einsum(
        "nhwc,co->nhwo", second_full, expand_full, preferred_element_type=jnp.float32
    )
    third_norm, third_inv, third_out = normalize_each(third, output_scale, output_shift, count)
    summed = third_out + features.astype(jnp.float32)
    block_out = jax.nn.silu(summed).astype(jnp.bfloat16)

    mask_columns = jnp.pad(
        masks_full.reshape(9, groups, canvases, pixels).transpose(1, 2, 3, 0),
        ((0, 0), (0, 0), (0, 0), (0, 7)),
    ).astype(jnp.bfloat16)
    half = lane // 2

    def mine(values):
        whole = lax.all_gather(values, "chan", axis=1, tiled=True)
        part = lax.dynamic_slice_in_dim(whole, place * width, width, axis=1)
        return lax.dynamic_slice_in_dim(part.reshape(2, 2 * width), half, 1, axis=0)

    my_scale, my_shift = mine(head_scale), mine(head_shift)
    heads_flat = head_weights.reshape(9, head_weights.shape[1], -1)
    block_all, head_acts, head_norm, head_inv = run_heads(
        count,
        block_out.reshape(canvases, pixels, -1),
        heads_flat.reshape(-1, heads_flat.shape[2]),
        mask_columns,
        my_scale,
        my_shift,
    )
    mixed = distil_matrix(distil_weights)
    mixed_back = mixed[::-1].transpose(0, 2, 1).reshape(-1, mixed.shape[1])
    heads_back = heads_flat[::-1].transpose(0, 2, 1).reshape(-1, heads_flat.shape[1])
    cots = jnp.stack([depth_cotangent, segment_cotangent]).reshape(2, canvases, pixels, 128)
    packed = jnp.stack(
        [
            jnp.concatenate([cots[0, :, :, :width], cots[1, :, :, :width]], axis=-1),
            jnp.concatenate([cots[0, :, :, width:], cots[1, :, :, width:]], axis=-1),
        ]
    )
    streams, distil_grad, gate_sums, head_grads, head_sums = run_distil(
        count,
        head_acts,
        mixed.reshape(-1, mixed.shape[2]),
        mixed_back,
        mask_columns,
        cots,
        packed,
        gate_bias,
        head_norm,
        head_inv,
        my_scale,
        my_shift,
    )
    outputs = streams.reshape((2,) + image_ids.shape + (128,))
    block_grad, heads_grad = run_back(head_grads, block_all, heads_back, mask_columns)
    block_grad = block_grad.reshape(features.shape)
    heads_grad = heads_grad.reshape(head_weights.shape)
    summed_grad = block_grad * silu_slope(summed)
    third_pre, third_shift, third_scale = normalize_each_back(
        summed_grad, third_norm, third_inv, output_scale, count
    )
    expand_grad = sum_batch(
        jnp.einsum("nhwc,nhwo->co", second_full, third_pre, preferred_element_type=jnp.float32), 0
    )
    second_grad = sum_chan(
        jnp.einsum("nhwo,co->nhwc", third_pre, expand_full, preferred_element_type=jnp.float32)
    ) * silu_slope(second_out)
    second_pre, second_shift, second_scale = normalize_each_back(
        second_grad, second_norm, second_inv, block_scale[1], count
    )
    spatial_grad = sum_batch(conv_weight_grad(first_full, second_pre, masks), 1)
    first_grad = sum_chan(conv_input_grad(second_pre, spatial_full, masks)) * silu_slope(first_out)
    first_pre, first_shift, first_scale = normalize_each_back(
        first_grad, first_norm, first_inv, block_scale[0], count
    )
    first_pre_full = gather_chan(first_pre)
    reduce_grad = sum_batch(
        jnp.einsum("nhwc,nhwo->co", features, first_pre_full, preferred_element_type=jnp.float32), 1
    )
    features_grad = summed_grad + jnp.einsum(
        "nhwo,co->nhwc", first_pre_full, reduce_full, preferred_element_type=jnp.float32
    )
    sums = head_sums.reshape(2, 1, 2, width)
    wide = jnp.zeros((2, 2, 2, groups * width), jnp.float32)
    sums = lax.dynamic_update_slice(wide, sums, (0, half, 0, place * width)).reshape(2, 4, -1)
    sums = lax.psum(sums, ("batch", "chan"))
    sums = lax.dynamic_slice_in_dim(sums, lane * 128, 128, axis=2)
    gate_total = lax.psum(gate_sums, "batch")
    return (
        outputs[0],
        outputs[1],
        features_grad,
        reduce_grad,
        spatial_grad,
        expand_grad,
        heads_grad,
        distil_grad,
        jnp.stack([jnp.sum(first_scale, 0), jnp.sum(second_scale, 0)]),
        jnp.stack([jnp.sum(first_shift, 0), jnp.sum(second_shift, 0)]),
        sums[0],
        sums[1],
        gate_total,
        jnp.sum(third_scale, 0),
        jnp.sum(third_shift, 0),
    )


def solution(mesh):
    local = stationary_local if dict(mesh.shape) == {"batch": 8, "chan": 4} else gathered_local
    placed = (
        P("batch", None, None, "chan"),
        P("batch", None, None),
        P("chan", "batch"),
        P(None, "batch", "chan"),
        P("batch", "chan"),
        P(None, "chan", None, "batch"),
        P(None, None, None, "batch", "chan"),
        P(None, "chan"),
        P(None, "chan"),
        P(None, "chan"),
        P(None, "chan"),
        P(None, "chan"),
        P("chan"),
        P("chan"),
        P("batch", None, None, "chan"),
        P("batch", None, None, "chan"),
    )
    return jax.shard_map(
        local,
        mesh=mesh,
        in_specs=placed,
        out_specs=(
            P("batch", None, None, "chan"),
            P("batch", None, None, "chan"),
            P("batch", None, None, "chan"),
            P("chan", "batch"),
            P(None, "batch", "chan"),
            P("batch", "chan"),
            P(None, "chan", None, "batch"),
            P(None, None, None, "batch", "chan"),
            P(None, "chan"),
            P(None, "chan"),
            P(None, "chan"),
            P(None, "chan"),
            P(None, "chan"),
            P("chan"),
            P("chan"),
        ),
        check_vma=False,
    )
```

```python
import functools

import jax
import jax.numpy as jnp
from jax import lax
from jax.experimental import pallas as pl
from jax.experimental.pallas import tpu as pltpu
from jax.sharding import PartitionSpec as P

EPSILON = 1e-05
OFFSETS = ((-1, -1), (-1, 0), (-1, 1), (0, -1), (0, 0), (0, 1), (1, -1), (1, 0), (1, 1))
OWN_HEAD = (0, 3)
SOURCE_START = (1, 0)


def silu_slope(values):
    sig = jax.nn.sigmoid(values)
    return sig * (1.0 + values * (1.0 - sig))


def shifted(values, vertical, lateral):
    row_count, column_count = (values.shape[1], values.shape[2])
    widths = [(0, 0)] * values.ndim
    widths[1] = (1, 1)
    widths[2] = (1, 1)
    padded = jnp.pad(values, widths)
    return padded[
        :, 1 + vertical : 1 + vertical + row_count, 1 + lateral : 1 + lateral + column_count
    ]


def tap_masks(image_ids):
    row_count, column_count = (image_ids.shape[1], image_ids.shape[2])
    padded = jnp.pad(image_ids, ((0, 0), (1, 1), (1, 1)), constant_values=-1)
    masks = []
    for vertical, lateral in OFFSETS:
        beside = padded[
            :, 1 + vertical : 1 + vertical + row_count, 1 + lateral : 1 + lateral + column_count
        ]
        masks.append((beside == image_ids).astype(jnp.float32))
    return jnp.stack(masks)


def conv_forward(inputs, weight, masks):
    total = 0.0
    for number, (vertical, lateral) in enumerate(OFFSETS):
        moved = shifted(inputs, vertical, lateral) * masks[number][..., None].astype(inputs.dtype)
        total = total + jnp.einsum(
            "nhwc,co->nhwo", moved, weight[number], preferred_element_type=jnp.float32
        )
    return total


def conv_input_grad(grads, weight, masks):
    total = 0.0
    for number, (vertical, lateral) in enumerate(OFFSETS):
        term = jnp.einsum(
            "nhwo,co->nhwc", grads, weight[number], preferred_element_type=jnp.float32
        )
        total = total + shifted(term * masks[number][..., None], -vertical, -lateral)
    return total


def conv_weight_grad(inputs, grads, masks):
    pieces = []
    for number, (vertical, lateral) in enumerate(OFFSETS):
        moved = shifted(inputs, vertical, lateral) * masks[number][..., None].astype(inputs.dtype)
        pieces.append(jnp.einsum("nhwc,nhwo->co", moved, grads, preferred_element_type=jnp.float32))
    return jnp.stack(pieces)


def pixel_sum(values):
    return jnp.sum(values, axis=(0, 1, 2))


def normalize(values, scale, shift, count):
    total, squares = lax.psum((pixel_sum(values), pixel_sum(values * values)), "batch")
    center = total / count
    inverse = lax.rsqrt(squares / count - center * center + EPSILON)
    normed = (values - center) * inverse
    return (normed, inverse, normed * scale + shift)


def grad_sums(first_sum, second_sum):
    return lax.psum((first_sum, second_sum), "batch")


def normalize_back(grads, normed, inverse, scale, shift_sum, scale_sum, count):
    return scale * inverse * (grads - (shift_sum + normed * scale_sum) / count)


def channel_gather(values):
    return lax.all_gather(values, "chan", axis=4, tiled=True)


def channel_sum(values):
    return lax.psum_scatter(
        values.astype(jnp.bfloat16), "chan", scatter_dimension=4, tiled=True
    ).astype(jnp.float32)


def fetch_weights(reduce_weight, spatial_weight, expand_weight, head_weights, distil_weights):
    return (
        lax.all_gather(reduce_weight, "batch", axis=1, tiled=True),
        lax.all_gather(spatial_weight, "batch", axis=1, tiled=True),
        lax.all_gather(expand_weight, "batch", axis=0, tiled=True),
        lax.all_gather(head_weights, "batch", axis=3, tiled=True),
        lax.all_gather(distil_weights, "batch", axis=3, tiled=True),
    )


def scatter_weights(grads):
    reduce_grad, spatial_grad, expand_grad, heads_grad, distil_grad = grads
    return (
        lax.psum_scatter(reduce_grad, "batch", scatter_dimension=1, tiled=True),
        lax.psum_scatter(spatial_grad, "batch", scatter_dimension=1, tiled=True),
        lax.psum_scatter(expand_grad, "batch", scatter_dimension=0, tiled=True),
        lax.psum_scatter(heads_grad, "batch", scatter_dimension=3, tiled=True),
        lax.psum_scatter(distil_grad, "batch", scatter_dimension=3, tiled=True),
    )


def micro_step(inputs, image_ids, depth_cot, segment_cot, gathered, small, batch_count):
    reduce_full, spatial_full, expand_full, heads_full, distil_full = gathered
    block_scale, block_shift, head_scale, head_shift, gate_bias, output_scale, output_shift = small
    masks = tap_masks(image_ids)
    canvases, row_count, column_count = image_ids.shape
    count = float(batch_count * canvases * row_count * column_count)
    first_partial = jnp.einsum(
        "nhwc,co->nhwo", inputs, reduce_full, preferred_element_type=jnp.float32
    )
    first = channel_sum(first_partial[:, :, :, None, :])
    first_norm, first_inv, first_out = normalize(first, block_scale[0:1], block_shift[0:1], count)
    first_act = jax.nn.silu(first_out).astype(jnp.bfloat16)
    first_full = channel_gather(first_act)[:, :, :, 0, :]
    second = conv_forward(first_full, spatial_full, masks)[:, :, :, None, :]
    second_norm, second_inv, second_out = normalize(
        second, block_scale[1:2], block_shift[1:2], count
    )
    second_act = jax.nn.silu(second_out).astype(jnp.bfloat16)
    second_full = channel_gather(second_act)[:, :, :, 0, :]
    third = jnp.einsum(
        "nhwc,co->nhwo", second_full, expand_full, preferred_element_type=jnp.float32
    )[:, :, :, None, :]
    third_norm, third_inv, third_out = normalize(
        third, output_scale[None], output_shift[None], count
    )
    summed = third_out[:, :, :, 0, :] + inputs.astype(jnp.float32)
    block_out = jax.nn.silu(summed).astype(jnp.bfloat16)
    heads_flat = heads_full.reshape(heads_full.shape[0], heads_full.shape[1], -1)
    head_partial = conv_forward(block_out, heads_flat, masks)
    head_pre = channel_sum(
        head_partial.reshape(head_partial.shape[:3] + (heads_full.shape[2], heads_full.shape[3]))
    )
    head_norm, head_inv, head_out = normalize(head_pre, head_scale, head_shift, count)
    head_act = jax.nn.silu(head_out).astype(jnp.bfloat16)
    head_full = channel_gather(head_act)
    head_width = head_full.shape[4]
    gate_pre = [0.0, 0.0]
    message = [0.0, 0.0]
    for number, (vertical, lateral) in enumerate(OFFSETS):
        moved = shifted(head_full, vertical, lateral) * masks[number][:, :, :, None, None].astype(
            jnp.bfloat16
        )
        for stream in range(2):
            weights_here = distil_full[stream, number]
            first_source = SOURCE_START[stream]
            sources = moved[:, :, :, first_source : first_source + 3].reshape(
                moved.shape[:3] + (3 * head_width,)
            )
            gate_pre[stream] = gate_pre[stream] + jnp.einsum(
                "nhwc,co->nhwo",
                moved[:, :, :, OWN_HEAD[stream]],
                weights_here[0],
                preferred_element_type=jnp.float32,
            )
            message[stream] = message[stream] + jnp.einsum(
                "nhwc,co->nhwo",
                sources,
                weights_here[1:].reshape(3 * head_width, -1),
                preferred_element_type=jnp.float32,
            )
    cotangents = (depth_cot.astype(jnp.float32), segment_cot.astype(jnp.float32))
    outputs, message_grads, gate_grads = ([], [], [])
    for stream in range(2):
        gate_value = jax.nn.sigmoid(gate_pre[stream] + gate_bias[stream])
        own_feature = head_act[:, :, :, OWN_HEAD[stream]].astype(jnp.float32)
        outputs.append((own_feature + gate_value * message[stream]).astype(jnp.bfloat16))
        message_grads.append((cotangents[stream] * gate_value).astype(jnp.bfloat16))
        gate_grads.append(
            (cotangents[stream] * message[stream] * gate_value * (1.0 - gate_value)).astype(
                jnp.bfloat16
            )
        )
    spread_grad = 0.0
    distil_parts = [[], []]
    for number, (vertical, lateral) in enumerate(OFFSETS):
        tap_mask = masks[number][:, :, :, None, None]
        moved = shifted(head_full, vertical, lateral) * tap_mask.astype(jnp.bfloat16)
        tap_grad = jnp.zeros(head_full.shape, jnp.float32)
        for stream in range(2):
            weights_here = distil_full[stream, number]
            first_source = SOURCE_START[stream]
            sources = moved[:, :, :, first_source : first_source + 3].reshape(
                moved.shape[:3] + (3 * head_width,)
            )
            own_grad = jnp.einsum(
                "nhwo,co->nhwc",
                gate_grads[stream],
                weights_here[0],
                preferred_element_type=jnp.float32,
            )
            source_grad = jnp.einsum(
                "nhwo,co->nhwc",
                message_grads[stream],
                weights_here[1:].reshape(3 * head_width, -1),
                preferred_element_type=jnp.float32,
            )
            tap_grad = tap_grad.at[:, :, :, OWN_HEAD[stream]].add(own_grad)
            tap_grad = tap_grad.at[:, :, :, first_source : first_source + 3].add(
                source_grad.reshape(source_grad.shape[:3] + (3, head_width))
            )
            gate_weight_grad = jnp.einsum(
                "nhwc,nhwo->co",
                moved[:, :, :, OWN_HEAD[stream]],
                gate_grads[stream],
                preferred_element_type=jnp.float32,
            )
            source_weight_grad = jnp.einsum(
                "nhwc,nhwo->co", sources, message_grads[stream], preferred_element_type=jnp.float32
            )
            distil_parts[stream].append(
                jnp.concatenate(
                    [gate_weight_grad[None], source_weight_grad.reshape(3, head_width, -1)], axis=0
                )
            )
        spread_grad = spread_grad + shifted(tap_grad * tap_mask, -vertical, -lateral)
    distil_grad = jnp.stack([jnp.stack(distil_parts[0]), jnp.stack(distil_parts[1])])
    head_grad = channel_sum(spread_grad)
    head_grad = (
        head_grad.at[:, :, :, OWN_HEAD[0]]
        .add(cotangents[0])
        .at[:, :, :, OWN_HEAD[1]]
        .add(cotangents[1])
    )
    head_grad = head_grad * silu_slope(head_out)
    gate_sums = jnp.stack(
        [pixel_sum(gate_grads[0].astype(jnp.float32)), pixel_sum(gate_grads[1].astype(jnp.float32))]
    )
    shift_sums, scale_sums = grad_sums(
        jnp.concatenate([pixel_sum(head_grad), gate_sums], axis=0), pixel_sum(head_grad * head_norm)
    )
    head_pre_grad = normalize_back(
        head_grad, head_norm, head_inv, head_scale, shift_sums[:4], scale_sums, count
    ).astype(jnp.bfloat16)
    head_pre_full = channel_gather(head_pre_grad)
    head_flat_grad = head_pre_full.reshape(head_pre_full.shape[:3] + (-1,))
    block_grad = conv_input_grad(head_flat_grad, heads_flat, masks)
    heads_grad = conv_weight_grad(block_out, head_flat_grad, masks).reshape(heads_full.shape)
    summed_grad = block_grad * silu_slope(summed)
    third_grad = summed_grad[:, :, :, None, :]
    third_shift, third_scale = grad_sums(pixel_sum(third_grad), pixel_sum(third_grad * third_norm))
    third_pre = normalize_back(
        third_grad, third_norm, third_inv, output_scale[None], third_shift, third_scale, count
    ).astype(jnp.bfloat16)[:, :, :, 0, :]
    expand_grad = jnp.einsum(
        "nhwc,nhwo->co", second_full, third_pre, preferred_element_type=jnp.float32
    )
    second_grad = channel_sum(
        jnp.einsum("nhwo,co->nhwc", third_pre, expand_full, preferred_element_type=jnp.float32)[
            :, :, :, None, :
        ]
    )
    second_grad = second_grad * silu_slope(second_out)
    second_shift, second_scale = grad_sums(
        pixel_sum(second_grad), pixel_sum(second_grad * second_norm)
    )
    second_pre = normalize_back(
        second_grad, second_norm, second_inv, block_scale[1:2], second_shift, second_scale, count
    ).astype(jnp.bfloat16)[:, :, :, 0, :]
    spatial_grad = conv_weight_grad(first_full, second_pre, masks)
    first_grad = channel_sum(conv_input_grad(second_pre, spatial_full, masks)[:, :, :, None, :])
    first_grad = first_grad * silu_slope(first_out)
    first_shift, first_scale = grad_sums(pixel_sum(first_grad), pixel_sum(first_grad * first_norm))
    first_pre = normalize_back(
        first_grad, first_norm, first_inv, block_scale[0:1], first_shift, first_scale, count
    ).astype(jnp.bfloat16)
    first_pre_full = channel_gather(first_pre)[:, :, :, 0, :]
    reduce_grad = jnp.einsum(
        "nhwc,nhwo->co", inputs, first_pre_full, preferred_element_type=jnp.float32
    )
    input_grad = summed_grad + jnp.einsum(
        "nhwo,co->nhwc", first_pre_full, reduce_full, preferred_element_type=jnp.float32
    )
    weight_grads = (reduce_grad, spatial_grad, expand_grad, heads_grad, distil_grad)
    small_grads = (
        jnp.concatenate([first_scale, second_scale], axis=0),
        jnp.concatenate([first_shift, second_shift], axis=0),
        scale_sums,
        shift_sums[:4],
        shift_sums[4:],
        third_scale[0],
        third_shift[0],
    )
    return (outputs[0], outputs[1], input_grad, weight_grads, small_grads)


def gathered_local(
    features,
    image_ids,
    reduce_weight,
    spatial_weight,
    expand_weight,
    head_weights,
    distil_weights,
    block_scale,
    block_shift,
    head_scale,
    head_shift,
    gate_bias,
    output_scale,
    output_shift,
    depth_cotangent,
    segment_cotangent,
):
    batch_count = lax.axis_size("batch")
    small = (
        block_scale,
        block_shift,
        head_scale,
        head_shift,
        gate_bias,
        output_scale,
        output_shift,
    )
    depth_list, segment_list, input_list = ([], [], [])
    weight_total = None
    small_total = None
    for micro_index in range(features.shape[0]):
        gathered = fetch_weights(
            reduce_weight, spatial_weight, expand_weight, head_weights, distil_weights
        )
        canvas_pick = slice(micro_index, micro_index + 1)
        depth_out, segment_out, input_grad, weight_grads, small_grads = micro_step(
            features[canvas_pick],
            image_ids[canvas_pick],
            depth_cotangent[canvas_pick],
            segment_cotangent[canvas_pick],
            gathered,
            small,
            batch_count,
        )
        weight_grads = scatter_weights(weight_grads)
        weight_total = (
            weight_grads
            if weight_total is None
            else jax.tree.map(jnp.add, weight_total, weight_grads)
        )
        small_total = (
            small_grads if small_total is None else jax.tree.map(jnp.add, small_total, small_grads)
        )
        depth_list.append(depth_out)
        segment_list.append(segment_out)
        input_list.append(input_grad)
    reduce_grad, spatial_grad, expand_grad, heads_grad, distil_grad = weight_total
    scale_mid, shift_mid, scale_heads, shift_heads, bias_gates, scale_out, shift_out = small_total
    return (
        jnp.concatenate(depth_list, axis=0),
        jnp.concatenate(segment_list, axis=0),
        jnp.concatenate(input_list, axis=0),
        reduce_grad,
        spatial_grad,
        expand_grad,
        heads_grad,
        distil_grad,
        scale_mid,
        shift_mid,
        scale_heads,
        shift_heads,
        bias_gates,
        scale_out,
        shift_out,
    )


MESH = pl.DeviceIdType.MESH
PIXELS = 256
PAD = 32
LANES = 128


def whereabouts():
    place, lane = lax.axis_index("batch"), lax.axis_index("chan")
    return place, lane, place // 2, place % 2, lane // 2, lane % 2


def ranked(depth, rank):
    high, low = depth // 2, depth % 2
    up, odd = rank // 2, rank % 2
    return (
        (1 - odd) * (1 - up) * depth
        + odd * (1 - up) * (1 + low)
        + (1 - odd) * up * (2 - 2 * low + high)
        + odd * up * (3 - 3 * high)
    )


def middle(depth):
    return (depth // 2 + depth % 2) % 2


def inner(depth):
    return 1 + depth % 2


def outer(depth):
    return 3 * (depth // 2)


def onward(depth, rank):
    second = (1 - rank % 2) * (rank // 2)
    return outer(depth) + second * (3 - depth - outer(depth))


def homeward(depth, rank):
    second = (1 - rank % 2) * (rank // 2) * middle(depth)
    return inner(depth) + second * (outer(depth) - inner(depth))


def staggered(step):
    late = ((step + 1) % 2) * ((step + 6) // 7) + step // 7
    return (1 - late) * ((step + 1) // 2) + late * (step // 2 - 1 + step // 7), late


def push(source, target, send_sem, recv_sem, place, lane):
    return pltpu.make_async_remote_copy(
        src_ref=source,
        dst_ref=target,
        send_sem=send_sem,
        recv_sem=recv_sem,
        device_id=(place, lane),
        device_id_type=MESH,
    )


def greet(peers):
    barrier = pltpu.get_barrier_semaphore()
    for place, lane in peers:
        pl.semaphore_signal(barrier, inc=1, device_id=(place, lane), device_id_type=MESH)
    pl.semaphore_wait(barrier, len(peers))


def batch_peers():
    place, lane, _, _, _, _ = whereabouts()
    return [((place + step) % 8, lane) for step in range(1, 8)]


def line_peers():
    place, lane, depth, side, _, _ = whereabouts()
    peers = [(ranked(depth, rank) * 2 + side, lane) for rank in range(1, 4)]
    return peers + [(depth * 2 + 1 - side, lane)]


def chan_peers():
    place, lane, _, _, _, _ = whereabouts()
    return [(place, (lane + step) % 4) for step in range(1, 4)]


class Gather:
    def __init__(self, values, recv, cross, line, parts):
        self.values, self.recv, self.cross, self.line, self.parts = values, recv, cross, line, parts

    def view(self, block, part):
        return self.values.at[block] if self.parts == 1 else self.values.at[block, part]

    def copy(self, block, part, sem, depth, side):
        lane = lax.axis_index("chan")
        here = self.view(block, part)
        return push(here, here, sem, self.recv.at[block, part], depth * 2 + side, lane)

    def start(self):
        place, lane, depth, side, _, _ = whereabouts()
        for part in range(self.parts):
            self.copy(place, part, self.line.at[0, 0, part], inner(depth), side).start()

            @pl.when(middle(depth) == 1)
            def _():
                self.copy(place, part, self.line.at[1, 0, part], outer(depth), side).start()

            self.copy(place, part, self.cross.at[0, part], depth, 1 - side).start()

    def near(self, rank):
        place, lane, depth, side, _, _ = whereabouts()
        block = ranked(depth, rank) * 2 + side
        for part in range(self.parts):
            self.copy(block, part, self.cross.at[rank, part], depth, side).wait_recv()

            @pl.when(middle(depth) == 1)
            def _():
                self.copy(
                    block, part, self.line.at[0, rank, part], onward(depth, rank), side
                ).start()

            self.copy(block, part, self.cross.at[rank, part], depth, 1 - side).start()
        return block

    def far(self, rank):
        place, lane, depth, side, _, _ = whereabouts()
        block = ranked(depth, rank) * 2 + 1 - side
        for part in range(self.parts):
            self.copy(block, part, self.cross.at[rank, part], depth, side).wait_recv()
        return block

    def next(self, step):
        place, lane, depth, side, _, _ = whereabouts()
        rank, late = staggered(step)

        @pl.when((late == 0) & (step > 0))
        def _():
            self.near(rank)

        @pl.when(late == 1)
        def _():
            self.far(rank)

        return ranked(depth, rank) * 2 + (side + late) % 2

    def close(self):
        place, lane, depth, side, _, _ = whereabouts()
        for part in range(self.parts):
            for rank in range(4):
                self.copy(place, part, self.cross.at[rank, part], depth, side).wait_send()
            self.copy(place, part, self.line.at[0, 0, part], depth, side).wait_send()

            @pl.when(middle(depth) == 1)
            def _():
                self.copy(place, part, self.line.at[1, 0, part], depth, side).wait_send()
                for rank in range(1, 4):
                    self.copy(place, part, self.line.at[0, rank, part], depth, side).wait_send()


def gather_sems(parts):
    return [
        pltpu.SemaphoreType.DMA((8, parts)),
        pltpu.SemaphoreType.DMA((4, parts)),
        pltpu.SemaphoreType.DMA((2, 4, parts)),
    ]


def clear_edges(turned):
    edge = jnp.zeros((3, PAD, turned.shape[2]), turned.dtype)
    turned[:, 0:PAD] = edge
    turned[:, PAD + PIXELS :] = edge


def fill_columns(value, mask, turned, columns, row):
    width = value.shape[1]
    wide = value.astype(jnp.float32)
    inside = slice(PAD, PAD + PIXELS)
    turned[0, inside] = pltpu.roll(wide, 1, 0).astype(jnp.bfloat16)
    turned[1, inside] = value
    turned[2, inside] = pltpu.roll(wide, PIXELS - 1, 0).astype(jnp.bfloat16)
    for number, (vertical, lateral) in enumerate(OFFSETS):
        start = PAD + 32 * vertical
        columns[row : row + PIXELS, number * width : (number + 1) * width] = (
            turned[lateral + 1, start : start + PIXELS] * mask[:, number : number + 1]
        )


def send_pieces(part, block, stage, got, stage_sem, got_sem):
    place, lane, _, _, _, _ = whereabouts()
    for micro in range(2):
        for half in range(2):
            piece = part[micro * PIXELS : (micro + 1) * PIXELS, half * LANES : (half + 1) * LANES]
            target = half * 2 + micro

            @pl.when(target == lane)
            def _():
                got[lane, block] = piece

            @pl.when(target != lane)
            def _():
                stage[target, block] = piece
                push(
                    stage.at[target, block],
                    got.at[lane, block],
                    stage_sem.at[target, block],
                    got_sem.at[lane, block],
                    place,
                    target,
                ).start()


def await_pieces(stage, got, stage_sem, got_sem):
    place, lane, _, _, _, _ = whereabouts()

    def body(block, _):
        for step in range(1, 4):
            other = (lane + step) % 4
            push(
                stage.at[other, block],
                got.at[other, block],
                stage_sem.at[other, block],
                got_sem.at[other, block],
                place,
                lane,
            ).wait()
        return 0

    lax.fori_loop(0, 8, body, 0)


CHUNKS = 4


def spread_chunk(chunk, values, out_sem, in_sem):
    place, lane, _, _, upper, core = whereabouts()
    here = values.at[upper, core, pl.ds(2 * chunk, 2)]
    push(
        here, here, out_sem.at[1, chunk], in_sem.at[upper, core, chunk], place, 2 - 2 * upper + core
    ).start()
    push(
        here, here, out_sem.at[0, chunk], in_sem.at[upper, core, chunk], place, upper * 2 + 1 - core
    ).start()


def finish_chunks(values, out_sem, in_sem):
    place, lane, _, _, upper, core = whereabouts()

    def relay(chunk, _):
        here = values.at[1 - upper, core, pl.ds(2 * chunk, 2)]
        copy = push(
            here,
            here,
            out_sem.at[2, chunk],
            in_sem.at[1 - upper, core, chunk],
            place,
            upper * 2 + 1 - core,
        )
        copy.wait_recv()
        copy.start()
        return 0

    lax.fori_loop(0, CHUNKS, relay, 0)

    def close(chunk, _):
        for half in range(2):
            here = values.at[half, 1 - core, pl.ds(2 * chunk, 2)]
            push(
                here, here, out_sem.at[0, chunk], in_sem.at[half, 1 - core, chunk], place, lane
            ).wait_recv()
        here = values.at[upper, core, pl.ds(2 * chunk, 2)]
        for path in range(3):
            push(
                here, here, out_sem.at[path, chunk], in_sem.at[upper, core, chunk], place, lane
            ).wait_send()
        return 0

    lax.fori_loop(0, CHUNKS, close, 0)


def vmem(count):
    return [pl.BlockSpec(memory_space=pltpu.VMEM)] * count


def chan_scratch():
    return [
        pltpu.VMEM((4, 8, PIXELS, LANES), jnp.bfloat16),
        pltpu.VMEM((4, 8, PIXELS, LANES), jnp.bfloat16),
    ]


def chan_sems():
    return [
        pltpu.SemaphoreType.DMA((4, 8)),
        pltpu.SemaphoreType.DMA((4, 8)),
        pltpu.SemaphoreType.DMA((3, CHUNKS)),
        pltpu.SemaphoreType.DMA((2, 2, CHUNKS)),
    ]


def kernel_params(number):
    return pltpu.CompilerParams(
        collective_id=number, has_side_effects=True, vmem_limit_bytes=60 * 2**20
    )


class Exchange:
    def __init__(self, values, send, recv, axis):
        self.values, self.send, self.recv, self.axis = values, send, recv, axis

    def steps(self):
        place, lane, _, _, _, _ = whereabouts()
        if self.axis == "batch":
            return [(step - 1, (place + step) % 8, lane, (place + step) % 8) for step in range(1, 8)]
        return [(step - 1, place, (lane + step) % 4, (lane + step) % 4) for step in range(1, 4)]

    def mine(self):
        place, lane, _, _, _, _ = whereabouts()
        return place if self.axis == "batch" else lane

    def start(self):
        here = self.values.at[self.mine()]
        for number, place, lane, _ in self.steps():
            push(here, here, self.send.at[number], self.recv.at[self.mine()], place, lane).start()

    def wait(self):
        for number, place, lane, slot in self.steps():
            there = self.values.at[slot]
            push(there, there, self.send.at[number], self.recv.at[slot], place, lane).wait_recv()

    def close(self):
        here = self.values.at[self.mine()]
        for number, place, lane, _ in self.steps():
            push(here, here, self.send.at[number], self.recv.at[self.mine()], place, lane).wait_send()

    def total(self):
        result = self.values[0]
        for slot in range(1, self.values.shape[0]):
            result = result + self.values[slot]
        return result


class Pieces:
    def __init__(self, stage, got, send, recv):
        self.stage, self.got, self.send, self.recv = stage, got, send, recv

    def start(self, part):
        place, lane, _, _, _, _ = whereabouts()
        for slot in range(4):
            self.stage[slot] = part[:, slot * LANES : (slot + 1) * LANES].astype(jnp.bfloat16)
        for step in (2, 1, 3):
            slot = (lane + step) % 4
            push(
                self.stage.at[slot],
                self.got.at[lane],
                self.send.at[slot],
                self.recv.at[lane],
                place,
                slot,
            ).start()

    def finish(self):
        place, lane, _, _, _, _ = whereabouts()
        self.got[lane] = self.stage[lane]
        for step in range(1, 4):
            slot = (lane + step) % 4
            push(
                self.stage.at[slot],
                self.got.at[slot],
                self.send.at[slot],
                self.recv.at[slot],
                place,
                lane,
            ).wait()
        result = self.got[0].astype(jnp.float32)
        for slot in range(1, 4):
            result = result + self.got[slot].astype(jnp.float32)
        return result


def micro_rows(micro):
    return slice(micro * PIXELS, (micro + 1) * PIXELS)


def moments(value, other):
    rows = []
    for micro in range(2):
        part = value[micro_rows(micro)]
        rows.append(jnp.sum(part, axis=0, keepdims=True))
        rows.append(jnp.sum(part * other[micro_rows(micro)], axis=0, keepdims=True))
    return rows


def tile_rows(rows, height):
    width = rows[0].shape[1]
    return jnp.concatenate(rows + [jnp.zeros((height - len(rows), width), jnp.float32)], axis=0)


def normed_part(value, totals, micro, count):
    center = totals[2 * micro : 2 * micro + 1] / count
    inverse = lax.rsqrt(totals[2 * micro + 1 : 2 * micro + 2] / count - center * center + EPSILON)
    return (value[micro_rows(micro)] - center) * inverse, inverse


def dot_last(first, second):
    return lax.dot_general(
        first, second, (((1,), (1,)), ((), ())), preferred_element_type=jnp.float32
    )


def front_kernel(
    count,
    x_ref,
    ids_ref,
    reduce_ref,
    spatial_ref,
    expand_ref,
    block_ref,
    output_ref,
    head_ref,
    y_ref,
    norm3_ref,
    inverse3_ref,
    norm12_ref,
    inverse12_ref,
    act1_ref,
    act2_ref,
    reduce_all,
    spatial_all,
    expand_all,
    mask_all,
    mine_ref,
    turned,
    columns,
    stage,
    got,
    sums1,
    sums2,
    sums3,
    head_all,
    *sems,
):
    place, lane, depth, side, upper, core = whereabouts()
    reduces = Gather(reduce_all, *sems[0:3], 1)
    spatials = Gather(spatial_all, *sems[3:6], 1)
    expands = Gather(expand_all, *sems[6:9], 1)
    masks = Gather(mask_all, *sems[9:12], 1)
    pieces = Pieces(stage, got, sems[12], sems[13])
    first_sums = Exchange(sums1, sems[14], sems[15], "batch")
    second_sums = Exchange(sums2, sems[16], sems[17], "batch")
    third_sums = Exchange(sums3, sems[18], sems[19], "batch")
    heads = Exchange(head_all, sems[20], sems[21], "chan")
    first_acts = Exchange(act1_ref, sems[22], sems[23], "chan")
    second_acts = Exchange(act2_ref, sems[24], sems[25], "chan")

    greet(batch_peers() + chan_peers())
    reduce_all[place] = reduce_ref[...]
    reduces.start()
    spatial_all[place] = spatial_ref[...]
    spatials.start()
    expand_all[place] = expand_ref[...]
    expands.start()
    head_all[lane] = head_ref[...]
    heads.start()
    clear_edges(turned)
    pixel = lax.broadcasted_iota(jnp.int32, (PIXELS, LANES), 0)
    column = lax.broadcasted_iota(jnp.int32, (PIXELS, LANES), 1)
    for micro in range(2):
        ids = ids_ref[micro]
        mask = jnp.zeros((PIXELS, LANES), jnp.float32)
        for number, (vertical, lateral) in enumerate(OFFSETS):
            offset = 32 * vertical + lateral
            beside = ids if offset == 0 else pltpu.roll(ids, (-offset) % PIXELS, 0)
            row, col = (pixel >> 5) + vertical, (pixel & 31) + lateral
            inside = (row >= 0) & (row < 8) & (col >= 0) & (col < 32)
            same = (beside == ids) & inside & (column == number)
            mask = jnp.where(same, 1.0, mask)
        mask_all[place, micro] = mask.astype(jnp.bfloat16)
    masks.start()

    for rank in range(1, 4):
        reduces.near(rank)
    for rank in range(4):
        reduces.far(rank)
    x = x_ref[...].reshape(2 * PIXELS, x_ref.shape[2])
    pieces.start(dot_last(x, reduce_all[...].reshape(512, 512)))
    for rank in range(1, 4):
        spatials.near(rank)
    first = pieces.finish()
    sums1[place] = tile_rows(moments(first, first), 8)
    first_sums.start()
    for rank in range(1, 4):
        expands.near(rank)
    first_sums.wait()
    totals = first_sums.total()
    rows = []
    for micro in range(2):
        normed, inverse = normed_part(first, totals, micro, count)
        norm12_ref[0, micro_rows(micro)] = normed
        rows.append(inverse)
        out = normed * block_ref[0:1] + block_ref[2:3]
        act1_ref[lane, micro_rows(micro)] = (out * jax.nn.sigmoid(out)).astype(jnp.bfloat16)
    first_acts.start()
    for rank in range(1, 4):
        masks.near(rank)
    for rank in range(4):
        spatials.far(rank)
    first_acts.wait()
    for micro in range(2):
        value = jnp.concatenate([act1_ref[slot, micro_rows(micro)] for slot in range(4)], axis=1)
        fill_columns(value, mask_all[place, micro], turned, columns, micro * PIXELS)
    second = jnp.zeros((2 * PIXELS, LANES), jnp.float32)
    for number in range(9):
        second = second + jnp.dot(
            columns[:, number * 512 : (number + 1) * 512],
            spatial_all[:, number].reshape(512, LANES),
            preferred_element_type=jnp.float32,
        )
    sums2[place] = tile_rows(moments(second, second), 8)
    second_sums.start()
    for rank in range(4):
        expands.far(rank)
    second_sums.wait()
    totals = second_sums.total()
    for micro in range(2):
        normed, inverse = normed_part(second, totals, micro, count)
        norm12_ref[1, micro_rows(micro)] = normed
        rows.append(inverse)
        out = normed * block_ref[1:2] + block_ref[3:4]
        act2_ref[lane, micro_rows(micro)] = (out * jax.nn.sigmoid(out)).astype(jnp.bfloat16)
    second_acts.start()
    inverse12_ref[...] = tile_rows(rows, 8)
    heads.wait()
    half_width = LANES // 2
    low = lax.broadcasted_iota(jnp.int32, (1, LANES), 1) < half_width
    source = place // 2
    even = place % 2 == 0
    for kind in range(2):
        upper_row = head_all[source, pl.ds(4 * kind + 2 * upper, 1)]
        lower_row = head_all[source, pl.ds(4 * kind + 2 * upper + 1, 1)]
        mine_ref[kind : kind + 1] = jnp.where(
            even,
            jnp.where(low, upper_row, pltpu.roll(lower_row, half_width, 1)),
            jnp.where(low, pltpu.roll(upper_row, half_width, 1), lower_row),
        )
    second_acts.wait()
    value = jnp.concatenate([act2_ref[slot] for slot in range(4)], axis=1)
    third = jnp.dot(
        value, expand_all[...].reshape(512, 512), preferred_element_type=jnp.float32
    )
    sums3[place] = tile_rows(moments(third, third), 8)
    third_sums.start()
    for rank in range(4):
        masks.far(rank)
    third_sums.wait()
    totals = third_sums.total()
    rows = []
    for micro in range(2):
        normed, inverse = normed_part(third, totals, micro, count)
        norm3_ref[micro_rows(micro)] = normed
        rows.append(inverse)
        out = normed * output_ref[0:1] + output_ref[1:2] + x_ref[micro].astype(jnp.float32)
        y_ref[micro] = (out * jax.nn.sigmoid(out)).astype(jnp.bfloat16)
    inverse3_ref[...] = tile_rows(rows, 8)
    for item in (reduces, spatials, expands, masks, heads, first_acts, second_acts):
        item.close()
    for item in (first_sums, second_sums, third_sums):
        item.close()


def exchange_sems(size):
    return [pltpu.SemaphoreType.DMA((size - 1,)), pltpu.SemaphoreType.DMA((size,))]


def run_front(count, x, ids, reduce_rows, spatial, expand, block, output, heads):
    f32, bf16 = jnp.float32, jnp.bfloat16
    return pl.pallas_call(
        functools.partial(front_kernel, count),
        name="front",
        out_shape=(
            jax.ShapeDtypeStruct((2, PIXELS, 512), bf16),
            jax.ShapeDtypeStruct((2 * PIXELS, 512), f32),
            jax.ShapeDtypeStruct((8, 512), f32),
            jax.ShapeDtypeStruct((2, 2 * PIXELS, LANES), f32),
            jax.ShapeDtypeStruct((8, LANES), f32),
            jax.ShapeDtypeStruct((4, 2 * PIXELS, LANES), bf16),
            jax.ShapeDtypeStruct((4, 2 * PIXELS, LANES), bf16),
            jax.ShapeDtypeStruct((8, 64, 512), bf16),
            jax.ShapeDtypeStruct((8, 9, 64, LANES), bf16),
            jax.ShapeDtypeStruct((8, 64, 512), bf16),
            jax.ShapeDtypeStruct((8, 2, PIXELS, LANES), bf16),
            jax.ShapeDtypeStruct((2, LANES), f32),
        ),
        in_specs=vmem(8),
        out_specs=tuple(vmem(12)),
        scratch_shapes=[
            pltpu.VMEM((3, 2 * PAD + PIXELS, 512), bf16),
            pltpu.VMEM((2 * PIXELS, 9 * 512), bf16),
            pltpu.VMEM((4, 2 * PIXELS, LANES), bf16),
            pltpu.VMEM((4, 2 * PIXELS, LANES), bf16),
            pltpu.VMEM((8, 8, LANES), f32),
            pltpu.VMEM((8, 8, LANES), f32),
            pltpu.VMEM((8, 8, 512), f32),
            pltpu.VMEM((4, 8, LANES), f32),
        ]
        + gather_sems(1) * 4
        + [pltpu.SemaphoreType.DMA((4,))] * 2
        + exchange_sems(8) * 3
        + exchange_sems(4) * 3,
        compiler_params=kernel_params(1),
    )(x, ids, reduce_rows, spatial, expand, block, output, heads)


class Scatter:
    def __init__(self, part, far_buf, far_got, near_buf, near_got, sems):
        self.part, self.far_buf, self.far_got = part, far_buf, far_got
        self.near_buf, self.near_got = near_buf, near_got
        self.far_send, self.far_recv, self.near_send, self.near_recv = sems

    def start(self):
        place, lane, depth, side, _, _ = whereabouts()
        for level in range(4):
            self.far_buf[level] = self.part[level * 2 + 1 - side].astype(jnp.bfloat16)
        push(
            self.far_buf, self.far_got, self.far_send, self.far_recv, depth * 2 + 1 - side, lane
        ).start()

    def middle(self):
        place, lane, depth, side, _, _ = whereabouts()
        push(self.far_buf, self.far_got, self.far_send, self.far_recv, place, lane).wait()
        for rank in range(1, 4):
            level = ranked(depth, rank)
            self.near_buf[rank - 1] = (
                self.part[level * 2 + side] + self.far_got[level].astype(jnp.float32)
            ).astype(jnp.bfloat16)
            push(
                self.near_buf.at[rank - 1],
                self.near_got.at[depth],
                self.near_send.at[rank - 1],
                self.near_recv.at[depth],
                level * 2 + side,
                lane,
            ).start()

    def finish(self):
        place, lane, depth, side, _, _ = whereabouts()
        result = self.part[place] + self.far_got[depth].astype(jnp.float32)
        for rank in range(1, 4):
            level = ranked(depth, rank)
            push(
                self.near_buf.at[rank - 1],
                self.near_got.at[level],
                self.near_send.at[rank - 1],
                self.near_recv.at[level],
                place,
                lane,
            ).wait()
            result = result + self.near_got[level].astype(jnp.float32)
        return result


def scatter_scratch(width):
    return [
        pltpu.VMEM((8, 64, width), jnp.float32),
        pltpu.VMEM((4, 64, width), jnp.bfloat16),
        pltpu.VMEM((4, 64, width), jnp.bfloat16),
        pltpu.VMEM((3, 64, width), jnp.bfloat16),
        pltpu.VMEM((4, 64, width), jnp.bfloat16),
    ]


def scatter_sems():
    return [
        pltpu.SemaphoreType.DMA,
        pltpu.SemaphoreType.DMA,
        pltpu.SemaphoreType.DMA((3,)),
        pltpu.SemaphoreType.DMA((4,)),
    ]


def back_part(value, normed, inverse, scale, shift_sum, scale_sum, count):
    return (scale * inverse * (value - (shift_sum + normed * scale_sum) / count)).astype(
        jnp.bfloat16
    )


def rear_kernel(
    count,
    grad_ref,
    x_ref,
    norm3_ref,
    inverse3_ref,
    norm12_ref,
    inverse12_ref,
    act1_ref,
    act2_ref,
    reduce_all,
    spatial_all,
    expand_all,
    mask_ref,
    block_ref,
    output_ref,
    head_ref,
    gate_ref,
    features_ref,
    reduce_out,
    spatial_out,
    expand_out,
    wide_out,
    small_out,
    turned,
    columns,
    stage,
    got,
    stage_next,
    got_next,
    sums_a,
    sums_b,
    sums_c,
    head_all,
    act_all,
    back3,
    *rest,
):
    expand_bufs, spatial_bufs, reduce_bufs, sems = rest[0:5], rest[5:10], rest[10:15], rest[15:]
    place, lane, depth, side, upper, core = whereabouts()
    pieces = Pieces(stage, got, sems[0], sems[1])
    first = Exchange(sums_a, sems[2], sems[3], "batch")
    second = Exchange(sums_b, sems[4], sems[5], "batch")
    third = Exchange(sums_c, sems[6], sems[7], "batch")
    heads = Exchange(head_all, sems[8], sems[9], "chan")
    acts = Exchange(act_all, sems[10], sems[11], "chan")
    expands = Scatter(*expand_bufs, sems[12:16])
    spatials = Scatter(*spatial_bufs, sems[16:20])
    reduces = Scatter(*reduce_bufs, sems[20:24])
    pieces_next = Pieces(stage_next, got_next, sems[24], sems[25])

    greet(batch_peers() + chan_peers())
    half_width = LANES // 2
    even = place % 2 == 0
    mine = lax.broadcasted_iota(jnp.int32, (1, LANES), 1) >> 6 == place % 2
    rows = []
    for kind in range(2):
        own = head_ref[kind : kind + 1]
        turned_own = pltpu.roll(own, half_width, 1)
        first_row = jnp.where(mine, jnp.where(even, own, turned_own), 0.0)
        second_row = jnp.where(mine, jnp.where(even, turned_own, own), 0.0)
        for half in range(2):
            for row in (first_row, second_row):
                rows.append(jnp.where(upper == half, row, 0.0))
    head_all[lane] = jnp.concatenate(rows, axis=0)
    heads.start()
    clear_edges(turned)
    rows = []
    for micro in range(2):
        normed = norm3_ref[micro_rows(micro)]
        out = normed * output_ref[0:1] + output_ref[1:2] + x_ref[micro].astype(jnp.float32)
        value = grad_ref[micro_rows(micro)] * silu_slope(out)
        features_ref[micro] = value
        rows.append(jnp.sum(value, axis=0, keepdims=True))
        rows.append(jnp.sum(value * normed, axis=0, keepdims=True))
    heads.wait()
    sums_a[place, 0:8] = tile_rows(rows, 8)
    sums_a[place, 8:16] = jnp.zeros((8, 512), jnp.float32)
    sums_a[place, 4:6, 0:LANES] = gate_ref[...]
    sums_a[place, 8:16, 0:LANES] = jnp.where(place // 2 == lane, heads.total(), 0.0)
    first.start()
    first.wait()
    totals = first.total()
    wide_out[...] = totals
    for micro in range(2):
        back3[micro_rows(micro)] = back_part(
            features_ref[micro],
            norm3_ref[micro_rows(micro)],
            inverse3_ref[micro : micro + 1],
            output_ref[0:1],
            totals[2 * micro : 2 * micro + 1],
            totals[2 * micro + 1 : 2 * micro + 2],
            count,
        )
    pieces.start(dot_last(back3[...], expand_all[...].reshape(512, 512)))
    value = jnp.concatenate([act2_ref[slot] for slot in range(4)], axis=1)
    expands.part[...] = jnp.dot(
        value.T, back3[...], preferred_element_type=jnp.float32
    ).reshape(8, 64, 512)
    expands.start()
    grad = pieces.finish()
    normed = norm12_ref[1]
    grad = grad * silu_slope(normed * block_ref[1:2] + block_ref[3:4])
    sums_b[place] = tile_rows(moments(grad, normed), 8)
    second.start()
    expands.middle()
    second.wait()
    totals = second.total()
    small_rows = [totals[1:2] + totals[3:4], totals[0:1] + totals[2:3]]
    for micro in range(2):
        value = back_part(
            grad[micro_rows(micro)],
            normed[micro_rows(micro)],
            inverse12_ref[2 + micro : 3 + micro],
            block_ref[1:2],
            totals[2 * micro : 2 * micro + 1],
            totals[2 * micro + 1 : 2 * micro + 2],
            count,
        )
        fill_columns(value, mask_ref[micro], turned, columns, micro * PIXELS)
    part = jnp.zeros((2 * PIXELS, 512), jnp.float32)
    for number in range(9):
        part = part + dot_last(
            columns[:, number * LANES : (number + 1) * LANES],
            spatial_all[:, 8 - number].reshape(512, LANES),
        )
    pieces_next.start(part)
    value = jnp.concatenate([act1_ref[slot] for slot in range(4)], axis=1)
    spatials.part[...] = jnp.dot(
        value.T, columns[...], preferred_element_type=jnp.float32
    ).reshape(8, 64, 9 * LANES)
    spatials.start()
    grad = pieces_next.finish()
    normed = norm12_ref[0]
    grad = grad * silu_slope(normed * block_ref[0:1] + block_ref[2:3])
    sums_c[place] = tile_rows(moments(grad, normed), 8)
    third.start()
    spatials.middle()
    expand_out[...] = expands.finish()
    third.wait()
    totals = third.total()
    small_rows = [totals[1:2] + totals[3:4], small_rows[0], totals[0:1] + totals[2:3], small_rows[1]]
    small_out[...] = tile_rows(small_rows, 8)
    for micro in range(2):
        act_all[lane, micro_rows(micro)] = back_part(
            grad[micro_rows(micro)],
            normed[micro_rows(micro)],
            inverse12_ref[micro : micro + 1],
            block_ref[0:1],
            totals[2 * micro : 2 * micro + 1],
            totals[2 * micro + 1 : 2 * micro + 2],
            count,
        )
    acts.start()
    acts.wait()
    value = jnp.concatenate([act_all[slot] for slot in range(4)], axis=1)
    x = x_ref[...].reshape(2 * PIXELS, 512)
    reduces.part[...] = jnp.dot(value.T, x, preferred_element_type=jnp.float32).reshape(8, 64, 512)
    reduces.start()
    more = jnp.dot(value, reduce_all[...].reshape(512, 512), preferred_element_type=jnp.float32)
    for micro in range(2):
        features_ref[micro] = features_ref[micro] + more[micro_rows(micro)]
    reduces.middle()
    result = spatials.finish()
    for number in range(9):
        spatial_out[8 - number] = result[:, number * LANES : (number + 1) * LANES]
    reduce_out[...] = reduces.finish().T
    for item in (first, second, third, heads, acts):
        item.close()


def run_rear(count, *arrays):
    f32, bf16 = jnp.float32, jnp.bfloat16
    return pl.pallas_call(
        functools.partial(rear_kernel, count),
        name="rear",
        out_shape=(
            jax.ShapeDtypeStruct((2, PIXELS, 512), f32),
            jax.ShapeDtypeStruct((512, 64), f32),
            jax.ShapeDtypeStruct((9, 64, LANES), f32),
            jax.ShapeDtypeStruct((64, 512), f32),
            jax.ShapeDtypeStruct((16, 512), f32),
            jax.ShapeDtypeStruct((8, LANES), f32),
        ),
        in_specs=vmem(16),
        out_specs=tuple(vmem(6)),
        scratch_shapes=[
            pltpu.VMEM((3, 2 * PAD + PIXELS, LANES), bf16),
            pltpu.VMEM((2 * PIXELS, 9 * LANES), bf16),
            pltpu.VMEM((4, 2 * PIXELS, LANES), bf16),
            pltpu.VMEM((4, 2 * PIXELS, LANES), bf16),
            pltpu.VMEM((4, 2 * PIXELS, LANES), bf16),
            pltpu.VMEM((4, 2 * PIXELS, LANES), bf16),
            pltpu.VMEM((8, 16, 512), f32),
            pltpu.VMEM((8, 8, LANES), f32),
            pltpu.VMEM((8, 8, LANES), f32),
            pltpu.VMEM((4, 8, LANES), f32),
            pltpu.VMEM((4, 2 * PIXELS, LANES), bf16),
            pltpu.VMEM((2 * PIXELS, 512), bf16),
        ]
        + scatter_scratch(512)
        + scatter_scratch(9 * LANES)
        + scatter_scratch(512)
        + [pltpu.SemaphoreType.DMA((4,))] * 2
        + exchange_sems(8) * 3
        + exchange_sems(4) * 2
        + scatter_sems() * 3
        + [pltpu.SemaphoreType.DMA((4,))] * 2,
        compiler_params=kernel_params(5),
    )(*arrays)


class Reduce:
    def __init__(self, part, keep, far_buf, far_got, line_buf, line_got, sems):
        self.part, self.keep, self.far_buf, self.far_got = part, keep, far_buf, far_got
        self.line_buf, self.line_got = line_buf, line_got
        self.far_send, self.far_recv, self.line_send, self.line_recv = sems

    def block(self, step):
        place, lane, depth, side, _, _ = whereabouts()
        rank, late = staggered(step)
        return ranked(depth, 3 - rank) * 2 + (side + 1 + late) % 2

    def line_wait(self, slot):
        place, lane, _, _, _, _ = whereabouts()
        push(
            self.line_buf.at[1],
            self.line_got.at[slot],
            self.line_send.at[1],
            self.line_recv.at[slot],
            place,
            lane,
        ).wait_recv()
        return self.line_got[slot].astype(jnp.float32)

    def step(self, step):
        place, lane, depth, side, _, _ = whereabouts()
        rank, late = staggered(step)
        rank = 3 - rank
        owner = ranked(depth, rank)

        @pl.when(late == 0)
        def _():
            self.far_buf[rank] = self.part[...].astype(jnp.bfloat16)
            push(
                self.far_buf.at[rank],
                self.far_got.at[rank],
                self.far_send.at[rank],
                self.far_recv.at[rank],
                depth * 2 + 1 - side,
                lane,
            ).start()

        @pl.when(late == 1)
        def _():
            push(
                self.far_buf.at[rank],
                self.far_got.at[rank],
                self.far_send.at[rank],
                self.far_recv.at[rank],
                place,
                lane,
            ).wait_recv()
            self.keep[...] = self.part[...] + self.far_got[rank].astype(jnp.float32)

            @pl.when((middle(depth) == 1) & (rank > 0))
            def _():
                self.keep[...] = self.keep[...] + self.line_wait(owner)

            @pl.when(rank > 0)
            def _():
                first = (rank % 2) * (1 - rank // 2) * (1 - middle(depth))
                slot = owner + first * (4 - owner)
                self.line_buf[rank] = self.keep[...].astype(jnp.bfloat16)
                push(
                    self.line_buf.at[rank],
                    self.line_got.at[slot],
                    self.line_send.at[rank],
                    self.line_recv.at[slot],
                    homeward(depth, rank) * 2 + side,
                    lane,
                ).start()

    def close(self):
        place, lane, depth, side, _, _ = whereabouts()
        self.keep[...] = self.keep[...] + self.line_wait(depth)

        @pl.when(middle(depth) == 1)
        def _():
            self.keep[...] = self.keep[...] + self.line_wait(4)

        for rank in range(4):
            push(
                self.far_buf.at[rank],
                self.far_got.at[rank],
                self.far_send.at[rank],
                self.far_recv.at[rank],
                place,
                lane,
            ).wait_send()
        for rank in range(1, 4):
            push(
                self.line_buf.at[rank],
                self.line_got.at[rank],
                self.line_send.at[rank],
                self.line_recv.at[rank],
                place,
                lane,
            ).wait_send()


def reduce_scratch():
    block = (2 * PIXELS, 512)
    return [
        pltpu.VMEM(block, jnp.float32),
        pltpu.VMEM(block, jnp.float32),
        pltpu.VMEM((4,) + block, jnp.bfloat16),
        pltpu.VMEM((4,) + block, jnp.bfloat16),
        pltpu.VMEM((4,) + block, jnp.bfloat16),
        pltpu.VMEM((5,) + block, jnp.bfloat16),
        pltpu.SemaphoreType.DMA((4,)),
        pltpu.SemaphoreType.DMA((4,)),
        pltpu.SemaphoreType.DMA((4,)),
        pltpu.SemaphoreType.DMA((5,)),
    ]


def heads_kernel(
    count,
    block_ref,
    weight_ref,
    mask_ref,
    mine_ref,
    all_ref,
    act_ref,
    norm_ref,
    inverse_ref,
    turned,
    columns,
    stage,
    got,
    recv_sem,
    x_sem,
    z_sem,
    stage_sem,
    got_sem,
    out_sem,
    in_sem,
):
    place, lane, depth, side, upper, core = whereabouts()
    gather = Gather(all_ref, recv_sem, x_sem, z_sem, 2)
    greet(line_peers() + chan_peers())
    all_ref[place] = block_ref[...]
    gather.start()
    clear_edges(turned)

    def body(step, _):
        block = gather.next(step)
        for micro in range(2):
            fill_columns(
                all_ref[block, micro], mask_ref[block, micro], turned, columns, micro * PIXELS
            )
        part = jnp.dot(columns[...], weight_ref[...], preferred_element_type=jnp.float32)
        send_pieces(part.astype(jnp.bfloat16), block, stage, got, stage_sem, got_sem)
        return 0

    lax.fori_loop(0, 8, body, 0)
    await_pieces(stage, got, stage_sem, got_sem)

    def collect(block, sums):
        value = got[0, block].astype(jnp.float32)
        for other in range(1, 4):
            value = value + got[other, block].astype(jnp.float32)
        norm_ref[block] = value
        return (
            sums[0] + jnp.sum(value, axis=0, keepdims=True),
            sums[1] + jnp.sum(value * value, axis=0, keepdims=True),
        )

    zero = jnp.zeros((1, LANES), jnp.float32)
    total, squares = lax.fori_loop(0, 8, collect, (zero, zero))
    center = total / count
    inverse = lax.rsqrt(squares / count - center * center + EPSILON)
    inverse_ref[...] = inverse

    def activate(chunk, _):
        for item in range(2):
            block = 2 * chunk + item
            normed = (norm_ref[block] - center) * inverse
            norm_ref[block] = normed
            out = normed * mine_ref[0:1] + mine_ref[1:2]
            act_ref[upper, core, block] = (out * jax.nn.sigmoid(out)).astype(jnp.bfloat16)
        spread_chunk(chunk, act_ref, out_sem, in_sem)
        return 0

    lax.fori_loop(0, CHUNKS, activate, 0)
    finish_chunks(act_ref, out_sem, in_sem)
    gather.close()


def run_heads(count, block_out, weight, masks, mine):
    return pl.pallas_call(
        functools.partial(heads_kernel, count),
        name="heads",
        out_shape=(
            jax.ShapeDtypeStruct((8, 2, PIXELS, 512), jnp.bfloat16),
            jax.ShapeDtypeStruct((2, 2, 8, PIXELS, LANES), jnp.bfloat16),
            jax.ShapeDtypeStruct((8, PIXELS, LANES), jnp.float32),
            jax.ShapeDtypeStruct((1, LANES), jnp.float32),
        ),
        in_specs=vmem(4),
        out_specs=tuple(vmem(4)),
        scratch_shapes=[
            pltpu.VMEM((3, 2 * PAD + PIXELS, 512), jnp.bfloat16),
            pltpu.VMEM((2 * PIXELS, 9 * 512), jnp.bfloat16),
        ]
        + chan_scratch()
        + gather_sems(2)
        + chan_sems(),
        compiler_params=kernel_params(2),
    )(block_out, weight, masks, mine)


def lane_index():
    return lax.broadcasted_iota(jnp.int32, (PIXELS, LANES), 1)


def distil_kernel(
    count,
    act_ref,
    mixed_ref,
    back_ref,
    mask_ref,
    cot_ref,
    packed_ref,
    bias_ref,
    norm_ref,
    inverse_ref,
    mine_ref,
    stream_ref,
    grad_ref,
    gate_ref,
    back_act_ref,
    sums_ref,
    turned,
    columns,
    turned_wide,
    columns_wide,
    grads_all,
    own_stage,
    own_got,
    cot_all,
    part_ref,
    keep,
    far_buf,
    far_got,
    line_buf,
    line_got,
    far_sem,
    far_recv,
    line_sem,
    line_recv,
    stage,
    got,
    own_sem,
    own_recv,
    cot_sem,
    cot_recv,
    recv_sem,
    x_sem,
    z_sem,
    stage_sem,
    got_sem,
    out_sem,
    in_sem,
):
    place, lane, depth, side, upper, core = whereabouts()
    half_width = LANES // 2
    greet(batch_peers() + chan_peers())
    low = lane_index() < half_width
    source = place // 2 == lane

    for parity in range(2):
        target = 2 * lane + parity

        @pl.when(target == place)
        def _():
            cot_all[place] = packed_ref[parity]

        @pl.when(target != place)
        def _():
            push(
                packed_ref.at[parity],
                cot_all.at[place],
                cot_sem.at[parity],
                cot_recv.at[place],
                target,
                lane,
            ).start()

    @pl.when(source)
    def _():
        def pack(step, _):
            block = (place + step) % 8
            for micro in range(2):
                own_stage[block, micro] = jnp.where(
                    low, act_ref[0, micro, block], act_ref[1, micro, block]
                )

            @pl.when(block == place)
            def _():
                own_got[place % 2] = own_stage[block]

            @pl.when(block != place)
            def _():
                push(
                    own_stage.at[block],
                    own_got.at[place % 2],
                    own_sem.at[block],
                    own_recv.at[place % 2],
                    block,
                    lane,
                ).start()

            return 0

        lax.fori_loop(0, 8, pack, 0)

    clear_edges(turned)
    clear_edges(turned_wide)
    grad_ref[...] = jnp.zeros_like(grad_ref)

    def partial(block):
        for micro in range(2):
            value = jnp.concatenate([act_ref[0, micro, block], act_ref[1, micro, block]], axis=1)
            fill_columns(value, mask_ref[block, micro], turned, columns, micro * PIXELS)
        return jnp.dot(columns[...], mixed_ref[...], preferred_element_type=jnp.float32)

    reduce = Reduce(
        part_ref,
        keep,
        far_buf,
        far_got,
        line_buf,
        line_got,
        (far_sem, far_recv, line_sem, line_recv),
    )

    def reduce_step(step, _):
        part_ref[...] = partial(reduce.block(step))
        reduce.step(step)
        return 0

    lax.fori_loop(0, 8, reduce_step, 0)
    for parity in range(2):
        owner = 2 * lane + parity

        @pl.when(owner != place)
        def _():
            push(
                own_got.at[parity],
                own_got.at[parity],
                own_sem.at[0],
                own_recv.at[parity],
                place,
                lane,
            ).wait_recv()

    reduce.close()
    for stream in range(2):
        bias_sum = jnp.zeros((1, LANES), jnp.float32)
        for micro in range(2):
            rows = slice(micro * PIXELS, (micro + 1) * PIXELS)
            first = own_got[0, micro].astype(jnp.float32)
            second = own_got[1, micro].astype(jnp.float32)
            if stream == 0:
                second = pltpu.roll(second, half_width, 1)
            else:
                first = pltpu.roll(first, half_width, 1)
            own = jnp.where(low, first, second)
            column = 2 * stream * LANES
            gate = jax.nn.sigmoid(
                keep[rows, column : column + LANES] + bias_ref[stream : stream + 1]
            )
            message = keep[rows, column + LANES : column + 2 * LANES]
            cot = cot_ref[stream, micro].astype(jnp.float32)
            stream_ref[stream, micro] = (own + gate * message).astype(jnp.bfloat16)
            gate_grad = (cot * message * gate * (1.0 - gate)).astype(jnp.bfloat16)
            bias_sum = bias_sum + jnp.sum(gate_grad.astype(jnp.float32), axis=0, keepdims=True)
            grads_all[place, micro, :, column : column + LANES] = gate_grad
            grads_all[place, micro, :, column + LANES : column + 2 * LANES] = (cot * gate).astype(
                jnp.bfloat16
            )
        gate_ref[stream : stream + 1] = bias_sum
    gather = Gather(grads_all, recv_sem, x_sem, z_sem, 2)
    gather.start()

    @pl.when(source)
    def _():
        for step in range(1, 8):
            other = (place + step) % 8
            push(
                cot_all.at[other],
                cot_all.at[other],
                cot_sem.at[0],
                cot_recv.at[other],
                place,
                lane,
            ).wait_recv()

    width = 2 * half_width // 2

    def body(step, _):
        block = gather.next(step)
        for micro in range(2):
            fill_columns(
                grads_all[block, micro],
                mask_ref[block, micro],
                turned_wide,
                columns_wide,
                micro * PIXELS,
            )
        part = jnp.dot(columns_wide[...], back_ref[...], preferred_element_type=jnp.float32)
        pieces = []
        for micro in range(2):
            extra = cot_all[block, micro].astype(jnp.float32)
            rows = part[micro * PIXELS : (micro + 1) * PIXELS]
            pieces.append(
                jnp.concatenate(
                    [
                        rows[:, :LANES] + jnp.where(low & source, extra, 0.0),
                        rows[:, LANES:] + jnp.where(low | ~source, 0.0, extra),
                    ],
                    axis=1,
                )
            )
        part = jnp.concatenate(pieces, axis=0).astype(jnp.bfloat16)
        send_pieces(part, block, stage, got, stage_sem, got_sem)
        value = jnp.concatenate(
            [
                jnp.concatenate([act_ref[half, micro, block] for half in range(2)], axis=1)
                for micro in range(2)
            ],
            axis=0,
        ).T
        for number in range(9):
            product = jnp.dot(
                value,
                columns_wide[:, number * 512 : (number + 1) * 512],
                preferred_element_type=jnp.float32,
            )
            for stream in range(2):
                for part_index in range(4):
                    head = (
                        OWN_HEAD[stream]
                        if part_index == 0
                        else SOURCE_START[stream] + part_index - 1
                    )
                    column = (2 * stream + (part_index > 0)) * LANES
                    grad_ref[stream, 8 - number, part_index] += product[
                        head * width : (head + 1) * width, column : column + LANES
                    ]
        return 0

    lax.fori_loop(0, 8, body, 0)
    await_pieces(stage, got, stage_sem, got_sem)
    normalize_gradient(
        count,
        got,
        norm_ref,
        inverse_ref,
        mine_ref,
        back_act_ref,
        sums_ref,
        keep,
        out_sem,
        in_sem,
    )
    gather.close()
    for parity in range(2):
        target = 2 * lane + parity

        @pl.when(target != place)
        def _():
            push(
                packed_ref.at[parity],
                cot_all.at[place],
                cot_sem.at[parity],
                cot_recv.at[place],
                target,
                lane,
            ).wait_send()

    @pl.when(source)
    def _():
        for step in range(1, 8):
            block = (place + step) % 8
            push(
                own_stage.at[block],
                own_got.at[0],
                own_sem.at[block],
                own_recv.at[0],
                block,
                lane,
            ).wait_send()


def normalize_gradient(
    count,
    got,
    norm_ref,
    inverse_ref,
    mine_ref,
    back_act_ref,
    sums_ref,
    keep,
    out_sem,
    in_sem,
):
    place, lane, depth, side, upper, core = whereabouts()

    def collect(block, sums):
        value = got[0, block].astype(jnp.float32)
        for other in range(1, 4):
            value = value + got[other, block].astype(jnp.float32)
        normed = norm_ref[block]
        value = value * silu_slope(normed * mine_ref[0:1] + mine_ref[1:2])
        keep[pl.ds(block // 4 * PIXELS, PIXELS), pl.ds(block % 4 * LANES, LANES)] = value
        return (
            sums[0] + jnp.sum(value, axis=0, keepdims=True),
            sums[1] + jnp.sum(value * normed, axis=0, keepdims=True),
        )

    zero = jnp.zeros((1, LANES), jnp.float32)
    shift_sum, scale_sum = lax.fori_loop(0, 8, collect, (zero, zero))
    sums_ref[0:1] = scale_sum
    sums_ref[1:2] = shift_sum
    factor = mine_ref[0:1] * inverse_ref[...]

    def activate(chunk, _):
        for item in range(2):
            block = 2 * chunk + item
            value = keep[pl.ds(block // 4 * PIXELS, PIXELS), pl.ds(block % 4 * LANES, LANES)]
            back_act_ref[upper, core, block] = (
                factor * (value - (shift_sum + norm_ref[block] * scale_sum) / count)
            ).astype(jnp.bfloat16)
        spread_chunk(chunk, back_act_ref, out_sem, in_sem)
        return 0

    lax.fori_loop(0, CHUNKS, activate, 0)
    finish_chunks(back_act_ref, out_sem, in_sem)


def run_distil(
    count, acts, mixed, mixed_back, masks, cots, packed, bias, norm, inverse, mine
):
    return pl.pallas_call(
        functools.partial(distil_kernel, count),
        name="distil",
        out_shape=(
            jax.ShapeDtypeStruct((2, 2, PIXELS, LANES), jnp.bfloat16),
            jax.ShapeDtypeStruct((2, 9, 4, 64, LANES), jnp.float32),
            jax.ShapeDtypeStruct((2, LANES), jnp.float32),
            jax.ShapeDtypeStruct((2, 2, 8, PIXELS, LANES), jnp.bfloat16),
            jax.ShapeDtypeStruct((2, LANES), jnp.float32),
        ),
        in_specs=vmem(10),
        out_specs=tuple(vmem(5)),
        scratch_shapes=[
            pltpu.VMEM((3, 2 * PAD + PIXELS, 256), jnp.bfloat16),
            pltpu.VMEM((2 * PIXELS, 9 * 256), jnp.bfloat16),
            pltpu.VMEM((3, 2 * PAD + PIXELS, 512), jnp.bfloat16),
            pltpu.VMEM((2 * PIXELS, 9 * 512), jnp.bfloat16),
            pltpu.VMEM((8, 2, PIXELS, 512), jnp.bfloat16),
            pltpu.VMEM((8, 2, PIXELS, LANES), jnp.bfloat16),
            pltpu.VMEM((2, 2, PIXELS, LANES), jnp.bfloat16),
            pltpu.VMEM((8, 2, PIXELS, LANES), jnp.bfloat16),
        ]
        + reduce_scratch()
        + chan_scratch()
        + [
            pltpu.SemaphoreType.DMA((8,)),
            pltpu.SemaphoreType.DMA((2,)),
            pltpu.SemaphoreType.DMA((2,)),
            pltpu.SemaphoreType.DMA((8,)),
        ]
        + gather_sems(2)
        + chan_sems(),
        compiler_params=kernel_params(3),
    )(acts, mixed, mixed_back, masks, cots, packed, bias, norm, inverse, mine)


def back_kernel(
    grads_ref,
    all_ref,
    weight_ref,
    mask_ref,
    out_ref,
    wgrad_ref,
    turned,
    columns,
    part_ref,
    keep,
    far_buf,
    far_got,
    line_buf,
    line_got,
    far_sem,
    far_recv,
    line_sem,
    line_recv,
):
    greet(line_peers())
    clear_edges(turned)
    wgrad_ref[...] = jnp.zeros_like(wgrad_ref)

    def partial(block):
        for micro in range(2):
            value = jnp.concatenate([grads_ref[0, micro, block], grads_ref[1, micro, block]], axis=1)
            fill_columns(value, mask_ref[block, micro], turned, columns, micro * PIXELS)
        return jnp.dot(columns[...], weight_ref[...], preferred_element_type=jnp.float32)

    def weigh(block):
        value = jnp.concatenate([all_ref[block, micro] for micro in range(2)], axis=0).T
        for number in range(9):
            wgrad_ref[8 - number] += jnp.dot(
                value,
                columns[:, number * 256 : (number + 1) * 256],
                preferred_element_type=jnp.float32,
            )

    reduce = Reduce(
        part_ref,
        keep,
        far_buf,
        far_got,
        line_buf,
        line_got,
        (far_sem, far_recv, line_sem, line_recv),
    )

    def step(step, _):
        block = reduce.block(step)
        part_ref[...] = partial(block)
        reduce.step(step)
        weigh(block)
        return 0

    lax.fori_loop(0, 8, step, 0)
    reduce.close()
    out_ref[...] = keep[...]


def run_back(grads, block_all, weight, masks):
    return pl.pallas_call(
        back_kernel,
        name="back",
        out_shape=(
            jax.ShapeDtypeStruct((2 * PIXELS, 512), jnp.float32),
            jax.ShapeDtypeStruct((9, 512, 256), jnp.float32),
        ),
        in_specs=vmem(4),
        out_specs=tuple(vmem(2)),
        scratch_shapes=[
            pltpu.VMEM((3, 2 * PAD + PIXELS, 256), jnp.bfloat16),
            pltpu.VMEM((2 * PIXELS, 9 * 256), jnp.bfloat16),
        ]
        + reduce_scratch(),
        compiler_params=kernel_params(4),
    )(grads, block_all, weight, masks)


def distil_matrix(weights):
    taps = weights.shape[1]
    width = weights.shape[3]
    columns = []
    for stream in range(2):
        for part in range(2):
            rows = []
            for head in range(4):
                source = head - SOURCE_START[stream]
                if part == 0 and head == OWN_HEAD[stream]:
                    rows.append(weights[stream, :, 0])
                elif part == 1 and 0 <= source < 3:
                    rows.append(weights[stream, :, 1 + source])
                else:
                    rows.append(jnp.zeros((taps, width, weights.shape[4]), weights.dtype))
            columns.append(jnp.concatenate(rows, axis=1))
    return jnp.concatenate(columns, axis=2)


def stationary_local(
    features,
    image_ids,
    reduce_weight,
    spatial_weight,
    expand_weight,
    head_weights,
    distil_weights,
    block_scale,
    block_shift,
    head_scale,
    head_shift,
    gate_bias,
    output_scale,
    output_shift,
    depth_cotangent,
    segment_cotangent,
):
    canvases, row_count, column_count = image_ids.shape
    pixels = row_count * column_count
    count = float(lax.axis_size("batch") * pixels)
    width = head_weights.shape[3]
    x = features.reshape(canvases, pixels, -1)
    ids = jnp.broadcast_to(
        image_ids.reshape(canvases, pixels, 1).astype(jnp.float32), (canvases, pixels, LANES)
    )
    block_params = jnp.concatenate([block_scale, block_shift], axis=0)
    output_params = jnp.stack([output_scale, output_shift])
    (
        block_out,
        norm3,
        inverse3,
        norm12,
        inverse12,
        act1,
        act2,
        reduce_all,
        spatial_all,
        expand_all,
        mask_all,
        mine,
    ) = run_front(
        count,
        x,
        ids,
        reduce_weight.T,
        spatial_weight,
        expand_weight,
        block_params,
        output_params,
        jnp.concatenate([head_scale, head_shift], axis=0),
    )
    heads_flat = head_weights.reshape(9, head_weights.shape[1], -1)
    block_all, head_acts, head_norm, head_inv = run_heads(
        count, block_out, heads_flat.reshape(-1, heads_flat.shape[2]), mask_all, mine
    )
    mixed = distil_matrix(distil_weights)
    mixed_back = mixed[::-1].transpose(0, 2, 1).reshape(-1, mixed.shape[1])
    heads_back = heads_flat[::-1].transpose(0, 2, 1).reshape(-1, heads_flat.shape[1])
    cots = jnp.stack([depth_cotangent, segment_cotangent]).reshape(2, canvases, pixels, LANES)
    packed = jnp.stack(
        [
            jnp.concatenate([cots[0, :, :, :width], cots[1, :, :, :width]], axis=-1),
            jnp.concatenate([cots[0, :, :, width:], cots[1, :, :, width:]], axis=-1),
        ]
    )
    streams, distil_grad, gate_sums, head_grads, head_sums = run_distil(
        count,
        head_acts,
        mixed.reshape(-1, mixed.shape[2]),
        mixed_back,
        mask_all,
        cots,
        packed,
        gate_bias,
        head_norm,
        head_inv,
        mine,
    )
    block_grad, heads_grad = run_back(head_grads, block_all, heads_back, mask_all)
    own_mask = lax.dynamic_index_in_dim(mask_all, lax.axis_index("batch"), 0, keepdims=False)
    features_grad, reduce_grad, spatial_grad, expand_grad, wide_sums, small_sums = run_rear(
        count,
        block_grad,
        x,
        norm3,
        inverse3,
        norm12,
        inverse12,
        act1,
        act2,
        reduce_all,
        spatial_all,
        expand_all,
        own_mask,
        block_params,
        output_params,
        head_sums,
        gate_sums,
    )
    streams = streams.reshape((2,) + image_ids.shape + (LANES,))
    return (
        streams[0],
        streams[1],
        features_grad.reshape(features.shape),
        reduce_grad,
        spatial_grad,
        expand_grad,
        heads_grad.reshape(head_weights.shape),
        distil_grad,
        small_sums[0:2],
        small_sums[2:4],
        wide_sums[8:12, :LANES],
        wide_sums[12:16, :LANES],
        wide_sums[4:6, :LANES],
        wide_sums[1] + wide_sums[3],
        wide_sums[0] + wide_sums[2],
    )


def solution(mesh):
    fits = dict(mesh.shape) == {"batch": 8, "chan": 4}
    local = stationary_local if fits else gathered_local
    placed = (
        P("batch", None, None, "chan"),
        P("batch", None, None),
        P("chan", "batch"),
        P(None, "batch", "chan"),
        P("batch", "chan"),
        P(None, "chan", None, "batch"),
        P(None, None, None, "batch", "chan"),
        P(None, "chan"),
        P(None, "chan"),
        P(None, "chan"),
        P(None, "chan"),
        P(None, "chan"),
        P("chan"),
        P("chan"),
        P("batch", None, None, "chan"),
        P("batch", None, None, "chan"),
    )
    return jax.shard_map(
        local,
        mesh=mesh,
        in_specs=placed,
        out_specs=(
            P("batch", None, None, "chan"),
            P("batch", None, None, "chan"),
            P("batch", None, None, "chan"),
            P("chan", "batch"),
            P(None, "batch", "chan"),
            P("batch", "chan"),
            P(None, "chan", None, "batch"),
            P(None, None, None, "batch", "chan"),
            P(None, "chan"),
            P(None, "chan"),
            P(None, "chan"),
            P(None, "chan"),
            P(None, "chan"),
            P("chan"),
            P("chan"),
        ),
        check_vma=False,
    )
```

```python
import functools

import jax
import jax.numpy as jnp
from jax import lax
from jax.experimental import pallas as pl
from jax.experimental.pallas import tpu as pltpu
from jax.sharding import PartitionSpec as P

EPSILON = 1e-05
OFFSETS = ((-1, -1), (-1, 0), (-1, 1), (0, -1), (0, 0), (0, 1), (1, -1), (1, 0), (1, 1))
OWN_HEAD = (0, 3)
SOURCE_START = (1, 0)


def silu_slope(values):
    sig = jax.nn.sigmoid(values)
    return sig * (1.0 + values * (1.0 - sig))


def shifted(values, vertical, lateral):
    row_count, column_count = (values.shape[1], values.shape[2])
    widths = [(0, 0)] * values.ndim
    widths[1] = (1, 1)
    widths[2] = (1, 1)
    padded = jnp.pad(values, widths)
    return padded[
        :, 1 + vertical : 1 + vertical + row_count, 1 + lateral : 1 + lateral + column_count
    ]


def tap_masks(image_ids):
    row_count, column_count = (image_ids.shape[1], image_ids.shape[2])
    padded = jnp.pad(image_ids, ((0, 0), (1, 1), (1, 1)), constant_values=-1)
    masks = []
    for vertical, lateral in OFFSETS:
        beside = padded[
            :, 1 + vertical : 1 + vertical + row_count, 1 + lateral : 1 + lateral + column_count
        ]
        masks.append((beside == image_ids).astype(jnp.float32))
    return jnp.stack(masks)


def conv_forward(inputs, weight, masks):
    total = 0.0
    for number, (vertical, lateral) in enumerate(OFFSETS):
        moved = shifted(inputs, vertical, lateral) * masks[number][..., None].astype(inputs.dtype)
        total = total + jnp.einsum(
            "nhwc,co->nhwo", moved, weight[number], preferred_element_type=jnp.float32
        )
    return total


def conv_input_grad(grads, weight, masks):
    total = 0.0
    for number, (vertical, lateral) in enumerate(OFFSETS):
        term = jnp.einsum(
            "nhwo,co->nhwc", grads, weight[number], preferred_element_type=jnp.float32
        )
        total = total + shifted(term * masks[number][..., None], -vertical, -lateral)
    return total


def conv_weight_grad(inputs, grads, masks):
    pieces = []
    for number, (vertical, lateral) in enumerate(OFFSETS):
        moved = shifted(inputs, vertical, lateral) * masks[number][..., None].astype(inputs.dtype)
        pieces.append(jnp.einsum("nhwc,nhwo->co", moved, grads, preferred_element_type=jnp.float32))
    return jnp.stack(pieces)


def pixel_sum(values):
    return jnp.sum(values, axis=(0, 1, 2))


def normalize(values, scale, shift, count):
    total, squares = lax.psum((pixel_sum(values), pixel_sum(values * values)), "batch")
    center = total / count
    inverse = lax.rsqrt(squares / count - center * center + EPSILON)
    normed = (values - center) * inverse
    return (normed, inverse, normed * scale + shift)


def grad_sums(first_sum, second_sum):
    return lax.psum((first_sum, second_sum), "batch")


def normalize_back(grads, normed, inverse, scale, shift_sum, scale_sum, count):
    return scale * inverse * (grads - (shift_sum + normed * scale_sum) / count)


def channel_gather(values):
    return lax.all_gather(values, "chan", axis=4, tiled=True)


def channel_sum(values):
    return lax.psum_scatter(
        values.astype(jnp.bfloat16), "chan", scatter_dimension=4, tiled=True
    ).astype(jnp.float32)


def fetch_weights(reduce_weight, spatial_weight, expand_weight, head_weights, distil_weights):
    return (
        lax.all_gather(reduce_weight, "batch", axis=1, tiled=True),
        lax.all_gather(spatial_weight, "batch", axis=1, tiled=True),
        lax.all_gather(expand_weight, "batch", axis=0, tiled=True),
        lax.all_gather(head_weights, "batch", axis=3, tiled=True),
        lax.all_gather(distil_weights, "batch", axis=3, tiled=True),
    )


def scatter_weights(grads):
    reduce_grad, spatial_grad, expand_grad, heads_grad, distil_grad = grads
    return (
        lax.psum_scatter(reduce_grad, "batch", scatter_dimension=1, tiled=True),
        lax.psum_scatter(spatial_grad, "batch", scatter_dimension=1, tiled=True),
        lax.psum_scatter(expand_grad, "batch", scatter_dimension=0, tiled=True),
        lax.psum_scatter(heads_grad, "batch", scatter_dimension=3, tiled=True),
        lax.psum_scatter(distil_grad, "batch", scatter_dimension=3, tiled=True),
    )


def micro_step(inputs, image_ids, depth_cot, segment_cot, gathered, small, batch_count):
    reduce_full, spatial_full, expand_full, heads_full, distil_full = gathered
    block_scale, block_shift, head_scale, head_shift, gate_bias, output_scale, output_shift = small
    masks = tap_masks(image_ids)
    canvases, row_count, column_count = image_ids.shape
    count = float(batch_count * canvases * row_count * column_count)
    first_partial = jnp.einsum(
        "nhwc,co->nhwo", inputs, reduce_full, preferred_element_type=jnp.float32
    )
    first = channel_sum(first_partial[:, :, :, None, :])
    first_norm, first_inv, first_out = normalize(first, block_scale[0:1], block_shift[0:1], count)
    first_act = jax.nn.silu(first_out).astype(jnp.bfloat16)
    first_full = channel_gather(first_act)[:, :, :, 0, :]
    second = conv_forward(first_full, spatial_full, masks)[:, :, :, None, :]
    second_norm, second_inv, second_out = normalize(
        second, block_scale[1:2], block_shift[1:2], count
    )
    second_act = jax.nn.silu(second_out).astype(jnp.bfloat16)
    second_full = channel_gather(second_act)[:, :, :, 0, :]
    third = jnp.einsum(
        "nhwc,co->nhwo", second_full, expand_full, preferred_element_type=jnp.float32
    )[:, :, :, None, :]
    third_norm, third_inv, third_out = normalize(
        third, output_scale[None], output_shift[None], count
    )
    summed = third_out[:, :, :, 0, :] + inputs.astype(jnp.float32)
    block_out = jax.nn.silu(summed).astype(jnp.bfloat16)
    heads_flat = heads_full.reshape(heads_full.shape[0], heads_full.shape[1], -1)
    head_partial = conv_forward(block_out, heads_flat, masks)
    head_pre = channel_sum(
        head_partial.reshape(head_partial.shape[:3] + (heads_full.shape[2], heads_full.shape[3]))
    )
    head_norm, head_inv, head_out = normalize(head_pre, head_scale, head_shift, count)
    head_act = jax.nn.silu(head_out).astype(jnp.bfloat16)
    head_full = channel_gather(head_act)
    head_width = head_full.shape[4]
    gate_pre = [0.0, 0.0]
    message = [0.0, 0.0]
    for number, (vertical, lateral) in enumerate(OFFSETS):
        moved = shifted(head_full, vertical, lateral) * masks[number][:, :, :, None, None].astype(
            jnp.bfloat16
        )
        for stream in range(2):
            weights_here = distil_full[stream, number]
            first_source = SOURCE_START[stream]
            sources = moved[:, :, :, first_source : first_source + 3].reshape(
                moved.shape[:3] + (3 * head_width,)
            )
            gate_pre[stream] = gate_pre[stream] + jnp.einsum(
                "nhwc,co->nhwo",
                moved[:, :, :, OWN_HEAD[stream]],
                weights_here[0],
                preferred_element_type=jnp.float32,
            )
            message[stream] = message[stream] + jnp.einsum(
                "nhwc,co->nhwo",
                sources,
                weights_here[1:].reshape(3 * head_width, -1),
                preferred_element_type=jnp.float32,
            )
    cotangents = (depth_cot.astype(jnp.float32), segment_cot.astype(jnp.float32))
    outputs, message_grads, gate_grads = ([], [], [])
    for stream in range(2):
        gate_value = jax.nn.sigmoid(gate_pre[stream] + gate_bias[stream])
        own_feature = head_act[:, :, :, OWN_HEAD[stream]].astype(jnp.float32)
        outputs.append((own_feature + gate_value * message[stream]).astype(jnp.bfloat16))
        message_grads.append((cotangents[stream] * gate_value).astype(jnp.bfloat16))
        gate_grads.append(
            (cotangents[stream] * message[stream] * gate_value * (1.0 - gate_value)).astype(
                jnp.bfloat16
            )
        )
    spread_grad = 0.0
    distil_parts = [[], []]
    for number, (vertical, lateral) in enumerate(OFFSETS):
        tap_mask = masks[number][:, :, :, None, None]
        moved = shifted(head_full, vertical, lateral) * tap_mask.astype(jnp.bfloat16)
        tap_grad = jnp.zeros(head_full.shape, jnp.float32)
        for stream in range(2):
            weights_here = distil_full[stream, number]
            first_source = SOURCE_START[stream]
            sources = moved[:, :, :, first_source : first_source + 3].reshape(
                moved.shape[:3] + (3 * head_width,)
            )
            own_grad = jnp.einsum(
                "nhwo,co->nhwc",
                gate_grads[stream],
                weights_here[0],
                preferred_element_type=jnp.float32,
            )
            source_grad = jnp.einsum(
                "nhwo,co->nhwc",
                message_grads[stream],
                weights_here[1:].reshape(3 * head_width, -1),
                preferred_element_type=jnp.float32,
            )
            tap_grad = tap_grad.at[:, :, :, OWN_HEAD[stream]].add(own_grad)
            tap_grad = tap_grad.at[:, :, :, first_source : first_source + 3].add(
                source_grad.reshape(source_grad.shape[:3] + (3, head_width))
            )
            gate_weight_grad = jnp.einsum(
                "nhwc,nhwo->co",
                moved[:, :, :, OWN_HEAD[stream]],
                gate_grads[stream],
                preferred_element_type=jnp.float32,
            )
            source_weight_grad = jnp.einsum(
                "nhwc,nhwo->co", sources, message_grads[stream], preferred_element_type=jnp.float32
            )
            distil_parts[stream].append(
                jnp.concatenate(
                    [gate_weight_grad[None], source_weight_grad.reshape(3, head_width, -1)], axis=0
                )
            )
        spread_grad = spread_grad + shifted(tap_grad * tap_mask, -vertical, -lateral)
    distil_grad = jnp.stack([jnp.stack(distil_parts[0]), jnp.stack(distil_parts[1])])
    head_grad = channel_sum(spread_grad)
    head_grad = (
        head_grad.at[:, :, :, OWN_HEAD[0]]
        .add(cotangents[0])
        .at[:, :, :, OWN_HEAD[1]]
        .add(cotangents[1])
    )
    head_grad = head_grad * silu_slope(head_out)
    gate_sums = jnp.stack(
        [pixel_sum(gate_grads[0].astype(jnp.float32)), pixel_sum(gate_grads[1].astype(jnp.float32))]
    )
    shift_sums, scale_sums = grad_sums(
        jnp.concatenate([pixel_sum(head_grad), gate_sums], axis=0), pixel_sum(head_grad * head_norm)
    )
    head_pre_grad = normalize_back(
        head_grad, head_norm, head_inv, head_scale, shift_sums[:4], scale_sums, count
    ).astype(jnp.bfloat16)
    head_pre_full = channel_gather(head_pre_grad)
    head_flat_grad = head_pre_full.reshape(head_pre_full.shape[:3] + (-1,))
    block_grad = conv_input_grad(head_flat_grad, heads_flat, masks)
    heads_grad = conv_weight_grad(block_out, head_flat_grad, masks).reshape(heads_full.shape)
    summed_grad = block_grad * silu_slope(summed)
    third_grad = summed_grad[:, :, :, None, :]
    third_shift, third_scale = grad_sums(pixel_sum(third_grad), pixel_sum(third_grad * third_norm))
    third_pre = normalize_back(
        third_grad, third_norm, third_inv, output_scale[None], third_shift, third_scale, count
    ).astype(jnp.bfloat16)[:, :, :, 0, :]
    expand_grad = jnp.einsum(
        "nhwc,nhwo->co", second_full, third_pre, preferred_element_type=jnp.float32
    )
    second_grad = channel_sum(
        jnp.einsum("nhwo,co->nhwc", third_pre, expand_full, preferred_element_type=jnp.float32)[
            :, :, :, None, :
        ]
    )
    second_grad = second_grad * silu_slope(second_out)
    second_shift, second_scale = grad_sums(
        pixel_sum(second_grad), pixel_sum(second_grad * second_norm)
    )
    second_pre = normalize_back(
        second_grad, second_norm, second_inv, block_scale[1:2], second_shift, second_scale, count
    ).astype(jnp.bfloat16)[:, :, :, 0, :]
    spatial_grad = conv_weight_grad(first_full, second_pre, masks)
    first_grad = channel_sum(conv_input_grad(second_pre, spatial_full, masks)[:, :, :, None, :])
    first_grad = first_grad * silu_slope(first_out)
    first_shift, first_scale = grad_sums(pixel_sum(first_grad), pixel_sum(first_grad * first_norm))
    first_pre = normalize_back(
        first_grad, first_norm, first_inv, block_scale[0:1], first_shift, first_scale, count
    ).astype(jnp.bfloat16)
    first_pre_full = channel_gather(first_pre)[:, :, :, 0, :]
    reduce_grad = jnp.einsum(
        "nhwc,nhwo->co", inputs, first_pre_full, preferred_element_type=jnp.float32
    )
    input_grad = summed_grad + jnp.einsum(
        "nhwo,co->nhwc", first_pre_full, reduce_full, preferred_element_type=jnp.float32
    )
    weight_grads = (reduce_grad, spatial_grad, expand_grad, heads_grad, distil_grad)
    small_grads = (
        jnp.concatenate([first_scale, second_scale], axis=0),
        jnp.concatenate([first_shift, second_shift], axis=0),
        scale_sums,
        shift_sums[:4],
        shift_sums[4:],
        third_scale[0],
        third_shift[0],
    )
    return (outputs[0], outputs[1], input_grad, weight_grads, small_grads)


def gathered_local(
    features,
    image_ids,
    reduce_weight,
    spatial_weight,
    expand_weight,
    head_weights,
    distil_weights,
    block_scale,
    block_shift,
    head_scale,
    head_shift,
    gate_bias,
    output_scale,
    output_shift,
    depth_cotangent,
    segment_cotangent,
):
    batch_count = lax.axis_size("batch")
    small = (
        block_scale,
        block_shift,
        head_scale,
        head_shift,
        gate_bias,
        output_scale,
        output_shift,
    )
    depth_list, segment_list, input_list = ([], [], [])
    weight_total = None
    small_total = None
    for micro_index in range(features.shape[0]):
        gathered = fetch_weights(
            reduce_weight, spatial_weight, expand_weight, head_weights, distil_weights
        )
        canvas_pick = slice(micro_index, micro_index + 1)
        depth_out, segment_out, input_grad, weight_grads, small_grads = micro_step(
            features[canvas_pick],
            image_ids[canvas_pick],
            depth_cotangent[canvas_pick],
            segment_cotangent[canvas_pick],
            gathered,
            small,
            batch_count,
        )
        weight_grads = scatter_weights(weight_grads)
        weight_total = (
            weight_grads
            if weight_total is None
            else jax.tree.map(jnp.add, weight_total, weight_grads)
        )
        small_total = (
            small_grads if small_total is None else jax.tree.map(jnp.add, small_total, small_grads)
        )
        depth_list.append(depth_out)
        segment_list.append(segment_out)
        input_list.append(input_grad)
    reduce_grad, spatial_grad, expand_grad, heads_grad, distil_grad = weight_total
    scale_mid, shift_mid, scale_heads, shift_heads, bias_gates, scale_out, shift_out = small_total
    return (
        jnp.concatenate(depth_list, axis=0),
        jnp.concatenate(segment_list, axis=0),
        jnp.concatenate(input_list, axis=0),
        reduce_grad,
        spatial_grad,
        expand_grad,
        heads_grad,
        distil_grad,
        scale_mid,
        shift_mid,
        scale_heads,
        shift_heads,
        bias_gates,
        scale_out,
        shift_out,
    )


MESH = pl.DeviceIdType.MESH
PIXELS = 256
PAD = 32
LANES = 128


def whereabouts():
    place, lane = lax.axis_index("batch"), lax.axis_index("chan")
    return place, lane, place // 2, place % 2, lane // 2, lane % 2


def ranked(depth, rank):
    high, low = depth // 2, depth % 2
    up, odd = rank // 2, rank % 2
    return (
        (1 - odd) * (1 - up) * depth
        + odd * (1 - up) * (1 + low)
        + (1 - odd) * up * (2 - 2 * low + high)
        + odd * up * (3 - 3 * high)
    )


def middle(depth):
    return (depth // 2 + depth % 2) % 2


def inner(depth):
    return 1 + depth % 2


def outer(depth):
    return 3 * (depth // 2)


def onward(depth, rank):
    second = (1 - rank % 2) * (rank // 2)
    return outer(depth) + second * (3 - depth - outer(depth))


def homeward(depth, rank):
    second = (1 - rank % 2) * (rank // 2) * middle(depth)
    return inner(depth) + second * (outer(depth) - inner(depth))


def staggered(step):
    late = ((step + 1) % 2) * ((step + 14) // 15) + step // 15
    return (1 - late) * ((step + 1) // 2) + late * (step // 2 - 1 + step // 15), late


def push(source, target, send_sem, recv_sem, place, lane):
    return pltpu.make_async_remote_copy(
        src_ref=source,
        dst_ref=target,
        send_sem=send_sem,
        recv_sem=recv_sem,
        device_id=(place, lane),
        device_id_type=MESH,
    )


def greet(peers):
    barrier = pltpu.get_barrier_semaphore()
    for place, lane in peers:
        pl.semaphore_signal(barrier, inc=1, device_id=(place, lane), device_id_type=MESH)
    pl.semaphore_wait(barrier, len(peers))


def batch_peers():
    place, lane, _, _, _, _ = whereabouts()
    return [((place + step) % 8, lane) for step in range(1, 8)]


def line_peers():
    place, lane, depth, side, _, _ = whereabouts()
    peers = [(ranked(depth, rank) * 2 + side, lane) for rank in range(1, 4)]
    return peers + [(depth * 2 + 1 - side, lane)]


def chan_peers():
    place, lane, _, _, _, _ = whereabouts()
    return [(place, (lane + step) % 4) for step in range(1, 4)]


class Gather:
    def __init__(self, values, recv, cross, line, parts):
        self.values, self.recv, self.cross, self.line, self.parts = values, recv, cross, line, parts

    def view(self, block, part):
        return self.values.at[block] if self.parts == 1 else self.values.at[block, part]

    def copy(self, block, part, sem, depth, side):
        lane = lax.axis_index("chan")
        here = self.view(block, part)
        return push(here, here, sem, self.recv.at[block, part], depth * 2 + side, lane)

    def start(self, part=0):
        place, lane, depth, side, _, _ = whereabouts()
        self.copy(place, part, self.line.at[0, 0, part], inner(depth), side).start()

        @pl.when(middle(depth) == 1)
        def _():
            self.copy(place, part, self.line.at[1, 0, part], outer(depth), side).start()

        self.copy(place, part, self.cross.at[0, part], depth, 1 - side).start()

    def near(self, rank, part=0):
        place, lane, depth, side, _, _ = whereabouts()
        block = ranked(depth, rank) * 2 + side
        self.copy(block, part, self.cross.at[rank, part], depth, side).wait_recv()

        @pl.when(middle(depth) == 1)
        def _():
            self.copy(block, part, self.line.at[0, rank, part], onward(depth, rank), side).start()

        self.copy(block, part, self.cross.at[rank, part], depth, 1 - side).start()

    def far(self, rank, part=0):
        place, lane, depth, side, _, _ = whereabouts()
        block = ranked(depth, rank) * 2 + 1 - side
        self.copy(block, part, self.cross.at[rank, part], depth, side).wait_recv()

    def next(self, step):
        place, lane, depth, side, _, _ = whereabouts()
        item, late = staggered(step)
        part, rank = item // 4, item % 4

        @pl.when((late == 0) & (rank > 0))
        def _():
            self.near(rank, part)

        @pl.when((late == 0) & (item == 3))
        def _():
            self.start(1)

        @pl.when(late == 1)
        def _():
            self.far(rank, part)

        return ranked(depth, rank) * 2 + (side + late) % 2, part

    def close(self):
        place, lane, depth, side, _, _ = whereabouts()
        for part in range(self.parts):
            for rank in range(4):
                self.copy(place, part, self.cross.at[rank, part], depth, side).wait_send()
            self.copy(place, part, self.line.at[0, 0, part], depth, side).wait_send()

            @pl.when(middle(depth) == 1)
            def _():
                self.copy(place, part, self.line.at[1, 0, part], depth, side).wait_send()
                for rank in range(1, 4):
                    self.copy(place, part, self.line.at[0, rank, part], depth, side).wait_send()


def gather_sems(parts):
    return [
        pltpu.SemaphoreType.DMA((8, parts)),
        pltpu.SemaphoreType.DMA((4, parts)),
        pltpu.SemaphoreType.DMA((2, 4, parts)),
    ]


def clear_edges(turned):
    edge = jnp.zeros((3, PAD, turned.shape[2]), turned.dtype)
    turned[:, 0:PAD] = edge
    turned[:, PAD + PIXELS :] = edge


def fill_columns(value, mask, turned, columns, row=0, flip=False):
    width = value.shape[1]
    lanes = slice(0, width)
    wide = value.astype(jnp.float32)
    inside = slice(PAD, PAD + PIXELS)
    turned[0, inside, lanes] = pltpu.roll(wide, 1, 0).astype(jnp.bfloat16)
    turned[1, inside, lanes] = value
    turned[2, inside, lanes] = pltpu.roll(wide, PIXELS - 1, 0).astype(jnp.bfloat16)
    for number, (vertical, lateral) in enumerate(OFFSETS):
        start = PAD + 32 * vertical
        slot = 8 - number if flip else number
        columns[row : row + PIXELS, slot * width : (slot + 1) * width] = (
            turned[lateral + 1, start : start + PIXELS, lanes] * mask[:, number : number + 1]
        )


def vmem(count):
    return [pl.BlockSpec(memory_space=pltpu.VMEM)] * count


def kernel_params(number):
    return pltpu.CompilerParams(
        collective_id=number, has_side_effects=True, vmem_limit_bytes=60 * 2**20
    )


class Exchange:
    def __init__(self, values, send, recv, axis):
        self.values, self.send, self.recv, self.axis = values, send, recv, axis

    def steps(self):
        place, lane, _, _, _, _ = whereabouts()
        if self.axis == "batch":
            return [(step - 1, (place + step) % 8, lane, (place + step) % 8) for step in range(1, 8)]
        return [(step - 1, place, (lane + step) % 4, (lane + step) % 4) for step in range(1, 4)]

    def mine(self):
        place, lane, _, _, _, _ = whereabouts()
        return place if self.axis == "batch" else lane

    def start(self):
        here = self.values.at[self.mine()]
        for number, place, lane, _ in self.steps():
            push(here, here, self.send.at[number], self.recv.at[self.mine()], place, lane).start()

    def wait(self):
        for number, place, lane, slot in self.steps():
            there = self.values.at[slot]
            push(there, there, self.send.at[number], self.recv.at[slot], place, lane).wait_recv()

    def close(self):
        here = self.values.at[self.mine()]
        for number, place, lane, _ in self.steps():
            push(here, here, self.send.at[number], self.recv.at[self.mine()], place, lane).wait_send()

    def total(self):
        result = self.values[0]
        for slot in range(1, self.values.shape[0]):
            result = result + self.values[slot]
        return result


class Pieces:
    def __init__(self, stage, got, send, recv):
        self.stage, self.got, self.send, self.recv = stage, got, send, recv

    def start(self, part):
        place, lane, _, _, _, _ = whereabouts()
        for slot in range(4):
            self.stage[slot] = part[:, slot * LANES : (slot + 1) * LANES].astype(jnp.bfloat16)
        for step in (2, 1, 3):
            slot = (lane + step) % 4
            push(
                self.stage.at[slot],
                self.got.at[lane],
                self.send.at[slot],
                self.recv.at[lane],
                place,
                slot,
            ).start()

    def finish(self):
        place, lane, _, _, _, _ = whereabouts()
        self.got[lane] = self.stage[lane]
        for step in range(1, 4):
            slot = (lane + step) % 4
            push(
                self.stage.at[slot],
                self.got.at[slot],
                self.send.at[slot],
                self.recv.at[slot],
                place,
                lane,
            ).wait()
        result = self.got[0].astype(jnp.float32)
        for slot in range(1, 4):
            result = result + self.got[slot].astype(jnp.float32)
        return result


def micro_rows(micro):
    return slice(micro * PIXELS, (micro + 1) * PIXELS)


def moments(value, other):
    rows = []
    for micro in range(2):
        part = value[micro_rows(micro)]
        rows.append(jnp.sum(part, axis=0, keepdims=True))
        rows.append(jnp.sum(part * other[micro_rows(micro)], axis=0, keepdims=True))
    return rows


def tile_rows(rows, height):
    width = rows[0].shape[1]
    return jnp.concatenate(rows + [jnp.zeros((height - len(rows), width), jnp.float32)], axis=0)


def normed_part(value, totals, micro, count):
    center = totals[2 * micro : 2 * micro + 1] / count
    inverse = lax.rsqrt(totals[2 * micro + 1 : 2 * micro + 2] / count - center * center + EPSILON)
    return (value[micro_rows(micro)] - center) * inverse, inverse


def dot_last(first, second):
    return lax.dot_general(
        first, second, (((1,), (1,)), ((), ())), preferred_element_type=jnp.float32
    )


def front_kernel(
    count,
    x_ref,
    ids_ref,
    reduce_ref,
    spatial_ref,
    expand_ref,
    block_scale,
    block_shift,
    output_scale,
    output_shift,
    head_scale,
    head_shift,
    y_ref,
    norm3_ref,
    inverse3_ref,
    norm12_ref,
    inverse12_ref,
    act1_ref,
    act2_ref,
    reduce_all,
    spatial_all,
    expand_all,
    mask_all,
    mine_ref,
    mask_ref,
    turned,
    columns,
    stage,
    got,
    sums1,
    sums2,
    sums3,
    head_all,
    *sems,
):
    place, lane, depth, side, upper, core = whereabouts()
    reduces = Gather(reduce_all, *sems[0:3], 1)
    spatials = Gather(spatial_all, *sems[3:6], 1)
    expands = Gather(expand_all, *sems[6:9], 1)
    masks = Gather(mask_all, *sems[9:12], 1)
    pieces = Pieces(stage, got, sems[12], sems[13])
    first_sums = Exchange(sums1, sems[14], sems[15], "batch")
    second_sums = Exchange(sums2, sems[16], sems[17], "batch")
    third_sums = Exchange(sums3, sems[18], sems[19], "batch")
    heads = Exchange(head_all, sems[20], sems[21], "chan")
    first_acts = Exchange(act1_ref, sems[22], sems[23], "chan")
    second_acts = Exchange(act2_ref, sems[24], sems[25], "chan")

    greet(batch_peers() + chan_peers())
    reduce_all[place] = reduce_ref[...]
    reduces.start()
    spatial_all[place] = spatial_ref[...]
    spatials.start()
    expand_all[place] = expand_ref[...]
    expands.start()
    head_all[lane, 0:4] = head_scale[...]
    head_all[lane, 4:8] = head_shift[...]
    heads.start()
    clear_edges(turned)
    pixel = lax.broadcasted_iota(jnp.int32, (PIXELS, LANES), 0)
    column = lax.broadcasted_iota(jnp.int32, (PIXELS, LANES), 1)
    for micro in range(2):
        ids = ids_ref[micro]
        mask = jnp.zeros((PIXELS, LANES), jnp.float32)
        for number, (vertical, lateral) in enumerate(OFFSETS):
            offset = 32 * vertical + lateral
            beside = ids if offset == 0 else pltpu.roll(ids, (-offset) % PIXELS, 0)
            row, col = (pixel >> 5) + vertical, (pixel & 31) + lateral
            inside = (row >= 0) & (row < 8) & (col >= 0) & (col < 32)
            same = (beside == ids) & inside & (column == number)
            mask = jnp.where(same, 1.0, mask)
        mask_ref[micro] = mask.astype(jnp.bfloat16)
        mask_all[place, micro] = mask_ref[micro]
    masks.start()

    for rank in range(1, 4):
        reduces.near(rank)
    for rank in range(4):
        reduces.far(rank)
    x = x_ref[...].reshape(2 * PIXELS, x_ref.shape[2])
    pieces.start(dot_last(x, reduce_all[...].reshape(512, 512)))
    for rank in range(1, 4):
        spatials.near(rank)
    first = pieces.finish()
    sums1[place] = tile_rows(moments(first, first), 8)
    first_sums.start()
    for rank in range(1, 4):
        expands.near(rank)
    first_sums.wait()
    totals = first_sums.total()
    rows = []
    for micro in range(2):
        normed, inverse = normed_part(first, totals, micro, count)
        norm12_ref[0, micro_rows(micro)] = normed
        rows.append(inverse)
        out = normed * block_scale[0:1] + block_shift[0:1]
        act1_ref[lane, micro_rows(micro)] = (out * jax.nn.sigmoid(out)).astype(jnp.bfloat16)
    first_acts.start()
    for rank in range(1, 4):
        masks.near(rank)
    for rank in range(4):
        spatials.far(rank)
    first_acts.wait()
    for micro in range(2):
        value = jnp.concatenate([act1_ref[slot, micro_rows(micro)] for slot in range(4)], axis=1)
        fill_columns(value, mask_all[place, micro], turned, columns, micro * PIXELS)
    second = jnp.zeros((2 * PIXELS, LANES), jnp.float32)
    for number in range(9):
        second = second + jnp.dot(
            columns[:, number * 512 : (number + 1) * 512],
            spatial_all[:, number].reshape(512, LANES),
            preferred_element_type=jnp.float32,
        )
    sums2[place] = tile_rows(moments(second, second), 8)
    second_sums.start()
    for rank in range(4):
        expands.far(rank)
    second_sums.wait()
    totals = second_sums.total()
    for micro in range(2):
        normed, inverse = normed_part(second, totals, micro, count)
        norm12_ref[1, micro_rows(micro)] = normed
        rows.append(inverse)
        out = normed * block_scale[1:2] + block_shift[1:2]
        act2_ref[lane, micro_rows(micro)] = (out * jax.nn.sigmoid(out)).astype(jnp.bfloat16)
    second_acts.start()
    inverse12_ref[...] = tile_rows(rows, 8)
    heads.wait()
    half_width = LANES // 2
    low = lax.broadcasted_iota(jnp.int32, (1, LANES), 1) < half_width
    source = place // 2
    even = place % 2 == 0
    for kind in range(2):
        upper_row = head_all[source, pl.ds(4 * kind + 2 * upper, 1)]
        lower_row = head_all[source, pl.ds(4 * kind + 2 * upper + 1, 1)]
        mine_ref[kind : kind + 1] = jnp.where(
            even,
            jnp.where(low, upper_row, pltpu.roll(lower_row, half_width, 1)),
            jnp.where(low, pltpu.roll(upper_row, half_width, 1), lower_row),
        )
    second_acts.wait()
    value = jnp.concatenate([act2_ref[slot] for slot in range(4)], axis=1)
    third = jnp.dot(
        value, expand_all[...].reshape(512, 512), preferred_element_type=jnp.float32
    )
    sums3[place] = tile_rows(moments(third, third), 8)
    third_sums.start()
    for rank in range(4):
        masks.far(rank)
    third_sums.wait()
    totals = third_sums.total()
    rows = []
    for micro in range(2):
        normed, inverse = normed_part(third, totals, micro, count)
        norm3_ref[micro_rows(micro)] = normed
        rows.append(inverse)
        out = normed * output_scale[...] + output_shift[...] + x_ref[micro].astype(jnp.float32)
        y_ref[micro] = (out * jax.nn.sigmoid(out)).astype(jnp.bfloat16)
    inverse3_ref[...] = tile_rows(rows, 8)
    for item in (reduces, spatials, expands, masks, heads, first_acts, second_acts):
        item.close()
    for item in (first_sums, second_sums, third_sums):
        item.close()


def exchange_sems(size):
    return [pltpu.SemaphoreType.DMA((size - 1,)), pltpu.SemaphoreType.DMA((size,))]


def run_front(count, *arrays):
    f32, bf16 = jnp.float32, jnp.bfloat16
    return pl.pallas_call(
        functools.partial(front_kernel, count),
        name="front",
        out_shape=(
            jax.ShapeDtypeStruct((2, PIXELS, 512), bf16),
            jax.ShapeDtypeStruct((2 * PIXELS, 512), f32),
            jax.ShapeDtypeStruct((8, 512), f32),
            jax.ShapeDtypeStruct((2, 2 * PIXELS, LANES), f32),
            jax.ShapeDtypeStruct((8, LANES), f32),
            jax.ShapeDtypeStruct((4, 2 * PIXELS, LANES), bf16),
            jax.ShapeDtypeStruct((4, 2 * PIXELS, LANES), bf16),
            jax.ShapeDtypeStruct((8, 64, 512), bf16),
            jax.ShapeDtypeStruct((8, 9, 64, LANES), bf16),
            jax.ShapeDtypeStruct((8, 64, 512), bf16),
            jax.ShapeDtypeStruct((8, 2, PIXELS, LANES), bf16),
            jax.ShapeDtypeStruct((2, LANES), f32),
            jax.ShapeDtypeStruct((2, PIXELS, LANES), bf16),
        ),
        in_specs=vmem(11),
        out_specs=tuple(vmem(13)),
        scratch_shapes=[
            pltpu.VMEM((3, 2 * PAD + PIXELS, 512), bf16),
            pltpu.VMEM((2 * PIXELS, 9 * 512), bf16),
            pltpu.VMEM((4, 2 * PIXELS, LANES), bf16),
            pltpu.VMEM((4, 2 * PIXELS, LANES), bf16),
            pltpu.VMEM((8, 8, LANES), f32),
            pltpu.VMEM((8, 8, LANES), f32),
            pltpu.VMEM((8, 8, 512), f32),
            pltpu.VMEM((4, 8, LANES), f32),
        ]
        + gather_sems(1) * 4
        + [pltpu.SemaphoreType.DMA((4,))] * 2
        + exchange_sems(8) * 3
        + exchange_sems(4) * 3,
        compiler_params=kernel_params(1),
    )(*arrays)


class Scatter:
    def __init__(self, part, far_buf, far_got, near_buf, near_got, sems):
        self.part, self.far_buf, self.far_got = part, far_buf, far_got
        self.near_buf, self.near_got = near_buf, near_got
        self.far_send, self.far_recv, self.near_send, self.near_recv = sems

    def start(self):
        place, lane, depth, side, _, _ = whereabouts()
        for level in range(4):
            self.far_buf[level] = self.part[level * 2 + 1 - side].astype(jnp.bfloat16)
        push(
            self.far_buf, self.far_got, self.far_send, self.far_recv, depth * 2 + 1 - side, lane
        ).start()

    def middle(self):
        place, lane, depth, side, _, _ = whereabouts()
        push(self.far_buf, self.far_got, self.far_send, self.far_recv, place, lane).wait()
        for rank in range(1, 4):
            level = ranked(depth, rank)
            self.near_buf[rank - 1] = (
                self.part[level * 2 + side] + self.far_got[level].astype(jnp.float32)
            ).astype(jnp.bfloat16)
            push(
                self.near_buf.at[rank - 1],
                self.near_got.at[depth],
                self.near_send.at[rank - 1],
                self.near_recv.at[depth],
                level * 2 + side,
                lane,
            ).start()

    def finish(self):
        place, lane, depth, side, _, _ = whereabouts()
        result = self.part[place] + self.far_got[depth].astype(jnp.float32)
        for rank in range(1, 4):
            level = ranked(depth, rank)
            push(
                self.near_buf.at[rank - 1],
                self.near_got.at[level],
                self.near_send.at[rank - 1],
                self.near_recv.at[level],
                place,
                lane,
            ).wait()
            result = result + self.near_got[level].astype(jnp.float32)
        return result


def scatter_scratch(width):
    return [
        pltpu.VMEM((8, 64, width), jnp.float32),
        pltpu.VMEM((4, 64, width), jnp.bfloat16),
        pltpu.VMEM((4, 64, width), jnp.bfloat16),
        pltpu.VMEM((3, 64, width), jnp.bfloat16),
        pltpu.VMEM((4, 64, width), jnp.bfloat16),
    ]


def scatter_sems():
    return [
        pltpu.SemaphoreType.DMA,
        pltpu.SemaphoreType.DMA,
        pltpu.SemaphoreType.DMA((3,)),
        pltpu.SemaphoreType.DMA((4,)),
    ]


def back_part(value, normed, inverse, scale, shift_sum, scale_sum, count):
    return (scale * inverse * (value - (shift_sum + normed * scale_sum) / count)).astype(
        jnp.bfloat16
    )


def rear_kernel(
    count,
    grad_ref,
    x_ref,
    norm3_ref,
    inverse3_ref,
    norm12_ref,
    inverse12_ref,
    act1_ref,
    act2_ref,
    reduce_all,
    spatial_all,
    expand_all,
    mask_ref,
    block_scale,
    block_shift,
    output_scale,
    output_shift,
    head_ref,
    gate_ref,
    features_ref,
    reduce_out,
    spatial_out,
    expand_out,
    block_scale_out,
    block_shift_out,
    head_scale_out,
    head_shift_out,
    gate_out,
    output_scale_out,
    output_shift_out,
    turned,
    columns,
    stage,
    got,
    stage_next,
    got_next,
    sums_a,
    sums_b,
    sums_c,
    head_all,
    act_all,
    back3,
    *rest,
):
    expand_bufs, spatial_bufs, reduce_bufs, sems = rest[0:5], rest[5:10], rest[10:15], rest[15:]
    place, lane, depth, side, upper, core = whereabouts()
    pieces = Pieces(stage, got, sems[0], sems[1])
    first = Exchange(sums_a, sems[2], sems[3], "batch")
    second = Exchange(sums_b, sems[4], sems[5], "batch")
    third = Exchange(sums_c, sems[6], sems[7], "batch")
    heads = Exchange(head_all, sems[8], sems[9], "chan")
    acts = Exchange(act_all, sems[10], sems[11], "chan")
    expands = Scatter(*expand_bufs, sems[12:16])
    spatials = Scatter(*spatial_bufs, sems[16:20])
    reduces = Scatter(*reduce_bufs, sems[20:24])
    pieces_next = Pieces(stage_next, got_next, sems[24], sems[25])

    greet(batch_peers() + chan_peers())
    half_width = LANES // 2
    even = place % 2 == 0
    mine = lax.broadcasted_iota(jnp.int32, (1, LANES), 1) >> 6 == place % 2
    rows = []
    for kind in range(2):
        own = head_ref[kind : kind + 1]
        turned_own = pltpu.roll(own, half_width, 1)
        first_row = jnp.where(mine, jnp.where(even, own, turned_own), 0.0)
        second_row = jnp.where(mine, jnp.where(even, turned_own, own), 0.0)
        for half in range(2):
            for row in (first_row, second_row):
                rows.append(jnp.where(upper == half, row, 0.0))
    head_all[lane] = jnp.concatenate(rows, axis=0)
    heads.start()
    clear_edges(turned)
    rows = []
    for micro in range(2):
        normed = norm3_ref[micro_rows(micro)]
        out = normed * output_scale[...] + output_shift[...] + x_ref[micro].astype(jnp.float32)
        value = grad_ref[micro_rows(micro)] * silu_slope(out)
        features_ref[micro] = value
        rows.append(jnp.sum(value, axis=0, keepdims=True))
        rows.append(jnp.sum(value * normed, axis=0, keepdims=True))
    heads.wait()
    sums_a[place, 0:8] = tile_rows(rows, 8)
    sums_a[place, 8:16] = jnp.zeros((8, 512), jnp.float32)
    sums_a[place, 4:6, 0:LANES] = gate_ref[...]
    sums_a[place, 8:16, 0:LANES] = jnp.where(place // 2 == lane, heads.total(), 0.0)
    first.start()
    first.wait()
    totals = first.total()
    head_scale_out[...] = totals[8:12, 0:LANES]
    head_shift_out[...] = totals[12:16, 0:LANES]
    gate_out[...] = totals[4:6, 0:LANES]
    output_scale_out[...] = totals[1:2] + totals[3:4]
    output_shift_out[...] = totals[0:1] + totals[2:3]
    for micro in range(2):
        back3[micro_rows(micro)] = back_part(
            features_ref[micro],
            norm3_ref[micro_rows(micro)],
            inverse3_ref[micro : micro + 1],
            output_scale[...],
            totals[2 * micro : 2 * micro + 1],
            totals[2 * micro + 1 : 2 * micro + 2],
            count,
        )
    pieces.start(dot_last(back3[...], expand_all[...].reshape(512, 512)))
    value = jnp.concatenate([act2_ref[slot] for slot in range(4)], axis=1)
    expands.part[...] = jnp.dot(
        value.T, back3[...], preferred_element_type=jnp.float32
    ).reshape(8, 64, 512)
    expands.start()
    grad = pieces.finish()
    normed = norm12_ref[1]
    grad = grad * silu_slope(normed * block_scale[1:2] + block_shift[1:2])
    sums_b[place] = tile_rows(moments(grad, normed), 8)
    second.start()
    expands.middle()
    second.wait()
    totals = second.total()
    block_scale_out[1:2] = totals[1:2] + totals[3:4]
    block_shift_out[1:2] = totals[0:1] + totals[2:3]
    for micro in range(2):
        value = back_part(
            grad[micro_rows(micro)],
            normed[micro_rows(micro)],
            inverse12_ref[2 + micro : 3 + micro],
            block_scale[1:2],
            totals[2 * micro : 2 * micro + 1],
            totals[2 * micro + 1 : 2 * micro + 2],
            count,
        )
        fill_columns(value, mask_ref[micro], turned, columns, micro * PIXELS, True)
    part = jnp.zeros((2 * PIXELS, 512), jnp.float32)
    for number in range(9):
        part = part + dot_last(
            columns[:, number * LANES : (number + 1) * LANES],
            spatial_all[:, number].reshape(512, LANES),
        )
    pieces_next.start(part)
    value = jnp.concatenate([act1_ref[slot] for slot in range(4)], axis=1)
    spatials.part[...] = jnp.dot(
        value.T, columns[...], preferred_element_type=jnp.float32
    ).reshape(8, 64, 9 * LANES)
    spatials.start()
    grad = pieces_next.finish()
    normed = norm12_ref[0]
    grad = grad * silu_slope(normed * block_scale[0:1] + block_shift[0:1])
    sums_c[place] = tile_rows(moments(grad, normed), 8)
    third.start()
    spatials.middle()
    expand_out[...] = expands.finish()
    third.wait()
    totals = third.total()
    block_scale_out[0:1] = totals[1:2] + totals[3:4]
    block_shift_out[0:1] = totals[0:1] + totals[2:3]
    for micro in range(2):
        act_all[lane, micro_rows(micro)] = back_part(
            grad[micro_rows(micro)],
            normed[micro_rows(micro)],
            inverse12_ref[micro : micro + 1],
            block_scale[0:1],
            totals[2 * micro : 2 * micro + 1],
            totals[2 * micro + 1 : 2 * micro + 2],
            count,
        )
    acts.start()
    acts.wait()
    value = jnp.concatenate([act_all[slot] for slot in range(4)], axis=1)
    x = x_ref[...].reshape(2 * PIXELS, 512)
    reduces.part[...] = jnp.dot(value.T, x, preferred_element_type=jnp.float32).reshape(8, 64, 512)
    reduces.start()
    more = jnp.dot(value, reduce_all[...].reshape(512, 512), preferred_element_type=jnp.float32)
    for micro in range(2):
        features_ref[micro] = features_ref[micro] + more[micro_rows(micro)]
    reduces.middle()
    result = spatials.finish()
    for number in range(9):
        spatial_out[number] = result[:, number * LANES : (number + 1) * LANES]
    reduce_out[...] = reduces.finish()
    for item in (first, second, third, heads, acts):
        item.close()


def run_rear(count, *arrays):
    f32, bf16 = jnp.float32, jnp.bfloat16
    return pl.pallas_call(
        functools.partial(rear_kernel, count),
        name="rear",
        out_shape=(
            jax.ShapeDtypeStruct((2, PIXELS, 512), f32),
            jax.ShapeDtypeStruct((64, 512), f32),
            jax.ShapeDtypeStruct((9, 64, LANES), f32),
            jax.ShapeDtypeStruct((64, 512), f32),
            jax.ShapeDtypeStruct((2, LANES), f32),
            jax.ShapeDtypeStruct((2, LANES), f32),
            jax.ShapeDtypeStruct((4, LANES), f32),
            jax.ShapeDtypeStruct((4, LANES), f32),
            jax.ShapeDtypeStruct((2, LANES), f32),
            jax.ShapeDtypeStruct((1, 512), f32),
            jax.ShapeDtypeStruct((1, 512), f32),
        ),
        in_specs=vmem(18),
        out_specs=tuple(vmem(11)),
        scratch_shapes=[
            pltpu.VMEM((3, 2 * PAD + PIXELS, LANES), bf16),
            pltpu.VMEM((2 * PIXELS, 9 * LANES), bf16),
            pltpu.VMEM((4, 2 * PIXELS, LANES), bf16),
            pltpu.VMEM((4, 2 * PIXELS, LANES), bf16),
            pltpu.VMEM((4, 2 * PIXELS, LANES), bf16),
            pltpu.VMEM((4, 2 * PIXELS, LANES), bf16),
            pltpu.VMEM((8, 16, 512), f32),
            pltpu.VMEM((8, 8, LANES), f32),
            pltpu.VMEM((8, 8, LANES), f32),
            pltpu.VMEM((4, 8, LANES), f32),
            pltpu.VMEM((4, 2 * PIXELS, LANES), bf16),
            pltpu.VMEM((2 * PIXELS, 512), bf16),
        ]
        + scatter_scratch(512)
        + scatter_scratch(9 * LANES)
        + scatter_scratch(512)
        + [pltpu.SemaphoreType.DMA((4,))] * 2
        + exchange_sems(8) * 3
        + exchange_sems(4) * 2
        + scatter_sems() * 3
        + [pltpu.SemaphoreType.DMA((4,))] * 2,
        compiler_params=kernel_params(5),
    )(*arrays)


class Reduce:
    def __init__(self, part, keep, far_buf, far_got, line_buf, line_got, sems):
        self.part, self.keep, self.far_buf, self.far_got = part, keep, far_buf, far_got
        self.line_buf, self.line_got = line_buf, line_got
        self.far_send, self.far_recv, self.line_send, self.line_recv = sems

    def block(self, step):
        place, lane, depth, side, _, _ = whereabouts()
        item, late = staggered(step)
        return ranked(depth, 3 - item % 4) * 2 + (side + 1 + late) % 2, item // 4

    def far_copy(self, micro, rank, place):
        return push(
            self.far_buf.at[micro, rank],
            self.far_got.at[micro, rank],
            self.far_send.at[micro, rank],
            self.far_recv.at[micro, rank],
            place,
            lax.axis_index("chan"),
        )

    def line_copy(self, micro, rank, slot, place):
        return push(
            self.line_buf.at[micro, rank],
            self.line_got.at[micro, slot],
            self.line_send.at[micro, rank],
            self.line_recv.at[micro, slot],
            place,
            lax.axis_index("chan"),
        )

    def line_value(self, micro, slot):
        self.line_copy(micro, 0, slot, lax.axis_index("batch")).wait_recv()
        return self.line_got[micro, slot].astype(jnp.float32)

    def step(self, step):
        place, lane, depth, side, _, _ = whereabouts()
        item, late = staggered(step)
        micro, rank = item // 4, 3 - item % 4
        owner = ranked(depth, rank)

        @pl.when(late == 0)
        def _():
            self.far_buf[micro, rank] = self.part[...].astype(jnp.bfloat16)
            self.far_copy(micro, rank, depth * 2 + 1 - side).start()

        @pl.when(late == 1)
        def _():
            self.far_copy(micro, rank, place).wait_recv()
            self.keep[micro] = self.part[...] + self.far_got[micro, rank].astype(jnp.float32)

            @pl.when((middle(depth) == 1) & (rank > 0))
            def _():
                self.keep[micro] = self.keep[micro] + self.line_value(micro, owner)

            @pl.when(rank > 0)
            def _():
                first = (rank % 2) * (1 - rank // 2) * (1 - middle(depth))
                slot = owner + first * (4 - owner)
                self.line_buf[micro, rank - 1] = self.keep[micro].astype(jnp.bfloat16)
                self.line_copy(
                    micro, rank - 1, slot, homeward(depth, rank) * 2 + side
                ).start()

    def close(self, micro):
        place, lane, depth, side, _, _ = whereabouts()
        self.keep[micro] = self.keep[micro] + self.line_value(micro, depth)

        @pl.when(middle(depth) == 1)
        def _():
            self.keep[micro] = self.keep[micro] + self.line_value(micro, 4)

        for rank in range(4):
            self.far_copy(micro, rank, place).wait_send()
        for rank in range(3):
            self.line_copy(micro, rank, 0, place).wait_send()


class Channels:
    def __init__(self, stage, got, stage_sem, got_sem, values, out_sem, in_sem):
        self.stage, self.got, self.stage_sem, self.got_sem = stage, got, stage_sem, got_sem
        self.values, self.out_sem, self.in_sem = values, out_sem, in_sem

    def piece(self, slot, target, block, lane):
        return push(
            self.stage.at[slot, block],
            self.got.at[lane, block],
            self.stage_sem.at[slot, block],
            self.got_sem.at[lane, block],
            lax.axis_index("batch"),
            target,
        )

    def send(self, part, block, micro):
        _, lane, _, _, upper, core = whereabouts()
        for half in range(2):
            piece = part[:, half * LANES : (half + 1) * LANES]
            target = half * 2 + micro

            @pl.when(target == lane)
            def _():
                self.got[lane, block] = piece

            @pl.when(target != lane)
            def _():
                self.stage[target, block] = piece
                self.piece(target, target, block, lane).start()

    def collect(self, micro, take):
        _, lane, _, _, _, core = whereabouts()

        @pl.when(core == micro)
        def _():
            def body(block, _):
                for step in range(1, 4):
                    other = (lane + step) % 4
                    self.piece(other, other, block, other).wait_recv()
                take(block)
                return 0

            lax.fori_loop(0, 8, body, 0)

    def value(self, block):
        result = self.got[0, block].astype(jnp.float32)
        for other in range(1, 4):
            result = result + self.got[other, block].astype(jnp.float32)
        return result

    def sent(self):
        _, lane, _, _, _, _ = whereabouts()

        def body(block, _):
            for step in range(1, 4):
                other = (lane + step) % 4
                self.piece(other, other, block, lane).wait_send()
            return 0

        lax.fori_loop(0, 8, body, 0)

    def chunk(self, path, half, micro, chunk, place_lane):
        here = self.values.at[half, micro, pl.ds(2 * chunk, 2)]
        return push(
            here,
            here,
            self.out_sem.at[path, chunk],
            self.in_sem.at[half, micro, chunk],
            lax.axis_index("batch"),
            place_lane,
        )

    def spread(self, chunk):
        _, lane, _, _, upper, core = whereabouts()
        self.chunk(0, upper, core, chunk, 2 - 2 * upper + core).start()
        self.chunk(1, upper, core, chunk, upper * 2 + 1 - core).start()

    def relay(self, micro):
        _, lane, _, _, upper, core = whereabouts()

        @pl.when(core == micro)
        def _():
            for chunk in range(4):
                copy = self.chunk(2, 1 - upper, core, chunk, upper * 2 + 1 - core)
                copy.wait_recv()
                copy.start()

    def finish(self, micro):
        _, lane, _, _, upper, core = whereabouts()

        @pl.when(core != micro)
        def _():
            for chunk in range(4):
                for half in range(2):
                    self.chunk(0, half, micro, chunk, lane).wait_recv()

    def close(self):
        _, lane, _, _, upper, core = whereabouts()
        for chunk in range(4):
            for path in range(3):
                self.chunk(path, upper, core, chunk, lane).wait_send()


def middle_kernel(
    count,
    block_ref,
    head_ref,
    distil_ref,
    mask_ref,
    depth_cot,
    segment_cot,
    bias_ref,
    mine_ref,
    depth_out,
    segment_out,
    distil_grad,
    gate_sums,
    head_sums,
    back_out,
    head_grad,
    block_all,
    head_weight,
    mixed,
    mixed_back,
    turned,
    columns,
    acts,
    norm_ref,
    head_back,
    grads_all,
    packed,
    own_stage,
    own_got,
    cot_all,
    stage,
    got,
    part_ref,
    keep,
    far_buf,
    far_got,
    line_buf,
    line_got,
    stats,
    *sems,
):
    place, lane, depth, side, upper, core = whereabouts()
    half_width = LANES // 2
    source = place // 2 == lane
    low = lax.broadcasted_iota(jnp.int32, (PIXELS, LANES), 1) < half_width
    gather = Gather(block_all, *sems[0:3], 2)
    gather_back = Gather(grads_all, *sems[3:6], 2)
    reduce = Reduce(part_ref, keep, far_buf, far_got, line_buf, line_got, sems[6:10])
    ahead = Channels(stage, got, sems[10], sems[11], acts, sems[12], sems[13])
    behind = Channels(stage, got, sems[10], sems[11], head_back, sems[14], sems[15])
    own_sem, own_recv, cot_sem, cot_recv = sems[16:20]

    greet(batch_peers() + chan_peers())
    block_all[place] = block_ref[...]
    gather.start(0)
    clear_edges(turned)
    for number in range(9):
        head_weight[number * 512 : (number + 1) * 512] = head_ref[number].T
    for micro in range(2):
        first, second = (ref[micro].astype(jnp.float32) for ref in (depth_cot, segment_cot))
        packed[0, micro] = jnp.where(low, first, pltpu.roll(second, half_width, 1)).astype(
            jnp.bfloat16
        )
        packed[1, micro] = jnp.where(low, pltpu.roll(first, half_width, 1), second).astype(
            jnp.bfloat16
        )

    def cot_copy(parity, slot, target):
        return push(
            packed.at[parity], cot_all.at[slot], cot_sem.at[parity], cot_recv.at[slot], target, lane
        )

    def forward_step(step, _):
        block, micro = gather.next(step)
        fill_columns(block_all[block, micro], mask_ref[block, micro], turned, columns)
        part = jnp.dot(columns[...], head_weight[...], preferred_element_type=jnp.float32)
        ahead.send(part.astype(jnp.bfloat16), block, micro)

        @pl.when(step == 0)
        def _():
            prepare_mixed()

        @pl.when(step == 2)
        def _():
            for parity in range(2):
                target = 2 * lane + parity

                @pl.when(target == place)
                def _():
                    cot_all[place] = packed[parity]

                @pl.when(target != place)
                def _():
                    cot_copy(parity, place, target).start()

        @pl.when(step == 4)
        def _():
            for number in range(9):
                mixed_back[number * 512 : (number + 1) * 512] = mixed[
                    number * 256 : (number + 1) * 256
                ].T

        @pl.when(step == 10)
        def _():
            normalize(0)

        @pl.when(step == 14)
        def _():
            ahead.relay(0)

        return 0

    def prepare_mixed():
        width = half_width
        for number in range(9):
            for stream in range(2):
                for head in range(4):
                    index = head - SOURCE_START[stream]
                    rows = slice(number * 256 + head * width, number * 256 + (head + 1) * width)
                    left = slice(2 * stream * LANES, (2 * stream + 1) * LANES)
                    right = slice((2 * stream + 1) * LANES, (2 * stream + 2) * LANES)
                    nothing = jnp.zeros((width, LANES), jnp.bfloat16)
                    mixed[rows, left] = (
                        distil_ref[stream, number, 0] if head == OWN_HEAD[stream] else nothing
                    )
                    mixed[rows, right] = (
                        distil_ref[stream, number, 1 + index] if 0 <= index < 3 else nothing
                    )

    def normalize(micro):
        zero = jnp.zeros((1, LANES), jnp.float32)

        @pl.when(core == micro)
        def _():
            stats[0:2] = jnp.zeros((2, LANES), jnp.float32)

        def take(block):
            value = ahead.value(block)
            norm_ref[block] = value
            stats[0:1] += jnp.sum(value, axis=0, keepdims=True)
            stats[1:2] += jnp.sum(value * value, axis=0, keepdims=True)

        ahead.collect(micro, take)

        @pl.when(core == micro)
        def _():
            center = stats[0:1] / count
            inverse = lax.rsqrt(stats[1:2] / count - center * center + EPSILON)
            stats[2:3] = inverse

            def activate(chunk, _):
                for item in range(2):
                    block = 2 * chunk + item
                    normed = (norm_ref[block] - center) * inverse
                    norm_ref[block] = normed
                    out = normed * mine_ref[0:1] + mine_ref[1:2]
                    acts[upper, core, block] = (out * jax.nn.sigmoid(out)).astype(jnp.bfloat16)
                ahead.spread(chunk)
                return 0

            lax.fori_loop(0, 4, activate, 0)

    lax.fori_loop(0, 16, forward_step, 0)
    ahead.finish(0)

    def own_copy(block, micro, slot, target):
        return push(
            own_stage.at[block, micro],
            own_got.at[slot, micro],
            own_sem.at[block, micro],
            own_recv.at[slot, micro],
            target,
            lane,
        )

    def send_own(micro):
        @pl.when(source)
        def _():
            own_got[place % 2, micro] = jnp.where(
                low, acts[0, micro, place], acts[1, micro, place]
            )

            def pack(step, _):
                block = (place + step) % 8
                own_stage[block, micro] = jnp.where(
                    low, acts[0, micro, block], acts[1, micro, block]
                )
                own_copy(block, micro, place % 2, block).start()
                return 0

            lax.fori_loop(1, 8, pack, 0)

    send_own(0)

    def act_value(block, micro):
        return jnp.concatenate([acts[half, micro, block] for half in range(2)], axis=1)

    def gate(micro):
        reduce.close(micro)
        for parity in range(2):
            @pl.when(2 * lane + parity != place)
            def _():
                own_copy(0, micro, parity, place).wait_recv()

        for stream, cot_ref in enumerate((depth_cot, segment_cot)):
            first = own_got[0, micro].astype(jnp.float32)
            second = own_got[1, micro].astype(jnp.float32)
            if stream == 0:
                second = pltpu.roll(second, half_width, 1)
            else:
                first = pltpu.roll(first, half_width, 1)
            own = jnp.where(low, first, second)
            column = 2 * stream * LANES
            gates = jax.nn.sigmoid(
                keep[micro, :, column : column + LANES] + bias_ref[stream : stream + 1]
            )
            message = keep[micro, :, column + LANES : column + 2 * LANES]
            cot = cot_ref[micro].astype(jnp.float32)
            out_ref = (depth_out, segment_out)[stream]
            out_ref[micro] = (own + gates * message).astype(jnp.bfloat16)
            gate_grad = (cot * message * gates * (1.0 - gates)).astype(jnp.bfloat16)
            bias_sum = jnp.sum(gate_grad.astype(jnp.float32), axis=0, keepdims=True)
            if micro == 0:
                gate_sums[stream : stream + 1] = bias_sum
            else:
                gate_sums[stream : stream + 1] += bias_sum
            grads_all[place, micro, :, column : column + LANES] = gate_grad
            grads_all[place, micro, :, column + LANES : column + 2 * LANES] = (cot * gates).astype(
                jnp.bfloat16
            )

    def distil_step(step, _):
        block, micro = reduce.block(step)
        fill_columns(act_value(block, micro), mask_ref[block, micro], turned, columns)
        part_ref[...] = jnp.dot(
            columns[:, 0 : 9 * 256], mixed[...], preferred_element_type=jnp.float32
        )
        reduce.step(step)

        @pl.when(step == 1)
        def _():
            normalize(1)

        @pl.when(step == 4)
        def _():
            ahead.relay(1)

        @pl.when(step == 6)
        def _():
            ahead.finish(1)
            send_own(1)

        @pl.when(step == 11)
        def _():
            gate(0)
            gather_back.start(0)

        return 0

    lax.fori_loop(0, 16, distil_step, 0)
    gate(1)
    ahead.sent()
    ahead.close()
    distil_grad[...] = jnp.zeros_like(distil_grad)

    @pl.when(source)
    def _():
        for step in range(1, 8):
            other = (place + step) % 8
            cot_copy(0, other, place).wait_recv()

    def back_step(step, _):
        block, micro = gather_back.next(step)
        fill_columns(
            grads_all[block, micro], mask_ref[block, micro], turned, columns, flip=True
        )
        part = jnp.dot(columns[...], mixed_back[...], preferred_element_type=jnp.float32)
        extra = cot_all[block, micro].astype(jnp.float32)
        part = jnp.concatenate(
            [
                part[:, :LANES] + jnp.where(low & source, extra, 0.0),
                part[:, LANES:] + jnp.where(low | ~source, 0.0, extra),
            ],
            axis=1,
        )
        behind.send(part.astype(jnp.bfloat16), block, micro)
        value = act_value(block, micro).T
        width = half_width
        for number in range(9):
            product = jnp.dot(
                value,
                columns[:, number * 512 : (number + 1) * 512],
                preferred_element_type=jnp.float32,
            )
            for stream in range(2):
                for index in range(4):
                    head = OWN_HEAD[stream] if index == 0 else SOURCE_START[stream] + index - 1
                    column = (2 * stream + (index > 0)) * LANES
                    distil_grad[stream, number, index] += product[
                        head * width : (head + 1) * width, column : column + LANES
                    ]

        @pl.when(step == 10)
        def _():
            normalize_back(0)

        @pl.when(step == 14)
        def _():
            behind.relay(0)

        return 0

    def normalize_back(micro):
        @pl.when(core == micro)
        def _():
            stats[4:6] = jnp.zeros((2, LANES), jnp.float32)

        def spot(block):
            return pl.ds(block % 2 * PIXELS, PIXELS), pl.ds(block // 2 * LANES, LANES)

        def take(block):
            normed = norm_ref[block]
            value = behind.value(block) * silu_slope(normed * mine_ref[0:1] + mine_ref[1:2])
            wide_ref = head_grad
            wide_ref[block, :, 0:LANES] = value
            stats[4:5] += jnp.sum(value, axis=0, keepdims=True)
            stats[5:6] += jnp.sum(value * normed, axis=0, keepdims=True)

        behind.collect(micro, take)

        @pl.when(core == micro)
        def _():
            shift_sum, scale_sum = stats[4:5], stats[5:6]
            head_sums[0:1] = scale_sum
            head_sums[1:2] = shift_sum
            factor = mine_ref[0:1] * stats[2:3]

            def activate(chunk, _):
                for item in range(2):
                    block = 2 * chunk + item
                    value = head_grad[block, :, 0:LANES]
                    head_back[upper, core, block] = (
                        factor * (value - (shift_sum + norm_ref[block] * scale_sum) / count)
                    ).astype(jnp.bfloat16)
                behind.spread(chunk)
                return 0

            lax.fori_loop(0, 4, activate, 0)

    lax.fori_loop(0, 16, back_step, 0)
    behind.finish(0)

    def head_value(block, micro):
        return jnp.concatenate([head_back[half, micro, block] for half in range(2)], axis=1)

    def weigh(block, micro):
        fill_columns(block_all[block, micro], mask_ref[block, micro], turned, columns)
        value = head_value(block, micro).T
        for number in range(9):
            head_grad[number] += jnp.dot(
                value,
                columns[:, number * 512 : (number + 1) * 512],
                preferred_element_type=jnp.float32,
            )

    def block_step(step, _):
        block, micro = reduce.block(step)
        fill_columns(
            head_value(block, micro), mask_ref[block, micro], turned, columns, flip=True
        )
        part_ref[...] = jnp.dot(
            columns[:, 0 : 9 * 256],
            head_ref[...].reshape(9 * 256, 512),
            preferred_element_type=jnp.float32,
        )
        reduce.step(step)

        @pl.when(step == 1)
        def _():
            normalize_back(1)
            head_grad[...] = jnp.zeros_like(head_grad)

        @pl.when(step == 4)
        def _():
            behind.relay(1)

        @pl.when(step == 6)
        def _():
            behind.finish(1)

        @pl.when(step > 1)
        def _():
            weigh(block, micro)

        return 0

    lax.fori_loop(0, 16, block_step, 0)
    for step in range(2):
        block, micro = reduce.block(step)
        weigh(block, micro)
    for micro in range(2):
        reduce.close(micro)
        back_out[micro_rows(micro)] = keep[micro]
    behind.sent()
    behind.close()
    gather.close()
    gather_back.close()
    for parity in range(2):
        @pl.when(2 * lane + parity != place)
        def _():
            cot_copy(parity, place, place).wait_send()

    @pl.when(source)
    def _():
        for micro in range(2):
            for step in range(1, 8):
                own_copy((place + step) % 8, micro, 0, place).wait_send()


def run_middle(count, *arrays):
    f32, bf16 = jnp.float32, jnp.bfloat16
    block = (PIXELS, 512)
    dma = pltpu.SemaphoreType.DMA
    return pl.pallas_call(
        functools.partial(middle_kernel, count),
        name="middle",
        out_shape=(
            jax.ShapeDtypeStruct((2, PIXELS, LANES), bf16),
            jax.ShapeDtypeStruct((2, PIXELS, LANES), bf16),
            jax.ShapeDtypeStruct((2, 9, 4, 64, LANES), f32),
            jax.ShapeDtypeStruct((2, LANES), f32),
            jax.ShapeDtypeStruct((2, LANES), f32),
            jax.ShapeDtypeStruct((2 * PIXELS, 512), f32),
            jax.ShapeDtypeStruct((9, 256, 512), f32),
        ),
        in_specs=vmem(8),
        out_specs=tuple(vmem(7)),
        scratch_shapes=[
            pltpu.VMEM((8, 2) + block, bf16),
            pltpu.VMEM((9 * 512, 256), bf16),
            pltpu.VMEM((9 * 256, 512), bf16),
            pltpu.VMEM((9 * 512, 256), bf16),
            pltpu.VMEM((3, 2 * PAD + PIXELS, 512), bf16),
            pltpu.VMEM((PIXELS, 9 * 512), bf16),
            pltpu.VMEM((2, 2, 8, PIXELS, LANES), bf16),
            pltpu.VMEM((8, PIXELS, LANES), f32),
            pltpu.VMEM((2, 2, 8, PIXELS, LANES), bf16),
            pltpu.VMEM((8, 2) + block, bf16),
            pltpu.VMEM((2, 2, PIXELS, LANES), bf16),
            pltpu.VMEM((8, 2, PIXELS, LANES), bf16),
            pltpu.VMEM((2, 2, PIXELS, LANES), bf16),
            pltpu.VMEM((8, 2, PIXELS, LANES), bf16),
            pltpu.VMEM((4, 8, PIXELS, LANES), bf16),
            pltpu.VMEM((4, 8, PIXELS, LANES), bf16),
            pltpu.VMEM(block, f32),
            pltpu.VMEM((2,) + block, f32),
            pltpu.VMEM((2, 4) + block, bf16),
            pltpu.VMEM((2, 4) + block, bf16),
            pltpu.VMEM((2, 3) + block, bf16),
            pltpu.VMEM((2, 5) + block, bf16),
            pltpu.VMEM((8, LANES), f32),
        ]
        + gather_sems(2) * 2
        + [dma((2, 4)), dma((2, 4)), dma((2, 3)), dma((2, 5))]
        + [dma((4, 8)), dma((4, 8))]
        + [dma((3, 4)), dma((2, 2, 4))] * 2
        + [dma((8, 2)), dma((2, 2)), dma((2,)), dma((8,))],
        compiler_params=kernel_params(2),
    )(*arrays)


def stationary_local(
    features,
    image_ids,
    reduce_weight,
    spatial_weight,
    expand_weight,
    head_weights,
    distil_weights,
    block_scale,
    block_shift,
    head_scale,
    head_shift,
    gate_bias,
    output_scale,
    output_shift,
    depth_cotangent,
    segment_cotangent,
):
    canvases, row_count, column_count = image_ids.shape
    pixels = row_count * column_count
    count = float(lax.axis_size("batch") * pixels)
    x = features.reshape(canvases, pixels, -1)
    ids = jnp.broadcast_to(
        image_ids.reshape(canvases, pixels, 1).astype(jnp.float32), (canvases, pixels, LANES)
    )
    block_params = (block_scale, block_shift)
    output_params = (output_scale[None], output_shift[None])
    (
        block_out,
        norm3,
        inverse3,
        norm12,
        inverse12,
        act1,
        act2,
        reduce_all,
        spatial_all,
        expand_all,
        mask_all,
        mine,
        mask,
    ) = run_front(
        count,
        x,
        ids,
        reduce_weight.T,
        spatial_weight,
        expand_weight,
        *block_params,
        *output_params,
        head_scale,
        head_shift,
    )
    depth_out, segment_out, distil_grad, gate_sums, head_sums, block_grad, heads_grad = run_middle(
        count,
        block_out,
        head_weights.transpose(0, 2, 3, 1).reshape(9, -1, head_weights.shape[1]),
        distil_weights,
        mask_all,
        depth_cotangent.reshape(canvases, pixels, LANES),
        segment_cotangent.reshape(canvases, pixels, LANES),
        gate_bias,
        mine,
    )
    (
        features_grad,
        reduce_grad,
        spatial_grad,
        expand_grad,
        block_scale_grad,
        block_shift_grad,
        head_scale_grad,
        head_shift_grad,
        gate_grad,
        output_scale_grad,
        output_shift_grad,
    ) = run_rear(
        count,
        block_grad,
        x,
        norm3,
        inverse3,
        norm12,
        inverse12,
        act1,
        act2,
        reduce_all,
        spatial_all,
        expand_all,
        mask,
        *block_params,
        *output_params,
        head_sums,
        gate_sums,
    )
    heads_grad = heads_grad.reshape(9, 4, -1, head_weights.shape[1]).transpose(0, 3, 1, 2)
    return (
        depth_out.reshape(depth_cotangent.shape),
        segment_out.reshape(depth_cotangent.shape),
        features_grad.reshape(features.shape),
        reduce_grad.T,
        spatial_grad,
        expand_grad,
        heads_grad,
        distil_grad,
        block_scale_grad,
        block_shift_grad,
        head_scale_grad,
        head_shift_grad,
        gate_grad,
        output_scale_grad[0],
        output_shift_grad[0],
    )


def solution(mesh):
    fits = dict(mesh.shape) == {"batch": 8, "chan": 4}
    local = stationary_local if fits else gathered_local
    placed = (
        P("batch", None, None, "chan"),
        P("batch", None, None),
        P("chan", "batch"),
        P(None, "batch", "chan"),
        P("batch", "chan"),
        P(None, "chan", None, "batch"),
        P(None, None, None, "batch", "chan"),
        P(None, "chan"),
        P(None, "chan"),
        P(None, "chan"),
        P(None, "chan"),
        P(None, "chan"),
        P("chan"),
        P("chan"),
        P("batch", None, None, "chan"),
        P("batch", None, None, "chan"),
    )
    return jax.shard_map(
        local,
        mesh=mesh,
        in_specs=placed,
        out_specs=(
            P("batch", None, None, "chan"),
            P("batch", None, None, "chan"),
            P("batch", None, None, "chan"),
            P("chan", "batch"),
            P(None, "batch", "chan"),
            P("batch", "chan"),
            P(None, "chan", None, "batch"),
            P(None, None, None, "batch", "chan"),
            P(None, "chan"),
            P(None, "chan"),
            P(None, "chan"),
            P(None, "chan"),
            P(None, "chan"),
            P("chan"),
            P("chan"),
        ),
        check_vma=False,
    )
```

```python
import functools

import jax
import jax.numpy as jnp
from jax import lax
from jax.experimental import pallas as pl
from jax.experimental.pallas import tpu as pltpu
from jax.sharding import PartitionSpec as P

EPSILON = 1e-05
OFFSETS = ((-1, -1), (-1, 0), (-1, 1), (0, -1), (0, 0), (0, 1), (1, -1), (1, 0), (1, 1))
OWN_HEAD = (0, 3)
SOURCE_START = (1, 0)


def silu_slope(values):
    sig = jax.nn.sigmoid(values)
    return sig * (1.0 + values * (1.0 - sig))


def shifted(values, vertical, lateral):
    row_count, column_count = (values.shape[1], values.shape[2])
    widths = [(0, 0)] * values.ndim
    widths[1] = (1, 1)
    widths[2] = (1, 1)
    padded = jnp.pad(values, widths)
    return padded[
        :, 1 + vertical : 1 + vertical + row_count, 1 + lateral : 1 + lateral + column_count
    ]


def tap_masks(image_ids):
    row_count, column_count = (image_ids.shape[1], image_ids.shape[2])
    padded = jnp.pad(image_ids, ((0, 0), (1, 1), (1, 1)), constant_values=-1)
    masks = []
    for vertical, lateral in OFFSETS:
        beside = padded[
            :, 1 + vertical : 1 + vertical + row_count, 1 + lateral : 1 + lateral + column_count
        ]
        masks.append((beside == image_ids).astype(jnp.float32))
    return jnp.stack(masks)


def conv_forward(inputs, weight, masks):
    total = 0.0
    for number, (vertical, lateral) in enumerate(OFFSETS):
        moved = shifted(inputs, vertical, lateral) * masks[number][..., None].astype(inputs.dtype)
        total = total + jnp.einsum(
            "nhwc,co->nhwo", moved, weight[number], preferred_element_type=jnp.float32
        )
    return total


def conv_input_grad(grads, weight, masks):
    total = 0.0
    for number, (vertical, lateral) in enumerate(OFFSETS):
        term = jnp.einsum(
            "nhwo,co->nhwc", grads, weight[number], preferred_element_type=jnp.float32
        )
        total = total + shifted(term * masks[number][..., None], -vertical, -lateral)
    return total


def conv_weight_grad(inputs, grads, masks):
    pieces = []
    for number, (vertical, lateral) in enumerate(OFFSETS):
        moved = shifted(inputs, vertical, lateral) * masks[number][..., None].astype(inputs.dtype)
        pieces.append(jnp.einsum("nhwc,nhwo->co", moved, grads, preferred_element_type=jnp.float32))
    return jnp.stack(pieces)


def pixel_sum(values):
    return jnp.sum(values, axis=(0, 1, 2))


def normalize(values, scale, shift, count):
    total, squares = lax.psum((pixel_sum(values), pixel_sum(values * values)), "batch")
    center = total / count
    inverse = lax.rsqrt(squares / count - center * center + EPSILON)
    normed = (values - center) * inverse
    return (normed, inverse, normed * scale + shift)


def grad_sums(first_sum, second_sum):
    return lax.psum((first_sum, second_sum), "batch")


def normalize_back(grads, normed, inverse, scale, shift_sum, scale_sum, count):
    return scale * inverse * (grads - (shift_sum + normed * scale_sum) / count)


def channel_gather(values):
    return lax.all_gather(values, "chan", axis=4, tiled=True)


def channel_sum(values):
    return lax.psum_scatter(
        values.astype(jnp.bfloat16), "chan", scatter_dimension=4, tiled=True
    ).astype(jnp.float32)


def fetch_weights(reduce_weight, spatial_weight, expand_weight, head_weights, distil_weights):
    return (
        lax.all_gather(reduce_weight, "batch", axis=1, tiled=True),
        lax.all_gather(spatial_weight, "batch", axis=1, tiled=True),
        lax.all_gather(expand_weight, "batch", axis=0, tiled=True),
        lax.all_gather(head_weights, "batch", axis=3, tiled=True),
        lax.all_gather(distil_weights, "batch", axis=3, tiled=True),
    )


def scatter_weights(grads):
    reduce_grad, spatial_grad, expand_grad, heads_grad, distil_grad = grads
    return (
        lax.psum_scatter(reduce_grad, "batch", scatter_dimension=1, tiled=True),
        lax.psum_scatter(spatial_grad, "batch", scatter_dimension=1, tiled=True),
        lax.psum_scatter(expand_grad, "batch", scatter_dimension=0, tiled=True),
        lax.psum_scatter(heads_grad, "batch", scatter_dimension=3, tiled=True),
        lax.psum_scatter(distil_grad, "batch", scatter_dimension=3, tiled=True),
    )


def micro_step(inputs, image_ids, depth_cot, segment_cot, gathered, small, batch_count):
    reduce_full, spatial_full, expand_full, heads_full, distil_full = gathered
    block_scale, block_shift, head_scale, head_shift, gate_bias, output_scale, output_shift = small
    masks = tap_masks(image_ids)
    canvases, row_count, column_count = image_ids.shape
    count = float(batch_count * canvases * row_count * column_count)
    first_partial = jnp.einsum(
        "nhwc,co->nhwo", inputs, reduce_full, preferred_element_type=jnp.float32
    )
    first = channel_sum(first_partial[:, :, :, None, :])
    first_norm, first_inv, first_out = normalize(first, block_scale[0:1], block_shift[0:1], count)
    first_act = jax.nn.silu(first_out).astype(jnp.bfloat16)
    first_full = channel_gather(first_act)[:, :, :, 0, :]
    second = conv_forward(first_full, spatial_full, masks)[:, :, :, None, :]
    second_norm, second_inv, second_out = normalize(
        second, block_scale[1:2], block_shift[1:2], count
    )
    second_act = jax.nn.silu(second_out).astype(jnp.bfloat16)
    second_full = channel_gather(second_act)[:, :, :, 0, :]
    third = jnp.einsum(
        "nhwc,co->nhwo", second_full, expand_full, preferred_element_type=jnp.float32
    )[:, :, :, None, :]
    third_norm, third_inv, third_out = normalize(
        third, output_scale[None], output_shift[None], count
    )
    summed = third_out[:, :, :, 0, :] + inputs.astype(jnp.float32)
    block_out = jax.nn.silu(summed).astype(jnp.bfloat16)
    heads_flat = heads_full.reshape(heads_full.shape[0], heads_full.shape[1], -1)
    head_partial = conv_forward(block_out, heads_flat, masks)
    head_pre = channel_sum(
        head_partial.reshape(head_partial.shape[:3] + (heads_full.shape[2], heads_full.shape[3]))
    )
    head_norm, head_inv, head_out = normalize(head_pre, head_scale, head_shift, count)
    head_act = jax.nn.silu(head_out).astype(jnp.bfloat16)
    head_full = channel_gather(head_act)
    head_width = head_full.shape[4]
    gate_pre = [0.0, 0.0]
    message = [0.0, 0.0]
    for number, (vertical, lateral) in enumerate(OFFSETS):
        moved = shifted(head_full, vertical, lateral) * masks[number][:, :, :, None, None].astype(
            jnp.bfloat16
        )
        for stream in range(2):
            weights_here = distil_full[stream, number]
            first_source = SOURCE_START[stream]
            sources = moved[:, :, :, first_source : first_source + 3].reshape(
                moved.shape[:3] + (3 * head_width,)
            )
            gate_pre[stream] = gate_pre[stream] + jnp.einsum(
                "nhwc,co->nhwo",
                moved[:, :, :, OWN_HEAD[stream]],
                weights_here[0],
                preferred_element_type=jnp.float32,
            )
            message[stream] = message[stream] + jnp.einsum(
                "nhwc,co->nhwo",
                sources,
                weights_here[1:].reshape(3 * head_width, -1),
                preferred_element_type=jnp.float32,
            )
    cotangents = (depth_cot.astype(jnp.float32), segment_cot.astype(jnp.float32))
    outputs, message_grads, gate_grads = ([], [], [])
    for stream in range(2):
        gate_value = jax.nn.sigmoid(gate_pre[stream] + gate_bias[stream])
        own_feature = head_act[:, :, :, OWN_HEAD[stream]].astype(jnp.float32)
        outputs.append((own_feature + gate_value * message[stream]).astype(jnp.bfloat16))
        message_grads.append((cotangents[stream] * gate_value).astype(jnp.bfloat16))
        gate_grads.append(
            (cotangents[stream] * message[stream] * gate_value * (1.0 - gate_value)).astype(
                jnp.bfloat16
            )
        )
    spread_grad = 0.0
    distil_parts = [[], []]
    for number, (vertical, lateral) in enumerate(OFFSETS):
        tap_mask = masks[number][:, :, :, None, None]
        moved = shifted(head_full, vertical, lateral) * tap_mask.astype(jnp.bfloat16)
        tap_grad = jnp.zeros(head_full.shape, jnp.float32)
        for stream in range(2):
            weights_here = distil_full[stream, number]
            first_source = SOURCE_START[stream]
            sources = moved[:, :, :, first_source : first_source + 3].reshape(
                moved.shape[:3] + (3 * head_width,)
            )
            own_grad = jnp.einsum(
                "nhwo,co->nhwc",
                gate_grads[stream],
                weights_here[0],
                preferred_element_type=jnp.float32,
            )
            source_grad = jnp.einsum(
                "nhwo,co->nhwc",
                message_grads[stream],
                weights_here[1:].reshape(3 * head_width, -1),
                preferred_element_type=jnp.float32,
            )
            tap_grad = tap_grad.at[:, :, :, OWN_HEAD[stream]].add(own_grad)
            tap_grad = tap_grad.at[:, :, :, first_source : first_source + 3].add(
                source_grad.reshape(source_grad.shape[:3] + (3, head_width))
            )
            gate_weight_grad = jnp.einsum(
                "nhwc,nhwo->co",
                moved[:, :, :, OWN_HEAD[stream]],
                gate_grads[stream],
                preferred_element_type=jnp.float32,
            )
            source_weight_grad = jnp.einsum(
                "nhwc,nhwo->co", sources, message_grads[stream], preferred_element_type=jnp.float32
            )
            distil_parts[stream].append(
                jnp.concatenate(
                    [gate_weight_grad[None], source_weight_grad.reshape(3, head_width, -1)], axis=0
                )
            )
        spread_grad = spread_grad + shifted(tap_grad * tap_mask, -vertical, -lateral)
    distil_grad = jnp.stack([jnp.stack(distil_parts[0]), jnp.stack(distil_parts[1])])
    head_grad = channel_sum(spread_grad)
    head_grad = (
        head_grad.at[:, :, :, OWN_HEAD[0]]
        .add(cotangents[0])
        .at[:, :, :, OWN_HEAD[1]]
        .add(cotangents[1])
    )
    head_grad = head_grad * silu_slope(head_out)
    gate_sums = jnp.stack(
        [pixel_sum(gate_grads[0].astype(jnp.float32)), pixel_sum(gate_grads[1].astype(jnp.float32))]
    )
    shift_sums, scale_sums = grad_sums(
        jnp.concatenate([pixel_sum(head_grad), gate_sums], axis=0), pixel_sum(head_grad * head_norm)
    )
    head_pre_grad = normalize_back(
        head_grad, head_norm, head_inv, head_scale, shift_sums[:4], scale_sums, count
    ).astype(jnp.bfloat16)
    head_pre_full = channel_gather(head_pre_grad)
    head_flat_grad = head_pre_full.reshape(head_pre_full.shape[:3] + (-1,))
    block_grad = conv_input_grad(head_flat_grad, heads_flat, masks)
    heads_grad = conv_weight_grad(block_out, head_flat_grad, masks).reshape(heads_full.shape)
    summed_grad = block_grad * silu_slope(summed)
    third_grad = summed_grad[:, :, :, None, :]
    third_shift, third_scale = grad_sums(pixel_sum(third_grad), pixel_sum(third_grad * third_norm))
    third_pre = normalize_back(
        third_grad, third_norm, third_inv, output_scale[None], third_shift, third_scale, count
    ).astype(jnp.bfloat16)[:, :, :, 0, :]
    expand_grad = jnp.einsum(
        "nhwc,nhwo->co", second_full, third_pre, preferred_element_type=jnp.float32
    )
    second_grad = channel_sum(
        jnp.einsum("nhwo,co->nhwc", third_pre, expand_full, preferred_element_type=jnp.float32)[
            :, :, :, None, :
        ]
    )
    second_grad = second_grad * silu_slope(second_out)
    second_shift, second_scale = grad_sums(
        pixel_sum(second_grad), pixel_sum(second_grad * second_norm)
    )
    second_pre = normalize_back(
        second_grad, second_norm, second_inv, block_scale[1:2], second_shift, second_scale, count
    ).astype(jnp.bfloat16)[:, :, :, 0, :]
    spatial_grad = conv_weight_grad(first_full, second_pre, masks)
    first_grad = channel_sum(conv_input_grad(second_pre, spatial_full, masks)[:, :, :, None, :])
    first_grad = first_grad * silu_slope(first_out)
    first_shift, first_scale = grad_sums(pixel_sum(first_grad), pixel_sum(first_grad * first_norm))
    first_pre = normalize_back(
        first_grad, first_norm, first_inv, block_scale[0:1], first_shift, first_scale, count
    ).astype(jnp.bfloat16)
    first_pre_full = channel_gather(first_pre)[:, :, :, 0, :]
    reduce_grad = jnp.einsum(
        "nhwc,nhwo->co", inputs, first_pre_full, preferred_element_type=jnp.float32
    )
    input_grad = summed_grad + jnp.einsum(
        "nhwo,co->nhwc", first_pre_full, reduce_full, preferred_element_type=jnp.float32
    )
    weight_grads = (reduce_grad, spatial_grad, expand_grad, heads_grad, distil_grad)
    small_grads = (
        jnp.concatenate([first_scale, second_scale], axis=0),
        jnp.concatenate([first_shift, second_shift], axis=0),
        scale_sums,
        shift_sums[:4],
        shift_sums[4:],
        third_scale[0],
        third_shift[0],
    )
    return (outputs[0], outputs[1], input_grad, weight_grads, small_grads)


def gathered_local(
    features,
    image_ids,
    reduce_weight,
    spatial_weight,
    expand_weight,
    head_weights,
    distil_weights,
    block_scale,
    block_shift,
    head_scale,
    head_shift,
    gate_bias,
    output_scale,
    output_shift,
    depth_cotangent,
    segment_cotangent,
):
    batch_count = lax.axis_size("batch")
    small = (
        block_scale,
        block_shift,
        head_scale,
        head_shift,
        gate_bias,
        output_scale,
        output_shift,
    )
    depth_list, segment_list, input_list = ([], [], [])
    weight_total = None
    small_total = None
    for micro_index in range(features.shape[0]):
        gathered = fetch_weights(
            reduce_weight, spatial_weight, expand_weight, head_weights, distil_weights
        )
        canvas_pick = slice(micro_index, micro_index + 1)
        depth_out, segment_out, input_grad, weight_grads, small_grads = micro_step(
            features[canvas_pick],
            image_ids[canvas_pick],
            depth_cotangent[canvas_pick],
            segment_cotangent[canvas_pick],
            gathered,
            small,
            batch_count,
        )
        weight_grads = scatter_weights(weight_grads)
        weight_total = (
            weight_grads
            if weight_total is None
            else jax.tree.map(jnp.add, weight_total, weight_grads)
        )
        small_total = (
            small_grads if small_total is None else jax.tree.map(jnp.add, small_total, small_grads)
        )
        depth_list.append(depth_out)
        segment_list.append(segment_out)
        input_list.append(input_grad)
    reduce_grad, spatial_grad, expand_grad, heads_grad, distil_grad = weight_total
    scale_mid, shift_mid, scale_heads, shift_heads, bias_gates, scale_out, shift_out = small_total
    return (
        jnp.concatenate(depth_list, axis=0),
        jnp.concatenate(segment_list, axis=0),
        jnp.concatenate(input_list, axis=0),
        reduce_grad,
        spatial_grad,
        expand_grad,
        heads_grad,
        distil_grad,
        scale_mid,
        shift_mid,
        scale_heads,
        shift_heads,
        bias_gates,
        scale_out,
        shift_out,
    )


MESH = pl.DeviceIdType.MESH
PIXELS = 256
PAD = 32
LANES = 128


def whereabouts():
    place, lane = lax.axis_index("batch"), lax.axis_index("chan")
    return place, lane, place // 2, place % 2, lane // 2, lane % 2


def ranked(depth, rank):
    high, low = depth // 2, depth % 2
    up, odd = rank // 2, rank % 2
    return (
        (1 - odd) * (1 - up) * depth
        + odd * (1 - up) * (1 + low)
        + (1 - odd) * up * (2 - 2 * low + high)
        + odd * up * (3 - 3 * high)
    )


def middle(depth):
    return (depth // 2 + depth % 2) % 2


def inner(depth):
    return 1 + depth % 2


def outer(depth):
    return 3 * (depth // 2)


def onward(depth, rank):
    second = (1 - rank % 2) * (rank // 2)
    return outer(depth) + second * (3 - depth - outer(depth))


def homeward(depth, rank):
    second = (1 - rank % 2) * (rank // 2) * middle(depth)
    return inner(depth) + second * (outer(depth) - inner(depth))


def staggered(step):
    late = ((step + 1) % 2) * ((step + 14) // 15) + step // 15
    return (1 - late) * ((step + 1) // 2) + late * (step // 2 - 1 + step // 15), late


def push(source, target, send_sem, recv_sem, place, lane):
    return pltpu.make_async_remote_copy(
        src_ref=source,
        dst_ref=target,
        send_sem=send_sem,
        recv_sem=recv_sem,
        device_id=(place, lane),
        device_id_type=MESH,
    )


def greet(peers):
    barrier = pltpu.get_barrier_semaphore()
    for place, lane in peers:
        pl.semaphore_signal(barrier, inc=1, device_id=(place, lane), device_id_type=MESH)
    pl.semaphore_wait(barrier, len(peers))


def batch_peers():
    place, lane, _, _, _, _ = whereabouts()
    return [((place + step) % 8, lane) for step in range(1, 8)]


def line_peers():
    place, lane, depth, side, _, _ = whereabouts()
    peers = [(ranked(depth, rank) * 2 + side, lane) for rank in range(1, 4)]
    return peers + [(depth * 2 + 1 - side, lane)]


def chan_peers():
    place, lane, _, _, _, _ = whereabouts()
    return [(place, (lane + step) % 4) for step in range(1, 4)]


class Gather:
    def __init__(self, values, recv, cross, line, parts):
        self.values, self.recv, self.cross, self.line, self.parts = values, recv, cross, line, parts

    def view(self, block, part):
        return self.values.at[block] if self.parts == 1 else self.values.at[block, part]

    def copy(self, block, part, sem, depth, side):
        lane = lax.axis_index("chan")
        here = self.view(block, part)
        return push(here, here, sem, self.recv.at[block, part], depth * 2 + side, lane)

    def start(self, part=0):
        place, lane, depth, side, _, _ = whereabouts()
        self.copy(place, part, self.line.at[0, 0, part], inner(depth), side).start()

        @pl.when(middle(depth) == 1)
        def _():
            self.copy(place, part, self.line.at[1, 0, part], outer(depth), side).start()

        self.copy(place, part, self.cross.at[0, part], depth, 1 - side).start()

    def near(self, rank, part=0):
        place, lane, depth, side, _, _ = whereabouts()
        block = ranked(depth, rank) * 2 + side
        self.copy(block, part, self.cross.at[rank, part], depth, side).wait_recv()

        @pl.when(middle(depth) == 1)
        def _():
            self.copy(block, part, self.line.at[0, rank, part], onward(depth, rank), side).start()

        self.copy(block, part, self.cross.at[rank, part], depth, 1 - side).start()

    def far(self, rank, part=0):
        place, lane, depth, side, _, _ = whereabouts()
        block = ranked(depth, rank) * 2 + 1 - side
        self.copy(block, part, self.cross.at[rank, part], depth, side).wait_recv()

    def next(self, step):
        place, lane, depth, side, _, _ = whereabouts()
        item, late = staggered(step)
        part, rank = item // 4, item % 4

        @pl.when((late == 0) & (rank > 0))
        def _():
            self.near(rank, part)

        @pl.when((late == 0) & (item == 1))
        def _():
            self.start(1)

        @pl.when(late == 1)
        def _():
            self.far(rank, part)

        return ranked(depth, rank) * 2 + (side + late) % 2, part

    def close(self):
        place, lane, depth, side, _, _ = whereabouts()
        for part in range(self.parts):
            for rank in range(4):
                self.copy(place, part, self.cross.at[rank, part], depth, side).wait_send()
            self.copy(place, part, self.line.at[0, 0, part], depth, side).wait_send()

            @pl.when(middle(depth) == 1)
            def _():
                self.copy(place, part, self.line.at[1, 0, part], depth, side).wait_send()
                for rank in range(1, 4):
                    self.copy(place, part, self.line.at[0, rank, part], depth, side).wait_send()


def gather_sems(parts):
    return [
        pltpu.SemaphoreType.DMA((8, parts)),
        pltpu.SemaphoreType.DMA((4, parts)),
        pltpu.SemaphoreType.DMA((2, 4, parts)),
    ]


def clear_edges(turned):
    edge = jnp.zeros((3, PAD, turned.shape[2]), turned.dtype)
    turned[:, 0:PAD] = edge
    turned[:, PAD + PIXELS :] = edge


def fill_columns(value, mask, turned, columns, row=0, flip=False):
    width = value.shape[1]
    lanes = slice(0, width)
    wide = value.astype(jnp.float32)
    inside = slice(PAD, PAD + PIXELS)
    turned[0, inside, lanes] = pltpu.roll(wide, 1, 0).astype(jnp.bfloat16)
    turned[1, inside, lanes] = value
    turned[2, inside, lanes] = pltpu.roll(wide, PIXELS - 1, 0).astype(jnp.bfloat16)
    for number, (vertical, lateral) in enumerate(OFFSETS):
        start = PAD + 32 * vertical
        slot = 8 - number if flip else number
        columns[row : row + PIXELS, slot * width : (slot + 1) * width] = (
            turned[lateral + 1, start : start + PIXELS, lanes] * mask[:, number : number + 1]
        )


def vmem(count):
    return [pl.BlockSpec(memory_space=pltpu.VMEM)] * count


def kernel_params(number):
    return pltpu.CompilerParams(
        collective_id=number, has_side_effects=True, vmem_limit_bytes=60 * 2**20
    )


class Exchange:
    def __init__(self, values, send, recv, axis):
        self.values, self.send, self.recv, self.axis = values, send, recv, axis

    def steps(self):
        place, lane, _, _, _, _ = whereabouts()
        if self.axis == "batch":
            return [(step - 1, (place + step) % 8, lane, (place + step) % 8) for step in range(1, 8)]
        return [(step - 1, place, (lane + step) % 4, (lane + step) % 4) for step in range(1, 4)]

    def mine(self):
        place, lane, _, _, _, _ = whereabouts()
        return place if self.axis == "batch" else lane

    def start(self):
        here = self.values.at[self.mine()]
        for number, place, lane, _ in self.steps():
            push(here, here, self.send.at[number], self.recv.at[self.mine()], place, lane).start()

    def wait(self):
        for number, place, lane, slot in self.steps():
            there = self.values.at[slot]
            push(there, there, self.send.at[number], self.recv.at[slot], place, lane).wait_recv()

    def close(self):
        here = self.values.at[self.mine()]
        for number, place, lane, _ in self.steps():
            push(here, here, self.send.at[number], self.recv.at[self.mine()], place, lane).wait_send()

    def total(self):
        result = self.values[0]
        for slot in range(1, self.values.shape[0]):
            result = result + self.values[slot]
        return result


class Pieces:
    def __init__(self, stage, got, send, recv):
        self.stage, self.got, self.send, self.recv = stage, got, send, recv

    def start(self, part):
        place, lane, _, _, _, _ = whereabouts()
        for slot in range(4):
            self.stage[slot] = part[:, slot * LANES : (slot + 1) * LANES].astype(jnp.bfloat16)
        for step in (2, 1, 3):
            slot = (lane + step) % 4
            push(
                self.stage.at[slot],
                self.got.at[lane],
                self.send.at[slot],
                self.recv.at[lane],
                place,
                slot,
            ).start()

    def finish(self):
        place, lane, _, _, _, _ = whereabouts()
        self.got[lane] = self.stage[lane]
        for step in range(1, 4):
            slot = (lane + step) % 4
            push(
                self.stage.at[slot],
                self.got.at[slot],
                self.send.at[slot],
                self.recv.at[slot],
                place,
                lane,
            ).wait()
        result = self.got[0].astype(jnp.float32)
        for slot in range(1, 4):
            result = result + self.got[slot].astype(jnp.float32)
        return result


def micro_rows(micro):
    return slice(micro * PIXELS, (micro + 1) * PIXELS)


def moments(value, other):
    rows = []
    for micro in range(2):
        part = value[micro_rows(micro)]
        rows.append(jnp.sum(part, axis=0, keepdims=True))
        rows.append(jnp.sum(part * other[micro_rows(micro)], axis=0, keepdims=True))
    return rows


def tile_rows(rows, height):
    width = rows[0].shape[1]
    return jnp.concatenate(rows + [jnp.zeros((height - len(rows), width), jnp.float32)], axis=0)


def normed_part(value, totals, micro, count):
    center = totals[2 * micro : 2 * micro + 1] / count
    inverse = lax.rsqrt(totals[2 * micro + 1 : 2 * micro + 2] / count - center * center + EPSILON)
    return (value[micro_rows(micro)] - center) * inverse, inverse


def dot_last(first, second):
    return lax.dot_general(
        first, second, (((1,), (1,)), ((), ())), preferred_element_type=jnp.float32
    )


def make_masks(ids_ref, mask_all):
    rows = 8 * ids_ref.shape[0]
    ids = ids_ref[...].reshape(rows, PIXELS).T
    pixel = lax.broadcasted_iota(jnp.int32, (PIXELS, rows), 0)
    taps = []
    for vertical, lateral in OFFSETS:
        offset = 32 * vertical + lateral
        beside = ids if offset == 0 else pltpu.roll(ids, (-offset) % PIXELS, 0)
        row, col = (pixel >> 5) + vertical, (pixel & 31) + lateral
        inside = (row >= 0) & (row < 8) & (col >= 0) & (col < 32)
        taps.append(jnp.where(inside & (beside == ids), 1.0, 0.0).astype(jnp.bfloat16))
    taps = jnp.concatenate(taps + [jnp.zeros_like(taps[0])], axis=1)
    item = lax.broadcasted_iota(jnp.int32, (10 * rows, LANES), 0)
    lane = lax.broadcasted_iota(jnp.int32, (10 * rows, LANES), 1)
    for block in range(8):
        for micro in range(2):
            chosen = jnp.where(item == lane * rows + (8 * block + micro), 1.0, 0.0)
            mask_all[block, micro] = jnp.dot(
                taps, chosen.astype(jnp.bfloat16), preferred_element_type=jnp.float32
            ).astype(jnp.bfloat16)


def front_kernel(
    count,
    x_ref,
    ids_ref,
    reduce_ref,
    spatial_ref,
    expand_ref,
    block_scale,
    block_shift,
    output_scale,
    output_shift,
    head_scale,
    head_shift,
    y_ref,
    norm3_ref,
    inverse3_ref,
    norm12_ref,
    inverse12_ref,
    act1_ref,
    act2_ref,
    reduce_all,
    spatial_all,
    expand_all,
    mask_all,
    mine_ref,
    mask_ref,
    turned,
    columns,
    stage,
    got,
    sums1,
    sums2,
    sums3,
    head_all,
    ids_all,
    *sems,
):
    place, lane, depth, side, upper, core = whereabouts()
    reduces = Gather(reduce_all, *sems[0:3], 1)
    spatials = Gather(spatial_all, *sems[3:6], 1)
    expands = Gather(expand_all, *sems[6:9], 1)
    ids = Exchange(ids_all, sems[9], sems[10], "batch")
    pieces = Pieces(stage, got, sems[11], sems[12])
    first_sums = Exchange(sums1, sems[13], sems[14], "batch")
    second_sums = Exchange(sums2, sems[15], sems[16], "batch")
    third_sums = Exchange(sums3, sems[17], sems[18], "batch")
    heads = Exchange(head_all, sems[19], sems[20], "chan")
    first_acts = Exchange(act1_ref, sems[21], sems[22], "chan")
    second_acts = Exchange(act2_ref, sems[23], sems[24], "chan")

    greet(batch_peers() + chan_peers())
    reduce_all[place] = reduce_ref[...]
    ids_all[place] = ids_ref[...]
    reduces.start()
    ids.start()
    spatial_all[place] = spatial_ref[...]
    expand_all[place] = expand_ref[...]
    head_all[lane, 0:4] = head_scale[...]
    head_all[lane, 4:8] = head_shift[...]
    heads.start()
    clear_edges(turned)
    for rank in range(1, 4):
        reduces.near(rank)
    spatials.start()
    for rank in range(4):
        reduces.far(rank)
    x = x_ref[...].reshape(2 * PIXELS, x_ref.shape[2])
    pieces.start(dot_last(x, reduce_all[...].reshape(512, 512)))
    ids.wait()
    make_masks(ids_all, mask_all)
    mask_ref[...] = mask_all[place]
    spatials.near(1)
    first = pieces.finish()
    sums1[place] = tile_rows(moments(first, first), 8)
    first_sums.start()
    spatials.near(2)
    expands.start()
    spatials.near(3)
    first_sums.wait()
    totals = first_sums.total()
    rows = []
    for micro in range(2):
        normed, inverse = normed_part(first, totals, micro, count)
        norm12_ref[0, micro_rows(micro)] = normed
        rows.append(inverse)
        out = normed * block_scale[0:1] + block_shift[0:1]
        act1_ref[lane, micro_rows(micro)] = (out * jax.nn.sigmoid(out)).astype(jnp.bfloat16)
    first_acts.start()
    expands.near(1)
    for rank in range(4):
        spatials.far(rank)
    expands.near(2)
    first_acts.wait()
    for micro in range(2):
        value = jnp.concatenate([act1_ref[slot, micro_rows(micro)] for slot in range(4)], axis=1)
        fill_columns(value, mask_all[place, micro], turned, columns, micro * PIXELS)
    second = jnp.zeros((2 * PIXELS, LANES), jnp.float32)
    for number in range(9):
        second = second + jnp.dot(
            columns[:, number * 512 : (number + 1) * 512],
            spatial_all[:, number].reshape(512, LANES),
            preferred_element_type=jnp.float32,
        )
    sums2[place] = tile_rows(moments(second, second), 8)
    second_sums.start()
    expands.near(3)
    second_sums.wait()
    totals = second_sums.total()
    for micro in range(2):
        normed, inverse = normed_part(second, totals, micro, count)
        norm12_ref[1, micro_rows(micro)] = normed
        rows.append(inverse)
        out = normed * block_scale[1:2] + block_shift[1:2]
        act2_ref[lane, micro_rows(micro)] = (out * jax.nn.sigmoid(out)).astype(jnp.bfloat16)
    second_acts.start()
    inverse12_ref[...] = tile_rows(rows, 8)
    heads.wait()
    half_width = LANES // 2
    low = lax.broadcasted_iota(jnp.int32, (1, LANES), 1) < half_width
    source = place // 2
    even = place % 2 == 0
    for kind in range(2):
        upper_row = head_all[source, pl.ds(4 * kind + 2 * upper, 1)]
        lower_row = head_all[source, pl.ds(4 * kind + 2 * upper + 1, 1)]
        mine_ref[kind : kind + 1] = jnp.where(
            even,
            jnp.where(low, upper_row, pltpu.roll(lower_row, half_width, 1)),
            jnp.where(low, pltpu.roll(upper_row, half_width, 1), lower_row),
        )
    for rank in range(4):
        expands.far(rank)
    second_acts.wait()
    value = jnp.concatenate([act2_ref[slot] for slot in range(4)], axis=1)
    third = jnp.dot(
        value, expand_all[...].reshape(512, 512), preferred_element_type=jnp.float32
    )
    sums3[place] = tile_rows(moments(third, third), 8)
    third_sums.start()
    third_sums.wait()
    totals = third_sums.total()
    rows = []
    for micro in range(2):
        normed, inverse = normed_part(third, totals, micro, count)
        norm3_ref[micro_rows(micro)] = normed
        rows.append(inverse)
        out = normed * output_scale[...] + output_shift[...] + x_ref[micro].astype(jnp.float32)
        y_ref[micro] = (out * jax.nn.sigmoid(out)).astype(jnp.bfloat16)
    inverse3_ref[...] = tile_rows(rows, 8)
    for item in (reduces, spatials, expands, ids, heads, first_acts, second_acts):
        item.close()
    for item in (first_sums, second_sums, third_sums):
        item.close()


def exchange_sems(size):
    return [pltpu.SemaphoreType.DMA((size - 1,)), pltpu.SemaphoreType.DMA((size,))]


def run_front(count, *arrays):
    f32, bf16 = jnp.float32, jnp.bfloat16
    return pl.pallas_call(
        functools.partial(front_kernel, count),
        name="front",
        out_shape=(
            jax.ShapeDtypeStruct((2, PIXELS, 512), bf16),
            jax.ShapeDtypeStruct((2 * PIXELS, 512), f32),
            jax.ShapeDtypeStruct((8, 512), f32),
            jax.ShapeDtypeStruct((2, 2 * PIXELS, LANES), f32),
            jax.ShapeDtypeStruct((8, LANES), f32),
            jax.ShapeDtypeStruct((4, 2 * PIXELS, LANES), bf16),
            jax.ShapeDtypeStruct((4, 2 * PIXELS, LANES), bf16),
            jax.ShapeDtypeStruct((8, 64, 512), bf16),
            jax.ShapeDtypeStruct((8, 9, 64, LANES), bf16),
            jax.ShapeDtypeStruct((8, 64, 512), bf16),
            jax.ShapeDtypeStruct((8, 2, PIXELS, LANES), bf16),
            jax.ShapeDtypeStruct((2, LANES), f32),
            jax.ShapeDtypeStruct((2, PIXELS, LANES), bf16),
        ),
        in_specs=vmem(11),
        out_specs=tuple(vmem(13)),
        scratch_shapes=[
            pltpu.VMEM((3, 2 * PAD + PIXELS, 512), bf16),
            pltpu.VMEM((2 * PIXELS, 9 * 512), bf16),
            pltpu.VMEM((4, 2 * PIXELS, LANES), bf16),
            pltpu.VMEM((4, 2 * PIXELS, LANES), bf16),
            pltpu.VMEM((8, 8, LANES), f32),
            pltpu.VMEM((8, 8, LANES), f32),
            pltpu.VMEM((8, 8, 512), f32),
            pltpu.VMEM((4, 8, LANES), f32),
            pltpu.VMEM((8, 8, PIXELS), f32),
        ]
        + gather_sems(1) * 3
        + exchange_sems(8)
        + [pltpu.SemaphoreType.DMA((4,))] * 2
        + exchange_sems(8) * 3
        + exchange_sems(4) * 3,
        compiler_params=kernel_params(1),
    )(*arrays)


class Scatter:
    def __init__(self, part, far_buf, far_got, near_buf, near_got, sems):
        self.part, self.far_buf, self.far_got = part, far_buf, far_got
        self.near_buf, self.near_got = near_buf, near_got
        self.far_send, self.far_recv, self.near_send, self.near_recv = sems

    def start(self):
        place, lane, depth, side, _, _ = whereabouts()
        for level in range(4):
            self.far_buf[level] = self.part[level * 2 + 1 - side].astype(jnp.bfloat16)
        push(
            self.far_buf, self.far_got, self.far_send, self.far_recv, depth * 2 + 1 - side, lane
        ).start()

    def middle(self):
        place, lane, depth, side, _, _ = whereabouts()
        push(self.far_buf, self.far_got, self.far_send, self.far_recv, place, lane).wait()
        for rank in range(1, 4):
            level = ranked(depth, rank)
            self.near_buf[rank - 1] = (
                self.part[level * 2 + side] + self.far_got[level].astype(jnp.float32)
            ).astype(jnp.bfloat16)
            push(
                self.near_buf.at[rank - 1],
                self.near_got.at[depth],
                self.near_send.at[rank - 1],
                self.near_recv.at[depth],
                level * 2 + side,
                lane,
            ).start()

    def finish(self):
        place, lane, depth, side, _, _ = whereabouts()
        result = self.part[place] + self.far_got[depth].astype(jnp.float32)
        for rank in range(1, 4):
            level = ranked(depth, rank)
            push(
                self.near_buf.at[rank - 1],
                self.near_got.at[level],
                self.near_send.at[rank - 1],
                self.near_recv.at[level],
                place,
                lane,
            ).wait()
            result = result + self.near_got[level].astype(jnp.float32)
        return result


def scatter_scratch(width):
    return [
        pltpu.VMEM((8, 64, width), jnp.float32),
        pltpu.VMEM((4, 64, width), jnp.bfloat16),
        pltpu.VMEM((4, 64, width), jnp.bfloat16),
        pltpu.VMEM((3, 64, width), jnp.bfloat16),
        pltpu.VMEM((4, 64, width), jnp.bfloat16),
    ]


def scatter_sems():
    return [
        pltpu.SemaphoreType.DMA,
        pltpu.SemaphoreType.DMA,
        pltpu.SemaphoreType.DMA((3,)),
        pltpu.SemaphoreType.DMA((4,)),
    ]


def back_part(value, normed, inverse, scale, shift_sum, scale_sum, count):
    return (scale * inverse * (value - (shift_sum + normed * scale_sum) / count)).astype(
        jnp.bfloat16
    )


def rear_kernel(
    count,
    grad_ref,
    x_ref,
    norm3_ref,
    inverse3_ref,
    norm12_ref,
    inverse12_ref,
    act1_ref,
    act2_ref,
    reduce_all,
    spatial_all,
    expand_all,
    mask_ref,
    block_scale,
    block_shift,
    output_scale,
    output_shift,
    head_ref,
    gate_ref,
    block_hbm,
    back_hbm,
    masks_hbm,
    features_ref,
    reduce_out,
    spatial_out,
    expand_out,
    block_scale_out,
    block_shift_out,
    head_scale_out,
    head_shift_out,
    gate_out,
    output_scale_out,
    output_shift_out,
    head_grad,
    block_all,
    head_back,
    mask_all,
    turned_wide,
    columns_wide,
    turned,
    columns,
    stage,
    got,
    stage_next,
    got_next,
    sums_a,
    sums_b,
    sums_c,
    head_all,
    act_all,
    back3,
    *rest,
):
    expand_bufs, spatial_bufs, reduce_bufs, sems = rest[0:5], rest[5:10], rest[10:15], rest[15:]
    place, lane, depth, side, upper, core = whereabouts()
    pieces = Pieces(stage, got, sems[0], sems[1])
    first = Exchange(sums_a, sems[2], sems[3], "batch")
    second = Exchange(sums_b, sems[4], sems[5], "batch")
    third = Exchange(sums_c, sems[6], sems[7], "batch")
    heads = Exchange(head_all, sems[8], sems[9], "chan")
    acts = Exchange(act_all, sems[10], sems[11], "chan")
    expands = Scatter(*expand_bufs, sems[12:16])
    spatials = Scatter(*spatial_bufs, sems[16:20])
    reduces = Scatter(*reduce_bufs, sems[20:24])
    pieces_next = Pieces(stage_next, got_next, sems[24], sems[25])

    loads = [
        pltpu.make_async_copy(source, target, sems[26].at[number])
        for number, (source, target) in enumerate(
            ((block_hbm, block_all), (back_hbm, head_back), (masks_hbm, mask_all))
        )
    ]
    for load in loads:
        load.start()

    def weigh(block):
        for micro in range(2):
            fill_columns(
                block_all[block, micro],
                mask_all[block, micro],
                turned_wide,
                columns_wide,
                micro * PIXELS,
            )
        value = jnp.concatenate(
            [
                jnp.concatenate([head_back[half, micro, block] for half in range(2)], axis=1)
                for micro in range(2)
            ],
            axis=0,
        ).T

        def tap(number, _):
            product = jnp.dot(
                value,
                columns_wide[:, pl.ds(pl.multiple_of(number * 512, 512), 512)],
                preferred_element_type=jnp.float32,
            )
            if block == 0:
                head_grad[number] = product
            else:
                head_grad[number] += product
            return 0

        lax.fori_loop(0, 9, tap, 0)

    greet(batch_peers() + chan_peers())
    clear_edges(turned_wide)
    half_width = LANES // 2
    even = place % 2 == 0
    mine = lax.broadcasted_iota(jnp.int32, (1, LANES), 1) >> 6 == place % 2
    rows = []
    for kind in range(2):
        own = head_ref[kind : kind + 1]
        turned_own = pltpu.roll(own, half_width, 1)
        first_row = jnp.where(mine, jnp.where(even, own, turned_own), 0.0)
        second_row = jnp.where(mine, jnp.where(even, turned_own, own), 0.0)
        for half in range(2):
            for row in (first_row, second_row):
                rows.append(jnp.where(upper == half, row, 0.0))
    head_all[lane] = jnp.concatenate(rows, axis=0)
    heads.start()
    clear_edges(turned)
    rows = []
    for micro in range(2):
        normed = norm3_ref[micro_rows(micro)]
        out = normed * output_scale[...] + output_shift[...] + x_ref[micro].astype(jnp.float32)
        value = grad_ref[micro_rows(micro)] * silu_slope(out)
        features_ref[micro] = value
        rows.append(jnp.sum(value, axis=0, keepdims=True))
        rows.append(jnp.sum(value * normed, axis=0, keepdims=True))
    heads.wait()
    sums_a[place, 0:8] = tile_rows(rows, 8)
    sums_a[place, 8:16] = jnp.zeros((8, 512), jnp.float32)
    sums_a[place, 4:6, 0:LANES] = gate_ref[...]
    sums_a[place, 8:16, 0:LANES] = jnp.where(place // 2 == lane, heads.total(), 0.0)
    first.start()
    for load in loads:
        load.wait()
    weigh(0)
    first.wait()
    totals = first.total()
    head_scale_out[...] = totals[8:12, 0:LANES]
    head_shift_out[...] = totals[12:16, 0:LANES]
    gate_out[...] = totals[4:6, 0:LANES]
    output_scale_out[...] = totals[1:2] + totals[3:4]
    output_shift_out[...] = totals[0:1] + totals[2:3]
    for micro in range(2):
        back3[micro_rows(micro)] = back_part(
            features_ref[micro],
            norm3_ref[micro_rows(micro)],
            inverse3_ref[micro : micro + 1],
            output_scale[...],
            totals[2 * micro : 2 * micro + 1],
            totals[2 * micro + 1 : 2 * micro + 2],
            count,
        )
    pieces.start(dot_last(back3[...], expand_all[...].reshape(512, 512)))
    value = jnp.concatenate([act2_ref[slot] for slot in range(4)], axis=1)
    expands.part[...] = jnp.dot(
        value.T, back3[...], preferred_element_type=jnp.float32
    ).reshape(8, 64, 512)
    expands.start()
    weigh(1)
    grad = pieces.finish()
    normed = norm12_ref[1]
    grad = grad * silu_slope(normed * block_scale[1:2] + block_shift[1:2])
    sums_b[place] = tile_rows(moments(grad, normed), 8)
    second.start()
    weigh(2)
    expands.middle()
    second.wait()
    totals = second.total()
    block_scale_out[1:2] = totals[1:2] + totals[3:4]
    block_shift_out[1:2] = totals[0:1] + totals[2:3]
    for micro in range(2):
        value = back_part(
            grad[micro_rows(micro)],
            normed[micro_rows(micro)],
            inverse12_ref[2 + micro : 3 + micro],
            block_scale[1:2],
            totals[2 * micro : 2 * micro + 1],
            totals[2 * micro + 1 : 2 * micro + 2],
            count,
        )
        fill_columns(value, mask_ref[micro], turned, columns, micro * PIXELS, True)
    part = jnp.zeros((2 * PIXELS, 512), jnp.float32)
    for number in range(9):
        part = part + dot_last(
            columns[:, number * LANES : (number + 1) * LANES],
            spatial_all[:, number].reshape(512, LANES),
        )
    pieces_next.start(part)
    value = jnp.concatenate([act1_ref[slot] for slot in range(4)], axis=1)
    spatials.part[...] = jnp.dot(
        value.T, columns[...], preferred_element_type=jnp.float32
    ).reshape(8, 64, 9 * LANES)
    spatials.start()
    weigh(3)
    grad = pieces_next.finish()
    normed = norm12_ref[0]
    grad = grad * silu_slope(normed * block_scale[0:1] + block_shift[0:1])
    sums_c[place] = tile_rows(moments(grad, normed), 8)
    third.start()
    weigh(4)
    spatials.middle()
    expand_out[...] = expands.finish()
    third.wait()
    totals = third.total()
    block_scale_out[0:1] = totals[1:2] + totals[3:4]
    block_shift_out[0:1] = totals[0:1] + totals[2:3]
    for micro in range(2):
        act_all[lane, micro_rows(micro)] = back_part(
            grad[micro_rows(micro)],
            normed[micro_rows(micro)],
            inverse12_ref[micro : micro + 1],
            block_scale[0:1],
            totals[2 * micro : 2 * micro + 1],
            totals[2 * micro + 1 : 2 * micro + 2],
            count,
        )
    acts.start()
    weigh(5)
    acts.wait()
    value = jnp.concatenate([act_all[slot] for slot in range(4)], axis=1)
    x = x_ref[...].reshape(2 * PIXELS, 512)
    reduces.part[...] = jnp.dot(value.T, x, preferred_element_type=jnp.float32).reshape(8, 64, 512)
    reduces.start()
    more = jnp.dot(value, reduce_all[...].reshape(512, 512), preferred_element_type=jnp.float32)
    for micro in range(2):
        features_ref[micro] = features_ref[micro] + more[micro_rows(micro)]
    weigh(6)
    reduces.middle()
    weigh(7)
    result = spatials.finish()
    for number in range(9):
        spatial_out[number] = result[:, number * LANES : (number + 1) * LANES]
    reduce_out[...] = reduces.finish()
    for item in (first, second, third, heads, acts):
        item.close()


def run_rear(count, *arrays):
    f32, bf16 = jnp.float32, jnp.bfloat16
    return pl.pallas_call(
        functools.partial(rear_kernel, count),
        name="rear",
        out_shape=(
            jax.ShapeDtypeStruct((2, PIXELS, 512), f32),
            jax.ShapeDtypeStruct((64, 512), f32),
            jax.ShapeDtypeStruct((9, 64, LANES), f32),
            jax.ShapeDtypeStruct((64, 512), f32),
            jax.ShapeDtypeStruct((2, LANES), f32),
            jax.ShapeDtypeStruct((2, LANES), f32),
            jax.ShapeDtypeStruct((4, LANES), f32),
            jax.ShapeDtypeStruct((4, LANES), f32),
            jax.ShapeDtypeStruct((2, LANES), f32),
            jax.ShapeDtypeStruct((1, 512), f32),
            jax.ShapeDtypeStruct((1, 512), f32),
            jax.ShapeDtypeStruct((9, 256, 512), f32),
        ),
        in_specs=vmem(18) + [pl.BlockSpec(memory_space=pl.ANY)] * 3,
        out_specs=tuple(vmem(12)),
        scratch_shapes=[
            pltpu.VMEM((8, 2, PIXELS, 512), bf16),
            pltpu.VMEM((2, 2, 8, PIXELS, LANES), bf16),
            pltpu.VMEM((8, 2, PIXELS, LANES), bf16),
            pltpu.VMEM((3, 2 * PAD + PIXELS, 512), bf16),
            pltpu.VMEM((2 * PIXELS, 9 * 512), bf16),
            pltpu.VMEM((3, 2 * PAD + PIXELS, LANES), bf16),
            pltpu.VMEM((2 * PIXELS, 9 * LANES), bf16),
            pltpu.VMEM((4, 2 * PIXELS, LANES), bf16),
            pltpu.VMEM((4, 2 * PIXELS, LANES), bf16),
            pltpu.VMEM((4, 2 * PIXELS, LANES), bf16),
            pltpu.VMEM((4, 2 * PIXELS, LANES), bf16),
            pltpu.VMEM((8, 16, 512), f32),
            pltpu.VMEM((8, 8, LANES), f32),
            pltpu.VMEM((8, 8, LANES), f32),
            pltpu.VMEM((4, 8, LANES), f32),
            pltpu.VMEM((4, 2 * PIXELS, LANES), bf16),
            pltpu.VMEM((2 * PIXELS, 512), bf16),
        ]
        + scatter_scratch(512)
        + scatter_scratch(9 * LANES)
        + scatter_scratch(512)
        + [pltpu.SemaphoreType.DMA((4,))] * 2
        + exchange_sems(8) * 3
        + exchange_sems(4) * 2
        + scatter_sems() * 3
        + [pltpu.SemaphoreType.DMA((4,))] * 2
        + [pltpu.SemaphoreType.DMA((3,))],
        compiler_params=kernel_params(5),
    )(*arrays)


class Reduce:
    def __init__(self, part, keep, far_buf, far_got, line_buf, line_got, sems):
        self.part, self.keep, self.far_buf, self.far_got = part, keep, far_buf, far_got
        self.line_buf, self.line_got = line_buf, line_got
        self.far_send, self.far_recv, self.line_send, self.line_recv = sems

    def block(self, step):
        place, lane, depth, side, _, _ = whereabouts()
        item, late = staggered(step)
        return ranked(depth, 3 - item % 4) * 2 + (side + 1 + late) % 2, item // 4

    def far_copy(self, micro, rank, place):
        return push(
            self.far_buf.at[micro, rank],
            self.far_got.at[micro, rank],
            self.far_send.at[micro, rank],
            self.far_recv.at[micro, rank],
            place,
            lax.axis_index("chan"),
        )

    def line_copy(self, micro, rank, slot, place):
        return push(
            self.line_buf.at[micro, rank],
            self.line_got.at[micro, slot],
            self.line_send.at[micro, rank],
            self.line_recv.at[micro, slot],
            place,
            lax.axis_index("chan"),
        )

    def line_value(self, micro, slot):
        self.line_copy(micro, 0, slot, lax.axis_index("batch")).wait_recv()
        return self.line_got[micro, slot].astype(jnp.float32)

    def step(self, step):
        place, lane, depth, side, _, _ = whereabouts()
        item, late = staggered(step)
        micro, rank = item // 4, 3 - item % 4
        owner = ranked(depth, rank)

        @pl.when(late == 0)
        def _():
            self.far_buf[micro, rank] = self.part[...].astype(jnp.bfloat16)
            self.far_copy(micro, rank, depth * 2 + 1 - side).start()

        @pl.when(late == 1)
        def _():
            self.far_copy(micro, rank, place).wait_recv()
            self.keep[micro] = self.part[...] + self.far_got[micro, rank].astype(jnp.float32)

            @pl.when((middle(depth) == 1) & (rank > 0))
            def _():
                self.keep[micro] = self.keep[micro] + self.line_value(micro, owner)

            @pl.when(rank > 0)
            def _():
                first = (rank % 2) * (1 - rank // 2) * (1 - middle(depth))
                slot = owner + first * (4 - owner)
                self.line_buf[micro, rank - 1] = self.keep[micro].astype(jnp.bfloat16)
                self.line_copy(
                    micro, rank - 1, slot, homeward(depth, rank) * 2 + side
                ).start()

    def close(self, micro):
        place, lane, depth, side, _, _ = whereabouts()
        self.keep[micro] = self.keep[micro] + self.line_value(micro, depth)

        @pl.when(middle(depth) == 1)
        def _():
            self.keep[micro] = self.keep[micro] + self.line_value(micro, 4)

        for rank in range(4):
            self.far_copy(micro, rank, place).wait_send()
        for rank in range(3):
            self.line_copy(micro, rank, 0, place).wait_send()


class Channels:
    def __init__(self, stage, got, stage_sem, got_sem, values, out_sem, in_sem):
        self.stage, self.got, self.stage_sem, self.got_sem = stage, got, stage_sem, got_sem
        self.values, self.out_sem, self.in_sem = values, out_sem, in_sem

    def piece(self, slot, target, block, lane):
        return push(
            self.stage.at[slot, block],
            self.got.at[lane, block],
            self.stage_sem.at[slot, block],
            self.got_sem.at[lane, block],
            lax.axis_index("batch"),
            target,
        )

    def send(self, part, block, micro):
        _, lane, _, _, upper, core = whereabouts()
        for half in range(2):
            piece = part[:, half * LANES : (half + 1) * LANES]
            target = half * 2 + micro

            @pl.when(target == lane)
            def _():
                self.got[lane, block] = piece

            @pl.when(target != lane)
            def _():
                self.stage[target, block] = piece
                self.piece(target, target, block, lane).start()

    def collect(self, micro, take):
        _, lane, _, _, _, core = whereabouts()

        @pl.when(core == micro)
        def _():
            def body(block, _):
                for step in range(1, 4):
                    other = (lane + step) % 4
                    self.piece(other, other, block, other).wait_recv()
                take(block)
                return 0

            lax.fori_loop(0, 8, body, 0)

    def value(self, block):
        result = self.got[0, block].astype(jnp.float32)
        for other in range(1, 4):
            result = result + self.got[other, block].astype(jnp.float32)
        return result

    def sent(self):
        _, lane, _, _, _, _ = whereabouts()

        def body(block, _):
            for step in range(1, 4):
                other = (lane + step) % 4
                self.piece(other, other, block, lane).wait_send()
            return 0

        lax.fori_loop(0, 8, body, 0)

    def chunk(self, path, half, micro, chunk, place_lane):
        here = self.values.at[half, micro, pl.ds(2 * chunk, 2)]
        return push(
            here,
            here,
            self.out_sem.at[path, chunk],
            self.in_sem.at[half, micro, chunk],
            lax.axis_index("batch"),
            place_lane,
        )

    def spread(self, chunk):
        _, lane, _, _, upper, core = whereabouts()
        self.chunk(0, upper, core, chunk, 2 - 2 * upper + core).start()
        self.chunk(1, upper, core, chunk, upper * 2 + 1 - core).start()

    def relay(self, micro):
        _, lane, _, _, upper, core = whereabouts()

        @pl.when(core == micro)
        def _():
            for chunk in range(4):
                copy = self.chunk(2, 1 - upper, core, chunk, upper * 2 + 1 - core)
                copy.wait_recv()
                copy.start()

    def finish(self, micro):
        _, lane, _, _, upper, core = whereabouts()

        @pl.when(core != micro)
        def _():
            for chunk in range(4):
                for half in range(2):
                    self.chunk(0, half, micro, chunk, lane).wait_recv()

    def close(self):
        _, lane, _, _, upper, core = whereabouts()
        for chunk in range(4):
            for path in range(3):
                self.chunk(path, upper, core, chunk, lane).wait_send()


def middle_kernel(
    count,
    block_ref,
    head_ref,
    distil_ref,
    mask_ref,
    depth_cot,
    segment_cot,
    bias_ref,
    mine_ref,
    depth_out,
    segment_out,
    distil_grad,
    gate_sums,
    head_sums,
    back_out,
    block_all,
    head_back,
    head_weight,
    mixed,
    mixed_back,
    turned,
    columns,
    acts,
    norm_ref,
    slope_ref,
    grads_all,
    packed,
    own_stage,
    own_got,
    cot_all,
    stage,
    got,
    part_ref,
    keep,
    far_buf,
    far_got,
    line_buf,
    line_got,
    stats,
    *sems,
):
    place, lane, depth, side, upper, core = whereabouts()
    half_width = LANES // 2
    source = place // 2 == lane
    low = lax.broadcasted_iota(jnp.int32, (PIXELS, LANES), 1) < half_width
    gather = Gather(block_all, *sems[0:3], 2)
    gather_back = Gather(grads_all, *sems[3:6], 2)
    reduce = Reduce(part_ref, keep, far_buf, far_got, line_buf, line_got, sems[6:10])
    ahead = Channels(stage, got, sems[10], sems[11], acts, sems[12], sems[13])
    behind = Channels(stage, got, sems[10], sems[11], head_back, sems[14], sems[15])
    own_sem, own_recv, cot_sem, cot_recv = sems[16:20]

    greet(batch_peers() + chan_peers())
    block_all[place] = block_ref[...]
    gather.start(0)
    clear_edges(turned)
    for number in range(9):
        head_weight[number * 512 : (number + 1) * 512] = head_ref[number].T
    for micro in range(2):
        first, second = (ref[micro].astype(jnp.float32) for ref in (depth_cot, segment_cot))
        packed[0, micro] = jnp.where(low, first, pltpu.roll(second, half_width, 1)).astype(
            jnp.bfloat16
        )
        packed[1, micro] = jnp.where(low, pltpu.roll(first, half_width, 1), second).astype(
            jnp.bfloat16
        )

    def cot_copy(parity, slot, target):
        return push(
            packed.at[parity], cot_all.at[slot], cot_sem.at[parity], cot_recv.at[slot], target, lane
        )

    def forward_step(step, _):
        block, micro = gather.next(step)
        fill_columns(block_all[block, micro], mask_ref[block, micro], turned, columns)
        part = jnp.dot(columns[0:PIXELS], head_weight[...], preferred_element_type=jnp.float32)
        ahead.send(part.astype(jnp.bfloat16), block, micro)

        @pl.when(step == 0)
        def _():
            prepare_mixed()

        @pl.when(step == 2)
        def _():
            for parity in range(2):
                target = 2 * lane + parity

                @pl.when(target == place)
                def _():
                    cot_all[place] = packed[parity]

                @pl.when(target != place)
                def _():
                    cot_copy(parity, place, target).start()

        @pl.when(step == 4)
        def _():
            for number in range(9):
                mixed_back[number * 512 : (number + 1) * 512] = mixed[
                    number * 256 : (number + 1) * 256
                ].T

        @pl.when(step == 10)
        def _():
            normalize(0)

        @pl.when(step == 14)
        def _():
            ahead.relay(0)

        return 0

    def prepare_mixed():
        width = half_width
        for number in range(9):
            for stream in range(2):
                for head in range(4):
                    index = head - SOURCE_START[stream]
                    rows = slice(number * 256 + head * width, number * 256 + (head + 1) * width)
                    left = slice(2 * stream * LANES, (2 * stream + 1) * LANES)
                    right = slice((2 * stream + 1) * LANES, (2 * stream + 2) * LANES)
                    nothing = jnp.zeros((width, LANES), jnp.bfloat16)
                    mixed[rows, left] = (
                        distil_ref[stream, number, 0] if head == OWN_HEAD[stream] else nothing
                    )
                    mixed[rows, right] = (
                        distil_ref[stream, number, 1 + index] if 0 <= index < 3 else nothing
                    )

    def normalize(micro):
        zero = jnp.zeros((1, LANES), jnp.float32)

        @pl.when(core == micro)
        def _():
            stats[0:2] = jnp.zeros((2, LANES), jnp.float32)

        def take(block):
            value = ahead.value(block)
            norm_ref[block] = value
            stats[0:1] += jnp.sum(value, axis=0, keepdims=True)
            stats[1:2] += jnp.sum(value * value, axis=0, keepdims=True)

        ahead.collect(micro, take)

        @pl.when(core == micro)
        def _():
            center = stats[0:1] / count
            inverse = lax.rsqrt(stats[1:2] / count - center * center + EPSILON)
            stats[2:3] = inverse

            def activate(chunk, _):
                for item in range(2):
                    block = 2 * chunk + item
                    normed = (norm_ref[block] - center) * inverse
                    norm_ref[block] = normed
                    out = normed * mine_ref[0:1] + mine_ref[1:2]
                    acts[upper, core, block] = (out * jax.nn.sigmoid(out)).astype(jnp.bfloat16)
                ahead.spread(chunk)
                return 0

            lax.fori_loop(0, 4, activate, 0)

    lax.fori_loop(0, 16, forward_step, 0)
    ahead.finish(0)

    def own_copy(block, micro, slot, target):
        return push(
            own_stage.at[block, micro],
            own_got.at[slot, micro],
            own_sem.at[block, micro],
            own_recv.at[slot, micro],
            target,
            lane,
        )

    def send_own(micro):
        @pl.when(source)
        def _():
            own_got[place % 2, micro] = jnp.where(
                low, acts[0, micro, place], acts[1, micro, place]
            )

            def pack(step, _):
                block = (place + step) % 8
                own_stage[block, micro] = jnp.where(
                    low, acts[0, micro, block], acts[1, micro, block]
                )
                own_copy(block, micro, place % 2, block).start()
                return 0

            lax.fori_loop(1, 8, pack, 0)

    send_own(0)

    def act_value(block, micro):
        return jnp.concatenate([acts[half, micro, block] for half in range(2)], axis=1)

    def gate(micro):
        reduce.close(micro)
        for parity in range(2):
            @pl.when(2 * lane + parity != place)
            def _():
                own_copy(0, micro, parity, place).wait_recv()

        for stream, cot_ref in enumerate((depth_cot, segment_cot)):
            first = own_got[0, micro].astype(jnp.float32)
            second = own_got[1, micro].astype(jnp.float32)
            if stream == 0:
                second = pltpu.roll(second, half_width, 1)
            else:
                first = pltpu.roll(first, half_width, 1)
            own = jnp.where(low, first, second)
            column = 2 * stream * LANES
            gates = jax.nn.sigmoid(
                keep[micro, :, column : column + LANES] + bias_ref[stream : stream + 1]
            )
            message = keep[micro, :, column + LANES : column + 2 * LANES]
            cot = cot_ref[micro].astype(jnp.float32)
            out_ref = (depth_out, segment_out)[stream]
            out_ref[micro] = (own + gates * message).astype(jnp.bfloat16)
            gate_grad = (cot * message * gates * (1.0 - gates)).astype(jnp.bfloat16)
            bias_sum = jnp.sum(gate_grad.astype(jnp.float32), axis=0, keepdims=True)
            if micro == 0:
                gate_sums[stream : stream + 1] = bias_sum
            else:
                gate_sums[stream : stream + 1] += bias_sum
            grads_all[place, micro, :, column : column + LANES] = gate_grad
            grads_all[place, micro, :, column + LANES : column + 2 * LANES] = (cot * gates).astype(
                jnp.bfloat16
            )

    def distil_step(step, _):
        block, micro = reduce.block(step)
        fill_columns(act_value(block, micro), mask_ref[block, micro], turned, columns)
        part_ref[...] = jnp.dot(
            columns[0:PIXELS, 0 : 9 * 256], mixed[...], preferred_element_type=jnp.float32
        )
        reduce.step(step)

        @pl.when(step == 1)
        def _():
            normalize(1)

        @pl.when(step == 4)
        def _():
            ahead.relay(1)

        @pl.when(step == 6)
        def _():
            ahead.finish(1)
            send_own(1)

        @pl.when(step == 11)
        def _():
            gate(0)
            gather_back.start(0)

        return 0

    lax.fori_loop(0, 16, distil_step, 0)
    gate(1)
    ahead.sent()
    ahead.close()
    distil_grad[...] = jnp.zeros_like(distil_grad)

    @pl.when(source)
    def _():
        for step in range(1, 8):
            other = (place + step) % 8
            cot_copy(0, other, place).wait_recv()

    def back_step(step, _):
        block, micro = gather_back.next(step)
        fill_columns(
            grads_all[block, micro], mask_ref[block, micro], turned, columns, flip=True
        )
        part = jnp.dot(columns[0:PIXELS], mixed_back[...], preferred_element_type=jnp.float32)
        extra = cot_all[block, micro].astype(jnp.float32)
        part = jnp.concatenate(
            [
                part[:, :LANES] + jnp.where(low & source, extra, 0.0),
                part[:, LANES:] + jnp.where(low | ~source, 0.0, extra),
            ],
            axis=1,
        )
        behind.send(part.astype(jnp.bfloat16), block, micro)
        @pl.when(step == 10)
        def _():
            normalize_back(0)

        @pl.when(step == 14)
        def _():
            behind.relay(0)

        return 0

    def normalize_back(micro):
        @pl.when(core == micro)
        def _():
            stats[4:6] = jnp.zeros((2, LANES), jnp.float32)

        def take(block):
            normed = norm_ref[block]
            value = behind.value(block) * silu_slope(normed * mine_ref[0:1] + mine_ref[1:2])
            slope_ref[block] = value
            stats[4:5] += jnp.sum(value, axis=0, keepdims=True)
            stats[5:6] += jnp.sum(value * normed, axis=0, keepdims=True)

        behind.collect(micro, take)

        @pl.when(core == micro)
        def _():
            shift_sum, scale_sum = stats[4:5], stats[5:6]
            head_sums[0:1] = scale_sum
            head_sums[1:2] = shift_sum
            factor = mine_ref[0:1] * stats[2:3]

            def activate(chunk, _):
                for item in range(2):
                    block = 2 * chunk + item
                    value = slope_ref[block]
                    head_back[upper, core, block] = (
                        factor * (value - (shift_sum + norm_ref[block] * scale_sum) / count)
                    ).astype(jnp.bfloat16)
                behind.spread(chunk)
                return 0

            lax.fori_loop(0, 4, activate, 0)

    lax.fori_loop(0, 16, back_step, 0)
    behind.finish(0)

    def head_value(block, micro):
        return jnp.concatenate([head_back[half, micro, block] for half in range(2)], axis=1)

    def weigh(block):
        for micro in range(2):
            fill_columns(
                grads_all[block, micro],
                mask_ref[block, micro],
                turned,
                columns,
                micro * PIXELS,
                True,
            )
        value = jnp.concatenate([act_value(block, micro) for micro in range(2)], axis=0).T
        width = half_width
        for number in range(9):
            product = jnp.dot(
                value,
                columns[:, number * 512 : (number + 1) * 512],
                preferred_element_type=jnp.float32,
            )
            for stream in range(2):
                for index in range(4):
                    head = OWN_HEAD[stream] if index == 0 else SOURCE_START[stream] + index - 1
                    column = (2 * stream + (index > 0)) * LANES
                    distil_grad[stream, number, index] += product[
                        head * width : (head + 1) * width, column : column + LANES
                    ]

    def block_step(step, _):
        block, micro = reduce.block(step)
        fill_columns(
            head_value(block, micro), mask_ref[block, micro], turned, columns, flip=True
        )
        part_ref[...] = jnp.dot(
            columns[0:PIXELS, 0 : 9 * 256],
            head_ref[...].reshape(9 * 256, 512),
            preferred_element_type=jnp.float32,
        )
        item, late = staggered(step)

        @pl.when(late == 1)
        def _():
            weigh(item)

        reduce.step(step)

        @pl.when(step == 1)
        def _():
            normalize_back(1)

        @pl.when(step == 4)
        def _():
            behind.relay(1)

        @pl.when(step == 6)
        def _():
            behind.finish(1)

        return 0

    lax.fori_loop(0, 16, block_step, 0)
    for micro in range(2):
        reduce.close(micro)
        back_out[micro_rows(micro)] = keep[micro]
    behind.sent()
    behind.close()
    gather.close()
    gather_back.close()
    for parity in range(2):
        @pl.when(2 * lane + parity != place)
        def _():
            cot_copy(parity, place, place).wait_send()

    @pl.when(source)
    def _():
        for micro in range(2):
            for step in range(1, 8):
                own_copy((place + step) % 8, micro, 0, place).wait_send()


def run_middle(count, *arrays):
    f32, bf16 = jnp.float32, jnp.bfloat16
    block = (PIXELS, 512)
    dma = pltpu.SemaphoreType.DMA
    return pl.pallas_call(
        functools.partial(middle_kernel, count),
        name="middle",
        out_shape=(
            jax.ShapeDtypeStruct((2, PIXELS, LANES), bf16),
            jax.ShapeDtypeStruct((2, PIXELS, LANES), bf16),
            jax.ShapeDtypeStruct((2, 9, 4, 64, LANES), f32),
            jax.ShapeDtypeStruct((2, LANES), f32),
            jax.ShapeDtypeStruct((2, LANES), f32),
            jax.ShapeDtypeStruct((2 * PIXELS, 512), f32),
            jax.ShapeDtypeStruct((8, 2) + block, bf16),
            jax.ShapeDtypeStruct((2, 2, 8, PIXELS, LANES), bf16),
        ),
        in_specs=vmem(8),
        out_specs=tuple(vmem(8)),
        scratch_shapes=[
            pltpu.VMEM((9 * 512, 256), bf16),
            pltpu.VMEM((9 * 256, 512), bf16),
            pltpu.VMEM((9 * 512, 256), bf16),
            pltpu.VMEM((3, 2 * PAD + PIXELS, 512), bf16),
            pltpu.VMEM((2 * PIXELS, 9 * 512), bf16),
            pltpu.VMEM((2, 2, 8, PIXELS, LANES), bf16),
            pltpu.VMEM((8, PIXELS, LANES), f32),
            pltpu.VMEM((8, PIXELS, LANES), f32),
            pltpu.VMEM((8, 2) + block, bf16),
            pltpu.VMEM((2, 2, PIXELS, LANES), bf16),
            pltpu.VMEM((8, 2, PIXELS, LANES), bf16),
            pltpu.VMEM((2, 2, PIXELS, LANES), bf16),
            pltpu.VMEM((8, 2, PIXELS, LANES), bf16),
            pltpu.VMEM((4, 8, PIXELS, LANES), bf16),
            pltpu.VMEM((4, 8, PIXELS, LANES), bf16),
            pltpu.VMEM(block, f32),
            pltpu.VMEM((2,) + block, f32),
            pltpu.VMEM((2, 4) + block, bf16),
            pltpu.VMEM((2, 4) + block, bf16),
            pltpu.VMEM((2, 3) + block, bf16),
            pltpu.VMEM((2, 5) + block, bf16),
            pltpu.VMEM((8, LANES), f32),
        ]
        + gather_sems(2) * 2
        + [dma((2, 4)), dma((2, 4)), dma((2, 3)), dma((2, 5))]
        + [dma((4, 8)), dma((4, 8))]
        + [dma((3, 4)), dma((2, 2, 4))] * 2
        + [dma((8, 2)), dma((2, 2)), dma((2,)), dma((8,))],
        compiler_params=kernel_params(2),
    )(*arrays)


def finish_kernel(count, *refs):
    sources, targets, held = refs[:count], refs[count : 2 * count], refs[2 * count : 3 * count]
    sem_in, sem_out = refs[3 * count :]

    def parts(ref):
        large = len(ref.shape) > 2
        return [ref.at[number] for number in range(ref.shape[0])] if large else [ref]

    number = 0
    loads, stores = [], []
    for source, target, hold in zip(sources, targets, held):
        for pieces in zip(parts(source), parts(hold), parts(target)):
            loads.append(pltpu.make_async_copy(pieces[0], pieces[1], sem_in.at[number]))
            stores.append(pltpu.make_async_copy(pieces[1], pieces[2], sem_out.at[number]))
            number += 1
    for load in loads:
        load.start()
    for load, store in zip(loads, stores):
        load.wait()
        store.start()
    for store in stores:
        store.wait()


def run_finish(*arrays):
    anywhere = [pl.BlockSpec(memory_space=pltpu.HBM)] * len(arrays)
    copies = sum(item.shape[0] if item.ndim > 2 else 1 for item in arrays)
    return pl.pallas_call(
        functools.partial(finish_kernel, len(arrays)),
        name="finish",
        out_shape=tuple(jax.ShapeDtypeStruct(item.shape, item.dtype) for item in arrays),
        in_specs=anywhere,
        out_specs=tuple(anywhere),
        scratch_shapes=[pltpu.VMEM(item.shape, item.dtype) for item in arrays]
        + [pltpu.SemaphoreType.DMA((copies,))] * 2,
        compiler_params=pltpu.CompilerParams(vmem_limit_bytes=60 * 2**20),
    )(*arrays)


def stationary_local(
    features,
    image_ids,
    reduce_weight,
    spatial_weight,
    expand_weight,
    head_weights,
    distil_weights,
    block_scale,
    block_shift,
    head_scale,
    head_shift,
    gate_bias,
    output_scale,
    output_shift,
    depth_cotangent,
    segment_cotangent,
):
    canvases, row_count, column_count = image_ids.shape
    pixels = row_count * column_count
    count = float(lax.axis_size("batch") * pixels)
    x = features.reshape(canvases, pixels, -1)
    ids = jnp.pad(image_ids.reshape(canvases, pixels).astype(jnp.float32), ((0, 6), (0, 0)))
    block_params = (block_scale, block_shift)
    output_params = (output_scale[None], output_shift[None])
    (
        block_out,
        norm3,
        inverse3,
        norm12,
        inverse12,
        act1,
        act2,
        reduce_all,
        spatial_all,
        expand_all,
        mask_all,
        mine,
        mask,
    ) = run_front(
        count,
        x,
        ids,
        reduce_weight.T,
        spatial_weight,
        expand_weight,
        *block_params,
        *output_params,
        head_scale,
        head_shift,
    )
    depth_out, segment_out, distil_grad, gate_sums, head_sums, block_grad, block_all, back_all = run_middle(
        count,
        block_out,
        head_weights.transpose(0, 2, 3, 1).reshape(9, -1, head_weights.shape[1]),
        distil_weights,
        mask_all,
        depth_cotangent.reshape(canvases, pixels, LANES),
        segment_cotangent.reshape(canvases, pixels, LANES),
        gate_bias,
        mine,
    )
    (
        features_grad,
        reduce_grad,
        spatial_grad,
        expand_grad,
        block_scale_grad,
        block_shift_grad,
        head_scale_grad,
        head_shift_grad,
        gate_grad,
        output_scale_grad,
        output_shift_grad,
        heads_grad,
    ) = run_rear(
        count,
        block_grad,
        x,
        norm3,
        inverse3,
        norm12,
        inverse12,
        act1,
        act2,
        reduce_all,
        spatial_all,
        expand_all,
        mask,
        *block_params,
        *output_params,
        head_sums,
        gate_sums,
        block_all,
        back_all,
        mask_all,
    )
    outs = run_finish(
        depth_out,
        segment_out,
        features_grad,
        reduce_grad,
        spatial_grad,
        expand_grad,
        heads_grad,
        distil_grad,
        block_scale_grad,
        block_shift_grad,
        head_scale_grad,
        head_shift_grad,
        gate_grad,
        output_scale_grad,
        output_shift_grad,
    )
    heads_grad = outs[6].reshape(9, 4, -1, head_weights.shape[1]).transpose(0, 3, 1, 2)
    return (
        outs[0].reshape(depth_cotangent.shape),
        outs[1].reshape(depth_cotangent.shape),
        outs[2].reshape(features.shape),
        outs[3].T,
        *outs[4:6],
        heads_grad,
        *outs[7:13],
        outs[13][0],
        outs[14][0],
    )


def solution(mesh):
    fits = dict(mesh.shape) == {"batch": 8, "chan": 4}
    local = stationary_local if fits else gathered_local
    placed = (
        P("batch", None, None, "chan"),
        P("batch", None, None),
        P("chan", "batch"),
        P(None, "batch", "chan"),
        P("batch", "chan"),
        P(None, "chan", None, "batch"),
        P(None, None, None, "batch", "chan"),
        P(None, "chan"),
        P(None, "chan"),
        P(None, "chan"),
        P(None, "chan"),
        P(None, "chan"),
        P("chan"),
        P("chan"),
        P("batch", None, None, "chan"),
        P("batch", None, None, "chan"),
    )
    return jax.shard_map(
        local,
        mesh=mesh,
        in_specs=placed,
        out_specs=(
            P("batch", None, None, "chan"),
            P("batch", None, None, "chan"),
            P("batch", None, None, "chan"),
            P("chan", "batch"),
            P(None, "batch", "chan"),
            P("batch", "chan"),
            P(None, "chan", None, "batch"),
            P(None, None, None, "batch", "chan"),
            P(None, "chan"),
            P(None, "chan"),
            P(None, "chan"),
            P(None, "chan"),
            P(None, "chan"),
            P("chan"),
            P("chan"),
        ),
        check_vma=False,
    )
```

```python
import functools

import jax
import jax.numpy as jnp
from jax import lax
from jax.experimental import pallas as pl
from jax.experimental.pallas import tpu as pltpu
from jax.sharding import PartitionSpec as P

EPSILON = 1e-05
OFFSETS = ((-1, -1), (-1, 0), (-1, 1), (0, -1), (0, 0), (0, 1), (1, -1), (1, 0), (1, 1))
OWN_HEAD = (0, 3)
SOURCE_START = (1, 0)


def silu_slope(values):
    sig = jax.nn.sigmoid(values)
    return sig * (1.0 + values * (1.0 - sig))


def shifted(values, vertical, lateral):
    row_count, column_count = (values.shape[1], values.shape[2])
    widths = [(0, 0)] * values.ndim
    widths[1] = (1, 1)
    widths[2] = (1, 1)
    padded = jnp.pad(values, widths)
    return padded[
        :, 1 + vertical : 1 + vertical + row_count, 1 + lateral : 1 + lateral + column_count
    ]


def tap_masks(image_ids):
    row_count, column_count = (image_ids.shape[1], image_ids.shape[2])
    padded = jnp.pad(image_ids, ((0, 0), (1, 1), (1, 1)), constant_values=-1)
    masks = []
    for vertical, lateral in OFFSETS:
        beside = padded[
            :, 1 + vertical : 1 + vertical + row_count, 1 + lateral : 1 + lateral + column_count
        ]
        masks.append((beside == image_ids).astype(jnp.float32))
    return jnp.stack(masks)


def conv_forward(inputs, weight, masks):
    total = 0.0
    for number, (vertical, lateral) in enumerate(OFFSETS):
        moved = shifted(inputs, vertical, lateral) * masks[number][..., None].astype(inputs.dtype)
        total = total + jnp.einsum(
            "nhwc,co->nhwo", moved, weight[number], preferred_element_type=jnp.float32
        )
    return total


def conv_input_grad(grads, weight, masks):
    total = 0.0
    for number, (vertical, lateral) in enumerate(OFFSETS):
        term = jnp.einsum(
            "nhwo,co->nhwc", grads, weight[number], preferred_element_type=jnp.float32
        )
        total = total + shifted(term * masks[number][..., None], -vertical, -lateral)
    return total


def conv_weight_grad(inputs, grads, masks):
    pieces = []
    for number, (vertical, lateral) in enumerate(OFFSETS):
        moved = shifted(inputs, vertical, lateral) * masks[number][..., None].astype(inputs.dtype)
        pieces.append(jnp.einsum("nhwc,nhwo->co", moved, grads, preferred_element_type=jnp.float32))
    return jnp.stack(pieces)


def pixel_sum(values):
    return jnp.sum(values, axis=(0, 1, 2))


def normalize(values, scale, shift, count):
    total, squares = lax.psum((pixel_sum(values), pixel_sum(values * values)), "batch")
    center = total / count
    inverse = lax.rsqrt(squares / count - center * center + EPSILON)
    normed = (values - center) * inverse
    return (normed, inverse, normed * scale + shift)


def grad_sums(first_sum, second_sum):
    return lax.psum((first_sum, second_sum), "batch")


def normalize_back(grads, normed, inverse, scale, shift_sum, scale_sum, count):
    return scale * inverse * (grads - (shift_sum + normed * scale_sum) / count)


def channel_gather(values):
    return lax.all_gather(values, "chan", axis=4, tiled=True)


def channel_sum(values):
    return lax.psum_scatter(
        values.astype(jnp.bfloat16), "chan", scatter_dimension=4, tiled=True
    ).astype(jnp.float32)


def fetch_weights(reduce_weight, spatial_weight, expand_weight, head_weights, distil_weights):
    return (
        lax.all_gather(reduce_weight, "batch", axis=1, tiled=True),
        lax.all_gather(spatial_weight, "batch", axis=1, tiled=True),
        lax.all_gather(expand_weight, "batch", axis=0, tiled=True),
        lax.all_gather(head_weights, "batch", axis=3, tiled=True),
        lax.all_gather(distil_weights, "batch", axis=3, tiled=True),
    )


def scatter_weights(grads):
    reduce_grad, spatial_grad, expand_grad, heads_grad, distil_grad = grads
    return (
        lax.psum_scatter(reduce_grad, "batch", scatter_dimension=1, tiled=True),
        lax.psum_scatter(spatial_grad, "batch", scatter_dimension=1, tiled=True),
        lax.psum_scatter(expand_grad, "batch", scatter_dimension=0, tiled=True),
        lax.psum_scatter(heads_grad, "batch", scatter_dimension=3, tiled=True),
        lax.psum_scatter(distil_grad, "batch", scatter_dimension=3, tiled=True),
    )


def micro_step(inputs, image_ids, depth_cot, segment_cot, gathered, small, batch_count):
    reduce_full, spatial_full, expand_full, heads_full, distil_full = gathered
    block_scale, block_shift, head_scale, head_shift, gate_bias, output_scale, output_shift = small
    masks = tap_masks(image_ids)
    canvases, row_count, column_count = image_ids.shape
    count = float(batch_count * canvases * row_count * column_count)
    first_partial = jnp.einsum(
        "nhwc,co->nhwo", inputs, reduce_full, preferred_element_type=jnp.float32
    )
    first = channel_sum(first_partial[:, :, :, None, :])
    first_norm, first_inv, first_out = normalize(first, block_scale[0:1], block_shift[0:1], count)
    first_act = jax.nn.silu(first_out).astype(jnp.bfloat16)
    first_full = channel_gather(first_act)[:, :, :, 0, :]
    second = conv_forward(first_full, spatial_full, masks)[:, :, :, None, :]
    second_norm, second_inv, second_out = normalize(
        second, block_scale[1:2], block_shift[1:2], count
    )
    second_act = jax.nn.silu(second_out).astype(jnp.bfloat16)
    second_full = channel_gather(second_act)[:, :, :, 0, :]
    third = jnp.einsum(
        "nhwc,co->nhwo", second_full, expand_full, preferred_element_type=jnp.float32
    )[:, :, :, None, :]
    third_norm, third_inv, third_out = normalize(
        third, output_scale[None], output_shift[None], count
    )
    summed = third_out[:, :, :, 0, :] + inputs.astype(jnp.float32)
    block_out = jax.nn.silu(summed).astype(jnp.bfloat16)
    heads_flat = heads_full.reshape(heads_full.shape[0], heads_full.shape[1], -1)
    head_partial = conv_forward(block_out, heads_flat, masks)
    head_pre = channel_sum(
        head_partial.reshape(head_partial.shape[:3] + (heads_full.shape[2], heads_full.shape[3]))
    )
    head_norm, head_inv, head_out = normalize(head_pre, head_scale, head_shift, count)
    head_act = jax.nn.silu(head_out).astype(jnp.bfloat16)
    head_full = channel_gather(head_act)
    head_width = head_full.shape[4]
    gate_pre = [0.0, 0.0]
    message = [0.0, 0.0]
    for number, (vertical, lateral) in enumerate(OFFSETS):
        moved = shifted(head_full, vertical, lateral) * masks[number][:, :, :, None, None].astype(
            jnp.bfloat16
        )
        for stream in range(2):
            weights_here = distil_full[stream, number]
            first_source = SOURCE_START[stream]
            sources = moved[:, :, :, first_source : first_source + 3].reshape(
                moved.shape[:3] + (3 * head_width,)
            )
            gate_pre[stream] = gate_pre[stream] + jnp.einsum(
                "nhwc,co->nhwo",
                moved[:, :, :, OWN_HEAD[stream]],
                weights_here[0],
                preferred_element_type=jnp.float32,
            )
            message[stream] = message[stream] + jnp.einsum(
                "nhwc,co->nhwo",
                sources,
                weights_here[1:].reshape(3 * head_width, -1),
                preferred_element_type=jnp.float32,
            )
    cotangents = (depth_cot.astype(jnp.float32), segment_cot.astype(jnp.float32))
    outputs, message_grads, gate_grads = ([], [], [])
    for stream in range(2):
        gate_value = jax.nn.sigmoid(gate_pre[stream] + gate_bias[stream])
        own_feature = head_act[:, :, :, OWN_HEAD[stream]].astype(jnp.float32)
        outputs.append((own_feature + gate_value * message[stream]).astype(jnp.bfloat16))
        message_grads.append((cotangents[stream] * gate_value).astype(jnp.bfloat16))
        gate_grads.append(
            (cotangents[stream] * message[stream] * gate_value * (1.0 - gate_value)).astype(
                jnp.bfloat16
            )
        )
    spread_grad = 0.0
    distil_parts = [[], []]
    for number, (vertical, lateral) in enumerate(OFFSETS):
        tap_mask = masks[number][:, :, :, None, None]
        moved = shifted(head_full, vertical, lateral) * tap_mask.astype(jnp.bfloat16)
        tap_grad = jnp.zeros(head_full.shape, jnp.float32)
        for stream in range(2):
            weights_here = distil_full[stream, number]
            first_source = SOURCE_START[stream]
            sources = moved[:, :, :, first_source : first_source + 3].reshape(
                moved.shape[:3] + (3 * head_width,)
            )
            own_grad = jnp.einsum(
                "nhwo,co->nhwc",
                gate_grads[stream],
                weights_here[0],
                preferred_element_type=jnp.float32,
            )
            source_grad = jnp.einsum(
                "nhwo,co->nhwc",
                message_grads[stream],
                weights_here[1:].reshape(3 * head_width, -1),
                preferred_element_type=jnp.float32,
            )
            tap_grad = tap_grad.at[:, :, :, OWN_HEAD[stream]].add(own_grad)
            tap_grad = tap_grad.at[:, :, :, first_source : first_source + 3].add(
                source_grad.reshape(source_grad.shape[:3] + (3, head_width))
            )
            gate_weight_grad = jnp.einsum(
                "nhwc,nhwo->co",
                moved[:, :, :, OWN_HEAD[stream]],
                gate_grads[stream],
                preferred_element_type=jnp.float32,
            )
            source_weight_grad = jnp.einsum(
                "nhwc,nhwo->co", sources, message_grads[stream], preferred_element_type=jnp.float32
            )
            distil_parts[stream].append(
                jnp.concatenate(
                    [gate_weight_grad[None], source_weight_grad.reshape(3, head_width, -1)], axis=0
                )
            )
        spread_grad = spread_grad + shifted(tap_grad * tap_mask, -vertical, -lateral)
    distil_grad = jnp.stack([jnp.stack(distil_parts[0]), jnp.stack(distil_parts[1])])
    head_grad = channel_sum(spread_grad)
    head_grad = (
        head_grad.at[:, :, :, OWN_HEAD[0]]
        .add(cotangents[0])
        .at[:, :, :, OWN_HEAD[1]]
        .add(cotangents[1])
    )
    head_grad = head_grad * silu_slope(head_out)
    gate_sums = jnp.stack(
        [pixel_sum(gate_grads[0].astype(jnp.float32)), pixel_sum(gate_grads[1].astype(jnp.float32))]
    )
    shift_sums, scale_sums = grad_sums(
        jnp.concatenate([pixel_sum(head_grad), gate_sums], axis=0), pixel_sum(head_grad * head_norm)
    )
    head_pre_grad = normalize_back(
        head_grad, head_norm, head_inv, head_scale, shift_sums[:4], scale_sums, count
    ).astype(jnp.bfloat16)
    head_pre_full = channel_gather(head_pre_grad)
    head_flat_grad = head_pre_full.reshape(head_pre_full.shape[:3] + (-1,))
    block_grad = conv_input_grad(head_flat_grad, heads_flat, masks)
    heads_grad = conv_weight_grad(block_out, head_flat_grad, masks).reshape(heads_full.shape)
    summed_grad = block_grad * silu_slope(summed)
    third_grad = summed_grad[:, :, :, None, :]
    third_shift, third_scale = grad_sums(pixel_sum(third_grad), pixel_sum(third_grad * third_norm))
    third_pre = normalize_back(
        third_grad, third_norm, third_inv, output_scale[None], third_shift, third_scale, count
    ).astype(jnp.bfloat16)[:, :, :, 0, :]
    expand_grad = jnp.einsum(
        "nhwc,nhwo->co", second_full, third_pre, preferred_element_type=jnp.float32
    )
    second_grad = channel_sum(
        jnp.einsum("nhwo,co->nhwc", third_pre, expand_full, preferred_element_type=jnp.float32)[
            :, :, :, None, :
        ]
    )
    second_grad = second_grad * silu_slope(second_out)
    second_shift, second_scale = grad_sums(
        pixel_sum(second_grad), pixel_sum(second_grad * second_norm)
    )
    second_pre = normalize_back(
        second_grad, second_norm, second_inv, block_scale[1:2], second_shift, second_scale, count
    ).astype(jnp.bfloat16)[:, :, :, 0, :]
    spatial_grad = conv_weight_grad(first_full, second_pre, masks)
    first_grad = channel_sum(conv_input_grad(second_pre, spatial_full, masks)[:, :, :, None, :])
    first_grad = first_grad * silu_slope(first_out)
    first_shift, first_scale = grad_sums(pixel_sum(first_grad), pixel_sum(first_grad * first_norm))
    first_pre = normalize_back(
        first_grad, first_norm, first_inv, block_scale[0:1], first_shift, first_scale, count
    ).astype(jnp.bfloat16)
    first_pre_full = channel_gather(first_pre)[:, :, :, 0, :]
    reduce_grad = jnp.einsum(
        "nhwc,nhwo->co", inputs, first_pre_full, preferred_element_type=jnp.float32
    )
    input_grad = summed_grad + jnp.einsum(
        "nhwo,co->nhwc", first_pre_full, reduce_full, preferred_element_type=jnp.float32
    )
    weight_grads = (reduce_grad, spatial_grad, expand_grad, heads_grad, distil_grad)
    small_grads = (
        jnp.concatenate([first_scale, second_scale], axis=0),
        jnp.concatenate([first_shift, second_shift], axis=0),
        scale_sums,
        shift_sums[:4],
        shift_sums[4:],
        third_scale[0],
        third_shift[0],
    )
    return (outputs[0], outputs[1], input_grad, weight_grads, small_grads)


def gathered_local(
    features,
    image_ids,
    reduce_weight,
    spatial_weight,
    expand_weight,
    head_weights,
    distil_weights,
    block_scale,
    block_shift,
    head_scale,
    head_shift,
    gate_bias,
    output_scale,
    output_shift,
    depth_cotangent,
    segment_cotangent,
):
    batch_count = lax.axis_size("batch")
    small = (
        block_scale,
        block_shift,
        head_scale,
        head_shift,
        gate_bias,
        output_scale,
        output_shift,
    )
    depth_list, segment_list, input_list = ([], [], [])
    weight_total = None
    small_total = None
    for micro_index in range(features.shape[0]):
        gathered = fetch_weights(
            reduce_weight, spatial_weight, expand_weight, head_weights, distil_weights
        )
        canvas_pick = slice(micro_index, micro_index + 1)
        depth_out, segment_out, input_grad, weight_grads, small_grads = micro_step(
            features[canvas_pick],
            image_ids[canvas_pick],
            depth_cotangent[canvas_pick],
            segment_cotangent[canvas_pick],
            gathered,
            small,
            batch_count,
        )
        weight_grads = scatter_weights(weight_grads)
        weight_total = (
            weight_grads
            if weight_total is None
            else jax.tree.map(jnp.add, weight_total, weight_grads)
        )
        small_total = (
            small_grads if small_total is None else jax.tree.map(jnp.add, small_total, small_grads)
        )
        depth_list.append(depth_out)
        segment_list.append(segment_out)
        input_list.append(input_grad)
    reduce_grad, spatial_grad, expand_grad, heads_grad, distil_grad = weight_total
    scale_mid, shift_mid, scale_heads, shift_heads, bias_gates, scale_out, shift_out = small_total
    return (
        jnp.concatenate(depth_list, axis=0),
        jnp.concatenate(segment_list, axis=0),
        jnp.concatenate(input_list, axis=0),
        reduce_grad,
        spatial_grad,
        expand_grad,
        heads_grad,
        distil_grad,
        scale_mid,
        shift_mid,
        scale_heads,
        shift_heads,
        bias_gates,
        scale_out,
        shift_out,
    )


MESH = pl.DeviceIdType.MESH
PIXELS = 256
PAD = 32
LANES = 128


def whereabouts():
    place, lane = lax.axis_index("batch"), lax.axis_index("chan")
    return place, lane, place // 2, place % 2, lane // 2, lane % 2


def ranked(depth, rank):
    high, low = depth // 2, depth % 2
    up, odd = rank // 2, rank % 2
    return (
        (1 - odd) * (1 - up) * depth
        + odd * (1 - up) * (1 + low)
        + (1 - odd) * up * (2 - 2 * low + high)
        + odd * up * (3 - 3 * high)
    )


def middle(depth):
    return (depth // 2 + depth % 2) % 2


def inner(depth):
    return 1 + depth % 2


def outer(depth):
    return 3 * (depth // 2)


def onward(depth, rank):
    second = (1 - rank % 2) * (rank // 2)
    return outer(depth) + second * (3 - depth - outer(depth))


def homeward(depth, rank):
    second = (1 - rank % 2) * (rank // 2) * middle(depth)
    return inner(depth) + second * (outer(depth) - inner(depth))


def staggered(step):
    late = ((step + 1) % 2) * ((step + 14) // 15) + step // 15
    return (1 - late) * ((step + 1) // 2) + late * (step // 2 - 1 + step // 15), late


def push(source, target, send_sem, recv_sem, place, lane):
    return pltpu.make_async_remote_copy(
        src_ref=source,
        dst_ref=target,
        send_sem=send_sem,
        recv_sem=recv_sem,
        device_id=(place, lane),
        device_id_type=MESH,
    )


def greet(peers):
    barrier = pltpu.get_barrier_semaphore()
    for place, lane in peers:
        pl.semaphore_signal(barrier, inc=1, device_id=(place, lane), device_id_type=MESH)
    pl.semaphore_wait(barrier, len(peers))


def batch_peers():
    place, lane, _, _, _, _ = whereabouts()
    return [((place + step) % 8, lane) for step in range(1, 8)]


def line_peers():
    place, lane, depth, side, _, _ = whereabouts()
    peers = [(ranked(depth, rank) * 2 + side, lane) for rank in range(1, 4)]
    return peers + [(depth * 2 + 1 - side, lane)]


def chan_peers():
    place, lane, _, _, _, _ = whereabouts()
    return [(place, (lane + step) % 4) for step in range(1, 4)]


class Gather:
    def __init__(self, values, recv, cross, line, parts):
        self.values, self.recv, self.cross, self.line, self.parts = values, recv, cross, line, parts

    def view(self, block, part):
        return self.values.at[block] if self.parts == 1 else self.values.at[block, part]

    def copy(self, block, part, sem, depth, side):
        lane = lax.axis_index("chan")
        here = self.view(block, part)
        return push(here, here, sem, self.recv.at[block, part], depth * 2 + side, lane)

    def start(self, part=0):
        place, lane, depth, side, _, _ = whereabouts()
        self.copy(place, part, self.line.at[0, 0, part], inner(depth), side).start()

        @pl.when(middle(depth) == 1)
        def _():
            self.copy(place, part, self.line.at[1, 0, part], outer(depth), side).start()

        self.copy(place, part, self.cross.at[0, part], depth, 1 - side).start()

    def near(self, rank, part=0):
        place, lane, depth, side, _, _ = whereabouts()
        block = ranked(depth, rank) * 2 + side
        self.copy(block, part, self.cross.at[rank, part], depth, side).wait_recv()

        @pl.when(middle(depth) == 1)
        def _():
            self.copy(block, part, self.line.at[0, rank, part], onward(depth, rank), side).start()

        self.copy(block, part, self.cross.at[rank, part], depth, 1 - side).start()

    def far(self, rank, part=0):
        place, lane, depth, side, _, _ = whereabouts()
        block = ranked(depth, rank) * 2 + 1 - side
        self.copy(block, part, self.cross.at[rank, part], depth, side).wait_recv()

    def next(self, step):
        place, lane, depth, side, _, _ = whereabouts()
        item, late = staggered(step)
        part, rank = item // 4, item % 4

        @pl.when((late == 0) & (rank > 0))
        def _():
            self.near(rank, part)

        @pl.when(late == 1)
        def _():
            self.far(rank, part)

        return ranked(depth, rank) * 2 + (side + late) % 2, part

    def close(self):
        place, lane, depth, side, _, _ = whereabouts()
        for part in range(self.parts):
            for rank in range(4):
                self.copy(place, part, self.cross.at[rank, part], depth, side).wait_send()
            self.copy(place, part, self.line.at[0, 0, part], depth, side).wait_send()

            @pl.when(middle(depth) == 1)
            def _():
                self.copy(place, part, self.line.at[1, 0, part], depth, side).wait_send()
                for rank in range(1, 4):
                    self.copy(place, part, self.line.at[0, rank, part], depth, side).wait_send()


def gather_sems(parts):
    return [
        pltpu.SemaphoreType.DMA((8, parts)),
        pltpu.SemaphoreType.DMA((4, parts)),
        pltpu.SemaphoreType.DMA((2, 4, parts)),
    ]


def clear_edges(turned):
    edge = jnp.zeros((3, PAD, turned.shape[2]), turned.dtype)
    turned[:, 0:PAD] = edge
    turned[:, PAD + PIXELS :] = edge


def fill_columns(value, mask, turned, columns, row=0, flip=False):
    width = value.shape[1]
    lanes = slice(0, width)
    wide = value.astype(jnp.float32)
    inside = slice(PAD, PAD + PIXELS)
    turned[0, inside, lanes] = pltpu.roll(wide, 1, 0).astype(jnp.bfloat16)
    turned[1, inside, lanes] = value
    turned[2, inside, lanes] = pltpu.roll(wide, PIXELS - 1, 0).astype(jnp.bfloat16)
    for number, (vertical, lateral) in enumerate(OFFSETS):
        start = PAD + 32 * vertical
        slot = 8 - number if flip else number
        columns[row : row + PIXELS, slot * width : (slot + 1) * width] = (
            turned[lateral + 1, start : start + PIXELS, lanes] * mask[:, number : number + 1]
        )


def vmem(count):
    return [pl.BlockSpec(memory_space=pltpu.VMEM)] * count


def kernel_params(number):
    return pltpu.CompilerParams(
        collective_id=number, has_side_effects=True, vmem_limit_bytes=60 * 2**20
    )


class Exchange:
    def __init__(self, values, send, recv, axis):
        self.values, self.send, self.recv, self.axis = values, send, recv, axis

    def steps(self):
        place, lane, _, _, _, _ = whereabouts()
        if self.axis == "batch":
            return [(step - 1, (place + step) % 8, lane, (place + step) % 8) for step in range(1, 8)]
        return [(step - 1, place, (lane + step) % 4, (lane + step) % 4) for step in range(1, 4)]

    def mine(self):
        place, lane, _, _, _, _ = whereabouts()
        return place if self.axis == "batch" else lane

    def start(self):
        here = self.values.at[self.mine()]
        for number, place, lane, _ in self.steps():
            push(here, here, self.send.at[number], self.recv.at[self.mine()], place, lane).start()

    def wait(self):
        for number, place, lane, slot in self.steps():
            there = self.values.at[slot]
            push(there, there, self.send.at[number], self.recv.at[slot], place, lane).wait_recv()

    def close(self):
        here = self.values.at[self.mine()]
        for number, place, lane, _ in self.steps():
            push(here, here, self.send.at[number], self.recv.at[self.mine()], place, lane).wait_send()

    def total(self):
        result = self.values[0]
        for slot in range(1, self.values.shape[0]):
            result = result + self.values[slot]
        return result


class Pieces:
    def __init__(self, stage, got, send, recv):
        self.stage, self.got, self.send, self.recv = stage, got, send, recv

    def start(self, part):
        place, lane, _, _, _, _ = whereabouts()
        for slot in range(4):
            self.stage[slot] = part[:, slot * LANES : (slot + 1) * LANES].astype(jnp.bfloat16)
        for step in (2, 1, 3):
            slot = (lane + step) % 4
            push(
                self.stage.at[slot],
                self.got.at[lane],
                self.send.at[slot],
                self.recv.at[lane],
                place,
                slot,
            ).start()

    def finish(self):
        place, lane, _, _, _, _ = whereabouts()
        self.got[lane] = self.stage[lane]
        for step in range(1, 4):
            slot = (lane + step) % 4
            push(
                self.stage.at[slot],
                self.got.at[slot],
                self.send.at[slot],
                self.recv.at[slot],
                place,
                lane,
            ).wait()
        result = self.got[0].astype(jnp.float32)
        for slot in range(1, 4):
            result = result + self.got[slot].astype(jnp.float32)
        return result


class Local:
    def __init__(self, pairs, sems):
        self.copies = [
            pltpu.make_async_copy(source, target, sems.at[number])
            for number, (source, target) in enumerate(pairs)
        ]

    def start(self, *numbers):
        for number in numbers:
            self.copies[number].start()

    def wait(self, *numbers):
        for number in numbers:
            self.copies[number].wait()


def anywhere(count):
    return [pl.BlockSpec(memory_space=pl.ANY)] * count


def micro_rows(micro):
    return slice(micro * PIXELS, (micro + 1) * PIXELS)


def moments(value, other):
    rows = []
    for micro in range(2):
        part = value[micro_rows(micro)]
        rows.append(jnp.sum(part, axis=0, keepdims=True))
        rows.append(jnp.sum(part * other[micro_rows(micro)], axis=0, keepdims=True))
    return rows


def tile_rows(rows, height):
    width = rows[0].shape[1]
    return jnp.concatenate(rows + [jnp.zeros((height - len(rows), width), jnp.float32)], axis=0)


def normed_part(value, totals, micro, count):
    center = totals[2 * micro : 2 * micro + 1] / count
    inverse = lax.rsqrt(totals[2 * micro + 1 : 2 * micro + 2] / count - center * center + EPSILON)
    return (value[micro_rows(micro)] - center) * inverse, inverse


def dot_last(first, second):
    return lax.dot_general(
        first, second, (((1,), (1,)), ((), ())), preferred_element_type=jnp.float32
    )


def make_masks(ids_ref, mask_all):
    rows = 8 * ids_ref.shape[0]
    ids = ids_ref[...].reshape(rows, PIXELS).T
    pixel = lax.broadcasted_iota(jnp.int32, (PIXELS, rows), 0)
    taps = []
    for vertical, lateral in OFFSETS:
        offset = 32 * vertical + lateral
        beside = ids if offset == 0 else pltpu.roll(ids, (-offset) % PIXELS, 0)
        row, col = (pixel >> 5) + vertical, (pixel & 31) + lateral
        inside = (row >= 0) & (row < 8) & (col >= 0) & (col < 32)
        taps.append(jnp.where(inside & (beside == ids), 1.0, 0.0).astype(jnp.bfloat16))
    taps = jnp.concatenate(taps + [jnp.zeros_like(taps[0])], axis=1)
    item = lax.broadcasted_iota(jnp.int32, (10 * rows, LANES), 0)
    lane = lax.broadcasted_iota(jnp.int32, (10 * rows, LANES), 1)
    for block in range(8):
        for micro in range(2):
            chosen = jnp.where(item == lane * rows + (8 * block + micro), 1.0, 0.0)
            mask_all[block, micro] = jnp.dot(
                taps, chosen.astype(jnp.bfloat16), preferred_element_type=jnp.float32
            ).astype(jnp.bfloat16)


def front_kernel(
    count,
    x_ref,
    ids_ref,
    reduce_ref,
    spatial_ref,
    expand_ref,
    block_scale,
    block_shift,
    output_scale,
    output_shift,
    head_scale,
    head_shift,
    depth_cot,
    segment_cot,
    y_ref,
    norm3_ref,
    inverse3_ref,
    norm12_ref,
    inverse12_ref,
    mine_ref,
    mask_ref,
    act1_out,
    act2_out,
    reduce_out,
    spatial_out,
    expand_out,
    mask_out,
    cot_out,
    act1_ref,
    act2_ref,
    reduce_all,
    spatial_all,
    expand_all,
    mask_all,
    cot_all,
    packed,
    turned,
    columns,
    stage,
    got,
    sums1,
    sums2,
    sums3,
    head_all,
    ids_all,
    *sems,
):
    place, lane, depth, side, upper, core = whereabouts()
    reduces = Gather(reduce_all, *sems[0:3], 1)
    spatials = Gather(spatial_all, *sems[3:6], 1)
    expands = Gather(expand_all, *sems[6:9], 1)
    ids = Exchange(ids_all, sems[9], sems[10], "batch")
    pieces = Pieces(stage, got, sems[11], sems[12])
    first_sums = Exchange(sums1, sems[13], sems[14], "batch")
    second_sums = Exchange(sums2, sems[15], sems[16], "batch")
    third_sums = Exchange(sums3, sems[17], sems[18], "batch")
    heads = Exchange(head_all, sems[19], sems[20], "chan")
    first_acts = Exchange(act1_ref, sems[21], sems[22], "chan")
    second_acts = Exchange(act2_ref, sems[23], sems[24], "chan")

    local = Local(
        (
            (act1_ref, act1_out),
            (act2_ref, act2_out),
            (reduce_all, reduce_out),
            (spatial_all, spatial_out),
            (expand_all, expand_out),
            (mask_all, mask_out),
            (cot_all, cot_out),
        ),
        sems[27],
    )
    cot_sem, cot_recv = sems[25:27]

    def cot_copy(parity, slot, target):
        return push(
            packed.at[parity], cot_all.at[slot], cot_sem.at[parity], cot_recv.at[slot], target, lane
        )

    greet(batch_peers() + chan_peers())
    reduce_all[place] = reduce_ref[...]
    ids_all[place, 0:2] = ids_ref[...].astype(jnp.float32)
    ids_all[place, 2:8] = jnp.zeros((6, PIXELS), jnp.float32)
    reduces.start()
    ids.start()
    spatial_all[place] = spatial_ref[...]
    expand_all[place] = expand_ref[...]
    head_all[lane, 0:4] = head_scale[...]
    head_all[lane, 4:8] = head_shift[...]
    heads.start()
    clear_edges(turned)
    for rank in range(1, 4):
        reduces.near(rank)
    spatials.start()
    for rank in range(4):
        reduces.far(rank)
    x = x_ref[...].reshape(2 * PIXELS, x_ref.shape[2])
    pieces.start(dot_last(x, reduce_all[...].reshape(512, 512)))
    ids.wait()
    make_masks(ids_all, mask_all)
    mask_ref[...] = mask_all[place]
    local.start(2, 5)
    spatials.near(1)
    first = pieces.finish()
    sums1[place] = tile_rows(moments(first, first), 8)
    first_sums.start()
    spatials.near(2)
    expands.start()
    spatials.near(3)
    half_width = LANES // 2
    left = lax.broadcasted_iota(jnp.int32, (PIXELS, LANES), 1) < half_width
    for micro in range(2):
        upper_cot, lower_cot = (ref[micro].astype(jnp.float32) for ref in (depth_cot, segment_cot))
        packed[0, micro] = jnp.where(left, upper_cot, pltpu.roll(lower_cot, half_width, 1)).astype(
            jnp.bfloat16
        )
        packed[1, micro] = jnp.where(left, pltpu.roll(upper_cot, half_width, 1), lower_cot).astype(
            jnp.bfloat16
        )
    first_sums.wait()
    totals = first_sums.total()
    rows = []
    for micro in range(2):
        normed, inverse = normed_part(first, totals, micro, count)
        norm12_ref[0, micro_rows(micro)] = normed
        rows.append(inverse)
        out = normed * block_scale[0:1] + block_shift[0:1]
        act1_ref[lane, micro_rows(micro)] = (out * jax.nn.sigmoid(out)).astype(jnp.bfloat16)
    first_acts.start()
    expands.near(1)
    for rank in range(4):
        spatials.far(rank)
    expands.near(2)
    first_acts.wait()
    local.start(0, 3)
    for micro in range(2):
        value = jnp.concatenate([act1_ref[slot, micro_rows(micro)] for slot in range(4)], axis=1)
        fill_columns(value, mask_all[place, micro], turned, columns, micro * PIXELS)
    second = jnp.zeros((2 * PIXELS, LANES), jnp.float32)
    for number in range(9):
        second = second + jnp.dot(
            columns[:, number * 512 : (number + 1) * 512],
            spatial_all[:, number].reshape(512, LANES),
            preferred_element_type=jnp.float32,
        )
    sums2[place] = tile_rows(moments(second, second), 8)
    second_sums.start()
    expands.near(3)
    for parity in range(2):
        target = 2 * lane + parity

        @pl.when(target == place)
        def _():
            cot_all[place] = packed[parity]

        @pl.when(target != place)
        def _():
            cot_copy(parity, place, target).start()

    second_sums.wait()
    totals = second_sums.total()
    for micro in range(2):
        normed, inverse = normed_part(second, totals, micro, count)
        norm12_ref[1, micro_rows(micro)] = normed
        rows.append(inverse)
        out = normed * block_scale[1:2] + block_shift[1:2]
        act2_ref[lane, micro_rows(micro)] = (out * jax.nn.sigmoid(out)).astype(jnp.bfloat16)
    second_acts.start()
    inverse12_ref[...] = tile_rows(rows, 8)
    heads.wait()
    low = lax.broadcasted_iota(jnp.int32, (1, LANES), 1) < half_width
    source = place // 2
    even = place % 2 == 0
    for kind in range(2):
        upper_row = head_all[source, pl.ds(4 * kind + 2 * upper, 1)]
        lower_row = head_all[source, pl.ds(4 * kind + 2 * upper + 1, 1)]
        mine_ref[kind : kind + 1] = jnp.where(
            even,
            jnp.where(low, upper_row, pltpu.roll(lower_row, half_width, 1)),
            jnp.where(low, pltpu.roll(upper_row, half_width, 1), lower_row),
        )
    for rank in range(4):
        expands.far(rank)
    second_acts.wait()
    local.start(1, 4)
    value = jnp.concatenate([act2_ref[slot] for slot in range(4)], axis=1)
    third = jnp.dot(
        value, expand_all[...].reshape(512, 512), preferred_element_type=jnp.float32
    )
    sums3[place] = tile_rows(moments(third, third), 8)
    third_sums.start()
    third_sums.wait()
    totals = third_sums.total()
    rows = []
    for micro in range(2):
        normed, inverse = normed_part(third, totals, micro, count)
        norm3_ref[micro_rows(micro)] = normed
        rows.append(inverse)
        out = normed * output_scale[...] + output_shift[...] + x_ref[micro].astype(jnp.float32)
        y_ref[micro] = (out * jax.nn.sigmoid(out)).astype(jnp.bfloat16)
    inverse3_ref[...] = tile_rows(rows, 8)
    @pl.when(place // 2 == lane)
    def _():
        for step in range(1, 8):
            cot_copy(0, (place + step) % 8, place).wait_recv()

    local.start(6)
    for parity in range(2):
        @pl.when(2 * lane + parity != place)
        def _():
            cot_copy(parity, place, place).wait_send()

    local.wait(0, 1, 2, 3, 4, 5, 6)
    for item in (reduces, spatials, expands, ids, heads, first_acts, second_acts):
        item.close()
    for item in (first_sums, second_sums, third_sums):
        item.close()


def exchange_sems(size):
    return [pltpu.SemaphoreType.DMA((size - 1,)), pltpu.SemaphoreType.DMA((size,))]


def run_front(count, *arrays):
    f32, bf16 = jnp.float32, jnp.bfloat16
    kept = (
        (4, 2 * PIXELS, LANES),
        (4, 2 * PIXELS, LANES),
        (8, 64, 512),
        (8, 9, 64, LANES),
        (8, 64, 512),
        (8, 2, PIXELS, LANES),
        (8, 2, PIXELS, LANES),
    )
    return pl.pallas_call(
        functools.partial(front_kernel, count),
        name="front",
        out_shape=(
            jax.ShapeDtypeStruct((2, PIXELS, 512), bf16),
            jax.ShapeDtypeStruct((2 * PIXELS, 512), f32),
            jax.ShapeDtypeStruct((8, 512), f32),
            jax.ShapeDtypeStruct((2, 2 * PIXELS, LANES), f32),
            jax.ShapeDtypeStruct((8, LANES), f32),
            jax.ShapeDtypeStruct((2, LANES), f32),
            jax.ShapeDtypeStruct((2, PIXELS, LANES), bf16),
        )
        + tuple(jax.ShapeDtypeStruct(shape, bf16) for shape in kept),
        in_specs=vmem(13),
        out_specs=tuple(vmem(7) + anywhere(7)),
        scratch_shapes=[pltpu.VMEM(shape, bf16) for shape in kept]
        + [
            pltpu.VMEM((2, 2, PIXELS, LANES), bf16),
            pltpu.VMEM((3, 2 * PAD + PIXELS, 512), bf16),
            pltpu.VMEM((2 * PIXELS, 9 * 512), bf16),
            pltpu.VMEM((4, 2 * PIXELS, LANES), bf16),
            pltpu.VMEM((4, 2 * PIXELS, LANES), bf16),
            pltpu.VMEM((8, 8, LANES), f32),
            pltpu.VMEM((8, 8, LANES), f32),
            pltpu.VMEM((8, 8, 512), f32),
            pltpu.VMEM((4, 8, LANES), f32),
            pltpu.VMEM((8, 8, PIXELS), f32),
        ]
        + gather_sems(1) * 3
        + exchange_sems(8)
        + [pltpu.SemaphoreType.DMA((4,))] * 2
        + exchange_sems(8) * 3
        + exchange_sems(4) * 3
        + [
            pltpu.SemaphoreType.DMA((2,)),
            pltpu.SemaphoreType.DMA((8,)),
            pltpu.SemaphoreType.DMA((7,)),
        ],
        compiler_params=kernel_params(1),
    )(*arrays)


class Scatter:
    def __init__(self, part, far_buf, far_got, near_buf, near_got, sems):
        self.part, self.far_buf, self.far_got = part, far_buf, far_got
        self.near_buf, self.near_got = near_buf, near_got
        self.far_send, self.far_recv, self.near_send, self.near_recv = sems

    def far_copy(self, level, place):
        return push(
            self.far_buf.at[level],
            self.far_got.at[level],
            self.far_send.at[level],
            self.far_recv.at[level],
            place,
            lax.axis_index("chan"),
        )

    def near_copy(self, rank, level, place):
        return push(
            self.near_buf.at[rank - 1],
            self.near_got.at[level],
            self.near_send.at[rank - 1],
            self.near_recv.at[level],
            place,
            lax.axis_index("chan"),
        )

    def start(self):
        place, lane, depth, side, _, _ = whereabouts()
        for rank in (3, 2, 1, 0):
            level = ranked(depth, rank)
            self.far_buf[level] = self.part[level * 2 + 1 - side].astype(jnp.bfloat16)
            self.far_copy(level, depth * 2 + 1 - side).start()

    def middle(self):
        place, lane, depth, side, _, _ = whereabouts()
        for rank in (3, 2, 1):
            level = ranked(depth, rank)
            self.far_copy(level, place).wait_recv()
            self.near_buf[rank - 1] = (
                self.part[level * 2 + side] + self.far_got[level].astype(jnp.float32)
            ).astype(jnp.bfloat16)
            self.near_copy(rank, depth, level * 2 + side).start()

    def finish(self):
        place, lane, depth, side, _, _ = whereabouts()
        self.far_copy(depth, place).wait_recv()
        result = self.part[place] + self.far_got[depth].astype(jnp.float32)
        for level in range(4):
            self.far_copy(level, place).wait_send()
        for rank in (3, 2, 1):
            level = ranked(depth, rank)
            self.near_copy(rank, level, place).wait()
            result = result + self.near_got[level].astype(jnp.float32)
        return result


def scatter_scratch(width):
    return [
        pltpu.VMEM((8, 64, width), jnp.float32),
        pltpu.VMEM((4, 64, width), jnp.bfloat16),
        pltpu.VMEM((4, 64, width), jnp.bfloat16),
        pltpu.VMEM((3, 64, width), jnp.bfloat16),
        pltpu.VMEM((4, 64, width), jnp.bfloat16),
    ]


def scatter_sems():
    return [
        pltpu.SemaphoreType.DMA((4,)),
        pltpu.SemaphoreType.DMA((4,)),
        pltpu.SemaphoreType.DMA((3,)),
        pltpu.SemaphoreType.DMA((4,)),
    ]


def back_part(value, normed, inverse, scale, shift_sum, scale_sum, count):
    return (scale * inverse * (value - (shift_sum + normed * scale_sum) / count)).astype(
        jnp.bfloat16
    )


def rear_kernel(
    count,
    grad_ref,
    x_ref,
    norm3_ref,
    inverse3_ref,
    norm12_ref,
    inverse12_ref,
    act1_ref,
    act2_ref,
    reduce_all,
    spatial_all,
    expand_all,
    mask_ref,
    block_scale,
    block_shift,
    output_scale,
    output_shift,
    head_ref,
    gate_ref,
    block_hbm,
    back_hbm,
    masks_hbm,
    features_ref,
    reduce_out,
    spatial_out,
    expand_out,
    block_scale_out,
    block_shift_out,
    head_scale_out,
    head_shift_out,
    gate_out,
    output_scale_out,
    output_shift_out,
    head_out,
    head_grad,
    block_all,
    head_back,
    mask_all,
    turned_wide,
    columns_wide,
    turned,
    columns,
    stage,
    got,
    stage_next,
    got_next,
    sums_a,
    sums_b,
    sums_c,
    head_all,
    act_all,
    back3,
    *rest,
):
    expand_bufs, spatial_bufs, reduce_bufs, sems = rest[0:5], rest[5:10], rest[10:15], rest[15:]
    place, lane, depth, side, upper, core = whereabouts()
    pieces = Pieces(stage, got, sems[0], sems[1])
    first = Exchange(sums_a, sems[2], sems[3], "batch")
    second = Exchange(sums_b, sems[4], sems[5], "batch")
    third = Exchange(sums_c, sems[6], sems[7], "batch")
    heads = Exchange(head_all, sems[8], sems[9], "chan")
    acts = Exchange(act_all, sems[10], sems[11], "chan")
    expands = Scatter(*expand_bufs, sems[12:16])
    spatials = Scatter(*spatial_bufs, sems[16:20])
    reduces = Scatter(*reduce_bufs, sems[20:24])
    pieces_next = Pieces(stage_next, got_next, sems[24], sems[25])

    loads = [
        pltpu.make_async_copy(source, target, sems[26].at[number])
        for number, (source, target) in enumerate(
            ((block_hbm, block_all), (back_hbm, head_back), (masks_hbm, mask_all))
        )
    ]
    for load in loads:
        load.start()

    def weigh(block):
        for micro in range(2):
            fill_columns(
                block_all[block, micro],
                mask_all[block, micro],
                turned_wide,
                columns_wide,
                micro * PIXELS,
            )
        value = jnp.concatenate(
            [
                jnp.concatenate([head_back[half, micro, block] for half in range(2)], axis=1)
                for micro in range(2)
            ],
            axis=0,
        ).T

        def tap(number, _):
            product = jnp.dot(
                value,
                columns_wide[:, pl.ds(pl.multiple_of(number * 512, 512), 512)],
                preferred_element_type=jnp.float32,
            )
            if block == 0:
                head_grad[number] = product
            else:
                head_grad[number] += product
            return 0

        lax.fori_loop(0, 9, tap, 0)

    greet(batch_peers() + chan_peers())
    clear_edges(turned_wide)
    half_width = LANES // 2
    even = place % 2 == 0
    mine = lax.broadcasted_iota(jnp.int32, (1, LANES), 1) >> 6 == place % 2
    rows = []
    for kind in range(2):
        own = head_ref[kind : kind + 1]
        turned_own = pltpu.roll(own, half_width, 1)
        first_row = jnp.where(mine, jnp.where(even, own, turned_own), 0.0)
        second_row = jnp.where(mine, jnp.where(even, turned_own, own), 0.0)
        for half in range(2):
            for row in (first_row, second_row):
                rows.append(jnp.where(upper == half, row, 0.0))
    head_all[lane] = jnp.concatenate(rows, axis=0)
    heads.start()
    clear_edges(turned)
    rows = []
    for micro in range(2):
        normed = norm3_ref[micro_rows(micro)]
        out = normed * output_scale[...] + output_shift[...] + x_ref[micro].astype(jnp.float32)
        value = grad_ref[micro_rows(micro)] * silu_slope(out)
        features_ref[micro] = value
        rows.append(jnp.sum(value, axis=0, keepdims=True))
        rows.append(jnp.sum(value * normed, axis=0, keepdims=True))
    heads.wait()
    sums_a[place, 0:8] = tile_rows(rows, 8)
    sums_a[place, 8:16] = jnp.zeros((8, 512), jnp.float32)
    sums_a[place, 4:6, 0:LANES] = gate_ref[...]
    sums_a[place, 8:16, 0:LANES] = jnp.where(place // 2 == lane, heads.total(), 0.0)
    first.start()
    for load in loads:
        load.wait()
    weigh(0)
    first.wait()
    totals = first.total()
    head_scale_out[...] = totals[8:12, 0:LANES]
    head_shift_out[...] = totals[12:16, 0:LANES]
    gate_out[...] = totals[4:6, 0:LANES]
    output_scale_out[...] = totals[1:2] + totals[3:4]
    output_shift_out[...] = totals[0:1] + totals[2:3]
    for micro in range(2):
        back3[micro_rows(micro)] = back_part(
            features_ref[micro],
            norm3_ref[micro_rows(micro)],
            inverse3_ref[micro : micro + 1],
            output_scale[...],
            totals[2 * micro : 2 * micro + 1],
            totals[2 * micro + 1 : 2 * micro + 2],
            count,
        )
    pieces.start(dot_last(back3[...], expand_all[...].reshape(512, 512)))
    value = jnp.concatenate([act2_ref[slot] for slot in range(4)], axis=1)
    expands.part[...] = jnp.dot(
        value.T, back3[...], preferred_element_type=jnp.float32
    ).reshape(8, 64, 512)
    expands.start()
    weigh(1)
    grad = pieces.finish()
    normed = norm12_ref[1]
    grad = grad * silu_slope(normed * block_scale[1:2] + block_shift[1:2])
    sums_b[place] = tile_rows(moments(grad, normed), 8)
    second.start()
    weigh(2)
    expands.middle()
    second.wait()
    totals = second.total()
    block_scale_out[1:2] = totals[1:2] + totals[3:4]
    block_shift_out[1:2] = totals[0:1] + totals[2:3]
    for micro in range(2):
        value = back_part(
            grad[micro_rows(micro)],
            normed[micro_rows(micro)],
            inverse12_ref[2 + micro : 3 + micro],
            block_scale[1:2],
            totals[2 * micro : 2 * micro + 1],
            totals[2 * micro + 1 : 2 * micro + 2],
            count,
        )
        fill_columns(value, mask_ref[micro], turned, columns, micro * PIXELS, True)
    part = jnp.zeros((2 * PIXELS, 512), jnp.float32)
    for number in range(9):
        part = part + dot_last(
            columns[:, number * LANES : (number + 1) * LANES],
            spatial_all[:, number].reshape(512, LANES),
        )
    pieces_next.start(part)
    value = jnp.concatenate([act1_ref[slot] for slot in range(4)], axis=1)
    spatials.part[...] = jnp.dot(
        value.T, columns[...], preferred_element_type=jnp.float32
    ).reshape(8, 64, 9 * LANES)
    spatials.start()
    weigh(3)
    grad = pieces_next.finish()
    normed = norm12_ref[0]
    grad = grad * silu_slope(normed * block_scale[0:1] + block_shift[0:1])
    sums_c[place] = tile_rows(moments(grad, normed), 8)
    third.start()
    weigh(4)
    spatials.middle()
    expand_out[...] = expands.finish()
    third.wait()
    totals = third.total()
    block_scale_out[0:1] = totals[1:2] + totals[3:4]
    block_shift_out[0:1] = totals[0:1] + totals[2:3]
    for micro in range(2):
        act_all[lane, micro_rows(micro)] = back_part(
            grad[micro_rows(micro)],
            normed[micro_rows(micro)],
            inverse12_ref[micro : micro + 1],
            block_scale[0:1],
            totals[2 * micro : 2 * micro + 1],
            totals[2 * micro + 1 : 2 * micro + 2],
            count,
        )
    acts.start()
    weigh(5)
    acts.wait()
    value = jnp.concatenate([act_all[slot] for slot in range(4)], axis=1)
    x = x_ref[...].reshape(2 * PIXELS, 512)
    reduces.part[...] = jnp.dot(value.T, x, preferred_element_type=jnp.float32).reshape(8, 64, 512)
    reduces.start()
    more = jnp.dot(value, reduce_all[...].reshape(512, 512), preferred_element_type=jnp.float32)
    for micro in range(2):
        features_ref[micro] = features_ref[micro] + more[micro_rows(micro)]
    weigh(6)
    weigh(7)
    store = pltpu.make_async_copy(head_grad, head_out, sems[26].at[3])
    store.start()
    reduces.middle()
    result = spatials.finish()
    for number in range(9):
        spatial_out[number] = result[:, number * LANES : (number + 1) * LANES]
    reduce_out[...] = reduces.finish()
    for item in (first, second, third, heads, acts):
        item.close()
    store.wait()


def run_rear(count, *arrays):
    f32, bf16 = jnp.float32, jnp.bfloat16
    return pl.pallas_call(
        functools.partial(rear_kernel, count),
        name="rear",
        out_shape=(
            jax.ShapeDtypeStruct((2, PIXELS, 512), f32),
            jax.ShapeDtypeStruct((64, 512), f32),
            jax.ShapeDtypeStruct((9, 64, LANES), f32),
            jax.ShapeDtypeStruct((64, 512), f32),
            jax.ShapeDtypeStruct((2, LANES), f32),
            jax.ShapeDtypeStruct((2, LANES), f32),
            jax.ShapeDtypeStruct((4, LANES), f32),
            jax.ShapeDtypeStruct((4, LANES), f32),
            jax.ShapeDtypeStruct((2, LANES), f32),
            jax.ShapeDtypeStruct((1, 512), f32),
            jax.ShapeDtypeStruct((1, 512), f32),
            jax.ShapeDtypeStruct((9, 256, 512), f32),
        ),
        in_specs=vmem(18) + [pl.BlockSpec(memory_space=pl.ANY)] * 3,
        out_specs=tuple(vmem(11) + anywhere(1)),
        scratch_shapes=[
            pltpu.VMEM((9, 256, 512), f32),
            pltpu.VMEM((8, 2, PIXELS, 512), bf16),
            pltpu.VMEM((2, 2, 8, PIXELS, LANES), bf16),
            pltpu.VMEM((8, 2, PIXELS, LANES), bf16),
            pltpu.VMEM((3, 2 * PAD + PIXELS, 512), bf16),
            pltpu.VMEM((2 * PIXELS, 9 * 512), bf16),
            pltpu.VMEM((3, 2 * PAD + PIXELS, LANES), bf16),
            pltpu.VMEM((2 * PIXELS, 9 * LANES), bf16),
            pltpu.VMEM((4, 2 * PIXELS, LANES), bf16),
            pltpu.VMEM((4, 2 * PIXELS, LANES), bf16),
            pltpu.VMEM((4, 2 * PIXELS, LANES), bf16),
            pltpu.VMEM((4, 2 * PIXELS, LANES), bf16),
            pltpu.VMEM((8, 16, 512), f32),
            pltpu.VMEM((8, 8, LANES), f32),
            pltpu.VMEM((8, 8, LANES), f32),
            pltpu.VMEM((4, 8, LANES), f32),
            pltpu.VMEM((4, 2 * PIXELS, LANES), bf16),
            pltpu.VMEM((2 * PIXELS, 512), bf16),
        ]
        + scatter_scratch(512)
        + scatter_scratch(9 * LANES)
        + scatter_scratch(512)
        + [pltpu.SemaphoreType.DMA((4,))] * 2
        + exchange_sems(8) * 3
        + exchange_sems(4) * 2
        + scatter_sems() * 3
        + [pltpu.SemaphoreType.DMA((4,))] * 2
        + [pltpu.SemaphoreType.DMA((4,))],
        compiler_params=kernel_params(5),
    )(*arrays)


class Reduce:
    def __init__(self, part, keep, far_buf, far_got, line_buf, line_got, sems):
        self.part, self.keep, self.far_buf, self.far_got = part, keep, far_buf, far_got
        self.line_buf, self.line_got = line_buf, line_got
        self.far_send, self.far_recv, self.line_send, self.line_recv = sems

    def block(self, step):
        place, lane, depth, side, _, _ = whereabouts()
        item, late = staggered(step)
        return ranked(depth, 3 - item % 4) * 2 + (side + 1 + late) % 2, item // 4

    def far_copy(self, micro, rank, place):
        return push(
            self.far_buf.at[micro, rank],
            self.far_got.at[micro, rank],
            self.far_send.at[micro, rank],
            self.far_recv.at[micro, rank],
            place,
            lax.axis_index("chan"),
        )

    def line_copy(self, micro, rank, slot, place):
        return push(
            self.line_buf.at[micro, rank],
            self.line_got.at[micro, slot],
            self.line_send.at[micro, rank],
            self.line_recv.at[micro, slot],
            place,
            lax.axis_index("chan"),
        )

    def line_value(self, micro, slot):
        self.line_copy(micro, 0, slot, lax.axis_index("batch")).wait_recv()
        return self.line_got[micro, slot].astype(jnp.float32)

    def step(self, step):
        place, lane, depth, side, _, _ = whereabouts()
        item, late = staggered(step)
        micro, rank = item // 4, 3 - item % 4
        owner = ranked(depth, rank)

        @pl.when(late == 0)
        def _():
            self.far_buf[micro, rank] = self.part[...].astype(jnp.bfloat16)
            self.far_copy(micro, rank, depth * 2 + 1 - side).start()

        @pl.when(late == 1)
        def _():
            self.far_copy(micro, rank, place).wait_recv()
            self.keep[micro] = self.part[...] + self.far_got[micro, rank].astype(jnp.float32)

            @pl.when((middle(depth) == 1) & (rank > 0))
            def _():
                self.keep[micro] = self.keep[micro] + self.line_value(micro, owner)

            @pl.when(rank > 0)
            def _():
                first = (rank % 2) * (1 - rank // 2) * (1 - middle(depth))
                slot = owner + first * (4 - owner)
                self.line_buf[micro, rank - 1] = self.keep[micro].astype(jnp.bfloat16)
                self.line_copy(
                    micro, rank - 1, slot, homeward(depth, rank) * 2 + side
                ).start()

    def close(self, micro):
        place, lane, depth, side, _, _ = whereabouts()
        self.keep[micro] = self.keep[micro] + self.line_value(micro, depth)

        @pl.when(middle(depth) == 1)
        def _():
            self.keep[micro] = self.keep[micro] + self.line_value(micro, 4)

        for rank in range(4):
            self.far_copy(micro, rank, place).wait_send()
        for rank in range(3):
            self.line_copy(micro, rank, 0, place).wait_send()


class Channels:
    def __init__(self, stage, got, stage_sem, got_sem, values, out_sem, in_sem):
        self.stage, self.got, self.stage_sem, self.got_sem = stage, got, stage_sem, got_sem
        self.values, self.out_sem, self.in_sem = values, out_sem, in_sem

    def piece(self, slot, target, block, lane):
        return push(
            self.stage.at[slot, block],
            self.got.at[lane, block],
            self.stage_sem.at[slot, block],
            self.got_sem.at[lane, block],
            lax.axis_index("batch"),
            target,
        )

    def send(self, part, block, micro):
        _, lane, _, _, upper, core = whereabouts()
        for half in range(2):
            piece = part[:, half * LANES : (half + 1) * LANES]
            target = half * 2 + micro

            @pl.when(target == lane)
            def _():
                self.got[lane, block] = piece

            @pl.when(target != lane)
            def _():
                self.stage[target, block] = piece
                self.piece(target, target, block, lane).start()

    def collect(self, micro, take):
        _, lane, _, _, _, core = whereabouts()

        @pl.when(core == micro)
        def _():
            def body(block, _):
                for step in range(1, 4):
                    other = (lane + step) % 4
                    self.piece(other, other, block, other).wait_recv()
                take(block)
                return 0

            lax.fori_loop(0, 8, body, 0)

    def value(self, block):
        result = self.got[0, block].astype(jnp.float32)
        for other in range(1, 4):
            result = result + self.got[other, block].astype(jnp.float32)
        return result

    def sent(self):
        _, lane, _, _, _, _ = whereabouts()

        def body(block, _):
            for step in range(1, 4):
                other = (lane + step) % 4
                self.piece(other, other, block, lane).wait_send()
            return 0

        lax.fori_loop(0, 8, body, 0)

    def chunk(self, path, half, micro, chunk, place_lane):
        here = self.values.at[half, micro, pl.ds(2 * chunk, 2)]
        return push(
            here,
            here,
            self.out_sem.at[path, chunk],
            self.in_sem.at[half, micro, chunk],
            lax.axis_index("batch"),
            place_lane,
        )

    def spread(self, chunk):
        _, lane, _, _, upper, core = whereabouts()
        self.chunk(0, upper, core, chunk, 2 - 2 * upper + core).start()
        self.chunk(1, upper, core, chunk, upper * 2 + 1 - core).start()

    def relay(self, micro):
        _, lane, _, _, upper, core = whereabouts()

        @pl.when(core == micro)
        def _():
            for chunk in range(4):
                copy = self.chunk(2, 1 - upper, core, chunk, upper * 2 + 1 - core)
                copy.wait_recv()
                copy.start()

    def finish(self, micro):
        _, lane, _, _, upper, core = whereabouts()

        @pl.when(core != micro)
        def _():
            for chunk in range(4):
                for half in range(2):
                    self.chunk(0, half, micro, chunk, lane).wait_recv()

    def close(self):
        _, lane, _, _, upper, core = whereabouts()
        for chunk in range(4):
            for path in range(3):
                self.chunk(path, upper, core, chunk, lane).wait_send()


def middle_kernel(
    count,
    block_ref,
    bias_ref,
    mine_ref,
    head_hbm,
    distil_hbm,
    mask_hbm,
    depth_hbm,
    segment_hbm,
    cot_hbm,
    depth_out,
    segment_out,
    distil_grad,
    gate_sums,
    head_sums,
    back_out,
    block_hbm,
    back_hbm,
    block_all,
    head_back,
    head_ref,
    distil_ref,
    mask_ref,
    depth_cot,
    segment_cot,
    cot_all,
    head_weight,
    mixed,
    mixed_back,
    turned,
    columns,
    acts,
    norm_ref,
    slope_ref,
    grads_all,
    own_stage,
    own_got,
    stage,
    got,
    part_ref,
    keep,
    far_buf,
    far_got,
    line_buf,
    line_got,
    stats,
    *sems,
):
    place, lane, depth, side, upper, core = whereabouts()
    half_width = LANES // 2
    source = place // 2 == lane
    low = lax.broadcasted_iota(jnp.int32, (PIXELS, LANES), 1) < half_width
    gather = Gather(block_all, *sems[0:3], 2)
    gather_back = Gather(grads_all, *sems[3:6], 2)
    reduce = Reduce(part_ref, keep, far_buf, far_got, line_buf, line_got, sems[6:10])
    ahead = Channels(stage, got, sems[10], sems[11], acts, sems[12], sems[13])
    behind = Channels(stage, got, sems[10], sems[11], head_back, sems[14], sems[15])
    own_sem, own_recv = sems[16:18]
    local = Local(
        (
            (head_hbm, head_ref),
            (mask_hbm, mask_ref),
            (distil_hbm, distil_ref),
            (depth_hbm, depth_cot),
            (segment_hbm, segment_cot),
            (cot_hbm, cot_all),
            (block_all, block_hbm),
            (head_back, back_hbm),
        ),
        sems[18],
    )
    local.start(0, 1, 2, 3, 4, 5)

    greet(batch_peers() + chan_peers())
    block_all[place] = block_ref[...]
    gather.start(0)
    clear_edges(turned)
    local.wait(0)
    for number in range(9):
        head_weight[number * 512 : (number + 1) * 512] = head_ref[number].T
    local.wait(1)

    def forward_step(step, _):
        block, micro = gather.next(step)
        fill_columns(block_all[block, micro], mask_ref[block, micro], turned, columns)
        part = jnp.dot(columns[0:PIXELS], head_weight[...], preferred_element_type=jnp.float32)
        ahead.send(part.astype(jnp.bfloat16), block, micro)

        @pl.when(step == 0)
        def _():
            local.wait(2)
            prepare_mixed()

        @pl.when(step == 1)
        def _():
            gather.start(1)

        @pl.when(step == 4)
        def _():
            for number in range(9):
                mixed_back[number * 512 : (number + 1) * 512] = mixed[
                    number * 256 : (number + 1) * 256
                ].T

        @pl.when(step == 10)
        def _():
            normalize(0)

        @pl.when(step == 14)
        def _():
            ahead.relay(0)

        return 0

    def prepare_mixed():
        width = half_width
        for number in range(9):
            for stream in range(2):
                for head in range(4):
                    index = head - SOURCE_START[stream]
                    rows = slice(number * 256 + head * width, number * 256 + (head + 1) * width)
                    left = slice(2 * stream * LANES, (2 * stream + 1) * LANES)
                    right = slice((2 * stream + 1) * LANES, (2 * stream + 2) * LANES)
                    nothing = jnp.zeros((width, LANES), jnp.bfloat16)
                    mixed[rows, left] = (
                        distil_ref[stream, number, 0] if head == OWN_HEAD[stream] else nothing
                    )
                    mixed[rows, right] = (
                        distil_ref[stream, number, 1 + index] if 0 <= index < 3 else nothing
                    )

    def normalize(micro):
        zero = jnp.zeros((1, LANES), jnp.float32)

        @pl.when(core == micro)
        def _():
            stats[0:2] = jnp.zeros((2, LANES), jnp.float32)

        def take(block):
            value = ahead.value(block)
            norm_ref[block] = value
            stats[0:1] += jnp.sum(value, axis=0, keepdims=True)
            stats[1:2] += jnp.sum(value * value, axis=0, keepdims=True)

        ahead.collect(micro, take)

        @pl.when(core == micro)
        def _():
            center = stats[0:1] / count
            inverse = lax.rsqrt(stats[1:2] / count - center * center + EPSILON)
            stats[2:3] = inverse

            def activate(chunk, _):
                for item in range(2):
                    block = 2 * chunk + item
                    normed = (norm_ref[block] - center) * inverse
                    norm_ref[block] = normed
                    out = normed * mine_ref[0:1] + mine_ref[1:2]
                    acts[upper, core, block] = (out * jax.nn.sigmoid(out)).astype(jnp.bfloat16)
                ahead.spread(chunk)
                return 0

            lax.fori_loop(0, 4, activate, 0)

    def own_copy(block, micro, slot, target):
        return push(
            own_stage.at[block, micro],
            own_got.at[slot, micro],
            own_sem.at[block, micro],
            own_recv.at[slot, micro],
            target,
            lane,
        )

    def send_own(micro):
        @pl.when(source)
        def _():
            own_got[place % 2, micro] = jnp.where(
                low, acts[0, micro, place], acts[1, micro, place]
            )

            def pack(step, _):
                block = (place + step) % 8
                own_stage[block, micro] = jnp.where(
                    low, acts[0, micro, block], acts[1, micro, block]
                )
                own_copy(block, micro, place % 2, block).start()
                return 0

            lax.fori_loop(1, 8, pack, 0)

    def act_value(block, micro):
        return jnp.concatenate([acts[half, micro, block] for half in range(2)], axis=1)

    def gate(micro):
        reduce.close(micro)
        for parity in range(2):
            @pl.when(2 * lane + parity != place)
            def _():
                own_copy(0, micro, parity, place).wait_recv()

        for stream, cot_ref in enumerate((depth_cot, segment_cot)):
            first = own_got[0, micro].astype(jnp.float32)
            second = own_got[1, micro].astype(jnp.float32)
            if stream == 0:
                second = pltpu.roll(second, half_width, 1)
            else:
                first = pltpu.roll(first, half_width, 1)
            own = jnp.where(low, first, second)
            column = 2 * stream * LANES
            gates = jax.nn.sigmoid(
                keep[micro, :, column : column + LANES] + bias_ref[stream : stream + 1]
            )
            message = keep[micro, :, column + LANES : column + 2 * LANES]
            cot = cot_ref[micro].astype(jnp.float32)
            out_ref = (depth_out, segment_out)[stream]
            out_ref[micro] = (own + gates * message).astype(jnp.bfloat16)
            gate_grad = (cot * message * gates * (1.0 - gates)).astype(jnp.bfloat16)
            bias_sum = jnp.sum(gate_grad.astype(jnp.float32), axis=0, keepdims=True)
            if micro == 0:
                gate_sums[stream : stream + 1] = bias_sum
            else:
                gate_sums[stream : stream + 1] += bias_sum
            grads_all[place, micro, :, column : column + LANES] = gate_grad
            grads_all[place, micro, :, column + LANES : column + 2 * LANES] = (cot * gates).astype(
                jnp.bfloat16
            )

    def distil_step(step, _):
        block, micro = reduce.block(step)
        fill_columns(act_value(block, micro), mask_ref[block, micro], turned, columns)
        part_ref[...] = jnp.dot(
            columns[0:PIXELS, 0 : 9 * 256], mixed[...], preferred_element_type=jnp.float32
        )
        reduce.step(step)

        @pl.when(step == 1)
        def _():
            normalize(1)

        @pl.when(step == 4)
        def _():
            ahead.relay(1)

        @pl.when(step == 6)
        def _():
            ahead.finish(1)
            ahead.sent()
            send_own(1)

        @pl.when(step == 11)
        def _():
            local.wait(3, 4)
            gate(0)
            gather_back.start(0)

        @pl.when(step == 15)
        def _():
            gate(1)
            gather_back.start(1)
            ahead.close()

        return 0

    distil_grad[...] = jnp.zeros_like(distil_grad)

    def back_step(step, _):
        block, micro = gather_back.next(step)
        fill_columns(
            grads_all[block, micro], mask_ref[block, micro], turned, columns, flip=True
        )
        part = jnp.dot(columns[0:PIXELS], mixed_back[...], preferred_element_type=jnp.float32)
        extra = cot_all[block, micro].astype(jnp.float32)
        part = jnp.concatenate(
            [
                part[:, :LANES] + jnp.where(low & source, extra, 0.0),
                part[:, LANES:] + jnp.where(low | ~source, 0.0, extra),
            ],
            axis=1,
        )
        behind.send(part.astype(jnp.bfloat16), block, micro)
        @pl.when(step == 10)
        def _():
            normalize_back(0)

        @pl.when(step == 14)
        def _():
            behind.relay(0)

        return 0

    def normalize_back(micro):
        @pl.when(core == micro)
        def _():
            stats[4:6] = jnp.zeros((2, LANES), jnp.float32)

        def take(block):
            normed = norm_ref[block]
            value = behind.value(block) * silu_slope(normed * mine_ref[0:1] + mine_ref[1:2])
            slope_ref[block] = value
            stats[4:5] += jnp.sum(value, axis=0, keepdims=True)
            stats[5:6] += jnp.sum(value * normed, axis=0, keepdims=True)

        behind.collect(micro, take)

        @pl.when(core == micro)
        def _():
            shift_sum, scale_sum = stats[4:5], stats[5:6]
            head_sums[0:1] = scale_sum
            head_sums[1:2] = shift_sum
            factor = mine_ref[0:1] * stats[2:3]

            def activate(chunk, _):
                for item in range(2):
                    block = 2 * chunk + item
                    value = slope_ref[block]
                    head_back[upper, core, block] = (
                        factor * (value - (shift_sum + norm_ref[block] * scale_sum) / count)
                    ).astype(jnp.bfloat16)
                behind.spread(chunk)
                return 0

            lax.fori_loop(0, 4, activate, 0)

    def head_value(block, micro):
        return jnp.concatenate([head_back[half, micro, block] for half in range(2)], axis=1)

    def weigh(block):
        for micro in range(2):
            fill_columns(
                grads_all[block, micro],
                mask_ref[block, micro],
                turned,
                columns,
                micro * PIXELS,
                True,
            )
        value = jnp.concatenate([act_value(block, micro) for micro in range(2)], axis=0).T
        width = half_width
        for number in range(9):
            product = jnp.dot(
                value,
                columns[:, number * 512 : (number + 1) * 512],
                preferred_element_type=jnp.float32,
            )
            for stream in range(2):
                for index in range(4):
                    head = OWN_HEAD[stream] if index == 0 else SOURCE_START[stream] + index - 1
                    column = (2 * stream + (index > 0)) * LANES
                    distil_grad[stream, number, index] += product[
                        head * width : (head + 1) * width, column : column + LANES
                    ]

    def block_step(step, _):
        block, micro = reduce.block(step)
        fill_columns(
            head_value(block, micro), mask_ref[block, micro], turned, columns, flip=True
        )
        part_ref[...] = jnp.dot(
            columns[0:PIXELS, 0 : 9 * 256],
            head_ref[...].reshape(9 * 256, 512),
            preferred_element_type=jnp.float32,
        )
        item, late = staggered(step)

        @pl.when(late == 1)
        def _():
            weigh(item)

        reduce.step(step)

        @pl.when(step == 1)
        def _():
            normalize_back(1)

        @pl.when(step == 4)
        def _():
            behind.relay(1)

        @pl.when(step == 6)
        def _():
            behind.finish(1)

        return 0

    def schedule(turn, _):
        phase = turn // 16
        place_in = turn % 16
        kind, step = phase, place_in
        late = (place_in + 1) // 16
        kind = phase + late
        step = place_in * (1 - late)
        back = (1 - (place_in + 15) // 16) * ((phase + 15) // 16)
        kind = kind - back
        step = step + 15 * back

        @pl.when(kind == 0)
        def _():
            forward_step(step, 0)

        @pl.when((kind == 1) & (step == 0))
        def _():
            ahead.finish(0)
            send_own(0)

        @pl.when(kind == 1)
        def _():
            distil_step(step, 0)

        @pl.when((kind == 2) & (step == 0))
        def _():
            local.wait(5)

        @pl.when(kind == 2)
        def _():
            back_step(step, 0)

        @pl.when((kind == 3) & (step == 0))
        def _():
            behind.finish(0)
            local.start(6)

        @pl.when(kind == 3)
        def _():
            block_step(step, 0)

        return 0

    lax.fori_loop(0, 65, schedule, 0)
    for micro in range(2):
        reduce.close(micro)
        back_out[micro_rows(micro)] = keep[micro]
    behind.sent()
    behind.close()
    gather.close()
    gather_back.close()
    local.start(7)

    @pl.when(source)
    def _():
        for micro in range(2):
            for step in range(1, 8):
                own_copy((place + step) % 8, micro, 0, place).wait_send()

    local.wait(6, 7)


def run_middle(count, *arrays):
    f32, bf16 = jnp.float32, jnp.bfloat16
    block = (PIXELS, 512)
    dma = pltpu.SemaphoreType.DMA
    return pl.pallas_call(
        functools.partial(middle_kernel, count),
        name="middle",
        out_shape=(
            jax.ShapeDtypeStruct((2, PIXELS, LANES), bf16),
            jax.ShapeDtypeStruct((2, PIXELS, LANES), bf16),
            jax.ShapeDtypeStruct((2, 9, 4, 64, LANES), f32),
            jax.ShapeDtypeStruct((2, LANES), f32),
            jax.ShapeDtypeStruct((2, LANES), f32),
            jax.ShapeDtypeStruct((2 * PIXELS, 512), f32),
            jax.ShapeDtypeStruct((8, 2) + block, bf16),
            jax.ShapeDtypeStruct((2, 2, 8, PIXELS, LANES), bf16),
        ),
        in_specs=vmem(3) + anywhere(6),
        out_specs=tuple(vmem(6) + anywhere(2)),
        scratch_shapes=[
            pltpu.VMEM((8, 2) + block, bf16),
            pltpu.VMEM((2, 2, 8, PIXELS, LANES), bf16),
            pltpu.VMEM((9, 256, 512), bf16),
            pltpu.VMEM((2, 9, 4, 64, LANES), bf16),
            pltpu.VMEM((8, 2, PIXELS, LANES), bf16),
            pltpu.VMEM((2, PIXELS, LANES), bf16),
            pltpu.VMEM((2, PIXELS, LANES), bf16),
            pltpu.VMEM((8, 2, PIXELS, LANES), bf16),
            pltpu.VMEM((9 * 512, 256), bf16),
            pltpu.VMEM((9 * 256, 512), bf16),
            pltpu.VMEM((9 * 512, 256), bf16),
            pltpu.VMEM((3, 2 * PAD + PIXELS, 512), bf16),
            pltpu.VMEM((2 * PIXELS, 9 * 512), bf16),
            pltpu.VMEM((2, 2, 8, PIXELS, LANES), bf16),
            pltpu.VMEM((8, PIXELS, LANES), f32),
            pltpu.VMEM((8, PIXELS, LANES), f32),
            pltpu.VMEM((8, 2) + block, bf16),
            pltpu.VMEM((8, 2, PIXELS, LANES), bf16),
            pltpu.VMEM((2, 2, PIXELS, LANES), bf16),
            pltpu.VMEM((4, 8, PIXELS, LANES), bf16),
            pltpu.VMEM((4, 8, PIXELS, LANES), bf16),
            pltpu.VMEM(block, f32),
            pltpu.VMEM((2,) + block, f32),
            pltpu.VMEM((2, 4) + block, bf16),
            pltpu.VMEM((2, 4) + block, bf16),
            pltpu.VMEM((2, 3) + block, bf16),
            pltpu.VMEM((2, 5) + block, bf16),
            pltpu.VMEM((8, LANES), f32),
        ]
        + gather_sems(2) * 2
        + [dma((2, 4)), dma((2, 4)), dma((2, 3)), dma((2, 5))]
        + [dma((4, 8)), dma((4, 8))]
        + [dma((3, 4)), dma((2, 2, 4))] * 2
        + [dma((8, 2)), dma((2, 2)), dma((8,))],
        compiler_params=kernel_params(2),
    )(*arrays)


def finish_kernel(count, *refs):
    sources, targets, held = refs[:count], refs[count : 2 * count], refs[2 * count : 3 * count]
    sem_in, sem_out = refs[3 * count :]

    def parts(ref):
        large = len(ref.shape) > 2
        return [ref.at[number] for number in range(ref.shape[0])] if large else [ref]

    number = 0
    loads, stores = [], []
    for source, target, hold in zip(sources, targets, held):
        for pieces in zip(parts(source), parts(hold), parts(target)):
            loads.append(pltpu.make_async_copy(pieces[0], pieces[1], sem_in.at[number]))
            stores.append(pltpu.make_async_copy(pieces[1], pieces[2], sem_out.at[number]))
            number += 1
    for load in loads:
        load.start()
    for load, store in zip(loads, stores):
        load.wait()
        store.start()
    for store in stores:
        store.wait()


def run_finish(*arrays):
    anywhere = [pl.BlockSpec(memory_space=pltpu.HBM)] * len(arrays)
    copies = sum(item.shape[0] if item.ndim > 2 else 1 for item in arrays)
    return pl.pallas_call(
        functools.partial(finish_kernel, len(arrays)),
        name="finish",
        out_shape=tuple(jax.ShapeDtypeStruct(item.shape, item.dtype) for item in arrays),
        in_specs=anywhere,
        out_specs=tuple(anywhere),
        scratch_shapes=[pltpu.VMEM(item.shape, item.dtype) for item in arrays]
        + [pltpu.SemaphoreType.DMA((copies,))] * 2,
        compiler_params=pltpu.CompilerParams(vmem_limit_bytes=60 * 2**20),
    )(*arrays)


def stationary_local(
    features,
    image_ids,
    reduce_weight,
    spatial_weight,
    expand_weight,
    head_weights,
    distil_weights,
    block_scale,
    block_shift,
    head_scale,
    head_shift,
    gate_bias,
    output_scale,
    output_shift,
    depth_cotangent,
    segment_cotangent,
):
    canvases, row_count, column_count = image_ids.shape
    pixels = row_count * column_count
    count = float(lax.axis_size("batch") * pixels)
    x = features.reshape(canvases, pixels, -1)
    cots = [item.reshape(canvases, pixels, LANES) for item in (depth_cotangent, segment_cotangent)]
    block_params = (block_scale, block_shift)
    output_params = (output_scale[None], output_shift[None])
    (
        block_out,
        norm3,
        inverse3,
        norm12,
        inverse12,
        mine,
        mask,
        act1,
        act2,
        reduce_all,
        spatial_all,
        expand_all,
        mask_all,
        cot_all,
    ) = run_front(
        count,
        x,
        image_ids.reshape(canvases, pixels),
        reduce_weight.T,
        spatial_weight,
        expand_weight,
        *block_params,
        *output_params,
        head_scale,
        head_shift,
        *cots,
    )
    depth_out, segment_out, distil_grad, gate_sums, head_sums, block_grad, block_all, back_all = run_middle(
        count,
        block_out,
        gate_bias,
        mine,
        head_weights.transpose(0, 2, 3, 1).reshape(9, -1, head_weights.shape[1]),
        distil_weights,
        mask_all,
        *cots,
        cot_all,
    )
    (
        features_grad,
        reduce_grad,
        spatial_grad,
        expand_grad,
        block_scale_grad,
        block_shift_grad,
        head_scale_grad,
        head_shift_grad,
        gate_grad,
        output_scale_grad,
        output_shift_grad,
        heads_grad,
    ) = run_rear(
        count,
        block_grad,
        x,
        norm3,
        inverse3,
        norm12,
        inverse12,
        act1,
        act2,
        reduce_all,
        spatial_all,
        expand_all,
        mask,
        *block_params,
        *output_params,
        head_sums,
        gate_sums,
        block_all,
        back_all,
        mask_all,
    )
    outs = run_finish(
        depth_out,
        segment_out,
        features_grad,
        reduce_grad,
        spatial_grad,
        expand_grad,
        heads_grad,
        distil_grad,
        block_scale_grad,
        block_shift_grad,
        head_scale_grad,
        head_shift_grad,
        gate_grad,
        output_scale_grad,
        output_shift_grad,
    )
    heads_grad = outs[6].reshape(9, 4, -1, head_weights.shape[1]).transpose(0, 3, 1, 2)
    return (
        outs[0].reshape(depth_cotangent.shape),
        outs[1].reshape(depth_cotangent.shape),
        outs[2].reshape(features.shape),
        outs[3].T,
        *outs[4:6],
        heads_grad,
        *outs[7:13],
        outs[13][0],
        outs[14][0],
    )


def solution(mesh):
    fits = dict(mesh.shape) == {"batch": 8, "chan": 4}
    local = stationary_local if fits else gathered_local
    placed = (
        P("batch", None, None, "chan"),
        P("batch", None, None),
        P("chan", "batch"),
        P(None, "batch", "chan"),
        P("batch", "chan"),
        P(None, "chan", None, "batch"),
        P(None, None, None, "batch", "chan"),
        P(None, "chan"),
        P(None, "chan"),
        P(None, "chan"),
        P(None, "chan"),
        P(None, "chan"),
        P("chan"),
        P("chan"),
        P("batch", None, None, "chan"),
        P("batch", None, None, "chan"),
    )
    return jax.shard_map(
        local,
        mesh=mesh,
        in_specs=placed,
        out_specs=(
            P("batch", None, None, "chan"),
            P("batch", None, None, "chan"),
            P("batch", None, None, "chan"),
            P("chan", "batch"),
            P(None, "batch", "chan"),
            P("batch", "chan"),
            P(None, "chan", None, "batch"),
            P(None, None, None, "batch", "chan"),
            P(None, "chan"),
            P(None, "chan"),
            P(None, "chan"),
            P(None, "chan"),
            P(None, "chan"),
            P("chan"),
            P("chan"),
        ),
        check_vma=False,
    )
```

```python
import functools

import jax
import jax.numpy as jnp
from jax import lax
from jax.experimental import pallas as pl
from jax.experimental.pallas import tpu as pltpu
from jax.sharding import PartitionSpec as P

EPSILON = 1e-05
OFFSETS = ((-1, -1), (-1, 0), (-1, 1), (0, -1), (0, 0), (0, 1), (1, -1), (1, 0), (1, 1))
OWN_HEAD = (0, 3)
SOURCE_START = (1, 0)


def silu_slope(values):
    sig = jax.nn.sigmoid(values)
    return sig * (1.0 + values * (1.0 - sig))


def shifted(values, vertical, lateral):
    row_count, column_count = (values.shape[1], values.shape[2])
    widths = [(0, 0)] * values.ndim
    widths[1] = (1, 1)
    widths[2] = (1, 1)
    padded = jnp.pad(values, widths)
    return padded[
        :, 1 + vertical : 1 + vertical + row_count, 1 + lateral : 1 + lateral + column_count
    ]


def tap_masks(image_ids):
    row_count, column_count = (image_ids.shape[1], image_ids.shape[2])
    padded = jnp.pad(image_ids, ((0, 0), (1, 1), (1, 1)), constant_values=-1)
    masks = []
    for vertical, lateral in OFFSETS:
        beside = padded[
            :, 1 + vertical : 1 + vertical + row_count, 1 + lateral : 1 + lateral + column_count
        ]
        masks.append((beside == image_ids).astype(jnp.float32))
    return jnp.stack(masks)


def conv_forward(inputs, weight, masks):
    total = 0.0
    for number, (vertical, lateral) in enumerate(OFFSETS):
        moved = shifted(inputs, vertical, lateral) * masks[number][..., None].astype(inputs.dtype)
        total = total + jnp.einsum(
            "nhwc,co->nhwo", moved, weight[number], preferred_element_type=jnp.float32
        )
    return total


def conv_input_grad(grads, weight, masks):
    total = 0.0
    for number, (vertical, lateral) in enumerate(OFFSETS):
        term = jnp.einsum(
            "nhwo,co->nhwc", grads, weight[number], preferred_element_type=jnp.float32
        )
        total = total + shifted(term * masks[number][..., None], -vertical, -lateral)
    return total


def conv_weight_grad(inputs, grads, masks):
    pieces = []
    for number, (vertical, lateral) in enumerate(OFFSETS):
        moved = shifted(inputs, vertical, lateral) * masks[number][..., None].astype(inputs.dtype)
        pieces.append(jnp.einsum("nhwc,nhwo->co", moved, grads, preferred_element_type=jnp.float32))
    return jnp.stack(pieces)


def pixel_sum(values):
    return jnp.sum(values, axis=(0, 1, 2))


def normalize(values, scale, shift, count):
    total, squares = lax.psum((pixel_sum(values), pixel_sum(values * values)), "batch")
    center = total / count
    inverse = lax.rsqrt(squares / count - center * center + EPSILON)
    normed = (values - center) * inverse
    return (normed, inverse, normed * scale + shift)


def grad_sums(first_sum, second_sum):
    return lax.psum((first_sum, second_sum), "batch")


def normalize_back(grads, normed, inverse, scale, shift_sum, scale_sum, count):
    return scale * inverse * (grads - (shift_sum + normed * scale_sum) / count)


def channel_gather(values):
    return lax.all_gather(values, "chan", axis=4, tiled=True)


def channel_sum(values):
    return lax.psum_scatter(
        values.astype(jnp.bfloat16), "chan", scatter_dimension=4, tiled=True
    ).astype(jnp.float32)


def fetch_weights(reduce_weight, spatial_weight, expand_weight, head_weights, distil_weights):
    return (
        lax.all_gather(reduce_weight, "batch", axis=1, tiled=True),
        lax.all_gather(spatial_weight, "batch", axis=1, tiled=True),
        lax.all_gather(expand_weight, "batch", axis=0, tiled=True),
        lax.all_gather(head_weights, "batch", axis=3, tiled=True),
        lax.all_gather(distil_weights, "batch", axis=3, tiled=True),
    )


def scatter_weights(grads):
    reduce_grad, spatial_grad, expand_grad, heads_grad, distil_grad = grads
    return (
        lax.psum_scatter(reduce_grad, "batch", scatter_dimension=1, tiled=True),
        lax.psum_scatter(spatial_grad, "batch", scatter_dimension=1, tiled=True),
        lax.psum_scatter(expand_grad, "batch", scatter_dimension=0, tiled=True),
        lax.psum_scatter(heads_grad, "batch", scatter_dimension=3, tiled=True),
        lax.psum_scatter(distil_grad, "batch", scatter_dimension=3, tiled=True),
    )


def micro_step(inputs, image_ids, depth_cot, segment_cot, gathered, small, batch_count):
    reduce_full, spatial_full, expand_full, heads_full, distil_full = gathered
    block_scale, block_shift, head_scale, head_shift, gate_bias, output_scale, output_shift = small
    masks = tap_masks(image_ids)
    canvases, row_count, column_count = image_ids.shape
    count = float(batch_count * canvases * row_count * column_count)
    first_partial = jnp.einsum(
        "nhwc,co->nhwo", inputs, reduce_full, preferred_element_type=jnp.float32
    )
    first = channel_sum(first_partial[:, :, :, None, :])
    first_norm, first_inv, first_out = normalize(first, block_scale[0:1], block_shift[0:1], count)
    first_act = jax.nn.silu(first_out).astype(jnp.bfloat16)
    first_full = channel_gather(first_act)[:, :, :, 0, :]
    second = conv_forward(first_full, spatial_full, masks)[:, :, :, None, :]
    second_norm, second_inv, second_out = normalize(
        second, block_scale[1:2], block_shift[1:2], count
    )
    second_act = jax.nn.silu(second_out).astype(jnp.bfloat16)
    second_full = channel_gather(second_act)[:, :, :, 0, :]
    third = jnp.einsum(
        "nhwc,co->nhwo", second_full, expand_full, preferred_element_type=jnp.float32
    )[:, :, :, None, :]
    third_norm, third_inv, third_out = normalize(
        third, output_scale[None], output_shift[None], count
    )
    summed = third_out[:, :, :, 0, :] + inputs.astype(jnp.float32)
    block_out = jax.nn.silu(summed).astype(jnp.bfloat16)
    heads_flat = heads_full.reshape(heads_full.shape[0], heads_full.shape[1], -1)
    head_partial = conv_forward(block_out, heads_flat, masks)
    head_pre = channel_sum(
        head_partial.reshape(head_partial.shape[:3] + (heads_full.shape[2], heads_full.shape[3]))
    )
    head_norm, head_inv, head_out = normalize(head_pre, head_scale, head_shift, count)
    head_act = jax.nn.silu(head_out).astype(jnp.bfloat16)
    head_full = channel_gather(head_act)
    head_width = head_full.shape[4]
    gate_pre = [0.0, 0.0]
    message = [0.0, 0.0]
    for number, (vertical, lateral) in enumerate(OFFSETS):
        moved = shifted(head_full, vertical, lateral) * masks[number][:, :, :, None, None].astype(
            jnp.bfloat16
        )
        for stream in range(2):
            weights_here = distil_full[stream, number]
            first_source = SOURCE_START[stream]
            sources = moved[:, :, :, first_source : first_source + 3].reshape(
                moved.shape[:3] + (3 * head_width,)
            )
            gate_pre[stream] = gate_pre[stream] + jnp.einsum(
                "nhwc,co->nhwo",
                moved[:, :, :, OWN_HEAD[stream]],
                weights_here[0],
                preferred_element_type=jnp.float32,
            )
            message[stream] = message[stream] + jnp.einsum(
                "nhwc,co->nhwo",
                sources,
                weights_here[1:].reshape(3 * head_width, -1),
                preferred_element_type=jnp.float32,
            )
    cotangents = (depth_cot.astype(jnp.float32), segment_cot.astype(jnp.float32))
    outputs, message_grads, gate_grads = ([], [], [])
    for stream in range(2):
        gate_value = jax.nn.sigmoid(gate_pre[stream] + gate_bias[stream])
        own_feature = head_act[:, :, :, OWN_HEAD[stream]].astype(jnp.float32)
        outputs.append((own_feature + gate_value * message[stream]).astype(jnp.bfloat16))
        message_grads.append((cotangents[stream] * gate_value).astype(jnp.bfloat16))
        gate_grads.append(
            (cotangents[stream] * message[stream] * gate_value * (1.0 - gate_value)).astype(
                jnp.bfloat16
            )
        )
    spread_grad = 0.0
    distil_parts = [[], []]
    for number, (vertical, lateral) in enumerate(OFFSETS):
        tap_mask = masks[number][:, :, :, None, None]
        moved = shifted(head_full, vertical, lateral) * tap_mask.astype(jnp.bfloat16)
        tap_grad = jnp.zeros(head_full.shape, jnp.float32)
        for stream in range(2):
            weights_here = distil_full[stream, number]
            first_source = SOURCE_START[stream]
            sources = moved[:, :, :, first_source : first_source + 3].reshape(
                moved.shape[:3] + (3 * head_width,)
            )
            own_grad = jnp.einsum(
                "nhwo,co->nhwc",
                gate_grads[stream],
                weights_here[0],
                preferred_element_type=jnp.float32,
            )
            source_grad = jnp.einsum(
                "nhwo,co->nhwc",
                message_grads[stream],
                weights_here[1:].reshape(3 * head_width, -1),
                preferred_element_type=jnp.float32,
            )
            tap_grad = tap_grad.at[:, :, :, OWN_HEAD[stream]].add(own_grad)
            tap_grad = tap_grad.at[:, :, :, first_source : first_source + 3].add(
                source_grad.reshape(source_grad.shape[:3] + (3, head_width))
            )
            gate_weight_grad = jnp.einsum(
                "nhwc,nhwo->co",
                moved[:, :, :, OWN_HEAD[stream]],
                gate_grads[stream],
                preferred_element_type=jnp.float32,
            )
            source_weight_grad = jnp.einsum(
                "nhwc,nhwo->co", sources, message_grads[stream], preferred_element_type=jnp.float32
            )
            distil_parts[stream].append(
                jnp.concatenate(
                    [gate_weight_grad[None], source_weight_grad.reshape(3, head_width, -1)], axis=0
                )
            )
        spread_grad = spread_grad + shifted(tap_grad * tap_mask, -vertical, -lateral)
    distil_grad = jnp.stack([jnp.stack(distil_parts[0]), jnp.stack(distil_parts[1])])
    head_grad = channel_sum(spread_grad)
    head_grad = (
        head_grad.at[:, :, :, OWN_HEAD[0]]
        .add(cotangents[0])
        .at[:, :, :, OWN_HEAD[1]]
        .add(cotangents[1])
    )
    head_grad = head_grad * silu_slope(head_out)
    gate_sums = jnp.stack(
        [pixel_sum(gate_grads[0].astype(jnp.float32)), pixel_sum(gate_grads[1].astype(jnp.float32))]
    )
    shift_sums, scale_sums = grad_sums(
        jnp.concatenate([pixel_sum(head_grad), gate_sums], axis=0), pixel_sum(head_grad * head_norm)
    )
    head_pre_grad = normalize_back(
        head_grad, head_norm, head_inv, head_scale, shift_sums[:4], scale_sums, count
    ).astype(jnp.bfloat16)
    head_pre_full = channel_gather(head_pre_grad)
    head_flat_grad = head_pre_full.reshape(head_pre_full.shape[:3] + (-1,))
    block_grad = conv_input_grad(head_flat_grad, heads_flat, masks)
    heads_grad = conv_weight_grad(block_out, head_flat_grad, masks).reshape(heads_full.shape)
    summed_grad = block_grad * silu_slope(summed)
    third_grad = summed_grad[:, :, :, None, :]
    third_shift, third_scale = grad_sums(pixel_sum(third_grad), pixel_sum(third_grad * third_norm))
    third_pre = normalize_back(
        third_grad, third_norm, third_inv, output_scale[None], third_shift, third_scale, count
    ).astype(jnp.bfloat16)[:, :, :, 0, :]
    expand_grad = jnp.einsum(
        "nhwc,nhwo->co", second_full, third_pre, preferred_element_type=jnp.float32
    )
    second_grad = channel_sum(
        jnp.einsum("nhwo,co->nhwc", third_pre, expand_full, preferred_element_type=jnp.float32)[
            :, :, :, None, :
        ]
    )
    second_grad = second_grad * silu_slope(second_out)
    second_shift, second_scale = grad_sums(
        pixel_sum(second_grad), pixel_sum(second_grad * second_norm)
    )
    second_pre = normalize_back(
        second_grad, second_norm, second_inv, block_scale[1:2], second_shift, second_scale, count
    ).astype(jnp.bfloat16)[:, :, :, 0, :]
    spatial_grad = conv_weight_grad(first_full, second_pre, masks)
    first_grad = channel_sum(conv_input_grad(second_pre, spatial_full, masks)[:, :, :, None, :])
    first_grad = first_grad * silu_slope(first_out)
    first_shift, first_scale = grad_sums(pixel_sum(first_grad), pixel_sum(first_grad * first_norm))
    first_pre = normalize_back(
        first_grad, first_norm, first_inv, block_scale[0:1], first_shift, first_scale, count
    ).astype(jnp.bfloat16)
    first_pre_full = channel_gather(first_pre)[:, :, :, 0, :]
    reduce_grad = jnp.einsum(
        "nhwc,nhwo->co", inputs, first_pre_full, preferred_element_type=jnp.float32
    )
    input_grad = summed_grad + jnp.einsum(
        "nhwo,co->nhwc", first_pre_full, reduce_full, preferred_element_type=jnp.float32
    )
    weight_grads = (reduce_grad, spatial_grad, expand_grad, heads_grad, distil_grad)
    small_grads = (
        jnp.concatenate([first_scale, second_scale], axis=0),
        jnp.concatenate([first_shift, second_shift], axis=0),
        scale_sums,
        shift_sums[:4],
        shift_sums[4:],
        third_scale[0],
        third_shift[0],
    )
    return (outputs[0], outputs[1], input_grad, weight_grads, small_grads)


def gathered_local(
    features,
    image_ids,
    reduce_weight,
    spatial_weight,
    expand_weight,
    head_weights,
    distil_weights,
    block_scale,
    block_shift,
    head_scale,
    head_shift,
    gate_bias,
    output_scale,
    output_shift,
    depth_cotangent,
    segment_cotangent,
):
    batch_count = lax.axis_size("batch")
    small = (
        block_scale,
        block_shift,
        head_scale,
        head_shift,
        gate_bias,
        output_scale,
        output_shift,
    )
    depth_list, segment_list, input_list = ([], [], [])
    weight_total = None
    small_total = None
    for micro_index in range(features.shape[0]):
        gathered = fetch_weights(
            reduce_weight, spatial_weight, expand_weight, head_weights, distil_weights
        )
        canvas_pick = slice(micro_index, micro_index + 1)
        depth_out, segment_out, input_grad, weight_grads, small_grads = micro_step(
            features[canvas_pick],
            image_ids[canvas_pick],
            depth_cotangent[canvas_pick],
            segment_cotangent[canvas_pick],
            gathered,
            small,
            batch_count,
        )
        weight_grads = scatter_weights(weight_grads)
        weight_total = (
            weight_grads
            if weight_total is None
            else jax.tree.map(jnp.add, weight_total, weight_grads)
        )
        small_total = (
            small_grads if small_total is None else jax.tree.map(jnp.add, small_total, small_grads)
        )
        depth_list.append(depth_out)
        segment_list.append(segment_out)
        input_list.append(input_grad)
    reduce_grad, spatial_grad, expand_grad, heads_grad, distil_grad = weight_total
    scale_mid, shift_mid, scale_heads, shift_heads, bias_gates, scale_out, shift_out = small_total
    return (
        jnp.concatenate(depth_list, axis=0),
        jnp.concatenate(segment_list, axis=0),
        jnp.concatenate(input_list, axis=0),
        reduce_grad,
        spatial_grad,
        expand_grad,
        heads_grad,
        distil_grad,
        scale_mid,
        shift_mid,
        scale_heads,
        shift_heads,
        bias_gates,
        scale_out,
        shift_out,
    )


MESH = pl.DeviceIdType.MESH
PIXELS = 256
PAD = 32
LANES = 128


def whereabouts():
    place, lane = lax.axis_index("batch"), lax.axis_index("chan")
    return place, lane, place // 2, place % 2, lane // 2, lane % 2


def ranked(depth, rank):
    high, low = depth // 2, depth % 2
    up, odd = rank // 2, rank % 2
    return (
        (1 - odd) * (1 - up) * depth
        + odd * (1 - up) * (1 + low)
        + (1 - odd) * up * (2 - 2 * low + high)
        + odd * up * (3 - 3 * high)
    )


def middle(depth):
    return (depth // 2 + depth % 2) % 2


def inner(depth):
    return 1 + depth % 2


def outer(depth):
    return 3 * (depth // 2)


def onward(depth, rank):
    second = (1 - rank % 2) * (rank // 2)
    return outer(depth) + second * (3 - depth - outer(depth))


def homeward(depth, rank):
    second = (1 - rank % 2) * (rank // 2) * middle(depth)
    return inner(depth) + second * (outer(depth) - inner(depth))


def staggered(step):
    late = ((step + 1) % 2) * ((step + 14) // 15) + step // 15
    return (1 - late) * ((step + 1) // 2) + late * (step // 2 - 1 + step // 15), late


def push(source, target, send_sem, recv_sem, place, lane):
    return pltpu.make_async_remote_copy(
        src_ref=source,
        dst_ref=target,
        send_sem=send_sem,
        recv_sem=recv_sem,
        device_id=(place, lane),
        device_id_type=MESH,
    )


def greet(peers):
    barrier = pltpu.get_barrier_semaphore()
    for place, lane in peers:
        pl.semaphore_signal(barrier, inc=1, device_id=(place, lane), device_id_type=MESH)
    pl.semaphore_wait(barrier, len(peers))


def batch_peers():
    place, lane, _, _, _, _ = whereabouts()
    return [((place + step) % 8, lane) for step in range(1, 8)]


def line_peers():
    place, lane, depth, side, _, _ = whereabouts()
    peers = [(ranked(depth, rank) * 2 + side, lane) for rank in range(1, 4)]
    return peers + [(depth * 2 + 1 - side, lane)]


def chan_peers():
    place, lane, _, _, _, _ = whereabouts()
    return [(place, (lane + step) % 4) for step in range(1, 4)]


class Gather:
    def __init__(self, values, recv, cross, line, parts, direct=False):
        self.values, self.recv, self.cross, self.line = values, recv, cross, line
        self.parts, self.direct = parts, direct

    def view(self, block, part):
        return self.values.at[block] if self.parts == 1 else self.values.at[block, part]

    def copy(self, block, part, sem, depth, side):
        lane = lax.axis_index("chan")
        here = self.view(block, part)
        return push(here, here, sem, self.recv.at[block, part], depth * 2 + side, lane)

    def start(self, part=0):
        place, lane, depth, side, _, _ = whereabouts()
        if self.direct:
            self.copy(place, part, self.cross.at[0, part], depth, 1 - side).start()
            for rank in range(1, 4):
                self.copy(
                    place, part, self.line.at[0, rank, part], ranked(depth, rank), side
                ).start()
            return
        self.copy(place, part, self.line.at[0, 0, part], inner(depth), side).start()

        @pl.when(middle(depth) == 1)
        def _():
            self.copy(place, part, self.line.at[1, 0, part], outer(depth), side).start()

        self.copy(place, part, self.cross.at[0, part], depth, 1 - side).start()

    def near(self, rank, part=0):
        place, lane, depth, side, _, _ = whereabouts()
        block = ranked(depth, rank) * 2 + side
        self.copy(block, part, self.cross.at[rank, part], depth, side).wait_recv()

        if not self.direct:

            @pl.when(middle(depth) == 1)
            def _():
                self.copy(
                    block, part, self.line.at[0, rank, part], onward(depth, rank), side
                ).start()

        self.copy(block, part, self.cross.at[rank, part], depth, 1 - side).start()

    def far(self, rank, part=0):
        place, lane, depth, side, _, _ = whereabouts()
        block = ranked(depth, rank) * 2 + 1 - side
        self.copy(block, part, self.cross.at[rank, part], depth, side).wait_recv()

    def next(self, step):
        place, lane, depth, side, _, _ = whereabouts()
        item, late = staggered(step)
        part, rank = item // 4, item % 4

        @pl.when((late == 0) & (rank > 0))
        def _():
            self.near(rank, part)

        @pl.when(late == 1)
        def _():
            self.far(rank, part)

        return ranked(depth, rank) * 2 + (side + late) % 2, part

    def close(self):
        place, lane, depth, side, _, _ = whereabouts()
        for part in range(self.parts):
            for rank in range(4):
                self.copy(place, part, self.cross.at[rank, part], depth, side).wait_send()
            if self.direct:
                for rank in range(1, 4):
                    self.copy(place, part, self.line.at[0, rank, part], depth, side).wait_send()
                continue
            self.copy(place, part, self.line.at[0, 0, part], depth, side).wait_send()

            @pl.when(middle(depth) == 1)
            def _():
                self.copy(place, part, self.line.at[1, 0, part], depth, side).wait_send()
                for rank in range(1, 4):
                    self.copy(place, part, self.line.at[0, rank, part], depth, side).wait_send()


def gather_sems(parts):
    return [
        pltpu.SemaphoreType.DMA((8, parts)),
        pltpu.SemaphoreType.DMA((4, parts)),
        pltpu.SemaphoreType.DMA((2, 4, parts)),
    ]


def clear_edges(turned):
    edge = jnp.zeros((3, PAD, turned.shape[2]), turned.dtype)
    turned[:, 0:PAD] = edge
    turned[:, PAD + PIXELS :] = edge


def fill_columns(value, mask, turned, columns, row=0, flip=False):
    width = value.shape[1]
    lanes = slice(0, width)
    wide = value.astype(jnp.float32)
    inside = slice(PAD, PAD + PIXELS)
    turned[0, inside, lanes] = pltpu.roll(wide, 1, 0).astype(jnp.bfloat16)
    turned[1, inside, lanes] = value
    turned[2, inside, lanes] = pltpu.roll(wide, PIXELS - 1, 0).astype(jnp.bfloat16)
    for number, (vertical, lateral) in enumerate(OFFSETS):
        start = PAD + 32 * vertical
        slot = 8 - number if flip else number
        columns[row : row + PIXELS, slot * width : (slot + 1) * width] = (
            turned[lateral + 1, start : start + PIXELS, lanes] * mask[:, number : number + 1]
        )


def vmem(count):
    return [pl.BlockSpec(memory_space=pltpu.VMEM)] * count


def kernel_params(number):
    return pltpu.CompilerParams(
        collective_id=number, has_side_effects=True, vmem_limit_bytes=60 * 2**20
    )


class Exchange:
    def __init__(self, values, send, recv, axis):
        self.values, self.send, self.recv, self.axis = values, send, recv, axis

    def steps(self):
        place, lane, _, _, _, _ = whereabouts()
        if self.axis == "batch":
            return [(step - 1, (place + step) % 8, lane, (place + step) % 8) for step in range(1, 8)]
        return [(step - 1, place, (lane + step) % 4, (lane + step) % 4) for step in range(1, 4)]

    def mine(self):
        place, lane, _, _, _, _ = whereabouts()
        return place if self.axis == "batch" else lane

    def start(self):
        here = self.values.at[self.mine()]
        for number, place, lane, _ in self.steps():
            push(here, here, self.send.at[number], self.recv.at[self.mine()], place, lane).start()

    def wait(self):
        for number, place, lane, slot in self.steps():
            there = self.values.at[slot]
            push(there, there, self.send.at[number], self.recv.at[slot], place, lane).wait_recv()

    def close(self):
        here = self.values.at[self.mine()]
        for number, place, lane, _ in self.steps():
            push(here, here, self.send.at[number], self.recv.at[self.mine()], place, lane).wait_send()

    def total(self):
        result = self.values[0]
        for slot in range(1, self.values.shape[0]):
            result = result + self.values[slot]
        return result


class Pieces:
    def __init__(self, stage, got, send, recv):
        self.stage, self.got, self.send, self.recv = stage, got, send, recv

    def start(self, part):
        place, lane, _, _, _, _ = whereabouts()
        for slot in range(4):
            self.stage[slot] = part[:, slot * LANES : (slot + 1) * LANES].astype(jnp.bfloat16)
        for step in (2, 1, 3):
            slot = (lane + step) % 4
            push(
                self.stage.at[slot],
                self.got.at[lane],
                self.send.at[slot],
                self.recv.at[lane],
                place,
                slot,
            ).start()

    def finish(self):
        place, lane, _, _, _, _ = whereabouts()
        self.got[lane] = self.stage[lane]
        for step in range(1, 4):
            slot = (lane + step) % 4
            push(
                self.stage.at[slot],
                self.got.at[slot],
                self.send.at[slot],
                self.recv.at[slot],
                place,
                lane,
            ).wait()
        result = self.got[0].astype(jnp.float32)
        for slot in range(1, 4):
            result = result + self.got[slot].astype(jnp.float32)
        return result


class Local:
    def __init__(self, pairs, sems):
        self.copies = [
            pltpu.make_async_copy(source, target, sems.at[number])
            for number, (source, target) in enumerate(pairs)
        ]

    def start(self, *numbers):
        for number in numbers:
            self.copies[number].start()

    def wait(self, *numbers):
        for number in numbers:
            self.copies[number].wait()


def anywhere(count):
    return [pl.BlockSpec(memory_space=pl.ANY)] * count


def micro_rows(micro):
    return slice(micro * PIXELS, (micro + 1) * PIXELS)


def moments(value, other):
    rows = []
    for micro in range(2):
        part = value[micro_rows(micro)]
        rows.append(jnp.sum(part, axis=0, keepdims=True))
        rows.append(jnp.sum(part * other[micro_rows(micro)], axis=0, keepdims=True))
    return rows


def tile_rows(rows, height):
    width = rows[0].shape[1]
    return jnp.concatenate(rows + [jnp.zeros((height - len(rows), width), jnp.float32)], axis=0)


def normed_part(value, totals, micro, count):
    center = totals[2 * micro : 2 * micro + 1] / count
    inverse = lax.rsqrt(totals[2 * micro + 1 : 2 * micro + 2] / count - center * center + EPSILON)
    return (value[micro_rows(micro)] - center) * inverse, inverse


def dot_last(first, second):
    return lax.dot_general(
        first, second, (((1,), (1,)), ((), ())), preferred_element_type=jnp.float32
    )


def make_masks(ids_ref, mask_all):
    rows = 8 * ids_ref.shape[0]
    ids = ids_ref[...].reshape(rows, PIXELS).T
    pixel = lax.broadcasted_iota(jnp.int32, (PIXELS, rows), 0)
    taps = []
    for vertical, lateral in OFFSETS:
        offset = 32 * vertical + lateral
        beside = ids if offset == 0 else pltpu.roll(ids, (-offset) % PIXELS, 0)
        row, col = (pixel >> 5) + vertical, (pixel & 31) + lateral
        inside = (row >= 0) & (row < 8) & (col >= 0) & (col < 32)
        taps.append(jnp.where(inside & (beside == ids), 1.0, 0.0).astype(jnp.bfloat16))
    taps = jnp.concatenate(taps + [jnp.zeros_like(taps[0])], axis=1)
    item = lax.broadcasted_iota(jnp.int32, (10 * rows, LANES), 0)
    lane = lax.broadcasted_iota(jnp.int32, (10 * rows, LANES), 1)
    for block in range(8):
        for micro in range(2):
            chosen = jnp.where(item == lane * rows + (8 * block + micro), 1.0, 0.0)
            mask_all[block, micro] = jnp.dot(
                taps, chosen.astype(jnp.bfloat16), preferred_element_type=jnp.float32
            ).astype(jnp.bfloat16)


def front_kernel(
    count,
    x_ref,
    ids_ref,
    reduce_ref,
    spatial_ref,
    expand_ref,
    block_scale,
    block_shift,
    output_scale,
    output_shift,
    head_scale,
    head_shift,
    depth_cot,
    segment_cot,
    y_ref,
    norm3_ref,
    inverse3_ref,
    norm12_ref,
    inverse12_ref,
    mine_ref,
    mask_ref,
    act1_out,
    act2_out,
    reduce_out,
    spatial_out,
    expand_out,
    mask_out,
    cot_out,
    act1_ref,
    act2_ref,
    reduce_all,
    spatial_all,
    expand_all,
    mask_all,
    cot_all,
    packed,
    turned,
    columns,
    stage,
    got,
    sums1,
    sums2,
    sums3,
    head_all,
    ids_all,
    raw1,
    raw2,
    fits1,
    fits2,
    *sems,
):
    place, lane, depth, side, upper, core = whereabouts()
    reduces = Gather(reduce_all, *sems[0:3], 1, True)
    spatials = Gather(spatial_all, *sems[3:6], 1)
    expands = Gather(expand_all, *sems[6:9], 1)
    ids = Exchange(ids_all, sems[9], sems[10], "batch")
    pieces = Pieces(stage, got, sems[11], sems[12])
    first_sums = Exchange(sums1, sems[13], sems[14], "batch")
    second_sums = Exchange(sums2, sems[15], sems[16], "batch")
    third_sums = Exchange(sums3, sems[17], sems[18], "batch")
    heads = Exchange(head_all, sems[19], sems[20], "chan")
    first_raw = Exchange(raw1, sems[21], sems[22], "chan")
    second_raw = Exchange(raw2, sems[23], sems[24], "chan")
    first_fits = Exchange(fits1, sems[28], sems[29], "chan")
    second_fits = Exchange(fits2, sems[30], sems[31], "chan")

    def centered(value, raw):
        rows = moments(value, value)
        for micro in range(2):
            raw[lane, micro_rows(micro)] = (
                value[micro_rows(micro)] - rows[2 * micro] / PIXELS
            ).astype(jnp.bfloat16)
        return rows

    def fit(value, rows, totals, layer, fits):
        inverses, lines = [], []
        for micro in range(2):
            normed, inverse = normed_part(value, totals, micro, count)
            norm12_ref[layer, micro_rows(micro)] = normed
            inverses.append(inverse)
            slope = inverse * block_scale[layer : layer + 1]
            center = totals[2 * micro : 2 * micro + 1] / count
            lines.append(slope)
            lines.append(
                (rows[2 * micro] / PIXELS - center) * slope + block_shift[layer : layer + 1]
            )
        fits[lane] = tile_rows(lines, 8)
        return inverses

    def activate(raw, fits, act):
        for slot in range(4):
            for micro in range(2):
                out = (
                    raw[slot, micro_rows(micro)].astype(jnp.float32)
                    * fits[slot, 2 * micro : 2 * micro + 1]
                    + fits[slot, 2 * micro + 1 : 2 * micro + 2]
                )
                act[slot, micro_rows(micro)] = (out * jax.nn.sigmoid(out)).astype(jnp.bfloat16)


    local = Local(
        (
            (act1_ref, act1_out),
            (act2_ref, act2_out),
            (reduce_all, reduce_out),
            (spatial_all, spatial_out),
            (expand_all, expand_out),
            (mask_all, mask_out),
            (cot_all, cot_out),
        ),
        sems[27],
    )
    cot_sem, cot_recv = sems[25:27]

    def cot_copy(parity, slot, target):
        return push(
            packed.at[parity], cot_all.at[slot], cot_sem.at[parity], cot_recv.at[slot], target, lane
        )

    greet(batch_peers() + chan_peers())
    reduce_all[place] = reduce_ref[...]
    reduces.start()
    ids_all[place] = jnp.zeros((8, PIXELS), jnp.float32)
    for micro in range(2):
        for row in range(8):
            ids_all[place, micro : micro + 1, row * 32 : (row + 1) * 32] = ids_ref[
                micro, row : row + 1
            ].astype(jnp.float32)
    ids.start()
    spatial_all[place] = spatial_ref[...]
    expand_all[place] = expand_ref[...]
    head_all[lane, 0:4] = head_scale[...]
    head_all[lane, 4:8] = head_shift[...]
    heads.start()
    clear_edges(turned)
    for rank in range(1, 4):
        reduces.near(rank)
    spatials.start()
    for rank in range(4):
        reduces.far(rank)
    x = x_ref[...].reshape(2 * PIXELS, x_ref.shape[2])
    pieces.start(dot_last(x, reduce_all[...].reshape(512, 512)))
    ids.wait()
    make_masks(ids_all, mask_all)
    mask_ref[...] = mask_all[place]
    local.start(2, 5)
    spatials.near(1)
    first = pieces.finish()
    first_rows = centered(first, raw1)
    sums1[place] = tile_rows(first_rows, 8)
    first_sums.start()
    first_raw.start()
    spatials.near(2)
    expands.start()
    spatials.near(3)
    half_width = LANES // 2
    left = lax.broadcasted_iota(jnp.int32, (PIXELS, LANES), 1) < half_width
    for micro in range(2):
        upper_cot, lower_cot = (ref[micro].astype(jnp.float32) for ref in (depth_cot, segment_cot))
        packed[0, micro] = jnp.where(left, upper_cot, pltpu.roll(lower_cot, half_width, 1)).astype(
            jnp.bfloat16
        )
        packed[1, micro] = jnp.where(left, pltpu.roll(upper_cot, half_width, 1), lower_cot).astype(
            jnp.bfloat16
        )
    first_sums.wait()
    rows = fit(first, first_rows, first_sums.total(), 0, fits1)
    first_fits.start()
    expands.near(1)
    for rank in range(4):
        spatials.far(rank)
    expands.near(2)
    first_raw.wait()
    first_fits.wait()
    activate(raw1, fits1, act1_ref)
    local.start(0, 3)
    for micro in range(2):
        value = jnp.concatenate([act1_ref[slot, micro_rows(micro)] for slot in range(4)], axis=1)
        fill_columns(value, mask_all[place, micro], turned, columns, micro * PIXELS)
    second = jnp.zeros((2 * PIXELS, LANES), jnp.float32)
    for number in range(9):
        second = second + jnp.dot(
            columns[:, number * 512 : (number + 1) * 512],
            spatial_all[:, number].reshape(512, LANES),
            preferred_element_type=jnp.float32,
        )
    second_rows = centered(second, raw2)
    sums2[place] = tile_rows(second_rows, 8)
    second_sums.start()
    second_raw.start()
    expands.near(3)
    for parity in range(2):
        target = 2 * lane + parity

        @pl.when(target == place)
        def _():
            cot_all[place] = packed[parity]

        @pl.when(target != place)
        def _():
            cot_copy(parity, place, target).start()

    second_sums.wait()
    rows = rows + fit(second, second_rows, second_sums.total(), 1, fits2)
    second_fits.start()
    inverse12_ref[...] = tile_rows(rows, 8)
    heads.wait()
    low = lax.broadcasted_iota(jnp.int32, (1, LANES), 1) < half_width
    source = place // 2
    even = place % 2 == 0
    for kind in range(2):
        upper_row = head_all[source, pl.ds(4 * kind + 2 * upper, 1)]
        lower_row = head_all[source, pl.ds(4 * kind + 2 * upper + 1, 1)]
        mine_ref[kind : kind + 1] = jnp.where(
            even,
            jnp.where(low, upper_row, pltpu.roll(lower_row, half_width, 1)),
            jnp.where(low, pltpu.roll(upper_row, half_width, 1), lower_row),
        )
    for rank in range(4):
        expands.far(rank)
    second_raw.wait()
    second_fits.wait()
    activate(raw2, fits2, act2_ref)
    local.start(1, 4)
    value = jnp.concatenate([act2_ref[slot] for slot in range(4)], axis=1)
    third = jnp.dot(
        value, expand_all[...].reshape(512, 512), preferred_element_type=jnp.float32
    )
    sums3[place] = tile_rows(moments(third, third), 8)
    third_sums.start()
    third_sums.wait()
    totals = third_sums.total()
    rows = []
    for micro in range(2):
        normed, inverse = normed_part(third, totals, micro, count)
        norm3_ref[micro_rows(micro)] = normed
        rows.append(inverse)
        out = normed * output_scale[...] + output_shift[...] + x_ref[micro].astype(jnp.float32)
        y_ref[micro] = (out * jax.nn.sigmoid(out)).astype(jnp.bfloat16)
    inverse3_ref[...] = tile_rows(rows, 8)
    @pl.when(place // 2 == lane)
    def _():
        for step in range(1, 8):
            cot_copy(0, (place + step) % 8, place).wait_recv()

    local.start(6)
    for parity in range(2):
        @pl.when(2 * lane + parity != place)
        def _():
            cot_copy(parity, place, place).wait_send()

    local.wait(0, 1, 2, 3, 4, 5, 6)
    for item in (reduces, spatials, expands, ids, heads, first_raw, second_raw):
        item.close()
    for item in (first_sums, second_sums, third_sums, first_fits, second_fits):
        item.close()


def exchange_sems(size):
    return [pltpu.SemaphoreType.DMA((size - 1,)), pltpu.SemaphoreType.DMA((size,))]


def run_front(count, *arrays):
    f32, bf16 = jnp.float32, jnp.bfloat16
    kept = (
        (4, 2 * PIXELS, LANES),
        (4, 2 * PIXELS, LANES),
        (8, 64, 512),
        (8, 9, 64, LANES),
        (8, 64, 512),
        (8, 2, PIXELS, LANES),
        (8, 2, PIXELS, LANES),
    )
    return pl.pallas_call(
        functools.partial(front_kernel, count),
        name="front",
        out_shape=(
            jax.ShapeDtypeStruct((2, PIXELS, 512), bf16),
            jax.ShapeDtypeStruct((2 * PIXELS, 512), f32),
            jax.ShapeDtypeStruct((8, 512), f32),
            jax.ShapeDtypeStruct((2, 2 * PIXELS, LANES), f32),
            jax.ShapeDtypeStruct((8, LANES), f32),
            jax.ShapeDtypeStruct((2, LANES), f32),
            jax.ShapeDtypeStruct((2, PIXELS, LANES), bf16),
        )
        + tuple(jax.ShapeDtypeStruct(shape, bf16) for shape in kept),
        in_specs=vmem(13),
        out_specs=tuple(vmem(7) + anywhere(7)),
        scratch_shapes=[pltpu.VMEM(shape, bf16) for shape in kept]
        + [
            pltpu.VMEM((2, 2, PIXELS, LANES), bf16),
            pltpu.VMEM((3, 2 * PAD + PIXELS, 512), bf16),
            pltpu.VMEM((2 * PIXELS, 9 * 512), bf16),
            pltpu.VMEM((4, 2 * PIXELS, LANES), bf16),
            pltpu.VMEM((4, 2 * PIXELS, LANES), bf16),
            pltpu.VMEM((8, 8, LANES), f32),
            pltpu.VMEM((8, 8, LANES), f32),
            pltpu.VMEM((8, 8, 512), f32),
            pltpu.VMEM((4, 8, LANES), f32),
            pltpu.VMEM((8, 8, PIXELS), f32),
            pltpu.VMEM((4, 2 * PIXELS, LANES), bf16),
            pltpu.VMEM((4, 2 * PIXELS, LANES), bf16),
            pltpu.VMEM((4, 8, LANES), f32),
            pltpu.VMEM((4, 8, LANES), f32),
        ]
        + gather_sems(1) * 3
        + exchange_sems(8)
        + [pltpu.SemaphoreType.DMA((4,))] * 2
        + exchange_sems(8) * 3
        + exchange_sems(4) * 3
        + [
            pltpu.SemaphoreType.DMA((2,)),
            pltpu.SemaphoreType.DMA((8,)),
            pltpu.SemaphoreType.DMA((7,)),
        ]
        + exchange_sems(4) * 2,
        compiler_params=kernel_params(1),
    )(*arrays)


class Scatter:
    def __init__(self, part, far_buf, far_got, near_buf, near_got, sems):
        self.part, self.far_buf, self.far_got = part, far_buf, far_got
        self.near_buf, self.near_got = near_buf, near_got
        self.far_send, self.far_recv, self.near_send, self.near_recv = sems

    def far_copy(self, level, place):
        return push(
            self.far_buf.at[level],
            self.far_got.at[level],
            self.far_send.at[level],
            self.far_recv.at[level],
            place,
            lax.axis_index("chan"),
        )

    def near_copy(self, rank, level, place):
        return push(
            self.near_buf.at[rank - 1],
            self.near_got.at[level],
            self.near_send.at[rank - 1],
            self.near_recv.at[level],
            place,
            lax.axis_index("chan"),
        )

    def start(self):
        place, lane, depth, side, _, _ = whereabouts()
        for rank in (3, 2, 1, 0):
            level = ranked(depth, rank)
            self.far_buf[level] = self.part[level * 2 + 1 - side].astype(jnp.bfloat16)
            self.far_copy(level, depth * 2 + 1 - side).start()

    def middle(self):
        place, lane, depth, side, _, _ = whereabouts()
        for rank in (3, 2, 1):
            level = ranked(depth, rank)
            self.far_copy(level, place).wait_recv()
            self.near_buf[rank - 1] = (
                self.part[level * 2 + side] + self.far_got[level].astype(jnp.float32)
            ).astype(jnp.bfloat16)
            self.near_copy(rank, depth, level * 2 + side).start()

    def finish(self):
        place, lane, depth, side, _, _ = whereabouts()
        self.far_copy(depth, place).wait_recv()
        result = self.part[place] + self.far_got[depth].astype(jnp.float32)
        for level in range(4):
            self.far_copy(level, place).wait_send()
        for rank in (3, 2, 1):
            level = ranked(depth, rank)
            self.near_copy(rank, level, place).wait()
            result = result + self.near_got[level].astype(jnp.float32)
        return result


def scatter_scratch(width):
    return [
        pltpu.VMEM((8, 64, width), jnp.float32),
        pltpu.VMEM((4, 64, width), jnp.bfloat16),
        pltpu.VMEM((4, 64, width), jnp.bfloat16),
        pltpu.VMEM((3, 64, width), jnp.bfloat16),
        pltpu.VMEM((4, 64, width), jnp.bfloat16),
    ]


def scatter_sems():
    return [
        pltpu.SemaphoreType.DMA((4,)),
        pltpu.SemaphoreType.DMA((4,)),
        pltpu.SemaphoreType.DMA((3,)),
        pltpu.SemaphoreType.DMA((4,)),
    ]


def back_part(value, normed, inverse, scale, shift_sum, scale_sum, count):
    return (scale * inverse * (value - (shift_sum + normed * scale_sum) / count)).astype(
        jnp.bfloat16
    )


def rear_kernel(
    count,
    grad_ref,
    x_ref,
    norm3_ref,
    inverse3_ref,
    norm12_ref,
    inverse12_ref,
    mask_ref,
    block_scale,
    block_shift,
    output_scale,
    output_shift,
    head_ref,
    gate_ref,
    block_hbm,
    back_hbm,
    masks_hbm,
    act1_hbm,
    act2_hbm,
    reduce_hbm,
    spatial_hbm,
    expand_hbm,
    features_ref,
    reduce_out,
    spatial_out,
    expand_out,
    block_scale_out,
    block_shift_out,
    head_scale_out,
    head_shift_out,
    gate_out,
    output_scale_out,
    output_shift_out,
    head_out,
    head_grad,
    block_all,
    head_back,
    mask_all,
    act1_ref,
    act2_ref,
    reduce_all,
    spatial_all,
    expand_all,
    turned_wide,
    columns_wide,
    turned,
    columns,
    stage,
    got,
    stage_next,
    got_next,
    sums_a,
    sums_b,
    sums_c,
    head_all,
    act_all,
    back3,
    *rest,
):
    expand_bufs, spatial_bufs, reduce_bufs, sems = rest[0:5], rest[5:10], rest[10:15], rest[15:]
    place, lane, depth, side, upper, core = whereabouts()
    pieces = Pieces(stage, got, sems[0], sems[1])
    first = Exchange(sums_a, sems[2], sems[3], "batch")
    second = Exchange(sums_b, sems[4], sems[5], "batch")
    third = Exchange(sums_c, sems[6], sems[7], "batch")
    heads = Exchange(head_all, sems[8], sems[9], "chan")
    acts = Exchange(act_all, sems[10], sems[11], "chan")
    expands = Scatter(*expand_bufs, sems[12:16])
    spatials = Scatter(*spatial_bufs, sems[16:20])
    reduces = Scatter(*reduce_bufs, sems[20:24])
    pieces_next = Pieces(stage_next, got_next, sems[24], sems[25])

    local = Local(
        (
            (expand_hbm, expand_all),
            (act2_hbm, act2_ref),
            (block_hbm, block_all),
            (back_hbm, head_back),
            (masks_hbm, mask_all),
            (spatial_hbm, spatial_all),
            (act1_hbm, act1_ref),
            (reduce_hbm, reduce_all),
            (head_grad, head_out),
        ),
        sems[26],
    )
    local.start(0, 1, 2, 3, 4, 5, 6, 7)

    def weigh(block):
        for micro in range(2):
            fill_columns(
                block_all[block, micro],
                mask_all[block, micro],
                turned_wide,
                columns_wide,
                micro * PIXELS,
            )
        value = jnp.concatenate(
            [
                jnp.concatenate([head_back[half, micro, block] for half in range(2)], axis=1)
                for micro in range(2)
            ],
            axis=0,
        ).T

        def tap(number, _):
            product = jnp.dot(
                value,
                columns_wide[:, pl.ds(pl.multiple_of(number * 512, 512), 512)],
                preferred_element_type=jnp.float32,
            )
            if block == 0:
                head_grad[number] = product
            else:
                head_grad[number] += product
            return 0

        lax.fori_loop(0, 9, tap, 0)

    greet(batch_peers() + chan_peers())
    clear_edges(turned_wide)
    half_width = LANES // 2
    even = place % 2 == 0
    mine = lax.broadcasted_iota(jnp.int32, (1, LANES), 1) >> 6 == place % 2
    rows = []
    for kind in range(2):
        own = head_ref[kind : kind + 1]
        turned_own = pltpu.roll(own, half_width, 1)
        first_row = jnp.where(mine, jnp.where(even, own, turned_own), 0.0)
        second_row = jnp.where(mine, jnp.where(even, turned_own, own), 0.0)
        for half in range(2):
            for row in (first_row, second_row):
                rows.append(jnp.where(upper == half, row, 0.0))
    head_all[lane] = jnp.concatenate(rows, axis=0)
    heads.start()
    clear_edges(turned)
    rows = []
    for micro in range(2):
        normed = norm3_ref[micro_rows(micro)]
        out = normed * output_scale[...] + output_shift[...] + x_ref[micro].astype(jnp.float32)
        value = grad_ref[micro_rows(micro)] * silu_slope(out)
        features_ref[micro] = value
        rows.append(jnp.sum(value, axis=0, keepdims=True))
        rows.append(jnp.sum(value * normed, axis=0, keepdims=True))
    heads.wait()
    sums_a[place, 0:8] = tile_rows(rows, 8)
    sums_a[place, 8:16] = jnp.zeros((8, 512), jnp.float32)
    sums_a[place, 4:6, 0:LANES] = gate_ref[...]
    sums_a[place, 8:16, 0:LANES] = jnp.where(place // 2 == lane, heads.total(), 0.0)
    first.start()
    local.wait(0, 1, 2, 3, 4)
    weigh(0)
    first.wait()
    totals = first.total()
    head_scale_out[...] = totals[8:12, 0:LANES]
    head_shift_out[...] = totals[12:16, 0:LANES]
    gate_out[...] = totals[4:6, 0:LANES]
    output_scale_out[...] = totals[1:2] + totals[3:4]
    output_shift_out[...] = totals[0:1] + totals[2:3]
    for micro in range(2):
        back3[micro_rows(micro)] = back_part(
            features_ref[micro],
            norm3_ref[micro_rows(micro)],
            inverse3_ref[micro : micro + 1],
            output_scale[...],
            totals[2 * micro : 2 * micro + 1],
            totals[2 * micro + 1 : 2 * micro + 2],
            count,
        )
    pieces.start(dot_last(back3[...], expand_all[...].reshape(512, 512)))
    value = jnp.concatenate([act2_ref[slot] for slot in range(4)], axis=1)
    expands.part[...] = jnp.dot(
        value.T, back3[...], preferred_element_type=jnp.float32
    ).reshape(8, 64, 512)
    expands.start()
    weigh(1)
    grad = pieces.finish()
    normed = norm12_ref[1]
    grad = grad * silu_slope(normed * block_scale[1:2] + block_shift[1:2])
    sums_b[place] = tile_rows(moments(grad, normed), 8)
    second.start()
    local.wait(5, 6, 7)
    weigh(2)
    expands.middle()
    second.wait()
    totals = second.total()
    block_scale_out[1:2] = totals[1:2] + totals[3:4]
    block_shift_out[1:2] = totals[0:1] + totals[2:3]
    for micro in range(2):
        value = back_part(
            grad[micro_rows(micro)],
            normed[micro_rows(micro)],
            inverse12_ref[2 + micro : 3 + micro],
            block_scale[1:2],
            totals[2 * micro : 2 * micro + 1],
            totals[2 * micro + 1 : 2 * micro + 2],
            count,
        )
        fill_columns(value, mask_ref[micro], turned, columns, micro * PIXELS, True)
    part = jnp.zeros((2 * PIXELS, 512), jnp.float32)
    for number in range(9):
        part = part + dot_last(
            columns[:, number * LANES : (number + 1) * LANES],
            spatial_all[:, number].reshape(512, LANES),
        )
    pieces_next.start(part)
    value = jnp.concatenate([act1_ref[slot] for slot in range(4)], axis=1)
    spatials.part[...] = jnp.dot(
        value.T, columns[...], preferred_element_type=jnp.float32
    ).reshape(8, 64, 9 * LANES)
    spatials.start()
    weigh(3)
    grad = pieces_next.finish()
    normed = norm12_ref[0]
    grad = grad * silu_slope(normed * block_scale[0:1] + block_shift[0:1])
    sums_c[place] = tile_rows(moments(grad, normed), 8)
    third.start()
    weigh(4)
    spatials.middle()
    expand_out[...] = expands.finish()
    third.wait()
    totals = third.total()
    block_scale_out[0:1] = totals[1:2] + totals[3:4]
    block_shift_out[0:1] = totals[0:1] + totals[2:3]
    for micro in range(2):
        act_all[lane, micro_rows(micro)] = back_part(
            grad[micro_rows(micro)],
            normed[micro_rows(micro)],
            inverse12_ref[micro : micro + 1],
            block_scale[0:1],
            totals[2 * micro : 2 * micro + 1],
            totals[2 * micro + 1 : 2 * micro + 2],
            count,
        )
    acts.start()
    weigh(5)
    acts.wait()
    value = jnp.concatenate([act_all[slot] for slot in range(4)], axis=1)
    x = x_ref[...].reshape(2 * PIXELS, 512)
    reduces.part[...] = jnp.dot(value.T, x, preferred_element_type=jnp.float32).reshape(8, 64, 512)
    reduces.start()
    more = jnp.dot(value, reduce_all[...].reshape(512, 512), preferred_element_type=jnp.float32)
    for micro in range(2):
        features_ref[micro] = features_ref[micro] + more[micro_rows(micro)]
    weigh(6)
    weigh(7)
    local.start(8)
    reduces.middle()
    result = spatials.finish()
    for number in range(9):
        spatial_out[number] = result[:, number * LANES : (number + 1) * LANES]
    reduce_out[...] = reduces.finish()
    for item in (first, second, third, heads, acts):
        item.close()
    local.wait(8)


def run_rear(count, *arrays):
    f32, bf16 = jnp.float32, jnp.bfloat16
    return pl.pallas_call(
        functools.partial(rear_kernel, count),
        name="rear",
        out_shape=(
            jax.ShapeDtypeStruct((2, PIXELS, 512), f32),
            jax.ShapeDtypeStruct((64, 512), f32),
            jax.ShapeDtypeStruct((9, 64, LANES), f32),
            jax.ShapeDtypeStruct((64, 512), f32),
            jax.ShapeDtypeStruct((2, LANES), f32),
            jax.ShapeDtypeStruct((2, LANES), f32),
            jax.ShapeDtypeStruct((4, LANES), f32),
            jax.ShapeDtypeStruct((4, LANES), f32),
            jax.ShapeDtypeStruct((2, LANES), f32),
            jax.ShapeDtypeStruct((1, 512), f32),
            jax.ShapeDtypeStruct((1, 512), f32),
            jax.ShapeDtypeStruct((9, 256, 512), f32),
        ),
        in_specs=vmem(13) + anywhere(8),
        out_specs=tuple(vmem(11) + anywhere(1)),
        scratch_shapes=[
            pltpu.VMEM((9, 256, 512), f32),
            pltpu.VMEM((8, 2, PIXELS, 512), bf16),
            pltpu.VMEM((2, 2, 8, PIXELS, LANES), bf16),
            pltpu.VMEM((8, 2, PIXELS, LANES), bf16),
            pltpu.VMEM((4, 2 * PIXELS, LANES), bf16),
            pltpu.VMEM((4, 2 * PIXELS, LANES), bf16),
            pltpu.VMEM((8, 64, 512), bf16),
            pltpu.VMEM((8, 9, 64, LANES), bf16),
            pltpu.VMEM((8, 64, 512), bf16),
            pltpu.VMEM((3, 2 * PAD + PIXELS, 512), bf16),
            pltpu.VMEM((2 * PIXELS, 9 * 512), bf16),
            pltpu.VMEM((3, 2 * PAD + PIXELS, LANES), bf16),
            pltpu.VMEM((2 * PIXELS, 9 * LANES), bf16),
            pltpu.VMEM((4, 2 * PIXELS, LANES), bf16),
            pltpu.VMEM((4, 2 * PIXELS, LANES), bf16),
            pltpu.VMEM((4, 2 * PIXELS, LANES), bf16),
            pltpu.VMEM((4, 2 * PIXELS, LANES), bf16),
            pltpu.VMEM((8, 16, 512), f32),
            pltpu.VMEM((8, 8, LANES), f32),
            pltpu.VMEM((8, 8, LANES), f32),
            pltpu.VMEM((4, 8, LANES), f32),
            pltpu.VMEM((4, 2 * PIXELS, LANES), bf16),
            pltpu.VMEM((2 * PIXELS, 512), bf16),
        ]
        + scatter_scratch(512)
        + scatter_scratch(9 * LANES)
        + scatter_scratch(512)
        + [pltpu.SemaphoreType.DMA((4,))] * 2
        + exchange_sems(8) * 3
        + exchange_sems(4) * 2
        + scatter_sems() * 3
        + [pltpu.SemaphoreType.DMA((4,))] * 2
        + [pltpu.SemaphoreType.DMA((9,))],
        compiler_params=kernel_params(5),
    )(*arrays)


class Reduce:
    def __init__(self, part, keep, far_buf, far_got, line_buf, line_got, sems):
        self.part, self.keep, self.far_buf, self.far_got = part, keep, far_buf, far_got
        self.line_buf, self.line_got = line_buf, line_got
        self.far_send, self.far_recv, self.line_send, self.line_recv = sems

    def block(self, step):
        place, lane, depth, side, _, _ = whereabouts()
        item, late = staggered(step)
        return ranked(depth, 3 - item % 4) * 2 + (side + 1 + late) % 2, item // 4

    def far_copy(self, micro, rank, place):
        return push(
            self.far_buf.at[micro, rank],
            self.far_got.at[micro, rank],
            self.far_send.at[micro, rank],
            self.far_recv.at[micro, rank],
            place,
            lax.axis_index("chan"),
        )

    def line_copy(self, micro, rank, slot, place):
        return push(
            self.line_buf.at[micro, rank],
            self.line_got.at[micro, slot],
            self.line_send.at[micro, rank],
            self.line_recv.at[micro, slot],
            place,
            lax.axis_index("chan"),
        )

    def line_value(self, micro, slot):
        self.line_copy(micro, 0, slot, lax.axis_index("batch")).wait_recv()
        return self.line_got[micro, slot].astype(jnp.float32)

    def step(self, step):
        place, lane, depth, side, _, _ = whereabouts()
        item, late = staggered(step)
        micro, rank = item // 4, 3 - item % 4
        owner = ranked(depth, rank)

        @pl.when(late == 0)
        def _():
            self.far_buf[micro, rank] = self.part[...].astype(jnp.bfloat16)
            self.far_copy(micro, rank, depth * 2 + 1 - side).start()

        @pl.when(late == 1)
        def _():
            self.far_copy(micro, rank, place).wait_recv()
            self.keep[micro] = self.part[...] + self.far_got[micro, rank].astype(jnp.float32)

            @pl.when((middle(depth) == 1) & (rank > 0))
            def _():
                self.keep[micro] = self.keep[micro] + self.line_value(micro, owner)

            @pl.when(rank > 0)
            def _():
                first = (rank % 2) * (1 - rank // 2) * (1 - middle(depth))
                slot = owner + first * (4 - owner)
                self.line_buf[micro, rank - 1] = self.keep[micro].astype(jnp.bfloat16)
                self.line_copy(
                    micro, rank - 1, slot, homeward(depth, rank) * 2 + side
                ).start()

    def close(self, micro):
        place, lane, depth, side, _, _ = whereabouts()
        self.keep[micro] = self.keep[micro] + self.line_value(micro, depth)

        @pl.when(middle(depth) == 1)
        def _():
            self.keep[micro] = self.keep[micro] + self.line_value(micro, 4)

        for rank in range(4):
            self.far_copy(micro, rank, place).wait_send()
        for rank in range(3):
            self.line_copy(micro, rank, 0, place).wait_send()


class Channels:
    def __init__(self, stage, got, stage_sem, got_sem, values, out_sem, in_sem):
        self.stage, self.got, self.stage_sem, self.got_sem = stage, got, stage_sem, got_sem
        self.values, self.out_sem, self.in_sem = values, out_sem, in_sem

    def piece(self, slot, target, block, lane):
        return push(
            self.stage.at[slot, block],
            self.got.at[lane, block],
            self.stage_sem.at[slot, block],
            self.got_sem.at[lane, block],
            lax.axis_index("batch"),
            target,
        )

    def send(self, part, block, micro):
        _, lane, _, _, upper, core = whereabouts()
        for half in range(2):
            piece = part[:, half * LANES : (half + 1) * LANES]
            target = half * 2 + micro

            @pl.when(target == lane)
            def _():
                self.got[lane, block] = piece

            @pl.when(target != lane)
            def _():
                self.stage[target, block] = piece
                self.piece(target, target, block, lane).start()

    def collect(self, micro, take):
        _, lane, _, _, _, core = whereabouts()

        @pl.when(core == micro)
        def _():
            def body(block, _):
                for step in range(1, 4):
                    other = (lane + step) % 4
                    self.piece(other, other, block, other).wait_recv()
                take(block)
                return 0

            lax.fori_loop(0, 8, body, 0)

    def value(self, block):
        result = self.got[0, block].astype(jnp.float32)
        for other in range(1, 4):
            result = result + self.got[other, block].astype(jnp.float32)
        return result

    def sent(self):
        _, lane, _, _, _, _ = whereabouts()

        def body(block, _):
            for step in range(1, 4):
                other = (lane + step) % 4
                self.piece(other, other, block, lane).wait_send()
            return 0

        lax.fori_loop(0, 8, body, 0)

    def chunk(self, path, half, micro, chunk, place_lane):
        here = self.values.at[half, micro, pl.ds(2 * chunk, 2)]
        return push(
            here,
            here,
            self.out_sem.at[path, chunk],
            self.in_sem.at[half, micro, chunk],
            lax.axis_index("batch"),
            place_lane,
        )

    def spread(self, chunk):
        _, lane, _, _, upper, core = whereabouts()
        self.chunk(0, upper, core, chunk, 2 - 2 * upper + core).start()
        self.chunk(1, upper, core, chunk, upper * 2 + 1 - core).start()

    def relay(self, micro):
        _, lane, _, _, upper, core = whereabouts()

        @pl.when(core == micro)
        def _():
            for chunk in range(4):
                copy = self.chunk(2, 1 - upper, core, chunk, upper * 2 + 1 - core)
                copy.wait_recv()
                copy.start()

    def finish(self, micro):
        _, lane, _, _, upper, core = whereabouts()

        @pl.when(core != micro)
        def _():
            for chunk in range(4):
                for half in range(2):
                    self.chunk(0, half, micro, chunk, lane).wait_recv()

    def close(self):
        _, lane, _, _, upper, core = whereabouts()
        for chunk in range(4):
            for path in range(3):
                self.chunk(path, upper, core, chunk, lane).wait_send()


def middle_kernel(
    count,
    block_ref,
    bias_ref,
    mine_ref,
    head_hbm,
    distil_hbm,
    mask_hbm,
    depth_hbm,
    segment_hbm,
    cot_hbm,
    depth_out,
    segment_out,
    distil_grad,
    gate_sums,
    head_sums,
    back_out,
    block_hbm,
    back_hbm,
    block_all,
    head_back,
    head_ref,
    distil_ref,
    mask_ref,
    depth_cot,
    segment_cot,
    cot_all,
    head_weight,
    mixed,
    mixed_back,
    turned,
    columns,
    acts,
    norm_ref,
    slope_ref,
    grads_all,
    own_stage,
    own_got,
    stage,
    got,
    part_ref,
    keep,
    far_buf,
    far_got,
    line_buf,
    line_got,
    stats,
    *sems,
):
    place, lane, depth, side, upper, core = whereabouts()
    half_width = LANES // 2
    source = place // 2 == lane
    low = lax.broadcasted_iota(jnp.int32, (PIXELS, LANES), 1) < half_width
    gather = Gather(block_all, *sems[0:3], 2)
    gather_back = Gather(grads_all, *sems[3:6], 2)
    reduce = Reduce(part_ref, keep, far_buf, far_got, line_buf, line_got, sems[6:10])
    ahead = Channels(stage, got, sems[10], sems[11], acts, sems[12], sems[13])
    behind = Channels(stage, got, sems[10], sems[11], head_back, sems[14], sems[15])
    own_sem, own_recv = sems[16:18]
    local = Local(
        (
            (head_hbm, head_ref),
            (mask_hbm, mask_ref),
            (distil_hbm, distil_ref),
            (depth_hbm, depth_cot),
            (segment_hbm, segment_cot),
            (cot_hbm, cot_all),
            (block_all, block_hbm),
            (head_back, back_hbm),
        ),
        sems[18],
    )
    local.start(0, 1, 2, 3, 4, 5)

    greet(batch_peers() + chan_peers())
    block_all[place] = block_ref[...]
    gather.start(0)
    clear_edges(turned)
    local.wait(0)
    for number in range(9):
        head_weight[number * 512 : (number + 1) * 512] = head_ref[number].T
    local.wait(1)

    def forward_step(step, _):
        block, micro = gather.next(step)
        fill_columns(block_all[block, micro], mask_ref[block, micro], turned, columns)
        part = jnp.dot(columns[0:PIXELS], head_weight[...], preferred_element_type=jnp.float32)
        ahead.send(part.astype(jnp.bfloat16), block, micro)

        @pl.when(step == 0)
        def _():
            local.wait(2)
            prepare_mixed()

        @pl.when(step == 1)
        def _():
            gather.start(1)

        @pl.when(step == 4)
        def _():
            for number in range(9):
                mixed_back[number * 512 : (number + 1) * 512] = mixed[
                    number * 256 : (number + 1) * 256
                ].T

        @pl.when(step == 10)
        def _():
            normalize(0)

        @pl.when(step == 13)
        def _():
            ahead.relay(0)

        return 0

    def prepare_mixed():
        width = half_width
        for number in range(9):
            for stream in range(2):
                for head in range(4):
                    index = head - SOURCE_START[stream]
                    rows = slice(number * 256 + head * width, number * 256 + (head + 1) * width)
                    left = slice(2 * stream * LANES, (2 * stream + 1) * LANES)
                    right = slice((2 * stream + 1) * LANES, (2 * stream + 2) * LANES)
                    nothing = jnp.zeros((width, LANES), jnp.bfloat16)
                    mixed[rows, left] = (
                        distil_ref[stream, number, 0] if head == OWN_HEAD[stream] else nothing
                    )
                    mixed[rows, right] = (
                        distil_ref[stream, number, 1 + index] if 0 <= index < 3 else nothing
                    )

    def normalize(micro):
        zero = jnp.zeros((1, LANES), jnp.float32)

        @pl.when(core == micro)
        def _():
            stats[0:2] = jnp.zeros((2, LANES), jnp.float32)

        def take(block):
            value = ahead.value(block)
            norm_ref[block] = value
            stats[0:1] += jnp.sum(value, axis=0, keepdims=True)
            stats[1:2] += jnp.sum(value * value, axis=0, keepdims=True)

        ahead.collect(micro, take)

        @pl.when(core == micro)
        def _():
            center = stats[0:1] / count
            inverse = lax.rsqrt(stats[1:2] / count - center * center + EPSILON)
            stats[2:3] = inverse

            def activate(chunk, _):
                for item in range(2):
                    block = 2 * chunk + item
                    normed = (norm_ref[block] - center) * inverse
                    norm_ref[block] = normed
                    out = normed * mine_ref[0:1] + mine_ref[1:2]
                    acts[upper, core, block] = (out * jax.nn.sigmoid(out)).astype(jnp.bfloat16)
                ahead.spread(chunk)
                return 0

            lax.fori_loop(0, 4, activate, 0)

    def own_copy(block, micro, slot, target):
        return push(
            own_stage.at[block, micro],
            own_got.at[slot, micro],
            own_sem.at[block, micro],
            own_recv.at[slot, micro],
            target,
            lane,
        )

    def send_own(micro):
        @pl.when(source)
        def _():
            own_got[place % 2, micro] = jnp.where(
                low, acts[0, micro, place], acts[1, micro, place]
            )

            def pack(step, _):
                block = (place + step) % 8
                own_stage[block, micro] = jnp.where(
                    low, acts[0, micro, block], acts[1, micro, block]
                )
                own_copy(block, micro, place % 2, block).start()
                return 0

            lax.fori_loop(1, 8, pack, 0)

    def act_value(block, micro):
        return jnp.concatenate([acts[half, micro, block] for half in range(2)], axis=1)

    def gate(micro):
        reduce.close(micro)
        for parity in range(2):
            @pl.when(2 * lane + parity != place)
            def _():
                own_copy(0, micro, parity, place).wait_recv()

        for stream, cot_ref in enumerate((depth_cot, segment_cot)):
            first = own_got[0, micro].astype(jnp.float32)
            second = own_got[1, micro].astype(jnp.float32)
            if stream == 0:
                second = pltpu.roll(second, half_width, 1)
            else:
                first = pltpu.roll(first, half_width, 1)
            own = jnp.where(low, first, second)
            column = 2 * stream * LANES
            gates = jax.nn.sigmoid(
                keep[micro, :, column : column + LANES] + bias_ref[stream : stream + 1]
            )
            message = keep[micro, :, column + LANES : column + 2 * LANES]
            cot = cot_ref[micro].astype(jnp.float32)
            out_ref = (depth_out, segment_out)[stream]
            out_ref[micro] = (own + gates * message).astype(jnp.bfloat16)
            gate_grad = (cot * message * gates * (1.0 - gates)).astype(jnp.bfloat16)
            bias_sum = jnp.sum(gate_grad.astype(jnp.float32), axis=0, keepdims=True)
            if micro == 0:
                gate_sums[stream : stream + 1] = bias_sum
            else:
                gate_sums[stream : stream + 1] += bias_sum
            grads_all[place, micro, :, column : column + LANES] = gate_grad
            grads_all[place, micro, :, column + LANES : column + 2 * LANES] = (cot * gates).astype(
                jnp.bfloat16
            )

    def distil_step(step, _):
        block, micro = reduce.block(step)
        fill_columns(act_value(block, micro), mask_ref[block, micro], turned, columns)
        part_ref[...] = jnp.dot(
            columns[0:PIXELS, 0 : 9 * 256], mixed[...], preferred_element_type=jnp.float32
        )
        reduce.step(step)

        @pl.when(step == 2)
        def _():
            normalize(1)

        @pl.when(step == 5)
        def _():
            ahead.relay(1)

        @pl.when(step == 6)
        def _():
            ahead.finish(1)
            ahead.sent()
            send_own(1)

        @pl.when(step == 11)
        def _():
            local.wait(3, 4)
            gate(0)
            gather_back.start(0)

        return 0

    distil_grad[...] = jnp.zeros_like(distil_grad)

    def back_step(step, _):
        block, micro = gather_back.next(step)
        fill_columns(
            grads_all[block, micro], mask_ref[block, micro], turned, columns, flip=True
        )
        part = jnp.dot(columns[0:PIXELS], mixed_back[...], preferred_element_type=jnp.float32)
        extra = cot_all[block, micro].astype(jnp.float32)
        part = jnp.concatenate(
            [
                part[:, :LANES] + jnp.where(low & source, extra, 0.0),
                part[:, LANES:] + jnp.where(low | ~source, 0.0, extra),
            ],
            axis=1,
        )
        behind.send(part.astype(jnp.bfloat16), block, micro)
        @pl.when(step == 10)
        def _():
            normalize_back(0)

        @pl.when(step == 13)
        def _():
            behind.relay(0)

        return 0

    def normalize_back(micro):
        @pl.when(core == micro)
        def _():
            stats[4:6] = jnp.zeros((2, LANES), jnp.float32)

        def take(block):
            normed = norm_ref[block]
            value = behind.value(block) * silu_slope(normed * mine_ref[0:1] + mine_ref[1:2])
            slope_ref[block] = value
            stats[4:5] += jnp.sum(value, axis=0, keepdims=True)
            stats[5:6] += jnp.sum(value * normed, axis=0, keepdims=True)

        behind.collect(micro, take)

        @pl.when(core == micro)
        def _():
            shift_sum, scale_sum = stats[4:5], stats[5:6]
            head_sums[0:1] = scale_sum
            head_sums[1:2] = shift_sum
            factor = mine_ref[0:1] * stats[2:3]

            def activate(chunk, _):
                for item in range(2):
                    block = 2 * chunk + item
                    value = slope_ref[block]
                    head_back[upper, core, block] = (
                        factor * (value - (shift_sum + norm_ref[block] * scale_sum) / count)
                    ).astype(jnp.bfloat16)
                behind.spread(chunk)
                return 0

            lax.fori_loop(0, 4, activate, 0)

    def head_value(block, micro):
        return jnp.concatenate([head_back[half, micro, block] for half in range(2)], axis=1)

    def weigh(block):
        for micro in range(2):
            fill_columns(
                grads_all[block, micro],
                mask_ref[block, micro],
                turned,
                columns,
                micro * PIXELS,
                True,
            )
        value = jnp.concatenate([act_value(block, micro) for micro in range(2)], axis=0).T
        width = half_width
        for number in range(9):
            product = jnp.dot(
                value,
                columns[:, number * 512 : (number + 1) * 512],
                preferred_element_type=jnp.float32,
            )
            for stream in range(2):
                for index in range(4):
                    head = OWN_HEAD[stream] if index == 0 else SOURCE_START[stream] + index - 1
                    column = (2 * stream + (index > 0)) * LANES
                    distil_grad[stream, number, index] += product[
                        head * width : (head + 1) * width, column : column + LANES
                    ]

    def block_step(step, _):
        block, micro = reduce.block(step)
        fill_columns(
            head_value(block, micro), mask_ref[block, micro], turned, columns, flip=True
        )
        part_ref[...] = jnp.dot(
            columns[0:PIXELS, 0 : 9 * 256],
            head_ref[...].reshape(9 * 256, 512),
            preferred_element_type=jnp.float32,
        )
        item, late = staggered(step)

        @pl.when(late == 1)
        def _():
            weigh(item)

        reduce.step(step)

        @pl.when(step == 2)
        def _():
            normalize_back(1)

        @pl.when(step == 5)
        def _():
            behind.relay(1)

        @pl.when(step == 6)
        def _():
            behind.finish(1)

        return 0

    def schedule(turn, _):
        phase, spot = (turn + 2) // 16, (turn + 2) % 16
        seam = (1 - (spot + 12) // 16) * ((phase + 3) // 4)
        odd = spot % 2
        kind = phase - seam * odd
        step = seam * (14 * odd + spot // 2) + (1 - seam) * (spot - 2)

        @pl.when(kind == 0)
        def _():
            forward_step(step, 0)

        @pl.when((kind == 1) & (step == 0))
        def _():
            ahead.finish(0)
            send_own(0)

        @pl.when(kind == 1)
        def _():
            distil_step(step, 0)

        @pl.when((kind == 2) & (step == 0))
        def _():
            local.wait(5)

        @pl.when((kind == 2) & (step == 4))
        def _():
            gate(1)
            gather_back.start(1)
            ahead.close()

        @pl.when(kind == 2)
        def _():
            back_step(step, 0)

        @pl.when((kind == 3) & (step == 0))
        def _():
            behind.finish(0)
            local.start(6)

        @pl.when(kind == 3)
        def _():
            block_step(step, 0)

        return 0

    lax.fori_loop(0, 66, schedule, 0)
    for micro in range(2):
        reduce.close(micro)
        back_out[micro_rows(micro)] = keep[micro]
    behind.sent()
    behind.close()
    gather.close()
    gather_back.close()
    local.start(7)

    @pl.when(source)
    def _():
        for micro in range(2):
            for step in range(1, 8):
                own_copy((place + step) % 8, micro, 0, place).wait_send()

    local.wait(6, 7)


def run_middle(count, *arrays):
    f32, bf16 = jnp.float32, jnp.bfloat16
    block = (PIXELS, 512)
    dma = pltpu.SemaphoreType.DMA
    return pl.pallas_call(
        functools.partial(middle_kernel, count),
        name="middle",
        out_shape=(
            jax.ShapeDtypeStruct((2, PIXELS, LANES), bf16),
            jax.ShapeDtypeStruct((2, PIXELS, LANES), bf16),
            jax.ShapeDtypeStruct((2, 9, 4, 64, LANES), f32),
            jax.ShapeDtypeStruct((2, LANES), f32),
            jax.ShapeDtypeStruct((2, LANES), f32),
            jax.ShapeDtypeStruct((2 * PIXELS, 512), f32),
            jax.ShapeDtypeStruct((8, 2) + block, bf16),
            jax.ShapeDtypeStruct((2, 2, 8, PIXELS, LANES), bf16),
        ),
        in_specs=vmem(3) + anywhere(6),
        out_specs=tuple(vmem(6) + anywhere(2)),
        scratch_shapes=[
            pltpu.VMEM((8, 2) + block, bf16),
            pltpu.VMEM((2, 2, 8, PIXELS, LANES), bf16),
            pltpu.VMEM((9, 256, 512), bf16),
            pltpu.VMEM((2, 9, 4, 64, LANES), bf16),
            pltpu.VMEM((8, 2, PIXELS, LANES), bf16),
            pltpu.VMEM((2, PIXELS, LANES), bf16),
            pltpu.VMEM((2, PIXELS, LANES), bf16),
            pltpu.VMEM((8, 2, PIXELS, LANES), bf16),
            pltpu.VMEM((9 * 512, 256), bf16),
            pltpu.VMEM((9 * 256, 512), bf16),
            pltpu.VMEM((9 * 512, 256), bf16),
            pltpu.VMEM((3, 2 * PAD + PIXELS, 512), bf16),
            pltpu.VMEM((2 * PIXELS, 9 * 512), bf16),
            pltpu.VMEM((2, 2, 8, PIXELS, LANES), bf16),
            pltpu.VMEM((8, PIXELS, LANES), f32),
            pltpu.VMEM((8, PIXELS, LANES), f32),
            pltpu.VMEM((8, 2) + block, bf16),
            pltpu.VMEM((8, 2, PIXELS, LANES), bf16),
            pltpu.VMEM((2, 2, PIXELS, LANES), bf16),
            pltpu.VMEM((4, 8, PIXELS, LANES), bf16),
            pltpu.VMEM((4, 8, PIXELS, LANES), bf16),
            pltpu.VMEM(block, f32),
            pltpu.VMEM((2,) + block, f32),
            pltpu.VMEM((2, 4) + block, bf16),
            pltpu.VMEM((2, 4) + block, bf16),
            pltpu.VMEM((2, 3) + block, bf16),
            pltpu.VMEM((2, 5) + block, bf16),
            pltpu.VMEM((8, LANES), f32),
        ]
        + gather_sems(2) * 2
        + [dma((2, 4)), dma((2, 4)), dma((2, 3)), dma((2, 5))]
        + [dma((4, 8)), dma((4, 8))]
        + [dma((3, 4)), dma((2, 2, 4))] * 2
        + [dma((8, 2)), dma((2, 2)), dma((8,))],
        compiler_params=kernel_params(2),
    )(*arrays)


def finish_kernel(count, *refs):
    sources, targets, held = refs[:count], refs[count : 2 * count], refs[2 * count : 3 * count]
    sem_in, sem_out = refs[3 * count :]

    def parts(ref):
        large = len(ref.shape) > 2
        return [ref.at[number] for number in range(ref.shape[0])] if large else [ref]

    number = 0
    loads, stores = [], []
    for source, target, hold in zip(sources, targets, held):
        for pieces in zip(parts(source), parts(hold), parts(target)):
            loads.append(pltpu.make_async_copy(pieces[0], pieces[1], sem_in.at[number]))
            stores.append(pltpu.make_async_copy(pieces[1], pieces[2], sem_out.at[number]))
            number += 1
    for load in loads:
        load.start()
    for load, store in zip(loads, stores):
        load.wait()
        store.start()
    for store in stores:
        store.wait()


def run_finish(*arrays):
    anywhere = [pl.BlockSpec(memory_space=pltpu.HBM)] * len(arrays)
    copies = sum(item.shape[0] if item.ndim > 2 else 1 for item in arrays)
    return pl.pallas_call(
        functools.partial(finish_kernel, len(arrays)),
        name="finish",
        out_shape=tuple(jax.ShapeDtypeStruct(item.shape, item.dtype) for item in arrays),
        in_specs=anywhere,
        out_specs=tuple(anywhere),
        scratch_shapes=[pltpu.VMEM(item.shape, item.dtype) for item in arrays]
        + [pltpu.SemaphoreType.DMA((copies,))] * 2,
        compiler_params=pltpu.CompilerParams(vmem_limit_bytes=60 * 2**20),
    )(*arrays)


def stationary_local(
    features,
    image_ids,
    reduce_weight,
    spatial_weight,
    expand_weight,
    head_weights,
    distil_weights,
    block_scale,
    block_shift,
    head_scale,
    head_shift,
    gate_bias,
    output_scale,
    output_shift,
    depth_cotangent,
    segment_cotangent,
):
    canvases, row_count, column_count = image_ids.shape
    pixels = row_count * column_count
    count = float(lax.axis_size("batch") * pixels)
    x = features.reshape(canvases, pixels, -1)
    cots = [item.reshape(canvases, pixels, LANES) for item in (depth_cotangent, segment_cotangent)]
    block_params = (block_scale, block_shift)
    output_params = (output_scale[None], output_shift[None])
    (
        block_out,
        norm3,
        inverse3,
        norm12,
        inverse12,
        mine,
        mask,
        act1,
        act2,
        reduce_all,
        spatial_all,
        expand_all,
        mask_all,
        cot_all,
    ) = run_front(
        count,
        x,
        image_ids,
        reduce_weight.T,
        spatial_weight,
        expand_weight,
        *block_params,
        *output_params,
        head_scale,
        head_shift,
        *cots,
    )
    depth_out, segment_out, distil_grad, gate_sums, head_sums, block_grad, block_all, back_all = run_middle(
        count,
        block_out,
        gate_bias,
        mine,
        head_weights.transpose(0, 2, 3, 1).reshape(9, -1, head_weights.shape[1]),
        distil_weights,
        mask_all,
        *cots,
        cot_all,
    )
    (
        features_grad,
        reduce_grad,
        spatial_grad,
        expand_grad,
        block_scale_grad,
        block_shift_grad,
        head_scale_grad,
        head_shift_grad,
        gate_grad,
        output_scale_grad,
        output_shift_grad,
        heads_grad,
    ) = run_rear(
        count,
        block_grad,
        x,
        norm3,
        inverse3,
        norm12,
        inverse12,
        mask,
        *block_params,
        *output_params,
        head_sums,
        gate_sums,
        block_all,
        back_all,
        mask_all,
        act1,
        act2,
        reduce_all,
        spatial_all,
        expand_all,
    )
    outs = run_finish(
        depth_out,
        segment_out,
        features_grad,
        reduce_grad,
        spatial_grad,
        expand_grad,
        heads_grad,
        distil_grad,
        block_scale_grad,
        block_shift_grad,
        head_scale_grad,
        head_shift_grad,
        gate_grad,
        output_scale_grad,
        output_shift_grad,
    )
    heads_grad = outs[6].reshape(9, 4, -1, head_weights.shape[1]).transpose(0, 3, 1, 2)
    return (
        outs[0].reshape(depth_cotangent.shape),
        outs[1].reshape(depth_cotangent.shape),
        outs[2].reshape(features.shape),
        outs[3].T,
        *outs[4:6],
        heads_grad,
        *outs[7:13],
        outs[13][0],
        outs[14][0],
    )


def solution(mesh):
    fits = dict(mesh.shape) == {"batch": 8, "chan": 4}
    local = stationary_local if fits else gathered_local
    placed = (
        P("batch", None, None, "chan"),
        P("batch", None, None),
        P("chan", "batch"),
        P(None, "batch", "chan"),
        P("batch", "chan"),
        P(None, "chan", None, "batch"),
        P(None, None, None, "batch", "chan"),
        P(None, "chan"),
        P(None, "chan"),
        P(None, "chan"),
        P(None, "chan"),
        P(None, "chan"),
        P("chan"),
        P("chan"),
        P("batch", None, None, "chan"),
        P("batch", None, None, "chan"),
    )
    return jax.shard_map(
        local,
        mesh=mesh,
        in_specs=placed,
        out_specs=(
            P("batch", None, None, "chan"),
            P("batch", None, None, "chan"),
            P("batch", None, None, "chan"),
            P("chan", "batch"),
            P(None, "batch", "chan"),
            P("batch", "chan"),
            P(None, "chan", None, "batch"),
            P(None, None, None, "batch", "chan"),
            P(None, "chan"),
            P(None, "chan"),
            P(None, "chan"),
            P(None, "chan"),
            P(None, "chan"),
            P("chan"),
            P("chan"),
        ),
        check_vma=False,
    )
```

```python
import functools

import jax
import jax.numpy as jnp
from jax import lax
from jax.experimental import pallas as pl
from jax.experimental.pallas import tpu as pltpu
from jax.sharding import PartitionSpec as P

EPSILON = 1e-05
OFFSETS = ((-1, -1), (-1, 0), (-1, 1), (0, -1), (0, 0), (0, 1), (1, -1), (1, 0), (1, 1))
OWN_HEAD = (0, 3)
SOURCE_START = (1, 0)


def silu_slope(values):
    sig = jax.nn.sigmoid(values)
    return sig * (1.0 + values * (1.0 - sig))


def shifted(values, vertical, lateral):
    row_count, column_count = (values.shape[1], values.shape[2])
    widths = [(0, 0)] * values.ndim
    widths[1] = (1, 1)
    widths[2] = (1, 1)
    padded = jnp.pad(values, widths)
    return padded[
        :, 1 + vertical : 1 + vertical + row_count, 1 + lateral : 1 + lateral + column_count
    ]


def tap_masks(image_ids):
    row_count, column_count = (image_ids.shape[1], image_ids.shape[2])
    padded = jnp.pad(image_ids, ((0, 0), (1, 1), (1, 1)), constant_values=-1)
    masks = []
    for vertical, lateral in OFFSETS:
        beside = padded[
            :, 1 + vertical : 1 + vertical + row_count, 1 + lateral : 1 + lateral + column_count
        ]
        masks.append((beside == image_ids).astype(jnp.float32))
    return jnp.stack(masks)


def conv_forward(inputs, weight, masks):
    total = 0.0
    for number, (vertical, lateral) in enumerate(OFFSETS):
        moved = shifted(inputs, vertical, lateral) * masks[number][..., None].astype(inputs.dtype)
        total = total + jnp.einsum(
            "nhwc,co->nhwo", moved, weight[number], preferred_element_type=jnp.float32
        )
    return total


def conv_input_grad(grads, weight, masks):
    total = 0.0
    for number, (vertical, lateral) in enumerate(OFFSETS):
        term = jnp.einsum(
            "nhwo,co->nhwc", grads, weight[number], preferred_element_type=jnp.float32
        )
        total = total + shifted(term * masks[number][..., None], -vertical, -lateral)
    return total


def conv_weight_grad(inputs, grads, masks):
    pieces = []
    for number, (vertical, lateral) in enumerate(OFFSETS):
        moved = shifted(inputs, vertical, lateral) * masks[number][..., None].astype(inputs.dtype)
        pieces.append(jnp.einsum("nhwc,nhwo->co", moved, grads, preferred_element_type=jnp.float32))
    return jnp.stack(pieces)


def pixel_sum(values):
    return jnp.sum(values, axis=(0, 1, 2))


def normalize(values, scale, shift, count):
    total, squares = lax.psum((pixel_sum(values), pixel_sum(values * values)), "batch")
    center = total / count
    inverse = lax.rsqrt(squares / count - center * center + EPSILON)
    normed = (values - center) * inverse
    return (normed, inverse, normed * scale + shift)


def grad_sums(first_sum, second_sum):
    return lax.psum((first_sum, second_sum), "batch")


def normalize_back(grads, normed, inverse, scale, shift_sum, scale_sum, count):
    return scale * inverse * (grads - (shift_sum + normed * scale_sum) / count)


def channel_gather(values):
    return lax.all_gather(values, "chan", axis=4, tiled=True)


def channel_sum(values):
    return lax.psum_scatter(
        values.astype(jnp.bfloat16), "chan", scatter_dimension=4, tiled=True
    ).astype(jnp.float32)


def fetch_weights(reduce_weight, spatial_weight, expand_weight, head_weights, distil_weights):
    return (
        lax.all_gather(reduce_weight, "batch", axis=1, tiled=True),
        lax.all_gather(spatial_weight, "batch", axis=1, tiled=True),
        lax.all_gather(expand_weight, "batch", axis=0, tiled=True),
        lax.all_gather(head_weights, "batch", axis=3, tiled=True),
        lax.all_gather(distil_weights, "batch", axis=3, tiled=True),
    )


def scatter_weights(grads):
    reduce_grad, spatial_grad, expand_grad, heads_grad, distil_grad = grads
    return (
        lax.psum_scatter(reduce_grad, "batch", scatter_dimension=1, tiled=True),
        lax.psum_scatter(spatial_grad, "batch", scatter_dimension=1, tiled=True),
        lax.psum_scatter(expand_grad, "batch", scatter_dimension=0, tiled=True),
        lax.psum_scatter(heads_grad, "batch", scatter_dimension=3, tiled=True),
        lax.psum_scatter(distil_grad, "batch", scatter_dimension=3, tiled=True),
    )


def micro_step(inputs, image_ids, depth_cot, segment_cot, gathered, small, batch_count):
    reduce_full, spatial_full, expand_full, heads_full, distil_full = gathered
    block_scale, block_shift, head_scale, head_shift, gate_bias, output_scale, output_shift = small
    masks = tap_masks(image_ids)
    canvases, row_count, column_count = image_ids.shape
    count = float(batch_count * canvases * row_count * column_count)
    first_partial = jnp.einsum(
        "nhwc,co->nhwo", inputs, reduce_full, preferred_element_type=jnp.float32
    )
    first = channel_sum(first_partial[:, :, :, None, :])
    first_norm, first_inv, first_out = normalize(first, block_scale[0:1], block_shift[0:1], count)
    first_act = jax.nn.silu(first_out).astype(jnp.bfloat16)
    first_full = channel_gather(first_act)[:, :, :, 0, :]
    second = conv_forward(first_full, spatial_full, masks)[:, :, :, None, :]
    second_norm, second_inv, second_out = normalize(
        second, block_scale[1:2], block_shift[1:2], count
    )
    second_act = jax.nn.silu(second_out).astype(jnp.bfloat16)
    second_full = channel_gather(second_act)[:, :, :, 0, :]
    third = jnp.einsum(
        "nhwc,co->nhwo", second_full, expand_full, preferred_element_type=jnp.float32
    )[:, :, :, None, :]
    third_norm, third_inv, third_out = normalize(
        third, output_scale[None], output_shift[None], count
    )
    summed = third_out[:, :, :, 0, :] + inputs.astype(jnp.float32)
    block_out = jax.nn.silu(summed).astype(jnp.bfloat16)
    heads_flat = heads_full.reshape(heads_full.shape[0], heads_full.shape[1], -1)
    head_partial = conv_forward(block_out, heads_flat, masks)
    head_pre = channel_sum(
        head_partial.reshape(head_partial.shape[:3] + (heads_full.shape[2], heads_full.shape[3]))
    )
    head_norm, head_inv, head_out = normalize(head_pre, head_scale, head_shift, count)
    head_act = jax.nn.silu(head_out).astype(jnp.bfloat16)
    head_full = channel_gather(head_act)
    head_width = head_full.shape[4]
    gate_pre = [0.0, 0.0]
    message = [0.0, 0.0]
    for number, (vertical, lateral) in enumerate(OFFSETS):
        moved = shifted(head_full, vertical, lateral) * masks[number][:, :, :, None, None].astype(
            jnp.bfloat16
        )
        for stream in range(2):
            weights_here = distil_full[stream, number]
            first_source = SOURCE_START[stream]
            sources = moved[:, :, :, first_source : first_source + 3].reshape(
                moved.shape[:3] + (3 * head_width,)
            )
            gate_pre[stream] = gate_pre[stream] + jnp.einsum(
                "nhwc,co->nhwo",
                moved[:, :, :, OWN_HEAD[stream]],
                weights_here[0],
                preferred_element_type=jnp.float32,
            )
            message[stream] = message[stream] + jnp.einsum(
                "nhwc,co->nhwo",
                sources,
                weights_here[1:].reshape(3 * head_width, -1),
                preferred_element_type=jnp.float32,
            )
    cotangents = (depth_cot.astype(jnp.float32), segment_cot.astype(jnp.float32))
    outputs, message_grads, gate_grads = ([], [], [])
    for stream in range(2):
        gate_value = jax.nn.sigmoid(gate_pre[stream] + gate_bias[stream])
        own_feature = head_act[:, :, :, OWN_HEAD[stream]].astype(jnp.float32)
        outputs.append((own_feature + gate_value * message[stream]).astype(jnp.bfloat16))
        message_grads.append((cotangents[stream] * gate_value).astype(jnp.bfloat16))
        gate_grads.append(
            (cotangents[stream] * message[stream] * gate_value * (1.0 - gate_value)).astype(
                jnp.bfloat16
            )
        )
    spread_grad = 0.0
    distil_parts = [[], []]
    for number, (vertical, lateral) in enumerate(OFFSETS):
        tap_mask = masks[number][:, :, :, None, None]
        moved = shifted(head_full, vertical, lateral) * tap_mask.astype(jnp.bfloat16)
        tap_grad = jnp.zeros(head_full.shape, jnp.float32)
        for stream in range(2):
            weights_here = distil_full[stream, number]
            first_source = SOURCE_START[stream]
            sources = moved[:, :, :, first_source : first_source + 3].reshape(
                moved.shape[:3] + (3 * head_width,)
            )
            own_grad = jnp.einsum(
                "nhwo,co->nhwc",
                gate_grads[stream],
                weights_here[0],
                preferred_element_type=jnp.float32,
            )
            source_grad = jnp.einsum(
                "nhwo,co->nhwc",
                message_grads[stream],
                weights_here[1:].reshape(3 * head_width, -1),
                preferred_element_type=jnp.float32,
            )
            tap_grad = tap_grad.at[:, :, :, OWN_HEAD[stream]].add(own_grad)
            tap_grad = tap_grad.at[:, :, :, first_source : first_source + 3].add(
                source_grad.reshape(source_grad.shape[:3] + (3, head_width))
            )
            gate_weight_grad = jnp.einsum(
                "nhwc,nhwo->co",
                moved[:, :, :, OWN_HEAD[stream]],
                gate_grads[stream],
                preferred_element_type=jnp.float32,
            )
            source_weight_grad = jnp.einsum(
                "nhwc,nhwo->co", sources, message_grads[stream], preferred_element_type=jnp.float32
            )
            distil_parts[stream].append(
                jnp.concatenate(
                    [gate_weight_grad[None], source_weight_grad.reshape(3, head_width, -1)], axis=0
                )
            )
        spread_grad = spread_grad + shifted(tap_grad * tap_mask, -vertical, -lateral)
    distil_grad = jnp.stack([jnp.stack(distil_parts[0]), jnp.stack(distil_parts[1])])
    head_grad = channel_sum(spread_grad)
    head_grad = (
        head_grad.at[:, :, :, OWN_HEAD[0]]
        .add(cotangents[0])
        .at[:, :, :, OWN_HEAD[1]]
        .add(cotangents[1])
    )
    head_grad = head_grad * silu_slope(head_out)
    gate_sums = jnp.stack(
        [pixel_sum(gate_grads[0].astype(jnp.float32)), pixel_sum(gate_grads[1].astype(jnp.float32))]
    )
    shift_sums, scale_sums = grad_sums(
        jnp.concatenate([pixel_sum(head_grad), gate_sums], axis=0), pixel_sum(head_grad * head_norm)
    )
    head_pre_grad = normalize_back(
        head_grad, head_norm, head_inv, head_scale, shift_sums[:4], scale_sums, count
    ).astype(jnp.bfloat16)
    head_pre_full = channel_gather(head_pre_grad)
    head_flat_grad = head_pre_full.reshape(head_pre_full.shape[:3] + (-1,))
    block_grad = conv_input_grad(head_flat_grad, heads_flat, masks)
    heads_grad = conv_weight_grad(block_out, head_flat_grad, masks).reshape(heads_full.shape)
    summed_grad = block_grad * silu_slope(summed)
    third_grad = summed_grad[:, :, :, None, :]
    third_shift, third_scale = grad_sums(pixel_sum(third_grad), pixel_sum(third_grad * third_norm))
    third_pre = normalize_back(
        third_grad, third_norm, third_inv, output_scale[None], third_shift, third_scale, count
    ).astype(jnp.bfloat16)[:, :, :, 0, :]
    expand_grad = jnp.einsum(
        "nhwc,nhwo->co", second_full, third_pre, preferred_element_type=jnp.float32
    )
    second_grad = channel_sum(
        jnp.einsum("nhwo,co->nhwc", third_pre, expand_full, preferred_element_type=jnp.float32)[
            :, :, :, None, :
        ]
    )
    second_grad = second_grad * silu_slope(second_out)
    second_shift, second_scale = grad_sums(
        pixel_sum(second_grad), pixel_sum(second_grad * second_norm)
    )
    second_pre = normalize_back(
        second_grad, second_norm, second_inv, block_scale[1:2], second_shift, second_scale, count
    ).astype(jnp.bfloat16)[:, :, :, 0, :]
    spatial_grad = conv_weight_grad(first_full, second_pre, masks)
    first_grad = channel_sum(conv_input_grad(second_pre, spatial_full, masks)[:, :, :, None, :])
    first_grad = first_grad * silu_slope(first_out)
    first_shift, first_scale = grad_sums(pixel_sum(first_grad), pixel_sum(first_grad * first_norm))
    first_pre = normalize_back(
        first_grad, first_norm, first_inv, block_scale[0:1], first_shift, first_scale, count
    ).astype(jnp.bfloat16)
    first_pre_full = channel_gather(first_pre)[:, :, :, 0, :]
    reduce_grad = jnp.einsum(
        "nhwc,nhwo->co", inputs, first_pre_full, preferred_element_type=jnp.float32
    )
    input_grad = summed_grad + jnp.einsum(
        "nhwo,co->nhwc", first_pre_full, reduce_full, preferred_element_type=jnp.float32
    )
    weight_grads = (reduce_grad, spatial_grad, expand_grad, heads_grad, distil_grad)
    small_grads = (
        jnp.concatenate([first_scale, second_scale], axis=0),
        jnp.concatenate([first_shift, second_shift], axis=0),
        scale_sums,
        shift_sums[:4],
        shift_sums[4:],
        third_scale[0],
        third_shift[0],
    )
    return (outputs[0], outputs[1], input_grad, weight_grads, small_grads)


def gathered_local(
    features,
    image_ids,
    reduce_weight,
    spatial_weight,
    expand_weight,
    head_weights,
    distil_weights,
    block_scale,
    block_shift,
    head_scale,
    head_shift,
    gate_bias,
    output_scale,
    output_shift,
    depth_cotangent,
    segment_cotangent,
):
    batch_count = lax.axis_size("batch")
    small = (
        block_scale,
        block_shift,
        head_scale,
        head_shift,
        gate_bias,
        output_scale,
        output_shift,
    )
    depth_list, segment_list, input_list = ([], [], [])
    weight_total = None
    small_total = None
    for micro_index in range(features.shape[0]):
        gathered = fetch_weights(
            reduce_weight, spatial_weight, expand_weight, head_weights, distil_weights
        )
        canvas_pick = slice(micro_index, micro_index + 1)
        depth_out, segment_out, input_grad, weight_grads, small_grads = micro_step(
            features[canvas_pick],
            image_ids[canvas_pick],
            depth_cotangent[canvas_pick],
            segment_cotangent[canvas_pick],
            gathered,
            small,
            batch_count,
        )
        weight_grads = scatter_weights(weight_grads)
        weight_total = (
            weight_grads
            if weight_total is None
            else jax.tree.map(jnp.add, weight_total, weight_grads)
        )
        small_total = (
            small_grads if small_total is None else jax.tree.map(jnp.add, small_total, small_grads)
        )
        depth_list.append(depth_out)
        segment_list.append(segment_out)
        input_list.append(input_grad)
    reduce_grad, spatial_grad, expand_grad, heads_grad, distil_grad = weight_total
    scale_mid, shift_mid, scale_heads, shift_heads, bias_gates, scale_out, shift_out = small_total
    return (
        jnp.concatenate(depth_list, axis=0),
        jnp.concatenate(segment_list, axis=0),
        jnp.concatenate(input_list, axis=0),
        reduce_grad,
        spatial_grad,
        expand_grad,
        heads_grad,
        distil_grad,
        scale_mid,
        shift_mid,
        scale_heads,
        shift_heads,
        bias_gates,
        scale_out,
        shift_out,
    )


MESH = pl.DeviceIdType.MESH
PIXELS = 256
PAD = 32
LANES = 128


def whereabouts():
    place, lane = lax.axis_index("batch"), lax.axis_index("chan")
    return place, lane, place // 2, place % 2, lane // 2, lane % 2


def ranked(depth, rank):
    high, low = depth // 2, depth % 2
    up, odd = rank // 2, rank % 2
    return (
        (1 - odd) * (1 - up) * depth
        + odd * (1 - up) * (1 + low)
        + (1 - odd) * up * (2 - 2 * low + high)
        + odd * up * (3 - 3 * high)
    )


def middle(depth):
    return (depth // 2 + depth % 2) % 2


def inner(depth):
    return 1 + depth % 2


def outer(depth):
    return 3 * (depth // 2)


def onward(depth, rank):
    second = (1 - rank % 2) * (rank // 2)
    return outer(depth) + second * (3 - depth - outer(depth))


def homeward(depth, rank):
    second = (1 - rank % 2) * (rank // 2) * middle(depth)
    return inner(depth) + second * (outer(depth) - inner(depth))


def staggered(step):
    late = ((step + 1) % 2) * ((step + 14) // 15) + step // 15
    return (1 - late) * ((step + 1) // 2) + late * (step // 2 - 1 + step // 15), late


def push(source, target, send_sem, recv_sem, place, lane):
    return pltpu.make_async_remote_copy(
        src_ref=source,
        dst_ref=target,
        send_sem=send_sem,
        recv_sem=recv_sem,
        device_id=(place, lane),
        device_id_type=MESH,
    )


def announce(peers):
    barrier = pltpu.get_barrier_semaphore()
    for place, lane in peers:
        pl.semaphore_signal(barrier, inc=1, device_id=(place, lane), device_id_type=MESH)


def gathered_peers(peers):
    pl.semaphore_wait(pltpu.get_barrier_semaphore(), len(peers))


def greet(peers):
    announce(peers)
    gathered_peers(peers)


def batch_peers():
    place, lane, _, _, _, _ = whereabouts()
    return [((place + step) % 8, lane) for step in range(1, 8)]


def line_peers():
    place, lane, depth, side, _, _ = whereabouts()
    peers = [(ranked(depth, rank) * 2 + side, lane) for rank in range(1, 4)]
    return peers + [(depth * 2 + 1 - side, lane)]


def chan_peers():
    place, lane, _, _, _, _ = whereabouts()
    return [(place, (lane + step) % 4) for step in range(1, 4)]


class Gather:
    def __init__(self, values, recv, cross, line, parts, direct=False):
        self.values, self.recv, self.cross, self.line = values, recv, cross, line
        self.parts, self.direct = parts, direct

    def view(self, block, part):
        return self.values.at[block] if self.parts == 1 else self.values.at[block, part]

    def copy(self, block, part, sem, depth, side):
        lane = lax.axis_index("chan")
        here = self.view(block, part)
        return push(here, here, sem, self.recv.at[block, part], depth * 2 + side, lane)

    def start(self, part=0):
        place, lane, depth, side, _, _ = whereabouts()
        if self.direct:
            self.copy(place, part, self.cross.at[0, part], depth, 1 - side).start()
            for rank in range(1, 4):
                self.copy(
                    place, part, self.line.at[0, rank, part], ranked(depth, rank), side
                ).start()
            return
        self.copy(place, part, self.line.at[0, 0, part], inner(depth), side).start()

        @pl.when(middle(depth) == 1)
        def _():
            self.copy(place, part, self.line.at[1, 0, part], outer(depth), side).start()

        self.copy(place, part, self.cross.at[0, part], depth, 1 - side).start()

    def near(self, rank, part=0):
        place, lane, depth, side, _, _ = whereabouts()
        block = ranked(depth, rank) * 2 + side
        self.copy(block, part, self.cross.at[rank, part], depth, side).wait_recv()

        if not self.direct:

            @pl.when(middle(depth) == 1)
            def _():
                self.copy(
                    block, part, self.line.at[0, rank, part], onward(depth, rank), side
                ).start()

        self.copy(block, part, self.cross.at[rank, part], depth, 1 - side).start()

    def far(self, rank, part=0):
        place, lane, depth, side, _, _ = whereabouts()
        block = ranked(depth, rank) * 2 + 1 - side
        self.copy(block, part, self.cross.at[rank, part], depth, side).wait_recv()

    def next(self, step):
        place, lane, depth, side, _, _ = whereabouts()
        item, late = staggered(step)
        part, rank = item // 4, item % 4

        @pl.when((late == 0) & (rank > 0))
        def _():
            self.near(rank, part)

        @pl.when(late == 1)
        def _():
            self.far(rank, part)

        return ranked(depth, rank) * 2 + (side + late) % 2, part

    def close(self):
        place, lane, depth, side, _, _ = whereabouts()
        for part in range(self.parts):
            for rank in range(4):
                self.copy(place, part, self.cross.at[rank, part], depth, side).wait_send()
            if self.direct:
                for rank in range(1, 4):
                    self.copy(place, part, self.line.at[0, rank, part], depth, side).wait_send()
                continue
            self.copy(place, part, self.line.at[0, 0, part], depth, side).wait_send()

            @pl.when(middle(depth) == 1)
            def _():
                self.copy(place, part, self.line.at[1, 0, part], depth, side).wait_send()
                for rank in range(1, 4):
                    self.copy(place, part, self.line.at[0, rank, part], depth, side).wait_send()


def gather_sems(parts):
    return [
        pltpu.SemaphoreType.DMA((8, parts)),
        pltpu.SemaphoreType.DMA((4, parts)),
        pltpu.SemaphoreType.DMA((2, 4, parts)),
    ]


def clear_edges(turned):
    edge = jnp.zeros((3, PAD, turned.shape[2]), turned.dtype)
    turned[:, 0:PAD] = edge
    turned[:, PAD + PIXELS :] = edge


def fill_columns(value, mask, turned, columns, row=0, flip=False):
    width = value.shape[1]
    lanes = slice(0, width)
    wide = value.astype(jnp.float32)
    inside = slice(PAD, PAD + PIXELS)
    turned[0, inside, lanes] = pltpu.roll(wide, 1, 0).astype(jnp.bfloat16)
    turned[1, inside, lanes] = value
    turned[2, inside, lanes] = pltpu.roll(wide, PIXELS - 1, 0).astype(jnp.bfloat16)
    for number, (vertical, lateral) in enumerate(OFFSETS):
        start = PAD + 32 * vertical
        slot = 8 - number if flip else number
        columns[row : row + PIXELS, slot * width : (slot + 1) * width] = (
            turned[lateral + 1, start : start + PIXELS, lanes] * mask[:, number : number + 1]
        )


def vmem(count):
    return [pl.BlockSpec(memory_space=pltpu.VMEM)] * count


def kernel_params(number):
    return pltpu.CompilerParams(
        collective_id=number, has_side_effects=True, vmem_limit_bytes=60 * 2**20
    )


class Exchange:
    def __init__(self, values, send, recv, axis):
        self.values, self.send, self.recv, self.axis = values, send, recv, axis

    def steps(self):
        place, lane, _, _, _, _ = whereabouts()
        if self.axis == "batch":
            return [(step - 1, (place + step) % 8, lane, (place + step) % 8) for step in range(1, 8)]
        return [(step - 1, place, (lane + step) % 4, (lane + step) % 4) for step in range(1, 4)]

    def mine(self):
        place, lane, _, _, _, _ = whereabouts()
        return place if self.axis == "batch" else lane

    def start(self):
        here = self.values.at[self.mine()]
        for number, place, lane, _ in self.steps():
            push(here, here, self.send.at[number], self.recv.at[self.mine()], place, lane).start()

    def wait(self):
        for number, place, lane, slot in self.steps():
            there = self.values.at[slot]
            push(there, there, self.send.at[number], self.recv.at[slot], place, lane).wait_recv()

    def close(self):
        here = self.values.at[self.mine()]
        for number, place, lane, _ in self.steps():
            push(here, here, self.send.at[number], self.recv.at[self.mine()], place, lane).wait_send()

    def total(self):
        result = self.values[0]
        for slot in range(1, self.values.shape[0]):
            result = result + self.values[slot]
        return result


class Pieces:
    def __init__(self, stage, got, send, recv):
        self.stage, self.got, self.send, self.recv = stage, got, send, recv

    def start(self, part):
        place, lane, _, _, _, _ = whereabouts()
        for slot in range(4):
            self.stage[slot] = part[:, slot * LANES : (slot + 1) * LANES].astype(jnp.bfloat16)
        for step in (2, 1, 3):
            slot = (lane + step) % 4
            push(
                self.stage.at[slot],
                self.got.at[lane],
                self.send.at[slot],
                self.recv.at[lane],
                place,
                slot,
            ).start()

    def finish(self):
        place, lane, _, _, _, _ = whereabouts()
        self.got[lane] = self.stage[lane]
        for step in range(1, 4):
            slot = (lane + step) % 4
            push(
                self.stage.at[slot],
                self.got.at[slot],
                self.send.at[slot],
                self.recv.at[slot],
                place,
                lane,
            ).wait()
        result = self.got[0].astype(jnp.float32)
        for slot in range(1, 4):
            result = result + self.got[slot].astype(jnp.float32)
        return result


class Local:
    def __init__(self, pairs, sems):
        self.copies = [
            pltpu.make_async_copy(source, target, sems.at[number])
            for number, (source, target) in enumerate(pairs)
        ]

    def start(self, *numbers):
        for number in numbers:
            self.copies[number].start()

    def wait(self, *numbers):
        for number in numbers:
            self.copies[number].wait()


def anywhere(count):
    return [pl.BlockSpec(memory_space=pl.ANY)] * count


def micro_rows(micro):
    return slice(micro * PIXELS, (micro + 1) * PIXELS)


def moments(value, other):
    rows = []
    for micro in range(2):
        part = value[micro_rows(micro)]
        rows.append(jnp.sum(part, axis=0, keepdims=True))
        rows.append(jnp.sum(part * other[micro_rows(micro)], axis=0, keepdims=True))
    return rows


def tile_rows(rows, height):
    width = rows[0].shape[1]
    return jnp.concatenate(rows + [jnp.zeros((height - len(rows), width), jnp.float32)], axis=0)


def normed_part(value, totals, micro, count):
    center = totals[2 * micro : 2 * micro + 1] / count
    inverse = lax.rsqrt(totals[2 * micro + 1 : 2 * micro + 2] / count - center * center + EPSILON)
    return (value[micro_rows(micro)] - center) * inverse, inverse


def dot_last(first, second):
    return lax.dot_general(
        first, second, (((1,), (1,)), ((), ())), preferred_element_type=jnp.float32
    )


def make_masks(ids_ref, mask_all):
    rows = 8 * ids_ref.shape[0]
    ids = ids_ref[...].reshape(rows, PIXELS).T
    pixel = lax.broadcasted_iota(jnp.int32, (PIXELS, rows), 0)
    taps = []
    for vertical, lateral in OFFSETS:
        offset = 32 * vertical + lateral
        beside = ids if offset == 0 else pltpu.roll(ids, (-offset) % PIXELS, 0)
        row, col = (pixel >> 5) + vertical, (pixel & 31) + lateral
        inside = (row >= 0) & (row < 8) & (col >= 0) & (col < 32)
        taps.append(jnp.where(inside & (beside == ids), 1.0, 0.0).astype(jnp.bfloat16))
    taps = jnp.concatenate(taps + [jnp.zeros_like(taps[0])], axis=1)
    item = lax.broadcasted_iota(jnp.int32, (10 * rows, LANES), 0)
    lane = lax.broadcasted_iota(jnp.int32, (10 * rows, LANES), 1)
    for block in range(8):
        for micro in range(2):
            chosen = jnp.where(item == lane * rows + (8 * block + micro), 1.0, 0.0)
            mask_all[block, micro] = jnp.dot(
                taps, chosen.astype(jnp.bfloat16), preferred_element_type=jnp.float32
            ).astype(jnp.bfloat16)


def front_kernel(
    count,
    x_ref,
    ids_ref,
    reduce_ref,
    spatial_ref,
    expand_ref,
    block_scale,
    block_shift,
    output_scale,
    output_shift,
    head_scale,
    head_shift,
    depth_cot,
    segment_cot,
    y_ref,
    norm3_ref,
    inverse3_ref,
    norm12_ref,
    inverse12_ref,
    mine_ref,
    mask_ref,
    act1_out,
    act2_out,
    reduce_out,
    spatial_out,
    expand_out,
    mask_out,
    cot_out,
    raw_out,
    act1_ref,
    act2_ref,
    reduce_all,
    spatial_all,
    expand_all,
    mask_all,
    cot_all,
    packed,
    turned,
    columns,
    stage,
    got,
    sums1,
    sums2,
    sums3,
    head_all,
    ids_all,
    raw1,
    raw2,
    fits1,
    fits2,
    *sems,
):
    place, lane, depth, side, upper, core = whereabouts()
    reduces = Gather(reduce_all, *sems[0:3], 1, True)
    spatials = Gather(spatial_all, *sems[3:6], 1)
    expands = Gather(expand_all, *sems[6:9], 1)
    ids = Exchange(ids_all, sems[9], sems[10], "batch")
    pieces = Pieces(stage, got, sems[11], sems[12])
    first_sums = Exchange(sums1, sems[13], sems[14], "batch")
    second_sums = Exchange(sums2, sems[15], sems[16], "batch")
    third_sums = Exchange(sums3, sems[17], sems[18], "batch")
    heads = Exchange(head_all, sems[19], sems[20], "chan")
    first_raw = Exchange(raw1, sems[21], sems[22], "chan")
    second_raw = Exchange(raw2, sems[23], sems[24], "chan")
    first_fits = Exchange(fits1, sems[28], sems[29], "chan")
    second_fits = Exchange(fits2, sems[30], sems[31], "chan")

    def centered(value, raw):
        rows = moments(value, value)
        for micro in range(2):
            raw[lane, micro_rows(micro)] = (
                value[micro_rows(micro)] - rows[2 * micro] / PIXELS
            ).astype(jnp.bfloat16)
        return rows

    def fit(value, rows, totals, layer, fits):
        inverses, offsets, lines = [], [], []
        for micro in range(2):
            normed, inverse = normed_part(value, totals, micro, count)
            norm12_ref[layer, micro_rows(micro)] = normed
            inverses.append(inverse)
            slope = inverse * block_scale[layer : layer + 1]
            center = totals[2 * micro : 2 * micro + 1] / count
            offset = rows[2 * micro] / PIXELS - center
            offsets.append(offset * inverse)
            lines.append(slope)
            lines.append(offset * slope + block_shift[layer : layer + 1])
        fits[lane] = tile_rows(lines, 8)
        return inverses, offsets

    def activate(raw, fits, act):
        for slot in range(4):
            for micro in range(2):
                out = (
                    raw[slot, micro_rows(micro)].astype(jnp.float32)
                    * fits[slot, 2 * micro : 2 * micro + 1]
                    + fits[slot, 2 * micro + 1 : 2 * micro + 2]
                )
                act[slot, micro_rows(micro)] = (out * jax.nn.sigmoid(out)).astype(jnp.bfloat16)


    local = Local(
        (
            (act1_ref, act1_out),
            (act2_ref, act2_out),
            (reduce_all, reduce_out),
            (spatial_all, spatial_out),
            (expand_all, expand_out),
            (mask_all, mask_out),
            (cot_all, cot_out),
            (raw1, raw_out),
        ),
        sems[27],
    )
    cot_sem, cot_recv = sems[25:27]

    def cot_copy(parity, slot, target):
        return push(
            packed.at[parity], cot_all.at[slot], cot_sem.at[parity], cot_recv.at[slot], target, lane
        )

    announce(batch_peers() + chan_peers())
    reduce_all[place] = reduce_ref[...]
    ids_all[place] = jnp.zeros((8, PIXELS), jnp.float32)
    for micro in range(2):
        for row in range(8):
            ids_all[place, micro : micro + 1, row * 32 : (row + 1) * 32] = ids_ref[
                micro, row : row + 1
            ].astype(jnp.float32)
    spatial_all[place] = spatial_ref[...]
    expand_all[place] = expand_ref[...]
    head_all[lane, 0:4] = head_scale[...]
    head_all[lane, 4:8] = head_shift[...]
    clear_edges(turned)
    gathered_peers(batch_peers() + chan_peers())
    reduces.start()
    ids.start()
    heads.start()
    for rank in range(1, 4):
        reduces.near(rank)
    spatials.start()
    for rank in range(4):
        reduces.far(rank)
    x = x_ref[...].reshape(2 * PIXELS, x_ref.shape[2])
    pieces.start(dot_last(x, reduce_all[...].reshape(512, 512)))
    ids.wait()
    make_masks(ids_all, mask_all)
    mask_ref[...] = mask_all[place]
    local.start(2, 5)
    spatials.near(1)
    first = pieces.finish()
    first_rows = centered(first, raw1)
    sums1[place] = tile_rows(first_rows, 8)
    first_sums.start()
    first_raw.start()
    spatials.near(2)
    expands.start()
    spatials.near(3)
    half_width = LANES // 2
    left = lax.broadcasted_iota(jnp.int32, (PIXELS, LANES), 1) < half_width
    for micro in range(2):
        upper_cot, lower_cot = (ref[micro].astype(jnp.float32) for ref in (depth_cot, segment_cot))
        packed[0, micro] = jnp.where(left, upper_cot, pltpu.roll(lower_cot, half_width, 1)).astype(
            jnp.bfloat16
        )
        packed[1, micro] = jnp.where(left, pltpu.roll(upper_cot, half_width, 1), lower_cot).astype(
            jnp.bfloat16
        )
    first_sums.wait()
    rows, offsets = fit(first, first_rows, first_sums.total(), 0, fits1)
    first_fits.start()
    expands.near(1)
    for rank in range(4):
        spatials.far(rank)
    expands.near(2)
    first_raw.wait()
    first_fits.wait()
    activate(raw1, fits1, act1_ref)
    local.start(0, 3, 7)
    for micro in range(2):
        value = jnp.concatenate([act1_ref[slot, micro_rows(micro)] for slot in range(4)], axis=1)
        fill_columns(value, mask_all[place, micro], turned, columns, micro * PIXELS)
    second = jnp.zeros((2 * PIXELS, LANES), jnp.float32)
    for number in range(9):
        second = second + jnp.dot(
            columns[:, number * 512 : (number + 1) * 512],
            spatial_all[:, number].reshape(512, LANES),
            preferred_element_type=jnp.float32,
        )
    second_rows = centered(second, raw2)
    sums2[place] = tile_rows(second_rows, 8)
    second_sums.start()
    second_raw.start()
    expands.near(3)
    for parity in range(2):
        target = 2 * lane + parity

        @pl.when(target == place)
        def _():
            cot_all[place] = packed[parity]

        @pl.when(target != place)
        def _():
            cot_copy(parity, place, target).start()

    second_sums.wait()
    rows = rows + fit(second, second_rows, second_sums.total(), 1, fits2)[0] + offsets
    second_fits.start()
    inverse12_ref[...] = tile_rows(rows, 8)
    heads.wait()
    low = lax.broadcasted_iota(jnp.int32, (1, LANES), 1) < half_width
    source = place // 2
    even = place % 2 == 0
    for kind in range(2):
        upper_row = head_all[source, pl.ds(4 * kind + 2 * upper, 1)]
        lower_row = head_all[source, pl.ds(4 * kind + 2 * upper + 1, 1)]
        mine_ref[kind : kind + 1] = jnp.where(
            even,
            jnp.where(low, upper_row, pltpu.roll(lower_row, half_width, 1)),
            jnp.where(low, pltpu.roll(upper_row, half_width, 1), lower_row),
        )
    for rank in range(4):
        expands.far(rank)
    second_raw.wait()
    second_fits.wait()
    activate(raw2, fits2, act2_ref)
    local.start(1, 4)
    value = jnp.concatenate([act2_ref[slot] for slot in range(4)], axis=1)
    third = jnp.dot(
        value, expand_all[...].reshape(512, 512), preferred_element_type=jnp.float32
    )
    sums3[place] = tile_rows(moments(third, third), 8)
    third_sums.start()
    third_sums.wait()
    totals = third_sums.total()
    rows = []
    for micro in range(2):
        normed, inverse = normed_part(third, totals, micro, count)
        norm3_ref[micro_rows(micro)] = normed
        rows.append(inverse)
        out = normed * output_scale[...] + output_shift[...] + x_ref[micro].astype(jnp.float32)
        y_ref[micro] = (out * jax.nn.sigmoid(out)).astype(jnp.bfloat16)
    inverse3_ref[...] = tile_rows(rows, 8)
    @pl.when(place // 2 == lane)
    def _():
        for step in range(1, 8):
            cot_copy(0, (place + step) % 8, place).wait_recv()

    local.start(6)
    for parity in range(2):
        @pl.when(2 * lane + parity != place)
        def _():
            cot_copy(parity, place, place).wait_send()

    local.wait(0, 1, 2, 3, 4, 5, 6, 7)
    for item in (reduces, spatials, expands, ids, heads, first_raw, second_raw):
        item.close()
    for item in (first_sums, second_sums, third_sums, first_fits, second_fits):
        item.close()


def exchange_sems(size):
    return [pltpu.SemaphoreType.DMA((size - 1,)), pltpu.SemaphoreType.DMA((size,))]


def run_front(count, *arrays):
    f32, bf16 = jnp.float32, jnp.bfloat16
    kept = (
        (4, 2 * PIXELS, LANES),
        (4, 2 * PIXELS, LANES),
        (8, 64, 512),
        (8, 9, 64, LANES),
        (8, 64, 512),
        (8, 2, PIXELS, LANES),
        (8, 2, PIXELS, LANES),
    )
    return pl.pallas_call(
        functools.partial(front_kernel, count),
        name="front",
        out_shape=(
            jax.ShapeDtypeStruct((2, PIXELS, 512), bf16),
            jax.ShapeDtypeStruct((2 * PIXELS, 512), f32),
            jax.ShapeDtypeStruct((8, 512), f32),
            jax.ShapeDtypeStruct((2, 2 * PIXELS, LANES), f32),
            jax.ShapeDtypeStruct((8, LANES), f32),
            jax.ShapeDtypeStruct((2, LANES), f32),
            jax.ShapeDtypeStruct((2, PIXELS, LANES), bf16),
        )
        + tuple(jax.ShapeDtypeStruct(shape, bf16) for shape in kept + (kept[0],)),
        in_specs=vmem(13),
        out_specs=tuple(vmem(7) + anywhere(8)),
        scratch_shapes=[pltpu.VMEM(shape, bf16) for shape in kept]
        + [
            pltpu.VMEM((2, 2, PIXELS, LANES), bf16),
            pltpu.VMEM((3, 2 * PAD + PIXELS, 512), bf16),
            pltpu.VMEM((2 * PIXELS, 9 * 512), bf16),
            pltpu.VMEM((4, 2 * PIXELS, LANES), bf16),
            pltpu.VMEM((4, 2 * PIXELS, LANES), bf16),
            pltpu.VMEM((8, 8, LANES), f32),
            pltpu.VMEM((8, 8, LANES), f32),
            pltpu.VMEM((8, 8, 512), f32),
            pltpu.VMEM((4, 8, LANES), f32),
            pltpu.VMEM((8, 8, PIXELS), f32),
            pltpu.VMEM((4, 2 * PIXELS, LANES), bf16),
            pltpu.VMEM((4, 2 * PIXELS, LANES), bf16),
            pltpu.VMEM((4, 8, LANES), f32),
            pltpu.VMEM((4, 8, LANES), f32),
        ]
        + gather_sems(1) * 3
        + exchange_sems(8)
        + [pltpu.SemaphoreType.DMA((4,))] * 2
        + exchange_sems(8) * 3
        + exchange_sems(4) * 3
        + [
            pltpu.SemaphoreType.DMA((2,)),
            pltpu.SemaphoreType.DMA((8,)),
            pltpu.SemaphoreType.DMA((8,)),
        ]
        + exchange_sems(4) * 2,
        compiler_params=kernel_params(1),
    )(*arrays)


class Scatter:
    def __init__(self, part, far_buf, far_got, near_buf, near_got, sems):
        self.part, self.far_buf, self.far_got = part, far_buf, far_got
        self.near_buf, self.near_got = near_buf, near_got
        self.far_send, self.far_recv, self.near_send, self.near_recv = sems

    def far_copy(self, level, place):
        return push(
            self.far_buf.at[level],
            self.far_got.at[level],
            self.far_send.at[level],
            self.far_recv.at[level],
            place,
            lax.axis_index("chan"),
        )

    def near_copy(self, rank, level, place):
        return push(
            self.near_buf.at[rank - 1],
            self.near_got.at[level],
            self.near_send.at[rank - 1],
            self.near_recv.at[level],
            place,
            lax.axis_index("chan"),
        )

    def start(self):
        place, lane, depth, side, _, _ = whereabouts()
        for rank in (3, 2, 1, 0):
            level = ranked(depth, rank)
            self.far_buf[level] = self.part[level * 2 + 1 - side].astype(jnp.bfloat16)
            self.far_copy(level, depth * 2 + 1 - side).start()

    def middle(self):
        place, lane, depth, side, _, _ = whereabouts()
        for rank in (3, 2, 1):
            level = ranked(depth, rank)
            self.far_copy(level, place).wait_recv()
            self.near_buf[rank - 1] = (
                self.part[level * 2 + side] + self.far_got[level].astype(jnp.float32)
            ).astype(jnp.bfloat16)
            self.near_copy(rank, depth, level * 2 + side).start()

    def finish(self):
        place, lane, depth, side, _, _ = whereabouts()
        self.far_copy(depth, place).wait_recv()
        result = self.part[place] + self.far_got[depth].astype(jnp.float32)
        for level in range(4):
            self.far_copy(level, place).wait_send()
        for rank in (3, 2, 1):
            level = ranked(depth, rank)
            self.near_copy(rank, level, place).wait()
            result = result + self.near_got[level].astype(jnp.float32)
        return result


def scatter_scratch(width):
    return [
        pltpu.VMEM((8, 64, width), jnp.float32),
        pltpu.VMEM((4, 64, width), jnp.bfloat16),
        pltpu.VMEM((4, 64, width), jnp.bfloat16),
        pltpu.VMEM((3, 64, width), jnp.bfloat16),
        pltpu.VMEM((4, 64, width), jnp.bfloat16),
    ]


def scatter_sems():
    return [
        pltpu.SemaphoreType.DMA((4,)),
        pltpu.SemaphoreType.DMA((4,)),
        pltpu.SemaphoreType.DMA((3,)),
        pltpu.SemaphoreType.DMA((4,)),
    ]


def back_part(value, normed, inverse, scale, shift_sum, scale_sum, count):
    return (scale * inverse * (value - (shift_sum + normed * scale_sum) / count)).astype(
        jnp.bfloat16
    )


def rear_kernel(
    count,
    grad_ref,
    x_ref,
    norm3_ref,
    inverse3_ref,
    norm12_ref,
    inverse12_ref,
    mask_ref,
    block_scale,
    block_shift,
    output_scale,
    output_shift,
    head_ref,
    gate_ref,
    block_hbm,
    back_hbm,
    masks_hbm,
    act1_hbm,
    act2_hbm,
    reduce_hbm,
    spatial_hbm,
    expand_hbm,
    raw_hbm,
    features_ref,
    reduce_out,
    spatial_out,
    expand_out,
    block_scale_out,
    block_shift_out,
    head_scale_out,
    head_shift_out,
    gate_out,
    output_scale_out,
    output_shift_out,
    head_out,
    head_grad,
    block_all,
    head_back,
    mask_all,
    act1_ref,
    act2_ref,
    reduce_all,
    spatial_all,
    expand_all,
    raw_ref,
    fits_all,
    turned_wide,
    columns_wide,
    turned,
    columns,
    stage,
    got,
    stage_next,
    got_next,
    sums_a,
    sums_b,
    sums_c,
    head_all,
    act_all,
    back3,
    *rest,
):
    expand_bufs, spatial_bufs, reduce_bufs, sems = rest[0:5], rest[5:10], rest[10:15], rest[15:]
    place, lane, depth, side, upper, core = whereabouts()
    pieces = Pieces(stage, got, sems[0], sems[1])
    first = Exchange(sums_a, sems[2], sems[3], "batch")
    second = Exchange(sums_b, sems[4], sems[5], "batch")
    third = Exchange(sums_c, sems[6], sems[7], "batch")
    heads = Exchange(head_all, sems[8], sems[9], "chan")
    acts = Exchange(act_all, sems[10], sems[11], "chan")
    fits = Exchange(fits_all, sems[27], sems[28], "chan")
    expands = Scatter(*expand_bufs, sems[12:16])
    spatials = Scatter(*spatial_bufs, sems[16:20])
    reduces = Scatter(*reduce_bufs, sems[20:24])
    pieces_next = Pieces(stage_next, got_next, sems[24], sems[25])

    local = Local(
        (
            (expand_hbm, expand_all),
            (act2_hbm, act2_ref),
            (block_hbm, block_all),
            (back_hbm, head_back),
            (masks_hbm, mask_all),
            (spatial_hbm, spatial_all),
            (act1_hbm, act1_ref),
            (reduce_hbm, reduce_all),
            (head_grad, head_out),
            (raw_hbm, raw_ref),
        ),
        sems[26],
    )
    local.start(0, 1, 2, 3, 4, 5, 6, 7, 9)

    def weigh(block):
        for micro in range(2):
            fill_columns(
                block_all[block, micro],
                mask_all[block, micro],
                turned_wide,
                columns_wide,
                micro * PIXELS,
            )
        value = jnp.concatenate(
            [
                jnp.concatenate([head_back[half, micro, block] for half in range(2)], axis=1)
                for micro in range(2)
            ],
            axis=0,
        ).T

        def tap(number, _):
            product = jnp.dot(
                value,
                columns_wide[:, pl.ds(pl.multiple_of(number * 512, 512), 512)],
                preferred_element_type=jnp.float32,
            )
            if block == 0:
                head_grad[number] = product
            else:
                head_grad[number] += product
            return 0

        lax.fori_loop(0, 9, tap, 0)

    announce(batch_peers() + chan_peers())
    clear_edges(turned_wide)
    half_width = LANES // 2
    even = place % 2 == 0
    mine = lax.broadcasted_iota(jnp.int32, (1, LANES), 1) >> 6 == place % 2
    rows = []
    for kind in range(2):
        own = head_ref[kind : kind + 1]
        turned_own = pltpu.roll(own, half_width, 1)
        first_row = jnp.where(mine, jnp.where(even, own, turned_own), 0.0)
        second_row = jnp.where(mine, jnp.where(even, turned_own, own), 0.0)
        for half in range(2):
            for row in (first_row, second_row):
                rows.append(jnp.where(upper == half, row, 0.0))
    head_all[lane] = jnp.concatenate(rows, axis=0)
    clear_edges(turned)
    wide_rows = []
    for micro in range(2):
        normed = norm3_ref[micro_rows(micro)]
        out = normed * output_scale[...] + output_shift[...] + x_ref[micro].astype(jnp.float32)
        value = grad_ref[micro_rows(micro)] * silu_slope(out)
        features_ref[micro] = value
        wide_rows.append(jnp.sum(value, axis=0, keepdims=True))
        wide_rows.append(jnp.sum(value * normed, axis=0, keepdims=True))
    gathered_peers(batch_peers() + chan_peers())
    sums_a[place] = tile_rows(wide_rows, 8)
    first.start()
    heads.start()
    local.wait(0, 1, 2, 3, 4)
    weigh(0)
    first.wait()
    totals = first.total()
    output_scale_out[...] = totals[1:2] + totals[3:4]
    output_shift_out[...] = totals[0:1] + totals[2:3]
    for micro in range(2):
        back3[micro_rows(micro)] = back_part(
            features_ref[micro],
            norm3_ref[micro_rows(micro)],
            inverse3_ref[micro : micro + 1],
            output_scale[...],
            totals[2 * micro : 2 * micro + 1],
            totals[2 * micro + 1 : 2 * micro + 2],
            count,
        )
    pieces.start(dot_last(back3[...], expand_all[...].reshape(512, 512)))
    value = jnp.concatenate([act2_ref[slot] for slot in range(4)], axis=1)
    expands.part[...] = jnp.dot(
        value.T, back3[...], preferred_element_type=jnp.float32
    ).reshape(8, 64, 512)
    expands.start()
    weigh(1)
    weigh(2)
    grad = pieces.finish()
    normed = norm12_ref[1]
    grad = grad * silu_slope(normed * block_scale[1:2] + block_shift[1:2])
    heads.wait()
    sums_b[place, 0:8] = tile_rows(moments(grad, normed), 8)
    sums_b[place, 4:6] = gate_ref[...]
    sums_b[place, 8:16] = jnp.where(place // 2 == lane, heads.total(), 0.0)
    second.start()
    local.wait(5, 6, 7, 9)
    weigh(3)
    expands.middle()
    second.wait()
    totals = second.total()
    head_scale_out[...] = totals[8:12]
    head_shift_out[...] = totals[12:16]
    gate_out[...] = totals[4:6]
    block_scale_out[1:2] = totals[1:2] + totals[3:4]
    block_shift_out[1:2] = totals[0:1] + totals[2:3]
    for micro in range(2):
        value = back_part(
            grad[micro_rows(micro)],
            normed[micro_rows(micro)],
            inverse12_ref[2 + micro : 3 + micro],
            block_scale[1:2],
            totals[2 * micro : 2 * micro + 1],
            totals[2 * micro + 1 : 2 * micro + 2],
            count,
        )
        fill_columns(value, mask_ref[micro], turned, columns, micro * PIXELS, True)
    part = jnp.zeros((2 * PIXELS, 512), jnp.float32)
    for number in range(9):
        part = part + dot_last(
            columns[:, number * LANES : (number + 1) * LANES],
            spatial_all[:, number].reshape(512, LANES),
        )
    pieces_next.start(part)
    value = jnp.concatenate([act1_ref[slot] for slot in range(4)], axis=1)
    spatials.part[...] = jnp.dot(
        value.T, columns[...], preferred_element_type=jnp.float32
    ).reshape(8, 64, 9 * LANES)
    spatials.start()
    weigh(4)
    weigh(5)
    grad = pieces_next.finish()
    normed = norm12_ref[0]
    grad = grad * silu_slope(normed * block_scale[0:1] + block_shift[0:1])
    rows = moments(grad, normed)
    sums_c[place] = tile_rows(rows, 8)
    third.start()
    for micro in range(2):
        act_all[lane, micro_rows(micro)] = (
            grad[micro_rows(micro)] - rows[2 * micro] / PIXELS
        ).astype(jnp.bfloat16)
    acts.start()
    weigh(6)
    spatials.middle()
    expand_out[...] = expands.finish()
    third.wait()
    totals = third.total()
    block_scale_out[0:1] = totals[1:2] + totals[3:4]
    block_shift_out[0:1] = totals[0:1] + totals[2:3]
    lines = []
    for micro in range(2):
        shift_sum = totals[2 * micro : 2 * micro + 1]
        scale_sum = totals[2 * micro + 1 : 2 * micro + 2]
        inverse = inverse12_ref[micro : micro + 1]
        factor = block_scale[0:1] * inverse
        lines.append(factor)
        lines.append(-factor * scale_sum * inverse / count)
        lines.append(
            factor
            * (
                rows[2 * micro] / PIXELS
                - (shift_sum + inverse12_ref[4 + micro : 5 + micro] * scale_sum) / count
            )
        )
    fits_all[lane] = tile_rows(lines, 8)
    fits.start()
    weigh(7)
    local.start(8)
    acts.wait()
    fits.wait()

    def whole(slot):
        parts = []
        for micro in range(2):
            line = [fits_all[slot, 3 * micro + row : 3 * micro + row + 1] for row in range(3)]
            parts.append(
                act_all[slot, micro_rows(micro)].astype(jnp.float32) * line[0]
                + raw_ref[slot, micro_rows(micro)].astype(jnp.float32) * line[1]
                + line[2]
            )
        return jnp.concatenate(parts, axis=0).astype(jnp.bfloat16)

    value = jnp.concatenate([whole(slot) for slot in range(4)], axis=1)
    x = x_ref[...].reshape(2 * PIXELS, 512)
    reduces.part[...] = jnp.dot(value.T, x, preferred_element_type=jnp.float32).reshape(8, 64, 512)
    reduces.start()
    more = jnp.dot(value, reduce_all[...].reshape(512, 512), preferred_element_type=jnp.float32)
    for micro in range(2):
        features_ref[micro] = features_ref[micro] + more[micro_rows(micro)]
    reduces.middle()
    result = spatials.finish()
    for number in range(9):
        spatial_out[number] = result[:, number * LANES : (number + 1) * LANES]
    reduce_out[...] = reduces.finish()
    for item in (first, second, third, heads, acts, fits):
        item.close()
    local.wait(8)


def run_rear(count, *arrays):
    f32, bf16 = jnp.float32, jnp.bfloat16
    return pl.pallas_call(
        functools.partial(rear_kernel, count),
        name="rear",
        out_shape=(
            jax.ShapeDtypeStruct((2, PIXELS, 512), f32),
            jax.ShapeDtypeStruct((64, 512), f32),
            jax.ShapeDtypeStruct((9, 64, LANES), f32),
            jax.ShapeDtypeStruct((64, 512), f32),
            jax.ShapeDtypeStruct((2, LANES), f32),
            jax.ShapeDtypeStruct((2, LANES), f32),
            jax.ShapeDtypeStruct((4, LANES), f32),
            jax.ShapeDtypeStruct((4, LANES), f32),
            jax.ShapeDtypeStruct((2, LANES), f32),
            jax.ShapeDtypeStruct((1, 512), f32),
            jax.ShapeDtypeStruct((1, 512), f32),
            jax.ShapeDtypeStruct((9, 256, 512), f32),
        ),
        in_specs=vmem(13) + anywhere(9),
        out_specs=tuple(vmem(11) + anywhere(1)),
        scratch_shapes=[
            pltpu.VMEM((9, 256, 512), f32),
            pltpu.VMEM((8, 2, PIXELS, 512), bf16),
            pltpu.VMEM((2, 2, 8, PIXELS, LANES), bf16),
            pltpu.VMEM((8, 2, PIXELS, LANES), bf16),
            pltpu.VMEM((4, 2 * PIXELS, LANES), bf16),
            pltpu.VMEM((4, 2 * PIXELS, LANES), bf16),
            pltpu.VMEM((8, 64, 512), bf16),
            pltpu.VMEM((8, 9, 64, LANES), bf16),
            pltpu.VMEM((8, 64, 512), bf16),
            pltpu.VMEM((4, 2 * PIXELS, LANES), bf16),
            pltpu.VMEM((4, 8, LANES), f32),
            pltpu.VMEM((3, 2 * PAD + PIXELS, 512), bf16),
            pltpu.VMEM((2 * PIXELS, 9 * 512), bf16),
            pltpu.VMEM((3, 2 * PAD + PIXELS, LANES), bf16),
            pltpu.VMEM((2 * PIXELS, 9 * LANES), bf16),
            pltpu.VMEM((4, 2 * PIXELS, LANES), bf16),
            pltpu.VMEM((4, 2 * PIXELS, LANES), bf16),
            pltpu.VMEM((4, 2 * PIXELS, LANES), bf16),
            pltpu.VMEM((4, 2 * PIXELS, LANES), bf16),
            pltpu.VMEM((8, 8, 512), f32),
            pltpu.VMEM((8, 16, LANES), f32),
            pltpu.VMEM((8, 8, LANES), f32),
            pltpu.VMEM((4, 8, LANES), f32),
            pltpu.VMEM((4, 2 * PIXELS, LANES), bf16),
            pltpu.VMEM((2 * PIXELS, 512), bf16),
        ]
        + scatter_scratch(512)
        + scatter_scratch(9 * LANES)
        + scatter_scratch(512)
        + [pltpu.SemaphoreType.DMA((4,))] * 2
        + exchange_sems(8) * 3
        + exchange_sems(4) * 2
        + scatter_sems() * 3
        + [pltpu.SemaphoreType.DMA((4,))] * 2
        + [pltpu.SemaphoreType.DMA((10,))]
        + exchange_sems(4),
        compiler_params=kernel_params(5),
    )(*arrays)


class Reduce:
    def __init__(self, part, keep, far_buf, far_got, line_buf, line_got, sems):
        self.part, self.keep, self.far_buf, self.far_got = part, keep, far_buf, far_got
        self.line_buf, self.line_got = line_buf, line_got
        self.far_send, self.far_recv, self.line_send, self.line_recv = sems

    def block(self, step):
        place, lane, depth, side, _, _ = whereabouts()
        item, late = staggered(step)
        return ranked(depth, 3 - item % 4) * 2 + (side + 1 + late) % 2, item // 4

    def far_copy(self, micro, rank, place):
        return push(
            self.far_buf.at[micro, rank],
            self.far_got.at[micro, rank],
            self.far_send.at[micro, rank],
            self.far_recv.at[micro, rank],
            place,
            lax.axis_index("chan"),
        )

    def line_copy(self, micro, rank, slot, place):
        return push(
            self.line_buf.at[micro, rank],
            self.line_got.at[micro, slot],
            self.line_send.at[micro, rank],
            self.line_recv.at[micro, slot],
            place,
            lax.axis_index("chan"),
        )

    def line_value(self, micro, slot):
        self.line_copy(micro, 0, slot, lax.axis_index("batch")).wait_recv()
        return self.line_got[micro, slot].astype(jnp.float32)

    def step(self, step):
        place, lane, depth, side, _, _ = whereabouts()
        item, late = staggered(step)
        micro, rank = item // 4, 3 - item % 4
        owner = ranked(depth, rank)

        @pl.when(late == 0)
        def _():
            self.far_buf[micro, rank] = self.part[...].astype(jnp.bfloat16)
            self.far_copy(micro, rank, depth * 2 + 1 - side).start()

        @pl.when(late == 1)
        def _():
            self.far_copy(micro, rank, place).wait_recv()
            self.keep[micro] = self.part[...] + self.far_got[micro, rank].astype(jnp.float32)

            @pl.when((middle(depth) == 1) & (rank > 0))
            def _():
                self.keep[micro] = self.keep[micro] + self.line_value(micro, owner)

            @pl.when(rank > 0)
            def _():
                first = (rank % 2) * (1 - rank // 2) * (1 - middle(depth))
                slot = owner + first * (4 - owner)
                self.line_buf[micro, rank - 1] = self.keep[micro].astype(jnp.bfloat16)
                self.line_copy(
                    micro, rank - 1, slot, homeward(depth, rank) * 2 + side
                ).start()

    def close(self, micro):
        place, lane, depth, side, _, _ = whereabouts()
        self.keep[micro] = self.keep[micro] + self.line_value(micro, depth)

        @pl.when(middle(depth) == 1)
        def _():
            self.keep[micro] = self.keep[micro] + self.line_value(micro, 4)

        for rank in range(4):
            self.far_copy(micro, rank, place).wait_send()
        for rank in range(3):
            self.line_copy(micro, rank, 0, place).wait_send()


class Channels:
    def __init__(self, stage, got, stage_sem, got_sem, values, out_sem, in_sem):
        self.stage, self.got, self.stage_sem, self.got_sem = stage, got, stage_sem, got_sem
        self.values, self.out_sem, self.in_sem = values, out_sem, in_sem

    def piece(self, slot, target, block, lane):
        return push(
            self.stage.at[slot, block],
            self.got.at[lane, block],
            self.stage_sem.at[slot, block],
            self.got_sem.at[lane, block],
            lax.axis_index("batch"),
            target,
        )

    def send(self, part, block, micro):
        _, lane, _, _, upper, core = whereabouts()
        for half in range(2):
            piece = part[:, half * LANES : (half + 1) * LANES]
            target = half * 2 + micro

            @pl.when(target == lane)
            def _():
                self.got[lane, block] = piece

            @pl.when(target != lane)
            def _():
                self.stage[target, block] = piece
                self.piece(target, target, block, lane).start()

    def collect(self, micro, take):
        _, lane, _, _, _, core = whereabouts()

        @pl.when(core == micro)
        def _():
            def body(block, _):
                for step in range(1, 4):
                    other = (lane + step) % 4
                    self.piece(other, other, block, other).wait_recv()
                take(block)
                return 0

            lax.fori_loop(0, 8, body, 0)

    def value(self, block):
        result = self.got[0, block].astype(jnp.float32)
        for other in range(1, 4):
            result = result + self.got[other, block].astype(jnp.float32)
        return result

    def sent(self):
        _, lane, _, _, _, _ = whereabouts()

        def body(block, _):
            for step in range(1, 4):
                other = (lane + step) % 4
                self.piece(other, other, block, lane).wait_send()
            return 0

        lax.fori_loop(0, 8, body, 0)

    def chunk(self, path, half, micro, chunk, place_lane):
        here = self.values.at[half, micro, pl.ds(2 * chunk, 2)]
        return push(
            here,
            here,
            self.out_sem.at[path, chunk],
            self.in_sem.at[half, micro, chunk],
            lax.axis_index("batch"),
            place_lane,
        )

    def spread(self, chunk):
        _, lane, _, _, upper, core = whereabouts()
        self.chunk(0, upper, core, chunk, 2 - 2 * upper + core).start()
        self.chunk(1, upper, core, chunk, upper * 2 + 1 - core).start()

    def relay(self, micro):
        _, lane, _, _, upper, core = whereabouts()

        @pl.when(core == micro)
        def _():
            for chunk in range(4):
                copy = self.chunk(2, 1 - upper, core, chunk, upper * 2 + 1 - core)
                copy.wait_recv()
                copy.start()

    def finish(self, micro):
        _, lane, _, _, upper, core = whereabouts()

        @pl.when(core != micro)
        def _():
            for chunk in range(4):
                for half in range(2):
                    self.chunk(0, half, micro, chunk, lane).wait_recv()

    def close(self):
        _, lane, _, _, upper, core = whereabouts()
        for chunk in range(4):
            for path in range(3):
                self.chunk(path, upper, core, chunk, lane).wait_send()


def middle_kernel(
    count,
    block_ref,
    bias_ref,
    mine_ref,
    head_hbm,
    distil_hbm,
    mask_hbm,
    depth_hbm,
    segment_hbm,
    cot_hbm,
    depth_out,
    segment_out,
    distil_grad,
    gate_sums,
    head_sums,
    back_out,
    block_hbm,
    back_hbm,
    block_all,
    head_back,
    head_ref,
    distil_ref,
    mask_ref,
    depth_cot,
    segment_cot,
    cot_all,
    head_weight,
    mixed,
    mixed_back,
    turned,
    columns,
    acts,
    norm_ref,
    slope_ref,
    grads_all,
    own_stage,
    own_got,
    stage,
    got,
    part_ref,
    keep,
    far_buf,
    far_got,
    line_buf,
    line_got,
    stats,
    *sems,
):
    place, lane, depth, side, upper, core = whereabouts()
    half_width = LANES // 2
    source = place // 2 == lane
    low = lax.broadcasted_iota(jnp.int32, (PIXELS, LANES), 1) < half_width
    gather = Gather(block_all, *sems[0:3], 2)
    gather_back = Gather(grads_all, *sems[3:6], 2)
    reduce = Reduce(part_ref, keep, far_buf, far_got, line_buf, line_got, sems[6:10])
    ahead = Channels(stage, got, sems[10], sems[11], acts, sems[12], sems[13])
    behind = Channels(stage, got, sems[10], sems[11], head_back, sems[14], sems[15])
    own_sem, own_recv = sems[16:18]
    local = Local(
        (
            (head_hbm, head_ref),
            (mask_hbm, mask_ref),
            (distil_hbm, distil_ref),
            (depth_hbm, depth_cot),
            (segment_hbm, segment_cot),
            (cot_hbm, cot_all),
            (block_all, block_hbm),
            (head_back, back_hbm),
        ),
        sems[18],
    )
    local.start(0, 1, 2, 3, 4, 5)

    greet(batch_peers() + chan_peers())
    block_all[place] = block_ref[...]
    gather.start(0)
    clear_edges(turned)
    local.wait(0)
    for number in range(9):
        head_weight[number * 512 : (number + 1) * 512] = head_ref[number].T
    local.wait(1)

    def forward_step(step, _):
        block, micro = gather.next(step)
        fill_columns(block_all[block, micro], mask_ref[block, micro], turned, columns)
        part = jnp.dot(columns[0:PIXELS], head_weight[...], preferred_element_type=jnp.float32)
        ahead.send(part.astype(jnp.bfloat16), block, micro)

        @pl.when(step == 0)
        def _():
            local.wait(2)
            prepare_mixed()

        @pl.when(step == 1)
        def _():
            gather.start(1)

        @pl.when(step == 4)
        def _():
            for number in range(9):
                mixed_back[number * 512 : (number + 1) * 512] = mixed[
                    number * 256 : (number + 1) * 256
                ].T

        @pl.when(step == 10)
        def _():
            normalize(0)

        @pl.when(step == 13)
        def _():
            ahead.relay(0)

        return 0

    def prepare_mixed():
        width = half_width
        for number in range(9):
            for stream in range(2):
                for head in range(4):
                    index = head - SOURCE_START[stream]
                    rows = slice(number * 256 + head * width, number * 256 + (head + 1) * width)
                    left = slice(2 * stream * LANES, (2 * stream + 1) * LANES)
                    right = slice((2 * stream + 1) * LANES, (2 * stream + 2) * LANES)
                    nothing = jnp.zeros((width, LANES), jnp.bfloat16)
                    mixed[rows, left] = (
                        distil_ref[stream, number, 0] if head == OWN_HEAD[stream] else nothing
                    )
                    mixed[rows, right] = (
                        distil_ref[stream, number, 1 + index] if 0 <= index < 3 else nothing
                    )

    def normalize(micro):
        zero = jnp.zeros((1, LANES), jnp.float32)

        @pl.when(core == micro)
        def _():
            stats[0:2] = jnp.zeros((2, LANES), jnp.float32)

        def take(block):
            value = ahead.value(block)
            norm_ref[block] = value
            stats[0:1] += jnp.sum(value, axis=0, keepdims=True)
            stats[1:2] += jnp.sum(value * value, axis=0, keepdims=True)

        ahead.collect(micro, take)

        @pl.when(core == micro)
        def _():
            center = stats[0:1] / count
            inverse = lax.rsqrt(stats[1:2] / count - center * center + EPSILON)
            stats[2:3] = inverse

            def activate(chunk, _):
                for item in range(2):
                    block = 2 * chunk + item
                    normed = (norm_ref[block] - center) * inverse
                    norm_ref[block] = normed
                    out = normed * mine_ref[0:1] + mine_ref[1:2]
                    acts[upper, core, block] = (out * jax.nn.sigmoid(out)).astype(jnp.bfloat16)
                ahead.spread(chunk)
                return 0

            lax.fori_loop(0, 4, activate, 0)

    def own_copy(block, micro, slot, target):
        return push(
            own_stage.at[block, micro],
            own_got.at[slot, micro],
            own_sem.at[block, micro],
            own_recv.at[slot, micro],
            target,
            lane,
        )

    def send_own(micro):
        @pl.when(source)
        def _():
            own_got[place % 2, micro] = jnp.where(
                low, acts[0, micro, place], acts[1, micro, place]
            )

            def pack(step, _):
                block = (place + step) % 8
                own_stage[block, micro] = jnp.where(
                    low, acts[0, micro, block], acts[1, micro, block]
                )
                own_copy(block, micro, place % 2, block).start()
                return 0

            lax.fori_loop(1, 8, pack, 0)

    def act_value(block, micro):
        return jnp.concatenate([acts[half, micro, block] for half in range(2)], axis=1)

    def gate(micro):
        reduce.close(micro)
        for parity in range(2):
            @pl.when(2 * lane + parity != place)
            def _():
                own_copy(0, micro, parity, place).wait_recv()

        for stream, cot_ref in enumerate((depth_cot, segment_cot)):
            first = own_got[0, micro].astype(jnp.float32)
            second = own_got[1, micro].astype(jnp.float32)
            if stream == 0:
                second = pltpu.roll(second, half_width, 1)
            else:
                first = pltpu.roll(first, half_width, 1)
            own = jnp.where(low, first, second)
            column = 2 * stream * LANES
            gates = jax.nn.sigmoid(
                keep[micro, :, column : column + LANES] + bias_ref[stream : stream + 1]
            )
            message = keep[micro, :, column + LANES : column + 2 * LANES]
            cot = cot_ref[micro].astype(jnp.float32)
            out_ref = (depth_out, segment_out)[stream]
            out_ref[micro] = (own + gates * message).astype(jnp.bfloat16)
            gate_grad = (cot * message * gates * (1.0 - gates)).astype(jnp.bfloat16)
            bias_sum = jnp.sum(gate_grad.astype(jnp.float32), axis=0, keepdims=True)
            if micro == 0:
                gate_sums[stream : stream + 1] = bias_sum
            else:
                gate_sums[stream : stream + 1] += bias_sum
            grads_all[place, micro, :, column : column + LANES] = gate_grad
            grads_all[place, micro, :, column + LANES : column + 2 * LANES] = (cot * gates).astype(
                jnp.bfloat16
            )

    def distil_step(step, _):
        block, micro = reduce.block(step)
        fill_columns(act_value(block, micro), mask_ref[block, micro], turned, columns)
        part_ref[...] = jnp.dot(
            columns[0:PIXELS, 0 : 9 * 256], mixed[...], preferred_element_type=jnp.float32
        )
        reduce.step(step)

        @pl.when(step == 2)
        def _():
            normalize(1)

        @pl.when(step == 5)
        def _():
            ahead.relay(1)

        @pl.when(step == 6)
        def _():
            ahead.finish(1)
            ahead.sent()
            send_own(1)

        @pl.when(step == 11)
        def _():
            local.wait(3, 4)
            gate(0)
            gather_back.start(0)

        return 0

    distil_grad[...] = jnp.zeros_like(distil_grad)

    def back_step(step, _):
        block, micro = gather_back.next(step)
        fill_columns(
            grads_all[block, micro], mask_ref[block, micro], turned, columns, flip=True
        )
        part = jnp.dot(columns[0:PIXELS], mixed_back[...], preferred_element_type=jnp.float32)
        extra = cot_all[block, micro].astype(jnp.float32)
        part = jnp.concatenate(
            [
                part[:, :LANES] + jnp.where(low & source, extra, 0.0),
                part[:, LANES:] + jnp.where(low | ~source, 0.0, extra),
            ],
            axis=1,
        )
        behind.send(part.astype(jnp.bfloat16), block, micro)
        @pl.when(step == 10)
        def _():
            normalize_back(0)

        @pl.when(step == 13)
        def _():
            behind.relay(0)

        return 0

    def normalize_back(micro):
        @pl.when(core == micro)
        def _():
            stats[4:6] = jnp.zeros((2, LANES), jnp.float32)

        def take(block):
            normed = norm_ref[block]
            value = behind.value(block) * silu_slope(normed * mine_ref[0:1] + mine_ref[1:2])
            slope_ref[block] = value
            stats[4:5] += jnp.sum(value, axis=0, keepdims=True)
            stats[5:6] += jnp.sum(value * normed, axis=0, keepdims=True)

        behind.collect(micro, take)

        @pl.when(core == micro)
        def _():
            shift_sum, scale_sum = stats[4:5], stats[5:6]
            head_sums[0:1] = scale_sum
            head_sums[1:2] = shift_sum
            factor = mine_ref[0:1] * stats[2:3]

            def activate(chunk, _):
                for item in range(2):
                    block = 2 * chunk + item
                    value = slope_ref[block]
                    head_back[upper, core, block] = (
                        factor * (value - (shift_sum + norm_ref[block] * scale_sum) / count)
                    ).astype(jnp.bfloat16)
                behind.spread(chunk)
                return 0

            lax.fori_loop(0, 4, activate, 0)

    def head_value(block, micro):
        return jnp.concatenate([head_back[half, micro, block] for half in range(2)], axis=1)

    def weigh(block):
        for micro in range(2):
            fill_columns(
                grads_all[block, micro],
                mask_ref[block, micro],
                turned,
                columns,
                micro * PIXELS,
                True,
            )
        value = jnp.concatenate([act_value(block, micro) for micro in range(2)], axis=0).T
        width = half_width
        for number in range(9):
            product = jnp.dot(
                value,
                columns[:, number * 512 : (number + 1) * 512],
                preferred_element_type=jnp.float32,
            )
            for stream in range(2):
                for index in range(4):
                    head = OWN_HEAD[stream] if index == 0 else SOURCE_START[stream] + index - 1
                    column = (2 * stream + (index > 0)) * LANES
                    distil_grad[stream, number, index] += product[
                        head * width : (head + 1) * width, column : column + LANES
                    ]

    def block_step(step, _):
        block, micro = reduce.block(step)
        fill_columns(
            head_value(block, micro), mask_ref[block, micro], turned, columns, flip=True
        )
        part_ref[...] = jnp.dot(
            columns[0:PIXELS, 0 : 9 * 256],
            head_ref[...].reshape(9 * 256, 512),
            preferred_element_type=jnp.float32,
        )
        item, late = staggered(step)

        reduce.step(step)

        @pl.when(late == 1)
        def _():
            weigh(item)

        @pl.when(step == 2)
        def _():
            normalize_back(1)

        @pl.when(step == 5)
        def _():
            behind.relay(1)

        @pl.when(step == 6)
        def _():
            behind.finish(1)

        return 0

    def schedule(turn, _):
        phase, spot = (turn + 2) // 16, (turn + 2) % 16
        seam = (1 - (spot + 12) // 16) * ((phase + 3) // 4)
        odd = spot % 2
        kind = phase - seam * odd
        step = seam * (14 * odd + spot // 2) + (1 - seam) * (spot - 2)

        @pl.when(kind == 0)
        def _():
            forward_step(step, 0)

        @pl.when((kind == 1) & (step == 0))
        def _():
            ahead.finish(0)
            send_own(0)

        @pl.when(kind == 1)
        def _():
            distil_step(step, 0)

        @pl.when((kind == 2) & (step == 0))
        def _():
            local.wait(5)

        @pl.when((kind == 2) & (step == 6))
        def _():
            gate(1)
            gather_back.start(1)
            ahead.close()

        @pl.when(kind == 2)
        def _():
            back_step(step, 0)

        @pl.when((kind == 3) & (step == 0))
        def _():
            behind.finish(0)
            local.start(6)

        @pl.when(kind == 3)
        def _():
            block_step(step, 0)

        return 0

    lax.fori_loop(0, 66, schedule, 0)
    for micro in range(2):
        reduce.close(micro)
        back_out[micro_rows(micro)] = keep[micro]
    behind.sent()
    behind.close()
    gather.close()
    gather_back.close()
    local.start(7)

    @pl.when(source)
    def _():
        for micro in range(2):
            for step in range(1, 8):
                own_copy((place + step) % 8, micro, 0, place).wait_send()

    local.wait(6, 7)


def run_middle(count, *arrays):
    f32, bf16 = jnp.float32, jnp.bfloat16
    block = (PIXELS, 512)
    dma = pltpu.SemaphoreType.DMA
    return pl.pallas_call(
        functools.partial(middle_kernel, count),
        name="middle",
        out_shape=(
            jax.ShapeDtypeStruct((2, PIXELS, LANES), bf16),
            jax.ShapeDtypeStruct((2, PIXELS, LANES), bf16),
            jax.ShapeDtypeStruct((2, 9, 4, 64, LANES), f32),
            jax.ShapeDtypeStruct((2, LANES), f32),
            jax.ShapeDtypeStruct((2, LANES), f32),
            jax.ShapeDtypeStruct((2 * PIXELS, 512), f32),
            jax.ShapeDtypeStruct((8, 2) + block, bf16),
            jax.ShapeDtypeStruct((2, 2, 8, PIXELS, LANES), bf16),
        ),
        in_specs=vmem(3) + anywhere(6),
        out_specs=tuple(vmem(6) + anywhere(2)),
        scratch_shapes=[
            pltpu.VMEM((8, 2) + block, bf16),
            pltpu.VMEM((2, 2, 8, PIXELS, LANES), bf16),
            pltpu.VMEM((9, 256, 512), bf16),
            pltpu.VMEM((2, 9, 4, 64, LANES), bf16),
            pltpu.VMEM((8, 2, PIXELS, LANES), bf16),
            pltpu.VMEM((2, PIXELS, LANES), bf16),
            pltpu.VMEM((2, PIXELS, LANES), bf16),
            pltpu.VMEM((8, 2, PIXELS, LANES), bf16),
            pltpu.VMEM((9 * 512, 256), bf16),
            pltpu.VMEM((9 * 256, 512), bf16),
            pltpu.VMEM((9 * 512, 256), bf16),
            pltpu.VMEM((3, 2 * PAD + PIXELS, 512), bf16),
            pltpu.VMEM((2 * PIXELS, 9 * 512), bf16),
            pltpu.VMEM((2, 2, 8, PIXELS, LANES), bf16),
            pltpu.VMEM((8, PIXELS, LANES), f32),
            pltpu.VMEM((8, PIXELS, LANES), f32),
            pltpu.VMEM((8, 2) + block, bf16),
            pltpu.VMEM((8, 2, PIXELS, LANES), bf16),
            pltpu.VMEM((2, 2, PIXELS, LANES), bf16),
            pltpu.VMEM((4, 8, PIXELS, LANES), bf16),
            pltpu.VMEM((4, 8, PIXELS, LANES), bf16),
            pltpu.VMEM(block, f32),
            pltpu.VMEM((2,) + block, f32),
            pltpu.VMEM((2, 4) + block, bf16),
            pltpu.VMEM((2, 4) + block, bf16),
            pltpu.VMEM((2, 3) + block, bf16),
            pltpu.VMEM((2, 5) + block, bf16),
            pltpu.VMEM((8, LANES), f32),
        ]
        + gather_sems(2) * 2
        + [dma((2, 4)), dma((2, 4)), dma((2, 3)), dma((2, 5))]
        + [dma((4, 8)), dma((4, 8))]
        + [dma((3, 4)), dma((2, 2, 4))] * 2
        + [dma((8, 2)), dma((2, 2)), dma((8,))],
        compiler_params=kernel_params(2),
    )(*arrays)


def finish_kernel(count, *refs):
    sources, targets, held = refs[:count], refs[count : 2 * count], refs[2 * count : 3 * count]
    sem_in, sem_out = refs[3 * count :]

    def parts(ref):
        large = len(ref.shape) > 2
        return [ref.at[number] for number in range(ref.shape[0])] if large else [ref]

    number = 0
    loads, stores = [], []
    for source, target, hold in zip(sources, targets, held):
        for pieces in zip(parts(source), parts(hold), parts(target)):
            loads.append(pltpu.make_async_copy(pieces[0], pieces[1], sem_in.at[number]))
            stores.append(pltpu.make_async_copy(pieces[1], pieces[2], sem_out.at[number]))
            number += 1
    for load in loads:
        load.start()
    for load, store in zip(loads, stores):
        load.wait()
        store.start()
    for store in stores:
        store.wait()


def run_finish(*arrays):
    anywhere = [pl.BlockSpec(memory_space=pltpu.HBM)] * len(arrays)
    copies = sum(item.shape[0] if item.ndim > 2 else 1 for item in arrays)
    return pl.pallas_call(
        functools.partial(finish_kernel, len(arrays)),
        name="finish",
        out_shape=tuple(jax.ShapeDtypeStruct(item.shape, item.dtype) for item in arrays),
        in_specs=anywhere,
        out_specs=tuple(anywhere),
        scratch_shapes=[pltpu.VMEM(item.shape, item.dtype) for item in arrays]
        + [pltpu.SemaphoreType.DMA((copies,))] * 2,
        compiler_params=pltpu.CompilerParams(vmem_limit_bytes=60 * 2**20),
    )(*arrays)


def stationary_local(
    features,
    image_ids,
    reduce_weight,
    spatial_weight,
    expand_weight,
    head_weights,
    distil_weights,
    block_scale,
    block_shift,
    head_scale,
    head_shift,
    gate_bias,
    output_scale,
    output_shift,
    depth_cotangent,
    segment_cotangent,
):
    canvases, row_count, column_count = image_ids.shape
    pixels = row_count * column_count
    count = float(lax.axis_size("batch") * pixels)
    x = features.reshape(canvases, pixels, -1)
    cots = [item.reshape(canvases, pixels, LANES) for item in (depth_cotangent, segment_cotangent)]
    block_params = (block_scale, block_shift)
    output_params = (output_scale[None], output_shift[None])
    (
        block_out,
        norm3,
        inverse3,
        norm12,
        inverse12,
        mine,
        mask,
        act1,
        act2,
        reduce_all,
        spatial_all,
        expand_all,
        mask_all,
        cot_all,
        raw,
    ) = run_front(
        count,
        x,
        image_ids,
        reduce_weight.T,
        spatial_weight,
        expand_weight,
        *block_params,
        *output_params,
        head_scale,
        head_shift,
        *cots,
    )
    depth_out, segment_out, distil_grad, gate_sums, head_sums, block_grad, block_all, back_all = run_middle(
        count,
        block_out,
        gate_bias,
        mine,
        head_weights.transpose(0, 2, 3, 1).reshape(9, -1, head_weights.shape[1]),
        distil_weights,
        mask_all,
        *cots,
        cot_all,
    )
    (
        features_grad,
        reduce_grad,
        spatial_grad,
        expand_grad,
        block_scale_grad,
        block_shift_grad,
        head_scale_grad,
        head_shift_grad,
        gate_grad,
        output_scale_grad,
        output_shift_grad,
        heads_grad,
    ) = run_rear(
        count,
        block_grad,
        x,
        norm3,
        inverse3,
        norm12,
        inverse12,
        mask,
        *block_params,
        *output_params,
        head_sums,
        gate_sums,
        block_all,
        back_all,
        mask_all,
        act1,
        act2,
        reduce_all,
        spatial_all,
        expand_all,
        raw,
    )
    outs = run_finish(
        depth_out,
        segment_out,
        features_grad,
        reduce_grad,
        spatial_grad,
        expand_grad,
        heads_grad,
        distil_grad,
        block_scale_grad,
        block_shift_grad,
        head_scale_grad,
        head_shift_grad,
        gate_grad,
        output_scale_grad,
        output_shift_grad,
    )
    heads_grad = outs[6].reshape(9, 4, -1, head_weights.shape[1]).transpose(0, 3, 1, 2)
    return (
        outs[0].reshape(depth_cotangent.shape),
        outs[1].reshape(depth_cotangent.shape),
        outs[2].reshape(features.shape),
        outs[3].T,
        *outs[4:6],
        heads_grad,
        *outs[7:13],
        outs[13][0],
        outs[14][0],
    )


def solution(mesh):
    fits = dict(mesh.shape) == {"batch": 8, "chan": 4}
    local = stationary_local if fits else gathered_local
    placed = (
        P("batch", None, None, "chan"),
        P("batch", None, None),
        P("chan", "batch"),
        P(None, "batch", "chan"),
        P("batch", "chan"),
        P(None, "chan", None, "batch"),
        P(None, None, None, "batch", "chan"),
        P(None, "chan"),
        P(None, "chan"),
        P(None, "chan"),
        P(None, "chan"),
        P(None, "chan"),
        P("chan"),
        P("chan"),
        P("batch", None, None, "chan"),
        P("batch", None, None, "chan"),
    )
    return jax.shard_map(
        local,
        mesh=mesh,
        in_specs=placed,
        out_specs=(
            P("batch", None, None, "chan"),
            P("batch", None, None, "chan"),
            P("batch", None, None, "chan"),
            P("chan", "batch"),
            P(None, "batch", "chan"),
            P("batch", "chan"),
            P(None, "chan", None, "batch"),
            P(None, None, None, "batch", "chan"),
            P(None, "chan"),
            P(None, "chan"),
            P(None, "chan"),
            P(None, "chan"),
            P(None, "chan"),
            P("chan"),
            P("chan"),
        ),
        check_vma=False,
    )
```

```python
import functools

import jax
import jax.numpy as jnp
from jax import lax
from jax.experimental import pallas as pl
from jax.experimental.pallas import tpu as pltpu
from jax.sharding import PartitionSpec as P

EPSILON = 1e-05
OFFSETS = ((-1, -1), (-1, 0), (-1, 1), (0, -1), (0, 0), (0, 1), (1, -1), (1, 0), (1, 1))
OWN_HEAD = (0, 3)
SOURCE_START = (1, 0)


def silu_slope(values):
    sig = jax.nn.sigmoid(values)
    return sig * (1.0 + values * (1.0 - sig))


def shifted(values, vertical, lateral):
    row_count, column_count = (values.shape[1], values.shape[2])
    widths = [(0, 0)] * values.ndim
    widths[1] = (1, 1)
    widths[2] = (1, 1)
    padded = jnp.pad(values, widths)
    return padded[
        :, 1 + vertical : 1 + vertical + row_count, 1 + lateral : 1 + lateral + column_count
    ]


def tap_masks(image_ids):
    row_count, column_count = (image_ids.shape[1], image_ids.shape[2])
    padded = jnp.pad(image_ids, ((0, 0), (1, 1), (1, 1)), constant_values=-1)
    masks = []
    for vertical, lateral in OFFSETS:
        beside = padded[
            :, 1 + vertical : 1 + vertical + row_count, 1 + lateral : 1 + lateral + column_count
        ]
        masks.append((beside == image_ids).astype(jnp.float32))
    return jnp.stack(masks)


def conv_forward(inputs, weight, masks):
    total = 0.0
    for number, (vertical, lateral) in enumerate(OFFSETS):
        moved = shifted(inputs, vertical, lateral) * masks[number][..., None].astype(inputs.dtype)
        total = total + jnp.einsum(
            "nhwc,co->nhwo", moved, weight[number], preferred_element_type=jnp.float32
        )
    return total


def conv_input_grad(grads, weight, masks):
    total = 0.0
    for number, (vertical, lateral) in enumerate(OFFSETS):
        term = jnp.einsum(
            "nhwo,co->nhwc", grads, weight[number], preferred_element_type=jnp.float32
        )
        total = total + shifted(term * masks[number][..., None], -vertical, -lateral)
    return total


def conv_weight_grad(inputs, grads, masks):
    pieces = []
    for number, (vertical, lateral) in enumerate(OFFSETS):
        moved = shifted(inputs, vertical, lateral) * masks[number][..., None].astype(inputs.dtype)
        pieces.append(jnp.einsum("nhwc,nhwo->co", moved, grads, preferred_element_type=jnp.float32))
    return jnp.stack(pieces)


def pixel_sum(values):
    return jnp.sum(values, axis=(0, 1, 2))


def normalize(values, scale, shift, count):
    total, squares = lax.psum((pixel_sum(values), pixel_sum(values * values)), "batch")
    center = total / count
    inverse = lax.rsqrt(squares / count - center * center + EPSILON)
    normed = (values - center) * inverse
    return (normed, inverse, normed * scale + shift)


def grad_sums(first_sum, second_sum):
    return lax.psum((first_sum, second_sum), "batch")


def normalize_back(grads, normed, inverse, scale, shift_sum, scale_sum, count):
    return scale * inverse * (grads - (shift_sum + normed * scale_sum) / count)


def channel_gather(values):
    return lax.all_gather(values, "chan", axis=4, tiled=True)


def channel_sum(values):
    return lax.psum_scatter(
        values.astype(jnp.bfloat16), "chan", scatter_dimension=4, tiled=True
    ).astype(jnp.float32)


def fetch_weights(reduce_weight, spatial_weight, expand_weight, head_weights, distil_weights):
    return (
        lax.all_gather(reduce_weight, "batch", axis=1, tiled=True),
        lax.all_gather(spatial_weight, "batch", axis=1, tiled=True),
        lax.all_gather(expand_weight, "batch", axis=0, tiled=True),
        lax.all_gather(head_weights, "batch", axis=3, tiled=True),
        lax.all_gather(distil_weights, "batch", axis=3, tiled=True),
    )


def scatter_weights(grads):
    reduce_grad, spatial_grad, expand_grad, heads_grad, distil_grad = grads
    return (
        lax.psum_scatter(reduce_grad, "batch", scatter_dimension=1, tiled=True),
        lax.psum_scatter(spatial_grad, "batch", scatter_dimension=1, tiled=True),
        lax.psum_scatter(expand_grad, "batch", scatter_dimension=0, tiled=True),
        lax.psum_scatter(heads_grad, "batch", scatter_dimension=3, tiled=True),
        lax.psum_scatter(distil_grad, "batch", scatter_dimension=3, tiled=True),
    )


def micro_step(inputs, image_ids, depth_cot, segment_cot, gathered, small, batch_count):
    reduce_full, spatial_full, expand_full, heads_full, distil_full = gathered
    block_scale, block_shift, head_scale, head_shift, gate_bias, output_scale, output_shift = small
    masks = tap_masks(image_ids)
    canvases, row_count, column_count = image_ids.shape
    count = float(batch_count * canvases * row_count * column_count)
    first_partial = jnp.einsum(
        "nhwc,co->nhwo", inputs, reduce_full, preferred_element_type=jnp.float32
    )
    first = channel_sum(first_partial[:, :, :, None, :])
    first_norm, first_inv, first_out = normalize(first, block_scale[0:1], block_shift[0:1], count)
    first_act = jax.nn.silu(first_out).astype(jnp.bfloat16)
    first_full = channel_gather(first_act)[:, :, :, 0, :]
    second = conv_forward(first_full, spatial_full, masks)[:, :, :, None, :]
    second_norm, second_inv, second_out = normalize(
        second, block_scale[1:2], block_shift[1:2], count
    )
    second_act = jax.nn.silu(second_out).astype(jnp.bfloat16)
    second_full = channel_gather(second_act)[:, :, :, 0, :]
    third = jnp.einsum(
        "nhwc,co->nhwo", second_full, expand_full, preferred_element_type=jnp.float32
    )[:, :, :, None, :]
    third_norm, third_inv, third_out = normalize(
        third, output_scale[None], output_shift[None], count
    )
    summed = third_out[:, :, :, 0, :] + inputs.astype(jnp.float32)
    block_out = jax.nn.silu(summed).astype(jnp.bfloat16)
    heads_flat = heads_full.reshape(heads_full.shape[0], heads_full.shape[1], -1)
    head_partial = conv_forward(block_out, heads_flat, masks)
    head_pre = channel_sum(
        head_partial.reshape(head_partial.shape[:3] + (heads_full.shape[2], heads_full.shape[3]))
    )
    head_norm, head_inv, head_out = normalize(head_pre, head_scale, head_shift, count)
    head_act = jax.nn.silu(head_out).astype(jnp.bfloat16)
    head_full = channel_gather(head_act)
    head_width = head_full.shape[4]
    gate_pre = [0.0, 0.0]
    message = [0.0, 0.0]
    for number, (vertical, lateral) in enumerate(OFFSETS):
        moved = shifted(head_full, vertical, lateral) * masks[number][:, :, :, None, None].astype(
            jnp.bfloat16
        )
        for stream in range(2):
            weights_here = distil_full[stream, number]
            first_source = SOURCE_START[stream]
            sources = moved[:, :, :, first_source : first_source + 3].reshape(
                moved.shape[:3] + (3 * head_width,)
            )
            gate_pre[stream] = gate_pre[stream] + jnp.einsum(
                "nhwc,co->nhwo",
                moved[:, :, :, OWN_HEAD[stream]],
                weights_here[0],
                preferred_element_type=jnp.float32,
            )
            message[stream] = message[stream] + jnp.einsum(
                "nhwc,co->nhwo",
                sources,
                weights_here[1:].reshape(3 * head_width, -1),
                preferred_element_type=jnp.float32,
            )
    cotangents = (depth_cot.astype(jnp.float32), segment_cot.astype(jnp.float32))
    outputs, message_grads, gate_grads = ([], [], [])
    for stream in range(2):
        gate_value = jax.nn.sigmoid(gate_pre[stream] + gate_bias[stream])
        own_feature = head_act[:, :, :, OWN_HEAD[stream]].astype(jnp.float32)
        outputs.append((own_feature + gate_value * message[stream]).astype(jnp.bfloat16))
        message_grads.append((cotangents[stream] * gate_value).astype(jnp.bfloat16))
        gate_grads.append(
            (cotangents[stream] * message[stream] * gate_value * (1.0 - gate_value)).astype(
                jnp.bfloat16
            )
        )
    spread_grad = 0.0
    distil_parts = [[], []]
    for number, (vertical, lateral) in enumerate(OFFSETS):
        tap_mask = masks[number][:, :, :, None, None]
        moved = shifted(head_full, vertical, lateral) * tap_mask.astype(jnp.bfloat16)
        tap_grad = jnp.zeros(head_full.shape, jnp.float32)
        for stream in range(2):
            weights_here = distil_full[stream, number]
            first_source = SOURCE_START[stream]
            sources = moved[:, :, :, first_source : first_source + 3].reshape(
                moved.shape[:3] + (3 * head_width,)
            )
            own_grad = jnp.einsum(
                "nhwo,co->nhwc",
                gate_grads[stream],
                weights_here[0],
                preferred_element_type=jnp.float32,
            )
            source_grad = jnp.einsum(
                "nhwo,co->nhwc",
                message_grads[stream],
                weights_here[1:].reshape(3 * head_width, -1),
                preferred_element_type=jnp.float32,
            )
            tap_grad = tap_grad.at[:, :, :, OWN_HEAD[stream]].add(own_grad)
            tap_grad = tap_grad.at[:, :, :, first_source : first_source + 3].add(
                source_grad.reshape(source_grad.shape[:3] + (3, head_width))
            )
            gate_weight_grad = jnp.einsum(
                "nhwc,nhwo->co",
                moved[:, :, :, OWN_HEAD[stream]],
                gate_grads[stream],
                preferred_element_type=jnp.float32,
            )
            source_weight_grad = jnp.einsum(
                "nhwc,nhwo->co", sources, message_grads[stream], preferred_element_type=jnp.float32
            )
            distil_parts[stream].append(
                jnp.concatenate(
                    [gate_weight_grad[None], source_weight_grad.reshape(3, head_width, -1)], axis=0
                )
            )
        spread_grad = spread_grad + shifted(tap_grad * tap_mask, -vertical, -lateral)
    distil_grad = jnp.stack([jnp.stack(distil_parts[0]), jnp.stack(distil_parts[1])])
    head_grad = channel_sum(spread_grad)
    head_grad = (
        head_grad.at[:, :, :, OWN_HEAD[0]]
        .add(cotangents[0])
        .at[:, :, :, OWN_HEAD[1]]
        .add(cotangents[1])
    )
    head_grad = head_grad * silu_slope(head_out)
    gate_sums = jnp.stack(
        [pixel_sum(gate_grads[0].astype(jnp.float32)), pixel_sum(gate_grads[1].astype(jnp.float32))]
    )
    shift_sums, scale_sums = grad_sums(
        jnp.concatenate([pixel_sum(head_grad), gate_sums], axis=0), pixel_sum(head_grad * head_norm)
    )
    head_pre_grad = normalize_back(
        head_grad, head_norm, head_inv, head_scale, shift_sums[:4], scale_sums, count
    ).astype(jnp.bfloat16)
    head_pre_full = channel_gather(head_pre_grad)
    head_flat_grad = head_pre_full.reshape(head_pre_full.shape[:3] + (-1,))
    block_grad = conv_input_grad(head_flat_grad, heads_flat, masks)
    heads_grad = conv_weight_grad(block_out, head_flat_grad, masks).reshape(heads_full.shape)
    summed_grad = block_grad * silu_slope(summed)
    third_grad = summed_grad[:, :, :, None, :]
    third_shift, third_scale = grad_sums(pixel_sum(third_grad), pixel_sum(third_grad * third_norm))
    third_pre = normalize_back(
        third_grad, third_norm, third_inv, output_scale[None], third_shift, third_scale, count
    ).astype(jnp.bfloat16)[:, :, :, 0, :]
    expand_grad = jnp.einsum(
        "nhwc,nhwo->co", second_full, third_pre, preferred_element_type=jnp.float32
    )
    second_grad = channel_sum(
        jnp.einsum("nhwo,co->nhwc", third_pre, expand_full, preferred_element_type=jnp.float32)[
            :, :, :, None, :
        ]
    )
    second_grad = second_grad * silu_slope(second_out)
    second_shift, second_scale = grad_sums(
        pixel_sum(second_grad), pixel_sum(second_grad * second_norm)
    )
    second_pre = normalize_back(
        second_grad, second_norm, second_inv, block_scale[1:2], second_shift, second_scale, count
    ).astype(jnp.bfloat16)[:, :, :, 0, :]
    spatial_grad = conv_weight_grad(first_full, second_pre, masks)
    first_grad = channel_sum(conv_input_grad(second_pre, spatial_full, masks)[:, :, :, None, :])
    first_grad = first_grad * silu_slope(first_out)
    first_shift, first_scale = grad_sums(pixel_sum(first_grad), pixel_sum(first_grad * first_norm))
    first_pre = normalize_back(
        first_grad, first_norm, first_inv, block_scale[0:1], first_shift, first_scale, count
    ).astype(jnp.bfloat16)
    first_pre_full = channel_gather(first_pre)[:, :, :, 0, :]
    reduce_grad = jnp.einsum(
        "nhwc,nhwo->co", inputs, first_pre_full, preferred_element_type=jnp.float32
    )
    input_grad = summed_grad + jnp.einsum(
        "nhwo,co->nhwc", first_pre_full, reduce_full, preferred_element_type=jnp.float32
    )
    weight_grads = (reduce_grad, spatial_grad, expand_grad, heads_grad, distil_grad)
    small_grads = (
        jnp.concatenate([first_scale, second_scale], axis=0),
        jnp.concatenate([first_shift, second_shift], axis=0),
        scale_sums,
        shift_sums[:4],
        shift_sums[4:],
        third_scale[0],
        third_shift[0],
    )
    return (outputs[0], outputs[1], input_grad, weight_grads, small_grads)


def gathered_local(
    features,
    image_ids,
    reduce_weight,
    spatial_weight,
    expand_weight,
    head_weights,
    distil_weights,
    block_scale,
    block_shift,
    head_scale,
    head_shift,
    gate_bias,
    output_scale,
    output_shift,
    depth_cotangent,
    segment_cotangent,
):
    batch_count = lax.axis_size("batch")
    small = (
        block_scale,
        block_shift,
        head_scale,
        head_shift,
        gate_bias,
        output_scale,
        output_shift,
    )
    depth_list, segment_list, input_list = ([], [], [])
    weight_total = None
    small_total = None
    for micro_index in range(features.shape[0]):
        gathered = fetch_weights(
            reduce_weight, spatial_weight, expand_weight, head_weights, distil_weights
        )
        canvas_pick = slice(micro_index, micro_index + 1)
        depth_out, segment_out, input_grad, weight_grads, small_grads = micro_step(
            features[canvas_pick],
            image_ids[canvas_pick],
            depth_cotangent[canvas_pick],
            segment_cotangent[canvas_pick],
            gathered,
            small,
            batch_count,
        )
        weight_grads = scatter_weights(weight_grads)
        weight_total = (
            weight_grads
            if weight_total is None
            else jax.tree.map(jnp.add, weight_total, weight_grads)
        )
        small_total = (
            small_grads if small_total is None else jax.tree.map(jnp.add, small_total, small_grads)
        )
        depth_list.append(depth_out)
        segment_list.append(segment_out)
        input_list.append(input_grad)
    reduce_grad, spatial_grad, expand_grad, heads_grad, distil_grad = weight_total
    scale_mid, shift_mid, scale_heads, shift_heads, bias_gates, scale_out, shift_out = small_total
    return (
        jnp.concatenate(depth_list, axis=0),
        jnp.concatenate(segment_list, axis=0),
        jnp.concatenate(input_list, axis=0),
        reduce_grad,
        spatial_grad,
        expand_grad,
        heads_grad,
        distil_grad,
        scale_mid,
        shift_mid,
        scale_heads,
        shift_heads,
        bias_gates,
        scale_out,
        shift_out,
    )


MESH = pl.DeviceIdType.MESH
PIXELS = 256
PAD = 32
LANES = 128


def whereabouts():
    place, lane = lax.axis_index("batch"), lax.axis_index("chan")
    return place, lane, place // 2, place % 2, lane // 2, lane % 2


def ranked(depth, rank):
    high, low = depth // 2, depth % 2
    up, odd = rank // 2, rank % 2
    return (
        (1 - odd) * (1 - up) * depth
        + odd * (1 - up) * (1 + low)
        + (1 - odd) * up * (2 - 2 * low + high)
        + odd * up * (3 - 3 * high)
    )


def middle(depth):
    return (depth // 2 + depth % 2) % 2


def inner(depth):
    return 1 + depth % 2


def outer(depth):
    return 3 * (depth // 2)


def onward(depth, rank):
    second = (1 - rank % 2) * (rank // 2)
    return outer(depth) + second * (3 - depth - outer(depth))


def homeward(depth, rank):
    second = (1 - rank % 2) * (rank // 2) * middle(depth)
    return inner(depth) + second * (outer(depth) - inner(depth))


def staggered(step):
    late = ((step + 1) % 2) * ((step + 14) // 15) + step // 15
    return (1 - late) * ((step + 1) // 2) + late * (step // 2 - 1 + step // 15), late


def push(source, target, send_sem, recv_sem, place, lane):
    return pltpu.make_async_remote_copy(
        src_ref=source,
        dst_ref=target,
        send_sem=send_sem,
        recv_sem=recv_sem,
        device_id=(place, lane),
        device_id_type=MESH,
    )


def announce(peers):
    barrier = pltpu.get_barrier_semaphore()
    for place, lane in peers:
        pl.semaphore_signal(barrier, inc=1, device_id=(place, lane), device_id_type=MESH)


def gathered_peers(peers):
    pl.semaphore_wait(pltpu.get_barrier_semaphore(), len(peers))


def greet(peers):
    announce(peers)
    gathered_peers(peers)


def batch_peers():
    place, lane, _, _, _, _ = whereabouts()
    return [((place + step) % 8, lane) for step in range(1, 8)]


def line_peers():
    place, lane, depth, side, _, _ = whereabouts()
    peers = [(ranked(depth, rank) * 2 + side, lane) for rank in range(1, 4)]
    return peers + [(depth * 2 + 1 - side, lane)]


def chan_peers():
    place, lane, _, _, _, _ = whereabouts()
    return [(place, (lane + step) % 4) for step in range(1, 4)]


class Gather:
    def __init__(self, values, recv, cross, line, parts, direct=False):
        self.values, self.recv, self.cross, self.line = values, recv, cross, line
        self.parts, self.direct = parts, direct

    def view(self, block, part):
        return self.values.at[block] if self.parts == 1 else self.values.at[block, part]

    def copy(self, block, part, sem, depth, side):
        lane = lax.axis_index("chan")
        here = self.view(block, part)
        return push(here, here, sem, self.recv.at[block, part], depth * 2 + side, lane)

    def start(self, part=0):
        place, lane, depth, side, _, _ = whereabouts()
        if self.direct:
            self.copy(place, part, self.cross.at[0, part], depth, 1 - side).start()
            for rank in range(1, 4):
                self.copy(
                    place, part, self.line.at[0, rank, part], ranked(depth, rank), side
                ).start()
            return
        self.copy(place, part, self.line.at[0, 0, part], inner(depth), side).start()

        @pl.when(middle(depth) == 1)
        def _():
            self.copy(place, part, self.line.at[1, 0, part], outer(depth), side).start()

        self.copy(place, part, self.cross.at[0, part], depth, 1 - side).start()

    def near(self, rank, part=0):
        place, lane, depth, side, _, _ = whereabouts()
        block = ranked(depth, rank) * 2 + side
        self.copy(block, part, self.cross.at[rank, part], depth, side).wait_recv()

        if not self.direct:

            @pl.when(middle(depth) == 1)
            def _():
                self.copy(
                    block, part, self.line.at[0, rank, part], onward(depth, rank), side
                ).start()

        self.copy(block, part, self.cross.at[rank, part], depth, 1 - side).start()

    def far(self, rank, part=0):
        place, lane, depth, side, _, _ = whereabouts()
        block = ranked(depth, rank) * 2 + 1 - side
        self.copy(block, part, self.cross.at[rank, part], depth, side).wait_recv()

    def next(self, step):
        place, lane, depth, side, _, _ = whereabouts()
        item, late = staggered(step)
        part, rank = item // 4, item % 4

        @pl.when((late == 0) & (rank > 0))
        def _():
            self.near(rank, part)

        @pl.when(late == 1)
        def _():
            self.far(rank, part)

        return ranked(depth, rank) * 2 + (side + late) % 2, part

    def close(self):
        place, lane, depth, side, _, _ = whereabouts()
        for part in range(self.parts):
            for rank in range(4):
                self.copy(place, part, self.cross.at[rank, part], depth, side).wait_send()
            if self.direct:
                for rank in range(1, 4):
                    self.copy(place, part, self.line.at[0, rank, part], depth, side).wait_send()
                continue
            self.copy(place, part, self.line.at[0, 0, part], depth, side).wait_send()

            @pl.when(middle(depth) == 1)
            def _():
                self.copy(place, part, self.line.at[1, 0, part], depth, side).wait_send()
                for rank in range(1, 4):
                    self.copy(place, part, self.line.at[0, rank, part], depth, side).wait_send()


def gather_sems(parts):
    return [
        pltpu.SemaphoreType.DMA((8, parts)),
        pltpu.SemaphoreType.DMA((4, parts)),
        pltpu.SemaphoreType.DMA((2, 4, parts)),
    ]


def clear_edges(turned):
    edge = jnp.zeros((3, PAD, turned.shape[2]), turned.dtype)
    turned[:, 0:PAD] = edge
    turned[:, PAD + PIXELS :] = edge


def fill_columns(value, mask, turned, columns, row=0, flip=False):
    width = value.shape[1]
    lanes = slice(0, width)
    wide = value.astype(jnp.float32)
    inside = slice(PAD, PAD + PIXELS)
    turned[0, inside, lanes] = pltpu.roll(wide, 1, 0).astype(jnp.bfloat16)
    turned[1, inside, lanes] = value
    turned[2, inside, lanes] = pltpu.roll(wide, PIXELS - 1, 0).astype(jnp.bfloat16)
    for number, (vertical, lateral) in enumerate(OFFSETS):
        start = PAD + 32 * vertical
        slot = 8 - number if flip else number
        columns[row : row + PIXELS, slot * width : (slot + 1) * width] = (
            turned[lateral + 1, start : start + PIXELS, lanes] * mask[:, number : number + 1]
        )


def vmem(count):
    return [pl.BlockSpec(memory_space=pltpu.VMEM)] * count


def kernel_params(number):
    return pltpu.CompilerParams(
        collective_id=number, has_side_effects=True, vmem_limit_bytes=60 * 2**20
    )


class Exchange:
    def __init__(self, values, send, recv, axis):
        self.values, self.send, self.recv, self.axis = values, send, recv, axis

    def steps(self):
        place, lane, _, _, _, _ = whereabouts()
        if self.axis == "batch":
            return [(step - 1, (place + step) % 8, lane, (place + step) % 8) for step in range(1, 8)]
        return [(step - 1, place, (lane + step) % 4, (lane + step) % 4) for step in range(1, 4)]

    def mine(self):
        place, lane, _, _, _, _ = whereabouts()
        return place if self.axis == "batch" else lane

    def start(self):
        here = self.values.at[self.mine()]
        for number, place, lane, _ in self.steps():
            push(here, here, self.send.at[number], self.recv.at[self.mine()], place, lane).start()

    def wait(self):
        for number, place, lane, slot in self.steps():
            there = self.values.at[slot]
            push(there, there, self.send.at[number], self.recv.at[slot], place, lane).wait_recv()

    def close(self):
        here = self.values.at[self.mine()]
        for number, place, lane, _ in self.steps():
            push(here, here, self.send.at[number], self.recv.at[self.mine()], place, lane).wait_send()

    def total(self):
        result = self.values[0]
        for slot in range(1, self.values.shape[0]):
            result = result + self.values[slot]
        return result


class Pieces:
    def __init__(self, stage, got, send, recv):
        self.stage, self.got, self.send, self.recv = stage, got, send, recv

    def start(self, part):
        place, lane, _, _, _, _ = whereabouts()
        for slot in range(4):
            self.stage[slot] = part[:, slot * LANES : (slot + 1) * LANES].astype(jnp.bfloat16)
        for step in (2, 1, 3):
            slot = (lane + step) % 4
            push(
                self.stage.at[slot],
                self.got.at[lane],
                self.send.at[slot],
                self.recv.at[lane],
                place,
                slot,
            ).start()

    def finish(self):
        place, lane, _, _, _, _ = whereabouts()
        self.got[lane] = self.stage[lane]
        for step in range(1, 4):
            slot = (lane + step) % 4
            push(
                self.stage.at[slot],
                self.got.at[slot],
                self.send.at[slot],
                self.recv.at[slot],
                place,
                lane,
            ).wait()
        result = self.got[0].astype(jnp.float32)
        for slot in range(1, 4):
            result = result + self.got[slot].astype(jnp.float32)
        return result


class Local:
    def __init__(self, pairs, sems):
        self.copies = [
            pltpu.make_async_copy(source, target, sems.at[number])
            for number, (source, target) in enumerate(pairs)
        ]

    def start(self, *numbers):
        for number in numbers:
            self.copies[number].start()

    def wait(self, *numbers):
        for number in numbers:
            self.copies[number].wait()


def anywhere(count):
    return [pl.BlockSpec(memory_space=pl.ANY)] * count


def micro_rows(micro):
    return slice(micro * PIXELS, (micro + 1) * PIXELS)


def moments(value, other):
    rows = []
    for micro in range(2):
        part = value[micro_rows(micro)]
        rows.append(jnp.sum(part, axis=0, keepdims=True))
        rows.append(jnp.sum(part * other[micro_rows(micro)], axis=0, keepdims=True))
    return rows


def tile_rows(rows, height):
    width = rows[0].shape[1]
    return jnp.concatenate(rows + [jnp.zeros((height - len(rows), width), jnp.float32)], axis=0)


def normed_part(value, totals, micro, count):
    center = totals[2 * micro : 2 * micro + 1] / count
    inverse = lax.rsqrt(totals[2 * micro + 1 : 2 * micro + 2] / count - center * center + EPSILON)
    return (value[micro_rows(micro)] - center) * inverse, inverse


def dot_last(first, second):
    return lax.dot_general(
        first, second, (((1,), (1,)), ((), ())), preferred_element_type=jnp.float32
    )


def make_masks(ids_ref, mask_all):
    rows = 8 * ids_ref.shape[0]
    ids = ids_ref[...].reshape(rows, PIXELS).T
    pixel = lax.broadcasted_iota(jnp.int32, (PIXELS, rows), 0)
    taps = []
    for vertical, lateral in OFFSETS:
        offset = 32 * vertical + lateral
        beside = ids if offset == 0 else pltpu.roll(ids, (-offset) % PIXELS, 0)
        row, col = (pixel >> 5) + vertical, (pixel & 31) + lateral
        inside = (row >= 0) & (row < 8) & (col >= 0) & (col < 32)
        taps.append(jnp.where(inside & (beside == ids), 1.0, 0.0).astype(jnp.bfloat16))
    taps = jnp.concatenate(taps + [jnp.zeros_like(taps[0])], axis=1)
    item = lax.broadcasted_iota(jnp.int32, (10 * rows, LANES), 0)
    lane = lax.broadcasted_iota(jnp.int32, (10 * rows, LANES), 1)
    for block in range(8):
        for micro in range(2):
            chosen = jnp.where(item == lane * rows + (8 * block + micro), 1.0, 0.0)
            mask_all[block, micro] = jnp.dot(
                taps, chosen.astype(jnp.bfloat16), preferred_element_type=jnp.float32
            ).astype(jnp.bfloat16)


def front_kernel(
    count,
    x_ref,
    ids_ref,
    reduce_ref,
    spatial_ref,
    expand_ref,
    block_scale,
    block_shift,
    output_scale,
    output_shift,
    head_scale,
    head_shift,
    depth_cot,
    segment_cot,
    y_ref,
    norm3_ref,
    inverse3_ref,
    norm12_ref,
    inverse12_ref,
    mine_ref,
    mask_ref,
    act1_out,
    act2_out,
    reduce_out,
    spatial_out,
    expand_out,
    mask_out,
    cot_out,
    raw_out,
    act1_ref,
    act2_ref,
    reduce_all,
    spatial_all,
    expand_all,
    mask_all,
    cot_all,
    packed,
    turned,
    columns,
    stage,
    got,
    sums1,
    sums2,
    sums3,
    head_all,
    ids_all,
    raw1,
    raw2,
    fits1,
    fits2,
    *sems,
):
    place, lane, depth, side, upper, core = whereabouts()
    reduces = Gather(reduce_all, *sems[0:3], 1, True)
    spatials = Gather(spatial_all, *sems[3:6], 1)
    expands = Gather(expand_all, *sems[6:9], 1)
    ids = Exchange(ids_all, sems[9], sems[10], "batch")
    pieces = Pieces(stage, got, sems[11], sems[12])
    first_sums = Exchange(sums1, sems[13], sems[14], "batch")
    second_sums = Exchange(sums2, sems[15], sems[16], "batch")
    third_sums = Exchange(sums3, sems[17], sems[18], "batch")
    heads = Exchange(head_all, sems[19], sems[20], "chan")
    first_raw = Exchange(raw1, sems[21], sems[22], "chan")
    second_raw = Exchange(raw2, sems[23], sems[24], "chan")
    first_fits = Exchange(fits1, sems[28], sems[29], "chan")
    second_fits = Exchange(fits2, sems[30], sems[31], "chan")

    def centered(value, raw):
        rows = moments(value, value)
        for micro in range(2):
            raw[lane, micro_rows(micro)] = (
                value[micro_rows(micro)] - rows[2 * micro] / PIXELS
            ).astype(jnp.bfloat16)
        return rows

    def fit(value, rows, totals, layer, fits):
        inverses, offsets, lines = [], [], []
        for micro in range(2):
            normed, inverse = normed_part(value, totals, micro, count)
            norm12_ref[layer, micro_rows(micro)] = normed
            inverses.append(inverse)
            slope = inverse * block_scale[layer : layer + 1]
            center = totals[2 * micro : 2 * micro + 1] / count
            offset = rows[2 * micro] / PIXELS - center
            offsets.append(offset * inverse)
            lines.append(slope)
            lines.append(offset * slope + block_shift[layer : layer + 1])
        fits[lane] = tile_rows(lines, 8)
        return inverses, offsets

    def activate(raw, fits, act):
        for slot in range(4):
            for micro in range(2):
                out = (
                    raw[slot, micro_rows(micro)].astype(jnp.float32)
                    * fits[slot, 2 * micro : 2 * micro + 1]
                    + fits[slot, 2 * micro + 1 : 2 * micro + 2]
                )
                act[slot, micro_rows(micro)] = (out * jax.nn.sigmoid(out)).astype(jnp.bfloat16)


    local = Local(
        (
            (act1_ref, act1_out),
            (act2_ref, act2_out),
            (reduce_all, reduce_out),
            (spatial_all, spatial_out),
            (expand_all, expand_out),
            (mask_all, mask_out),
            (cot_all, cot_out),
            (raw1, raw_out),
        ),
        sems[27],
    )
    cot_sem, cot_recv = sems[25:27]

    def cot_copy(parity, slot, target):
        return push(
            packed.at[parity], cot_all.at[slot], cot_sem.at[parity], cot_recv.at[slot], target, lane
        )

    announce(batch_peers() + chan_peers())
    reduce_all[place] = reduce_ref[...]
    ids_all[place] = jnp.zeros((8, PIXELS), jnp.float32)
    for micro in range(2):
        for row in range(8):
            ids_all[place, micro : micro + 1, row * 32 : (row + 1) * 32] = ids_ref[
                micro, row : row + 1
            ].astype(jnp.float32)
    spatial_all[place] = spatial_ref[...]
    expand_all[place] = expand_ref[...]
    head_all[lane, 0:4] = head_scale[...]
    head_all[lane, 4:8] = head_shift[...]
    clear_edges(turned)
    gathered_peers(batch_peers() + chan_peers())
    reduces.start()
    ids.start()
    heads.start()
    for rank in range(1, 4):
        reduces.near(rank)
    spatials.start()
    for rank in range(4):
        reduces.far(rank)
    x = x_ref[...].reshape(2 * PIXELS, x_ref.shape[2])
    pieces.start(dot_last(x, reduce_all[...].reshape(512, 512)))
    ids.wait()
    make_masks(ids_all, mask_all)
    mask_ref[...] = mask_all[place]
    local.start(2, 5)
    spatials.near(1)
    first = pieces.finish()
    first_rows = centered(first, raw1)
    sums1[place] = tile_rows(first_rows, 8)
    first_sums.start()
    first_raw.start()
    spatials.near(2)
    expands.start()
    spatials.near(3)
    half_width = LANES // 2
    left = lax.broadcasted_iota(jnp.int32, (PIXELS, LANES), 1) < half_width
    for micro in range(2):
        upper_cot, lower_cot = (ref[micro].astype(jnp.float32) for ref in (depth_cot, segment_cot))
        packed[0, micro] = jnp.where(left, upper_cot, pltpu.roll(lower_cot, half_width, 1)).astype(
            jnp.bfloat16
        )
        packed[1, micro] = jnp.where(left, pltpu.roll(upper_cot, half_width, 1), lower_cot).astype(
            jnp.bfloat16
        )
    first_sums.wait()
    rows, offsets = fit(first, first_rows, first_sums.total(), 0, fits1)
    first_fits.start()
    expands.near(1)
    for rank in range(4):
        spatials.far(rank)
    expands.near(2)
    first_raw.wait()
    first_fits.wait()
    activate(raw1, fits1, act1_ref)
    local.start(0, 3, 7)
    for micro in range(2):
        value = jnp.concatenate([act1_ref[slot, micro_rows(micro)] for slot in range(4)], axis=1)
        fill_columns(value, mask_all[place, micro], turned, columns, micro * PIXELS)
    second = jnp.zeros((2 * PIXELS, LANES), jnp.float32)
    for number in range(9):
        second = second + jnp.dot(
            columns[:, number * 512 : (number + 1) * 512],
            spatial_all[:, number].reshape(512, LANES),
            preferred_element_type=jnp.float32,
        )
    second_rows = centered(second, raw2)
    sums2[place] = tile_rows(second_rows, 8)
    second_sums.start()
    second_raw.start()
    expands.near(3)
    for parity in range(2):
        target = 2 * lane + parity

        @pl.when(target == place)
        def _():
            cot_all[place] = packed[parity]

        @pl.when(target != place)
        def _():
            cot_copy(parity, place, target).start()

    second_sums.wait()
    rows = rows + fit(second, second_rows, second_sums.total(), 1, fits2)[0] + offsets
    second_fits.start()
    inverse12_ref[...] = tile_rows(rows, 8)
    heads.wait()
    low = lax.broadcasted_iota(jnp.int32, (1, LANES), 1) < half_width
    source = place // 2
    even = place % 2 == 0
    for kind in range(2):
        upper_row = head_all[source, pl.ds(4 * kind + 2 * upper, 1)]
        lower_row = head_all[source, pl.ds(4 * kind + 2 * upper + 1, 1)]
        mine_ref[kind : kind + 1] = jnp.where(
            even,
            jnp.where(low, upper_row, pltpu.roll(lower_row, half_width, 1)),
            jnp.where(low, pltpu.roll(upper_row, half_width, 1), lower_row),
        )
    for rank in range(4):
        expands.far(rank)
    second_raw.wait()
    second_fits.wait()
    activate(raw2, fits2, act2_ref)
    local.start(1, 4)
    value = jnp.concatenate([act2_ref[slot] for slot in range(4)], axis=1)
    third = jnp.dot(
        value, expand_all[...].reshape(512, 512), preferred_element_type=jnp.float32
    )
    sums3[place] = tile_rows(moments(third, third), 8)
    third_sums.start()
    third_sums.wait()
    totals = third_sums.total()
    rows = []
    for micro in range(2):
        normed, inverse = normed_part(third, totals, micro, count)
        norm3_ref[micro_rows(micro)] = normed
        rows.append(inverse)
        out = normed * output_scale[...] + output_shift[...] + x_ref[micro].astype(jnp.float32)
        y_ref[micro] = (out * jax.nn.sigmoid(out)).astype(jnp.bfloat16)
    inverse3_ref[...] = tile_rows(rows, 8)
    @pl.when(place // 2 == lane)
    def _():
        for step in range(1, 8):
            cot_copy(0, (place + step) % 8, place).wait_recv()

    local.start(6)
    for parity in range(2):
        @pl.when(2 * lane + parity != place)
        def _():
            cot_copy(parity, place, place).wait_send()

    local.wait(0, 1, 2, 3, 4, 5, 6, 7)
    for item in (reduces, spatials, expands, ids, heads, first_raw, second_raw):
        item.close()
    for item in (first_sums, second_sums, third_sums, first_fits, second_fits):
        item.close()


def exchange_sems(size):
    return [pltpu.SemaphoreType.DMA((size - 1,)), pltpu.SemaphoreType.DMA((size,))]


def run_front(count, *arrays):
    f32, bf16 = jnp.float32, jnp.bfloat16
    kept = (
        (4, 2 * PIXELS, LANES),
        (4, 2 * PIXELS, LANES),
        (8, 64, 512),
        (8, 9, 64, LANES),
        (8, 64, 512),
        (8, 2, PIXELS, LANES),
        (8, 2, PIXELS, LANES),
    )
    return pl.pallas_call(
        functools.partial(front_kernel, count),
        name="front",
        out_shape=(
            jax.ShapeDtypeStruct((2, PIXELS, 512), bf16),
            jax.ShapeDtypeStruct((2 * PIXELS, 512), f32),
            jax.ShapeDtypeStruct((8, 512), f32),
            jax.ShapeDtypeStruct((2, 2 * PIXELS, LANES), f32),
            jax.ShapeDtypeStruct((8, LANES), f32),
            jax.ShapeDtypeStruct((2, LANES), f32),
            jax.ShapeDtypeStruct((2, PIXELS, LANES), bf16),
        )
        + tuple(jax.ShapeDtypeStruct(shape, bf16) for shape in kept + (kept[0],)),
        in_specs=vmem(13),
        out_specs=tuple(vmem(7) + anywhere(8)),
        scratch_shapes=[pltpu.VMEM(shape, bf16) for shape in kept]
        + [
            pltpu.VMEM((2, 2, PIXELS, LANES), bf16),
            pltpu.VMEM((3, 2 * PAD + PIXELS, 512), bf16),
            pltpu.VMEM((2 * PIXELS, 9 * 512), bf16),
            pltpu.VMEM((4, 2 * PIXELS, LANES), bf16),
            pltpu.VMEM((4, 2 * PIXELS, LANES), bf16),
            pltpu.VMEM((8, 8, LANES), f32),
            pltpu.VMEM((8, 8, LANES), f32),
            pltpu.VMEM((8, 8, 512), f32),
            pltpu.VMEM((4, 8, LANES), f32),
            pltpu.VMEM((8, 8, PIXELS), f32),
            pltpu.VMEM((4, 2 * PIXELS, LANES), bf16),
            pltpu.VMEM((4, 2 * PIXELS, LANES), bf16),
            pltpu.VMEM((4, 8, LANES), f32),
            pltpu.VMEM((4, 8, LANES), f32),
        ]
        + gather_sems(1) * 3
        + exchange_sems(8)
        + [pltpu.SemaphoreType.DMA((4,))] * 2
        + exchange_sems(8) * 3
        + exchange_sems(4) * 3
        + [
            pltpu.SemaphoreType.DMA((2,)),
            pltpu.SemaphoreType.DMA((8,)),
            pltpu.SemaphoreType.DMA((8,)),
        ]
        + exchange_sems(4) * 2,
        compiler_params=kernel_params(1),
    )(*arrays)


class Scatter:
    def __init__(self, part, far_buf, far_got, near_buf, near_got, sems):
        self.part, self.far_buf, self.far_got = part, far_buf, far_got
        self.near_buf, self.near_got = near_buf, near_got
        self.far_send, self.far_recv, self.near_send, self.near_recv = sems

    def far_copy(self, level, place):
        return push(
            self.far_buf.at[level],
            self.far_got.at[level],
            self.far_send.at[level],
            self.far_recv.at[level],
            place,
            lax.axis_index("chan"),
        )

    def near_copy(self, rank, level, place):
        return push(
            self.near_buf.at[rank - 1],
            self.near_got.at[level],
            self.near_send.at[rank - 1],
            self.near_recv.at[level],
            place,
            lax.axis_index("chan"),
        )

    def start(self):
        place, lane, depth, side, _, _ = whereabouts()
        for rank in (3, 2, 1, 0):
            level = ranked(depth, rank)
            self.far_buf[level] = self.part[level * 2 + 1 - side].astype(jnp.bfloat16)
            self.far_copy(level, depth * 2 + 1 - side).start()

    def middle(self):
        place, lane, depth, side, _, _ = whereabouts()
        for rank in (3, 2, 1):
            level = ranked(depth, rank)
            self.far_copy(level, place).wait_recv()
            self.near_buf[rank - 1] = (
                self.part[level * 2 + side] + self.far_got[level].astype(jnp.float32)
            ).astype(jnp.bfloat16)
            self.near_copy(rank, depth, level * 2 + side).start()

    def finish(self):
        place, lane, depth, side, _, _ = whereabouts()
        self.far_copy(depth, place).wait_recv()
        result = self.part[place] + self.far_got[depth].astype(jnp.float32)
        for level in range(4):
            self.far_copy(level, place).wait_send()
        for rank in (3, 2, 1):
            level = ranked(depth, rank)
            self.near_copy(rank, level, place).wait()
            result = result + self.near_got[level].astype(jnp.float32)
        return result


def scatter_scratch(width):
    return [
        pltpu.VMEM((8, 64, width), jnp.float32),
        pltpu.VMEM((4, 64, width), jnp.bfloat16),
        pltpu.VMEM((4, 64, width), jnp.bfloat16),
        pltpu.VMEM((3, 64, width), jnp.bfloat16),
        pltpu.VMEM((4, 64, width), jnp.bfloat16),
    ]


def scatter_sems():
    return [
        pltpu.SemaphoreType.DMA((4,)),
        pltpu.SemaphoreType.DMA((4,)),
        pltpu.SemaphoreType.DMA((3,)),
        pltpu.SemaphoreType.DMA((4,)),
    ]


def back_part(value, normed, inverse, scale, shift_sum, scale_sum, count):
    return (scale * inverse * (value - (shift_sum + normed * scale_sum) / count)).astype(
        jnp.bfloat16
    )


def rear_kernel(
    count,
    grad_ref,
    x_ref,
    norm3_ref,
    inverse3_ref,
    norm12_ref,
    inverse12_ref,
    mask_ref,
    block_scale,
    block_shift,
    output_scale,
    output_shift,
    head_ref,
    gate_ref,
    block_hbm,
    back_hbm,
    masks_hbm,
    act1_hbm,
    act2_hbm,
    reduce_hbm,
    spatial_hbm,
    expand_hbm,
    raw_hbm,
    features_ref,
    reduce_out,
    spatial_out,
    expand_out,
    block_scale_out,
    block_shift_out,
    head_scale_out,
    head_shift_out,
    gate_out,
    output_scale_out,
    output_shift_out,
    head_out,
    head_grad,
    block_all,
    head_back,
    mask_all,
    act1_ref,
    act2_ref,
    reduce_all,
    spatial_all,
    expand_all,
    raw_ref,
    fits_all,
    turned_wide,
    columns_wide,
    turned,
    columns,
    stage,
    got,
    stage_next,
    got_next,
    sums_a,
    sums_b,
    sums_c,
    head_all,
    act_all,
    back3,
    *rest,
):
    expand_bufs, spatial_bufs, reduce_bufs, sems = rest[0:5], rest[5:10], rest[10:15], rest[15:]
    place, lane, depth, side, upper, core = whereabouts()
    pieces = Pieces(stage, got, sems[0], sems[1])
    first = Exchange(sums_a, sems[2], sems[3], "batch")
    second = Exchange(sums_b, sems[4], sems[5], "batch")
    third = Exchange(sums_c, sems[6], sems[7], "batch")
    heads = Exchange(head_all, sems[8], sems[9], "chan")
    acts = Exchange(act_all, sems[10], sems[11], "chan")
    fits = Exchange(fits_all, sems[27], sems[28], "chan")
    expands = Scatter(*expand_bufs, sems[12:16])
    spatials = Scatter(*spatial_bufs, sems[16:20])
    reduces = Scatter(*reduce_bufs, sems[20:24])
    pieces_next = Pieces(stage_next, got_next, sems[24], sems[25])

    local = Local(
        (
            (expand_hbm, expand_all),
            (act2_hbm, act2_ref),
            (block_hbm, block_all),
            (back_hbm, head_back),
            (masks_hbm, mask_all),
            (spatial_hbm, spatial_all),
            (act1_hbm, act1_ref),
            (reduce_hbm, reduce_all),
            (head_grad, head_out),
            (raw_hbm, raw_ref),
        ),
        sems[26],
    )
    local.start(0, 1, 2, 3, 4, 5, 6, 7, 9)

    def weigh(block):
        for micro in range(2):
            fill_columns(
                block_all[block, micro],
                mask_all[block, micro],
                turned_wide,
                columns_wide,
                micro * PIXELS,
            )
        value = jnp.concatenate(
            [
                jnp.concatenate([head_back[half, micro, block] for half in range(2)], axis=1)
                for micro in range(2)
            ],
            axis=0,
        ).T

        def tap(number, _):
            product = jnp.dot(
                value,
                columns_wide[:, pl.ds(pl.multiple_of(number * 512, 512), 512)],
                preferred_element_type=jnp.float32,
            )
            if block == 0:
                head_grad[number] = product
            else:
                head_grad[number] += product
            return 0

        lax.fori_loop(0, 9, tap, 0)

    announce(batch_peers() + chan_peers())
    clear_edges(turned_wide)
    half_width = LANES // 2
    even = place % 2 == 0
    mine = lax.broadcasted_iota(jnp.int32, (1, LANES), 1) >> 6 == place % 2
    rows = []
    for kind in range(2):
        own = head_ref[kind : kind + 1]
        turned_own = pltpu.roll(own, half_width, 1)
        first_row = jnp.where(mine, jnp.where(even, own, turned_own), 0.0)
        second_row = jnp.where(mine, jnp.where(even, turned_own, own), 0.0)
        for half in range(2):
            for row in (first_row, second_row):
                rows.append(jnp.where(upper == half, row, 0.0))
    head_all[lane] = jnp.concatenate(rows, axis=0)
    clear_edges(turned)
    wide_rows = []
    for micro in range(2):
        normed = norm3_ref[micro_rows(micro)]
        out = normed * output_scale[...] + output_shift[...] + x_ref[micro].astype(jnp.float32)
        value = grad_ref[micro_rows(micro)] * silu_slope(out)
        features_ref[micro] = value
        wide_rows.append(jnp.sum(value, axis=0, keepdims=True))
        wide_rows.append(jnp.sum(value * normed, axis=0, keepdims=True))
    gathered_peers(batch_peers() + chan_peers())
    sums_a[place] = tile_rows(wide_rows, 8)
    first.start()
    heads.start()
    local.wait(0, 1, 2, 3, 4)
    weigh(0)
    first.wait()
    totals = first.total()
    output_scale_out[...] = totals[1:2] + totals[3:4]
    output_shift_out[...] = totals[0:1] + totals[2:3]
    for micro in range(2):
        back3[micro_rows(micro)] = back_part(
            features_ref[micro],
            norm3_ref[micro_rows(micro)],
            inverse3_ref[micro : micro + 1],
            output_scale[...],
            totals[2 * micro : 2 * micro + 1],
            totals[2 * micro + 1 : 2 * micro + 2],
            count,
        )
    pieces.start(dot_last(back3[...], expand_all[...].reshape(512, 512)))
    value = jnp.concatenate([act2_ref[slot] for slot in range(4)], axis=1)
    expands.part[...] = jnp.dot(
        value.T, back3[...], preferred_element_type=jnp.float32
    ).reshape(8, 64, 512)
    expands.start()
    weigh(1)
    weigh(2)
    grad = pieces.finish()
    normed = norm12_ref[1]
    grad = grad * silu_slope(normed * block_scale[1:2] + block_shift[1:2])
    heads.wait()
    sums_b[place, 0:8] = tile_rows(moments(grad, normed), 8)
    sums_b[place, 4:6] = gate_ref[...]
    sums_b[place, 8:16] = jnp.where(place // 2 == lane, heads.total(), 0.0)
    second.start()
    local.wait(5, 6, 7, 9)
    weigh(3)
    expands.middle()
    second.wait()
    totals = second.total()
    head_scale_out[...] = totals[8:12]
    head_shift_out[...] = totals[12:16]
    gate_out[...] = totals[4:6]
    block_scale_out[1:2] = totals[1:2] + totals[3:4]
    block_shift_out[1:2] = totals[0:1] + totals[2:3]
    for micro in range(2):
        value = back_part(
            grad[micro_rows(micro)],
            normed[micro_rows(micro)],
            inverse12_ref[2 + micro : 3 + micro],
            block_scale[1:2],
            totals[2 * micro : 2 * micro + 1],
            totals[2 * micro + 1 : 2 * micro + 2],
            count,
        )
        fill_columns(value, mask_ref[micro], turned, columns, micro * PIXELS, True)
    part = jnp.zeros((2 * PIXELS, 512), jnp.float32)
    for number in range(9):
        part = part + dot_last(
            columns[:, number * LANES : (number + 1) * LANES],
            spatial_all[:, number].reshape(512, LANES),
        )
    pieces_next.start(part)
    value = jnp.concatenate([act1_ref[slot] for slot in range(4)], axis=1)
    spatials.part[...] = jnp.dot(
        value.T, columns[...], preferred_element_type=jnp.float32
    ).reshape(8, 64, 9 * LANES)
    spatials.start()
    weigh(4)
    weigh(5)
    grad = pieces_next.finish()
    normed = norm12_ref[0]
    grad = grad * silu_slope(normed * block_scale[0:1] + block_shift[0:1])
    rows = moments(grad, normed)
    sums_c[place] = tile_rows(rows, 8)
    third.start()
    for micro in range(2):
        act_all[lane, micro_rows(micro)] = (
            grad[micro_rows(micro)] - rows[2 * micro] / PIXELS
        ).astype(jnp.bfloat16)
    acts.start()
    weigh(6)
    spatials.middle()
    expand_out[...] = expands.finish()
    third.wait()
    totals = third.total()
    block_scale_out[0:1] = totals[1:2] + totals[3:4]
    block_shift_out[0:1] = totals[0:1] + totals[2:3]
    lines = []
    for micro in range(2):
        shift_sum = totals[2 * micro : 2 * micro + 1]
        scale_sum = totals[2 * micro + 1 : 2 * micro + 2]
        inverse = inverse12_ref[micro : micro + 1]
        factor = block_scale[0:1] * inverse
        lines.append(factor)
        lines.append(-factor * scale_sum * inverse / count)
        lines.append(
            factor
            * (
                rows[2 * micro] / PIXELS
                - (shift_sum + inverse12_ref[4 + micro : 5 + micro] * scale_sum) / count
            )
        )
    fits_all[lane] = tile_rows(lines, 8)
    fits.start()
    weigh(7)
    local.start(8)
    acts.wait()
    fits.wait()

    def whole(slot):
        parts = []
        for micro in range(2):
            line = [fits_all[slot, 3 * micro + row : 3 * micro + row + 1] for row in range(3)]
            parts.append(
                act_all[slot, micro_rows(micro)].astype(jnp.float32) * line[0]
                + raw_ref[slot, micro_rows(micro)].astype(jnp.float32) * line[1]
                + line[2]
            )
        return jnp.concatenate(parts, axis=0).astype(jnp.bfloat16)

    value = jnp.concatenate([whole(slot) for slot in range(4)], axis=1)
    x = x_ref[...].reshape(2 * PIXELS, 512)
    reduces.part[...] = jnp.dot(value.T, x, preferred_element_type=jnp.float32).reshape(8, 64, 512)
    reduces.start()
    more = jnp.dot(value, reduce_all[...].reshape(512, 512), preferred_element_type=jnp.float32)
    for micro in range(2):
        features_ref[micro] = features_ref[micro] + more[micro_rows(micro)]
    reduces.middle()
    result = spatials.finish()
    for number in range(9):
        spatial_out[number] = result[:, number * LANES : (number + 1) * LANES]
    reduce_out[...] = reduces.finish()
    for item in (first, second, third, heads, acts, fits):
        item.close()
    local.wait(8)


def run_rear(count, *arrays):
    f32, bf16 = jnp.float32, jnp.bfloat16
    return pl.pallas_call(
        functools.partial(rear_kernel, count),
        name="rear",
        out_shape=(
            jax.ShapeDtypeStruct((2, PIXELS, 512), f32),
            jax.ShapeDtypeStruct((64, 512), f32),
            jax.ShapeDtypeStruct((9, 64, LANES), f32),
            jax.ShapeDtypeStruct((64, 512), f32),
            jax.ShapeDtypeStruct((2, LANES), f32),
            jax.ShapeDtypeStruct((2, LANES), f32),
            jax.ShapeDtypeStruct((4, LANES), f32),
            jax.ShapeDtypeStruct((4, LANES), f32),
            jax.ShapeDtypeStruct((2, LANES), f32),
            jax.ShapeDtypeStruct((1, 512), f32),
            jax.ShapeDtypeStruct((1, 512), f32),
            jax.ShapeDtypeStruct((9, 256, 512), f32),
        ),
        in_specs=vmem(13) + anywhere(9),
        out_specs=tuple(vmem(11) + anywhere(1)),
        scratch_shapes=[
            pltpu.VMEM((9, 256, 512), f32),
            pltpu.VMEM((8, 2, PIXELS, 512), bf16),
            pltpu.VMEM((2, 2, 8, PIXELS, LANES), bf16),
            pltpu.VMEM((8, 2, PIXELS, LANES), bf16),
            pltpu.VMEM((4, 2 * PIXELS, LANES), bf16),
            pltpu.VMEM((4, 2 * PIXELS, LANES), bf16),
            pltpu.VMEM((8, 64, 512), bf16),
            pltpu.VMEM((8, 9, 64, LANES), bf16),
            pltpu.VMEM((8, 64, 512), bf16),
            pltpu.VMEM((4, 2 * PIXELS, LANES), bf16),
            pltpu.VMEM((4, 8, LANES), f32),
            pltpu.VMEM((3, 2 * PAD + PIXELS, 512), bf16),
            pltpu.VMEM((2 * PIXELS, 9 * 512), bf16),
            pltpu.VMEM((3, 2 * PAD + PIXELS, LANES), bf16),
            pltpu.VMEM((2 * PIXELS, 9 * LANES), bf16),
            pltpu.VMEM((4, 2 * PIXELS, LANES), bf16),
            pltpu.VMEM((4, 2 * PIXELS, LANES), bf16),
            pltpu.VMEM((4, 2 * PIXELS, LANES), bf16),
            pltpu.VMEM((4, 2 * PIXELS, LANES), bf16),
            pltpu.VMEM((8, 8, 512), f32),
            pltpu.VMEM((8, 16, LANES), f32),
            pltpu.VMEM((8, 8, LANES), f32),
            pltpu.VMEM((4, 8, LANES), f32),
            pltpu.VMEM((4, 2 * PIXELS, LANES), bf16),
            pltpu.VMEM((2 * PIXELS, 512), bf16),
        ]
        + scatter_scratch(512)
        + scatter_scratch(9 * LANES)
        + scatter_scratch(512)
        + [pltpu.SemaphoreType.DMA((4,))] * 2
        + exchange_sems(8) * 3
        + exchange_sems(4) * 2
        + scatter_sems() * 3
        + [pltpu.SemaphoreType.DMA((4,))] * 2
        + [pltpu.SemaphoreType.DMA((10,))]
        + exchange_sems(4),
        compiler_params=kernel_params(5),
    )(*arrays)


class Reduce:
    def __init__(self, part, keep, far_buf, far_got, line_buf, line_got, sems):
        self.part, self.keep, self.far_buf, self.far_got = part, keep, far_buf, far_got
        self.line_buf, self.line_got = line_buf, line_got
        self.far_send, self.far_recv, self.line_send, self.line_recv = sems

    def block(self, step):
        place, lane, depth, side, _, _ = whereabouts()
        item, late = staggered(step)
        return ranked(depth, 3 - item % 4) * 2 + (side + 1 + late) % 2, item // 4

    def far_copy(self, micro, rank, place):
        return push(
            self.far_buf.at[micro, rank],
            self.far_got.at[micro, rank],
            self.far_send.at[micro, rank],
            self.far_recv.at[micro, rank],
            place,
            lax.axis_index("chan"),
        )

    def line_copy(self, micro, rank, slot, place):
        return push(
            self.line_buf.at[micro, rank],
            self.line_got.at[micro, slot],
            self.line_send.at[micro, rank],
            self.line_recv.at[micro, slot],
            place,
            lax.axis_index("chan"),
        )

    def line_value(self, micro, slot):
        self.line_copy(micro, 0, slot, lax.axis_index("batch")).wait_recv()
        return self.line_got[micro, slot].astype(jnp.float32)

    def step(self, step):
        place, lane, depth, side, _, _ = whereabouts()
        item, late = staggered(step)
        micro, rank = item // 4, 3 - item % 4
        owner = ranked(depth, rank)

        @pl.when(late == 0)
        def _():
            self.far_buf[micro, rank] = self.part[...].astype(jnp.bfloat16)
            self.far_copy(micro, rank, depth * 2 + 1 - side).start()

        @pl.when(late == 1)
        def _():
            self.far_copy(micro, rank, place).wait_recv()
            self.keep[micro] = self.part[...] + self.far_got[micro, rank].astype(jnp.float32)

            @pl.when((middle(depth) == 1) & (rank > 0))
            def _():
                self.keep[micro] = self.keep[micro] + self.line_value(micro, owner)

            @pl.when(rank > 0)
            def _():
                first = (rank % 2) * (1 - rank // 2) * (1 - middle(depth))
                slot = owner + first * (4 - owner)
                self.line_buf[micro, rank - 1] = self.keep[micro].astype(jnp.bfloat16)
                self.line_copy(
                    micro, rank - 1, slot, homeward(depth, rank) * 2 + side
                ).start()

    def close(self, micro):
        place, lane, depth, side, _, _ = whereabouts()
        self.keep[micro] = self.keep[micro] + self.line_value(micro, depth)

        @pl.when(middle(depth) == 1)
        def _():
            self.keep[micro] = self.keep[micro] + self.line_value(micro, 4)

        for rank in range(4):
            self.far_copy(micro, rank, place).wait_send()
        for rank in range(3):
            self.line_copy(micro, rank, 0, place).wait_send()


class Channels:
    def __init__(self, stage, got, stage_sem, got_sem, values, out_sem, in_sem):
        self.stage, self.got, self.stage_sem, self.got_sem = stage, got, stage_sem, got_sem
        self.values, self.out_sem, self.in_sem = values, out_sem, in_sem

    def piece(self, slot, target, block, lane):
        return push(
            self.stage.at[slot, block],
            self.got.at[lane, block],
            self.stage_sem.at[slot, block],
            self.got_sem.at[lane, block],
            lax.axis_index("batch"),
            target,
        )

    def send(self, part, block, micro):
        _, lane, _, _, upper, core = whereabouts()
        for half in range(2):
            piece = part[:, half * LANES : (half + 1) * LANES]
            target = half * 2 + micro

            @pl.when(target == lane)
            def _():
                self.got[lane, block] = piece

            @pl.when(target != lane)
            def _():
                self.stage[target, block] = piece
                self.piece(target, target, block, lane).start()

    def collect(self, micro, take):
        _, lane, _, _, _, core = whereabouts()

        @pl.when(core == micro)
        def _():
            def body(block, _):
                for step in range(1, 4):
                    other = (lane + step) % 4
                    self.piece(other, other, block, other).wait_recv()
                take(block)
                return 0

            lax.fori_loop(0, 8, body, 0)

    def value(self, block):
        result = self.got[0, block].astype(jnp.float32)
        for other in range(1, 4):
            result = result + self.got[other, block].astype(jnp.float32)
        return result

    def sent(self):
        _, lane, _, _, _, _ = whereabouts()

        def body(block, _):
            for step in range(1, 4):
                other = (lane + step) % 4
                self.piece(other, other, block, lane).wait_send()
            return 0

        lax.fori_loop(0, 8, body, 0)

    def chunk(self, path, half, micro, chunk, place_lane):
        here = self.values.at[half, micro, pl.ds(2 * chunk, 2)]
        return push(
            here,
            here,
            self.out_sem.at[path, chunk],
            self.in_sem.at[half, micro, chunk],
            lax.axis_index("batch"),
            place_lane,
        )

    def spread(self, chunk):
        _, lane, _, _, upper, core = whereabouts()
        self.chunk(0, upper, core, chunk, 2 - 2 * upper + core).start()
        self.chunk(1, upper, core, chunk, upper * 2 + 1 - core).start()

    def relay(self, micro):
        _, lane, _, _, upper, core = whereabouts()

        @pl.when(core == micro)
        def _():
            for chunk in range(4):
                copy = self.chunk(2, 1 - upper, core, chunk, upper * 2 + 1 - core)
                copy.wait_recv()
                copy.start()

    def finish(self, micro):
        _, lane, _, _, upper, core = whereabouts()

        @pl.when(core != micro)
        def _():
            for chunk in range(4):
                for half in range(2):
                    self.chunk(0, half, micro, chunk, lane).wait_recv()

    def close(self):
        _, lane, _, _, upper, core = whereabouts()
        for chunk in range(4):
            for path in range(3):
                self.chunk(path, upper, core, chunk, lane).wait_send()


def middle_kernel(
    count,
    block_ref,
    bias_ref,
    mine_ref,
    head_hbm,
    distil_hbm,
    mask_hbm,
    depth_hbm,
    segment_hbm,
    cot_hbm,
    depth_out,
    segment_out,
    gate_sums,
    head_sums,
    back_out,
    block_hbm,
    back_hbm,
    distil_out,
    distil_grad,
    block_all,
    head_back,
    head_ref,
    distil_ref,
    mask_ref,
    depth_cot,
    segment_cot,
    cot_all,
    head_weight,
    mixed,
    mixed_back,
    turned,
    columns,
    acts,
    norm_ref,
    slope_ref,
    grads_all,
    own_stage,
    own_got,
    stage,
    got,
    part_ref,
    keep,
    far_buf,
    far_got,
    line_buf,
    line_got,
    stats,
    *sems,
):
    place, lane, depth, side, upper, core = whereabouts()
    half_width = LANES // 2
    source = place // 2 == lane
    low = lax.broadcasted_iota(jnp.int32, (PIXELS, LANES), 1) < half_width
    gather = Gather(block_all, *sems[0:3], 2)
    gather_back = Gather(grads_all, *sems[3:6], 2)
    reduce = Reduce(part_ref, keep, far_buf, far_got, line_buf, line_got, sems[6:10])
    ahead = Channels(stage, got, sems[10], sems[11], acts, sems[12], sems[13])
    behind = Channels(stage, got, sems[10], sems[11], head_back, sems[14], sems[15])
    own_sem, own_recv = sems[16:18]
    local = Local(
        (
            (head_hbm, head_ref),
            (mask_hbm, mask_ref),
            (distil_hbm, distil_ref),
            (depth_hbm, depth_cot),
            (segment_hbm, segment_cot),
            (cot_hbm, cot_all),
            (block_all, block_hbm),
            (head_back, back_hbm),
            (distil_grad, distil_out),
        ),
        sems[18],
    )
    local.start(0, 1, 2, 3, 4, 5)

    greet(batch_peers() + chan_peers())
    block_all[place] = block_ref[...]
    gather.start(0)
    clear_edges(turned)
    local.wait(0)
    for number in range(9):
        head_weight[number * 512 : (number + 1) * 512] = head_ref[number].T
    local.wait(1)

    def forward_step(step, _):
        block, micro = gather.next(step)
        fill_columns(block_all[block, micro], mask_ref[block, micro], turned, columns)
        part = jnp.dot(columns[0:PIXELS], head_weight[...], preferred_element_type=jnp.float32)
        ahead.send(part.astype(jnp.bfloat16), block, micro)

        @pl.when(step == 0)
        def _():
            local.wait(2)
            prepare_mixed()

        @pl.when(step == 1)
        def _():
            gather.start(1)

        @pl.when(step == 4)
        def _():
            for number in range(9):
                mixed_back[number * 512 : (number + 1) * 512] = mixed[
                    number * 256 : (number + 1) * 256
                ].T

        @pl.when(step == 10)
        def _():
            normalize(0)

        @pl.when(step == 13)
        def _():
            ahead.relay(0)

        return 0

    def prepare_mixed():
        width = half_width
        for number in range(9):
            for stream in range(2):
                for head in range(4):
                    index = head - SOURCE_START[stream]
                    rows = slice(number * 256 + head * width, number * 256 + (head + 1) * width)
                    left = slice(2 * stream * LANES, (2 * stream + 1) * LANES)
                    right = slice((2 * stream + 1) * LANES, (2 * stream + 2) * LANES)
                    nothing = jnp.zeros((width, LANES), jnp.bfloat16)
                    mixed[rows, left] = (
                        distil_ref[stream, number, 0] if head == OWN_HEAD[stream] else nothing
                    )
                    mixed[rows, right] = (
                        distil_ref[stream, number, 1 + index] if 0 <= index < 3 else nothing
                    )

    def normalize(micro):
        zero = jnp.zeros((1, LANES), jnp.float32)

        @pl.when(core == micro)
        def _():
            stats[0:2] = jnp.zeros((2, LANES), jnp.float32)

        def take(block):
            value = ahead.value(block)
            norm_ref[block] = value
            stats[0:1] += jnp.sum(value, axis=0, keepdims=True)
            stats[1:2] += jnp.sum(value * value, axis=0, keepdims=True)

        ahead.collect(micro, take)

        @pl.when(core == micro)
        def _():
            center = stats[0:1] / count
            inverse = lax.rsqrt(stats[1:2] / count - center * center + EPSILON)
            stats[2:3] = inverse

            def activate(chunk, _):
                for item in range(2):
                    block = 2 * chunk + item
                    normed = (norm_ref[block] - center) * inverse
                    norm_ref[block] = normed
                    out = normed * mine_ref[0:1] + mine_ref[1:2]
                    acts[upper, core, block] = (out * jax.nn.sigmoid(out)).astype(jnp.bfloat16)
                ahead.spread(chunk)
                return 0

            lax.fori_loop(0, 4, activate, 0)

    def own_copy(block, micro, slot, target):
        return push(
            own_stage.at[block, micro],
            own_got.at[slot, micro],
            own_sem.at[block, micro],
            own_recv.at[slot, micro],
            target,
            lane,
        )

    def send_own(micro):
        @pl.when(source)
        def _():
            own_got[place % 2, micro] = jnp.where(
                low, acts[0, micro, place], acts[1, micro, place]
            )

            def pack(step, _):
                block = (place + step) % 8
                own_stage[block, micro] = jnp.where(
                    low, acts[0, micro, block], acts[1, micro, block]
                )
                own_copy(block, micro, place % 2, block).start()
                return 0

            lax.fori_loop(1, 8, pack, 0)

    def act_value(block, micro):
        return jnp.concatenate([acts[half, micro, block] for half in range(2)], axis=1)

    def gate(micro):
        reduce.close(micro)
        for parity in range(2):
            @pl.when(2 * lane + parity != place)
            def _():
                own_copy(0, micro, parity, place).wait_recv()

        for stream, cot_ref in enumerate((depth_cot, segment_cot)):
            first = own_got[0, micro].astype(jnp.float32)
            second = own_got[1, micro].astype(jnp.float32)
            if stream == 0:
                second = pltpu.roll(second, half_width, 1)
            else:
                first = pltpu.roll(first, half_width, 1)
            own = jnp.where(low, first, second)
            column = 2 * stream * LANES
            gates = jax.nn.sigmoid(
                keep[micro, :, column : column + LANES] + bias_ref[stream : stream + 1]
            )
            message = keep[micro, :, column + LANES : column + 2 * LANES]
            cot = cot_ref[micro].astype(jnp.float32)
            out_ref = (depth_out, segment_out)[stream]
            out_ref[micro] = (own + gates * message).astype(jnp.bfloat16)
            gate_grad = (cot * message * gates * (1.0 - gates)).astype(jnp.bfloat16)
            bias_sum = jnp.sum(gate_grad.astype(jnp.float32), axis=0, keepdims=True)
            if micro == 0:
                gate_sums[stream : stream + 1] = bias_sum
            else:
                gate_sums[stream : stream + 1] += bias_sum
            grads_all[place, micro, :, column : column + LANES] = gate_grad
            grads_all[place, micro, :, column + LANES : column + 2 * LANES] = (cot * gates).astype(
                jnp.bfloat16
            )

    def distil_step(step, _):
        block, micro = reduce.block(step)
        fill_columns(act_value(block, micro), mask_ref[block, micro], turned, columns)
        part_ref[...] = jnp.dot(
            columns[0:PIXELS, 0 : 9 * 256], mixed[...], preferred_element_type=jnp.float32
        )
        reduce.step(step)

        @pl.when(step == 2)
        def _():
            normalize(1)

        @pl.when(step == 5)
        def _():
            ahead.relay(1)

        @pl.when(step == 6)
        def _():
            ahead.finish(1)
            ahead.sent()
            send_own(1)

        @pl.when(step == 11)
        def _():
            local.wait(3, 4)
            gate(0)
            gather_back.start(0)

        return 0

    distil_grad[...] = jnp.zeros_like(distil_grad)

    def back_step(step, _):
        block, micro = gather_back.next(step)
        fill_columns(
            grads_all[block, micro], mask_ref[block, micro], turned, columns, flip=True
        )
        part = jnp.dot(columns[0:PIXELS], mixed_back[...], preferred_element_type=jnp.float32)
        extra = cot_all[block, micro].astype(jnp.float32)
        part = jnp.concatenate(
            [
                part[:, :LANES] + jnp.where(low & source, extra, 0.0),
                part[:, LANES:] + jnp.where(low | ~source, 0.0, extra),
            ],
            axis=1,
        )
        behind.send(part.astype(jnp.bfloat16), block, micro)
        @pl.when(step == 10)
        def _():
            normalize_back(0)

        @pl.when(step == 13)
        def _():
            behind.relay(0)

        return 0

    def normalize_back(micro):
        @pl.when(core == micro)
        def _():
            stats[4:6] = jnp.zeros((2, LANES), jnp.float32)

        def take(block):
            normed = norm_ref[block]
            value = behind.value(block) * silu_slope(normed * mine_ref[0:1] + mine_ref[1:2])
            slope_ref[block] = value
            stats[4:5] += jnp.sum(value, axis=0, keepdims=True)
            stats[5:6] += jnp.sum(value * normed, axis=0, keepdims=True)

        behind.collect(micro, take)

        @pl.when(core == micro)
        def _():
            shift_sum, scale_sum = stats[4:5], stats[5:6]
            head_sums[0:1] = scale_sum
            head_sums[1:2] = shift_sum
            factor = mine_ref[0:1] * stats[2:3]

            def activate(chunk, _):
                for item in range(2):
                    block = 2 * chunk + item
                    value = slope_ref[block]
                    head_back[upper, core, block] = (
                        factor * (value - (shift_sum + norm_ref[block] * scale_sum) / count)
                    ).astype(jnp.bfloat16)
                behind.spread(chunk)
                return 0

            lax.fori_loop(0, 4, activate, 0)

    def head_value(block, micro):
        return jnp.concatenate([head_back[half, micro, block] for half in range(2)], axis=1)

    def weigh(block):
        for micro in range(2):
            fill_columns(
                grads_all[block, micro],
                mask_ref[block, micro],
                turned,
                columns,
                micro * PIXELS,
                True,
            )
        value = jnp.concatenate([act_value(block, micro) for micro in range(2)], axis=0).T
        width = half_width
        for number in range(9):
            product = jnp.dot(
                value,
                columns[:, number * 512 : (number + 1) * 512],
                preferred_element_type=jnp.float32,
            )
            for stream in range(2):
                for index in range(4):
                    head = OWN_HEAD[stream] if index == 0 else SOURCE_START[stream] + index - 1
                    column = (2 * stream + (index > 0)) * LANES
                    distil_grad[stream, number, index] += product[
                        head * width : (head + 1) * width, column : column + LANES
                    ]

    def block_step(step, _):
        block, micro = reduce.block(step)
        fill_columns(
            head_value(block, micro), mask_ref[block, micro], turned, columns, flip=True
        )
        part_ref[...] = jnp.dot(
            columns[0:PIXELS, 0 : 9 * 256],
            head_ref[...].reshape(9 * 256, 512),
            preferred_element_type=jnp.float32,
        )
        item, late = staggered(step)

        reduce.step(step)

        @pl.when(late == 1)
        def _():
            weigh(item)

        @pl.when(step == 2)
        def _():
            normalize_back(1)

        @pl.when(step == 5)
        def _():
            behind.relay(1)

        @pl.when(step == 6)
        def _():
            behind.finish(1)
            local.start(7)

        return 0

    def schedule(turn, _):
        phase, spot = (turn + 2) // 16, (turn + 2) % 16
        seam = (1 - (spot + 12) // 16) * ((phase + 3) // 4)
        odd = spot % 2
        kind = phase - seam * odd
        step = seam * (14 * odd + spot // 2) + (1 - seam) * (spot - 2)

        @pl.when(kind == 0)
        def _():
            forward_step(step, 0)

        @pl.when((kind == 1) & (step == 0))
        def _():
            ahead.finish(0)
            send_own(0)

        @pl.when(kind == 1)
        def _():
            distil_step(step, 0)

        @pl.when((kind == 2) & (step == 0))
        def _():
            local.wait(5)

        @pl.when((kind == 2) & (step == 6))
        def _():
            gate(1)
            gather_back.start(1)
            ahead.close()

        @pl.when(kind == 2)
        def _():
            back_step(step, 0)

        @pl.when((kind == 3) & (step == 0))
        def _():
            behind.finish(0)
            local.start(6)

        @pl.when(kind == 3)
        def _():
            block_step(step, 0)

        return 0

    lax.fori_loop(0, 66, schedule, 0)
    local.start(8)
    for micro in range(2):
        reduce.close(micro)
        back_out[micro_rows(micro)] = keep[micro]
    behind.sent()
    behind.close()
    gather.close()
    gather_back.close()

    @pl.when(source)
    def _():
        for micro in range(2):
            for step in range(1, 8):
                own_copy((place + step) % 8, micro, 0, place).wait_send()

    local.wait(6, 7, 8)


def run_middle(count, *arrays):
    f32, bf16 = jnp.float32, jnp.bfloat16
    block = (PIXELS, 512)
    dma = pltpu.SemaphoreType.DMA
    return pl.pallas_call(
        functools.partial(middle_kernel, count),
        name="middle",
        out_shape=(
            jax.ShapeDtypeStruct((2, PIXELS, LANES), bf16),
            jax.ShapeDtypeStruct((2, PIXELS, LANES), bf16),
            jax.ShapeDtypeStruct((2, LANES), f32),
            jax.ShapeDtypeStruct((2, LANES), f32),
            jax.ShapeDtypeStruct((2 * PIXELS, 512), f32),
            jax.ShapeDtypeStruct((8, 2) + block, bf16),
            jax.ShapeDtypeStruct((2, 2, 8, PIXELS, LANES), bf16),
            jax.ShapeDtypeStruct((2, 9, 4, 64, LANES), f32),
        ),
        in_specs=vmem(3) + anywhere(6),
        out_specs=tuple(vmem(5) + anywhere(3)),
        scratch_shapes=[
            pltpu.VMEM((2, 9, 4, 64, LANES), f32),
            pltpu.VMEM((8, 2) + block, bf16),
            pltpu.VMEM((2, 2, 8, PIXELS, LANES), bf16),
            pltpu.VMEM((9, 256, 512), bf16),
            pltpu.VMEM((2, 9, 4, 64, LANES), bf16),
            pltpu.VMEM((8, 2, PIXELS, LANES), bf16),
            pltpu.VMEM((2, PIXELS, LANES), bf16),
            pltpu.VMEM((2, PIXELS, LANES), bf16),
            pltpu.VMEM((8, 2, PIXELS, LANES), bf16),
            pltpu.VMEM((9 * 512, 256), bf16),
            pltpu.VMEM((9 * 256, 512), bf16),
            pltpu.VMEM((9 * 512, 256), bf16),
            pltpu.VMEM((3, 2 * PAD + PIXELS, 512), bf16),
            pltpu.VMEM((2 * PIXELS, 9 * 512), bf16),
            pltpu.VMEM((2, 2, 8, PIXELS, LANES), bf16),
            pltpu.VMEM((8, PIXELS, LANES), f32),
            pltpu.VMEM((8, PIXELS, LANES), f32),
            pltpu.VMEM((8, 2) + block, bf16),
            pltpu.VMEM((8, 2, PIXELS, LANES), bf16),
            pltpu.VMEM((2, 2, PIXELS, LANES), bf16),
            pltpu.VMEM((4, 8, PIXELS, LANES), bf16),
            pltpu.VMEM((4, 8, PIXELS, LANES), bf16),
            pltpu.VMEM(block, f32),
            pltpu.VMEM((2,) + block, f32),
            pltpu.VMEM((2, 4) + block, bf16),
            pltpu.VMEM((2, 4) + block, bf16),
            pltpu.VMEM((2, 3) + block, bf16),
            pltpu.VMEM((2, 5) + block, bf16),
            pltpu.VMEM((8, LANES), f32),
        ]
        + gather_sems(2) * 2
        + [dma((2, 4)), dma((2, 4)), dma((2, 3)), dma((2, 5))]
        + [dma((4, 8)), dma((4, 8))]
        + [dma((3, 4)), dma((2, 2, 4))] * 2
        + [dma((8, 2)), dma((2, 2)), dma((9,))],
        compiler_params=kernel_params(2),
    )(*arrays)


def finish_kernel(count, *refs):
    sources, targets, held = refs[:count], refs[count : 2 * count], refs[2 * count : 3 * count]
    sem_in, sem_out = refs[3 * count :]

    def parts(ref):
        large = len(ref.shape) > 2
        return [ref.at[number] for number in range(ref.shape[0])] if large else [ref]

    number = 0
    loads, stores = [], []
    for source, target, hold in zip(sources, targets, held):
        for pieces in zip(parts(source), parts(hold), parts(target)):
            loads.append(pltpu.make_async_copy(pieces[0], pieces[1], sem_in.at[number]))
            stores.append(pltpu.make_async_copy(pieces[1], pieces[2], sem_out.at[number]))
            number += 1
    for load in loads:
        load.start()
    for load, store in zip(loads, stores):
        load.wait()
        store.start()
    for store in stores:
        store.wait()


def run_finish(*arrays):
    anywhere = [pl.BlockSpec(memory_space=pltpu.HBM)] * len(arrays)
    copies = sum(item.shape[0] if item.ndim > 2 else 1 for item in arrays)
    return pl.pallas_call(
        functools.partial(finish_kernel, len(arrays)),
        name="finish",
        out_shape=tuple(jax.ShapeDtypeStruct(item.shape, item.dtype) for item in arrays),
        in_specs=anywhere,
        out_specs=tuple(anywhere),
        scratch_shapes=[pltpu.VMEM(item.shape, item.dtype) for item in arrays]
        + [pltpu.SemaphoreType.DMA((copies,))] * 2,
        compiler_params=pltpu.CompilerParams(vmem_limit_bytes=60 * 2**20),
    )(*arrays)


def stationary_local(
    features,
    image_ids,
    reduce_weight,
    spatial_weight,
    expand_weight,
    head_weights,
    distil_weights,
    block_scale,
    block_shift,
    head_scale,
    head_shift,
    gate_bias,
    output_scale,
    output_shift,
    depth_cotangent,
    segment_cotangent,
):
    canvases, row_count, column_count = image_ids.shape
    pixels = row_count * column_count
    count = float(lax.axis_size("batch") * pixels)
    x = features.reshape(canvases, pixels, -1)
    cots = [item.reshape(canvases, pixels, LANES) for item in (depth_cotangent, segment_cotangent)]
    block_params = (block_scale, block_shift)
    output_params = (output_scale[None], output_shift[None])
    (
        block_out,
        norm3,
        inverse3,
        norm12,
        inverse12,
        mine,
        mask,
        act1,
        act2,
        reduce_all,
        spatial_all,
        expand_all,
        mask_all,
        cot_all,
        raw,
    ) = run_front(
        count,
        x,
        image_ids,
        reduce_weight.T,
        spatial_weight,
        expand_weight,
        *block_params,
        *output_params,
        head_scale,
        head_shift,
        *cots,
    )
    depth_out, segment_out, gate_sums, head_sums, block_grad, block_all, back_all, distil_grad = run_middle(
        count,
        block_out,
        gate_bias,
        mine,
        head_weights.transpose(0, 2, 3, 1).reshape(9, -1, head_weights.shape[1]),
        distil_weights,
        mask_all,
        *cots,
        cot_all,
    )
    (
        features_grad,
        reduce_grad,
        spatial_grad,
        expand_grad,
        block_scale_grad,
        block_shift_grad,
        head_scale_grad,
        head_shift_grad,
        gate_grad,
        output_scale_grad,
        output_shift_grad,
        heads_grad,
    ) = run_rear(
        count,
        block_grad,
        x,
        norm3,
        inverse3,
        norm12,
        inverse12,
        mask,
        *block_params,
        *output_params,
        head_sums,
        gate_sums,
        block_all,
        back_all,
        mask_all,
        act1,
        act2,
        reduce_all,
        spatial_all,
        expand_all,
        raw,
    )
    outs = run_finish(
        depth_out,
        segment_out,
        features_grad,
        reduce_grad,
        spatial_grad,
        expand_grad,
        heads_grad,
        distil_grad,
        block_scale_grad,
        block_shift_grad,
        head_scale_grad,
        head_shift_grad,
        gate_grad,
        output_scale_grad,
        output_shift_grad,
    )
    heads_grad = outs[6].reshape(9, 4, -1, head_weights.shape[1]).transpose(0, 3, 1, 2)
    return (
        outs[0].reshape(depth_cotangent.shape),
        outs[1].reshape(depth_cotangent.shape),
        outs[2].reshape(features.shape),
        outs[3].T,
        *outs[4:6],
        heads_grad,
        *outs[7:13],
        outs[13][0],
        outs[14][0],
    )


def solution(mesh):
    fits = dict(mesh.shape) == {"batch": 8, "chan": 4}
    local = stationary_local if fits else gathered_local
    placed = (
        P("batch", None, None, "chan"),
        P("batch", None, None),
        P("chan", "batch"),
        P(None, "batch", "chan"),
        P("batch", "chan"),
        P(None, "chan", None, "batch"),
        P(None, None, None, "batch", "chan"),
        P(None, "chan"),
        P(None, "chan"),
        P(None, "chan"),
        P(None, "chan"),
        P(None, "chan"),
        P("chan"),
        P("chan"),
        P("batch", None, None, "chan"),
        P("batch", None, None, "chan"),
    )
    return jax.shard_map(
        local,
        mesh=mesh,
        in_specs=placed,
        out_specs=(
            P("batch", None, None, "chan"),
            P("batch", None, None, "chan"),
            P("batch", None, None, "chan"),
            P("chan", "batch"),
            P(None, "batch", "chan"),
            P("batch", "chan"),
            P(None, "chan", None, "batch"),
            P(None, None, None, "batch", "chan"),
            P(None, "chan"),
            P(None, "chan"),
            P(None, "chan"),
            P(None, "chan"),
            P(None, "chan"),
            P("chan"),
            P("chan"),
        ),
        check_vma=False,
    )
```

```python
import functools

import jax
import jax.numpy as jnp
from jax import lax
from jax.experimental import pallas as pl
from jax.experimental.pallas import tpu as pltpu
from jax.sharding import PartitionSpec as P

EPSILON = 1e-05
OFFSETS = ((-1, -1), (-1, 0), (-1, 1), (0, -1), (0, 0), (0, 1), (1, -1), (1, 0), (1, 1))
OWN_HEAD = (0, 3)
SOURCE_START = (1, 0)


def silu_slope(values):
    sig = jax.nn.sigmoid(values)
    return sig * (1.0 + values * (1.0 - sig))


def shifted(values, vertical, lateral):
    row_count, column_count = (values.shape[1], values.shape[2])
    widths = [(0, 0)] * values.ndim
    widths[1] = (1, 1)
    widths[2] = (1, 1)
    padded = jnp.pad(values, widths)
    return padded[
        :, 1 + vertical : 1 + vertical + row_count, 1 + lateral : 1 + lateral + column_count
    ]


def tap_masks(image_ids):
    row_count, column_count = (image_ids.shape[1], image_ids.shape[2])
    padded = jnp.pad(image_ids, ((0, 0), (1, 1), (1, 1)), constant_values=-1)
    masks = []
    for vertical, lateral in OFFSETS:
        beside = padded[
            :, 1 + vertical : 1 + vertical + row_count, 1 + lateral : 1 + lateral + column_count
        ]
        masks.append((beside == image_ids).astype(jnp.float32))
    return jnp.stack(masks)


def conv_forward(inputs, weight, masks):
    total = 0.0
    for number, (vertical, lateral) in enumerate(OFFSETS):
        moved = shifted(inputs, vertical, lateral) * masks[number][..., None].astype(inputs.dtype)
        total = total + jnp.einsum(
            "nhwc,co->nhwo", moved, weight[number], preferred_element_type=jnp.float32
        )
    return total


def conv_input_grad(grads, weight, masks):
    total = 0.0
    for number, (vertical, lateral) in enumerate(OFFSETS):
        term = jnp.einsum(
            "nhwo,co->nhwc", grads, weight[number], preferred_element_type=jnp.float32
        )
        total = total + shifted(term * masks[number][..., None], -vertical, -lateral)
    return total


def conv_weight_grad(inputs, grads, masks):
    pieces = []
    for number, (vertical, lateral) in enumerate(OFFSETS):
        moved = shifted(inputs, vertical, lateral) * masks[number][..., None].astype(inputs.dtype)
        pieces.append(jnp.einsum("nhwc,nhwo->co", moved, grads, preferred_element_type=jnp.float32))
    return jnp.stack(pieces)


def pixel_sum(values):
    return jnp.sum(values, axis=(0, 1, 2))


def normalize(values, scale, shift, count):
    total, squares = lax.psum((pixel_sum(values), pixel_sum(values * values)), "batch")
    center = total / count
    inverse = lax.rsqrt(squares / count - center * center + EPSILON)
    normed = (values - center) * inverse
    return (normed, inverse, normed * scale + shift)


def grad_sums(first_sum, second_sum):
    return lax.psum((first_sum, second_sum), "batch")


def normalize_back(grads, normed, inverse, scale, shift_sum, scale_sum, count):
    return scale * inverse * (grads - (shift_sum + normed * scale_sum) / count)


def channel_gather(values):
    return lax.all_gather(values, "chan", axis=4, tiled=True)


def channel_sum(values):
    return lax.psum_scatter(
        values.astype(jnp.bfloat16), "chan", scatter_dimension=4, tiled=True
    ).astype(jnp.float32)


def fetch_weights(reduce_weight, spatial_weight, expand_weight, head_weights, distil_weights):
    return (
        lax.all_gather(reduce_weight, "batch", axis=1, tiled=True),
        lax.all_gather(spatial_weight, "batch", axis=1, tiled=True),
        lax.all_gather(expand_weight, "batch", axis=0, tiled=True),
        lax.all_gather(head_weights, "batch", axis=3, tiled=True),
        lax.all_gather(distil_weights, "batch", axis=3, tiled=True),
    )


def scatter_weights(grads):
    reduce_grad, spatial_grad, expand_grad, heads_grad, distil_grad = grads
    return (
        lax.psum_scatter(reduce_grad, "batch", scatter_dimension=1, tiled=True),
        lax.psum_scatter(spatial_grad, "batch", scatter_dimension=1, tiled=True),
        lax.psum_scatter(expand_grad, "batch", scatter_dimension=0, tiled=True),
        lax.psum_scatter(heads_grad, "batch", scatter_dimension=3, tiled=True),
        lax.psum_scatter(distil_grad, "batch", scatter_dimension=3, tiled=True),
    )


def micro_step(inputs, image_ids, depth_cot, segment_cot, gathered, small, batch_count):
    reduce_full, spatial_full, expand_full, heads_full, distil_full = gathered
    block_scale, block_shift, head_scale, head_shift, gate_bias, output_scale, output_shift = small
    masks = tap_masks(image_ids)
    canvases, row_count, column_count = image_ids.shape
    count = float(batch_count * canvases * row_count * column_count)
    first_partial = jnp.einsum(
        "nhwc,co->nhwo", inputs, reduce_full, preferred_element_type=jnp.float32
    )
    first = channel_sum(first_partial[:, :, :, None, :])
    first_norm, first_inv, first_out = normalize(first, block_scale[0:1], block_shift[0:1], count)
    first_act = jax.nn.silu(first_out).astype(jnp.bfloat16)
    first_full = channel_gather(first_act)[:, :, :, 0, :]
    second = conv_forward(first_full, spatial_full, masks)[:, :, :, None, :]
    second_norm, second_inv, second_out = normalize(
        second, block_scale[1:2], block_shift[1:2], count
    )
    second_act = jax.nn.silu(second_out).astype(jnp.bfloat16)
    second_full = channel_gather(second_act)[:, :, :, 0, :]
    third = jnp.einsum(
        "nhwc,co->nhwo", second_full, expand_full, preferred_element_type=jnp.float32
    )[:, :, :, None, :]
    third_norm, third_inv, third_out = normalize(
        third, output_scale[None], output_shift[None], count
    )
    summed = third_out[:, :, :, 0, :] + inputs.astype(jnp.float32)
    block_out = jax.nn.silu(summed).astype(jnp.bfloat16)
    heads_flat = heads_full.reshape(heads_full.shape[0], heads_full.shape[1], -1)
    head_partial = conv_forward(block_out, heads_flat, masks)
    head_pre = channel_sum(
        head_partial.reshape(head_partial.shape[:3] + (heads_full.shape[2], heads_full.shape[3]))
    )
    head_norm, head_inv, head_out = normalize(head_pre, head_scale, head_shift, count)
    head_act = jax.nn.silu(head_out).astype(jnp.bfloat16)
    head_full = channel_gather(head_act)
    head_width = head_full.shape[4]
    gate_pre = [0.0, 0.0]
    message = [0.0, 0.0]
    for number, (vertical, lateral) in enumerate(OFFSETS):
        moved = shifted(head_full, vertical, lateral) * masks[number][:, :, :, None, None].astype(
            jnp.bfloat16
        )
        for stream in range(2):
            weights_here = distil_full[stream, number]
            first_source = SOURCE_START[stream]
            sources = moved[:, :, :, first_source : first_source + 3].reshape(
                moved.shape[:3] + (3 * head_width,)
            )
            gate_pre[stream] = gate_pre[stream] + jnp.einsum(
                "nhwc,co->nhwo",
                moved[:, :, :, OWN_HEAD[stream]],
                weights_here[0],
                preferred_element_type=jnp.float32,
            )
            message[stream] = message[stream] + jnp.einsum(
                "nhwc,co->nhwo",
                sources,
                weights_here[1:].reshape(3 * head_width, -1),
                preferred_element_type=jnp.float32,
            )
    cotangents = (depth_cot.astype(jnp.float32), segment_cot.astype(jnp.float32))
    outputs, message_grads, gate_grads = ([], [], [])
    for stream in range(2):
        gate_value = jax.nn.sigmoid(gate_pre[stream] + gate_bias[stream])
        own_feature = head_act[:, :, :, OWN_HEAD[stream]].astype(jnp.float32)
        outputs.append((own_feature + gate_value * message[stream]).astype(jnp.bfloat16))
        message_grads.append((cotangents[stream] * gate_value).astype(jnp.bfloat16))
        gate_grads.append(
            (cotangents[stream] * message[stream] * gate_value * (1.0 - gate_value)).astype(
                jnp.bfloat16
            )
        )
    spread_grad = 0.0
    distil_parts = [[], []]
    for number, (vertical, lateral) in enumerate(OFFSETS):
        tap_mask = masks[number][:, :, :, None, None]
        moved = shifted(head_full, vertical, lateral) * tap_mask.astype(jnp.bfloat16)
        tap_grad = jnp.zeros(head_full.shape, jnp.float32)
        for stream in range(2):
            weights_here = distil_full[stream, number]
            first_source = SOURCE_START[stream]
            sources = moved[:, :, :, first_source : first_source + 3].reshape(
                moved.shape[:3] + (3 * head_width,)
            )
            own_grad = jnp.einsum(
                "nhwo,co->nhwc",
                gate_grads[stream],
                weights_here[0],
                preferred_element_type=jnp.float32,
            )
            source_grad = jnp.einsum(
                "nhwo,co->nhwc",
                message_grads[stream],
                weights_here[1:].reshape(3 * head_width, -1),
                preferred_element_type=jnp.float32,
            )
            tap_grad = tap_grad.at[:, :, :, OWN_HEAD[stream]].add(own_grad)
            tap_grad = tap_grad.at[:, :, :, first_source : first_source + 3].add(
                source_grad.reshape(source_grad.shape[:3] + (3, head_width))
            )
            gate_weight_grad = jnp.einsum(
                "nhwc,nhwo->co",
                moved[:, :, :, OWN_HEAD[stream]],
                gate_grads[stream],
                preferred_element_type=jnp.float32,
            )
            source_weight_grad = jnp.einsum(
                "nhwc,nhwo->co", sources, message_grads[stream], preferred_element_type=jnp.float32
            )
            distil_parts[stream].append(
                jnp.concatenate(
                    [gate_weight_grad[None], source_weight_grad.reshape(3, head_width, -1)], axis=0
                )
            )
        spread_grad = spread_grad + shifted(tap_grad * tap_mask, -vertical, -lateral)
    distil_grad = jnp.stack([jnp.stack(distil_parts[0]), jnp.stack(distil_parts[1])])
    head_grad = channel_sum(spread_grad)
    head_grad = (
        head_grad.at[:, :, :, OWN_HEAD[0]]
        .add(cotangents[0])
        .at[:, :, :, OWN_HEAD[1]]
        .add(cotangents[1])
    )
    head_grad = head_grad * silu_slope(head_out)
    gate_sums = jnp.stack(
        [pixel_sum(gate_grads[0].astype(jnp.float32)), pixel_sum(gate_grads[1].astype(jnp.float32))]
    )
    shift_sums, scale_sums = grad_sums(
        jnp.concatenate([pixel_sum(head_grad), gate_sums], axis=0), pixel_sum(head_grad * head_norm)
    )
    head_pre_grad = normalize_back(
        head_grad, head_norm, head_inv, head_scale, shift_sums[:4], scale_sums, count
    ).astype(jnp.bfloat16)
    head_pre_full = channel_gather(head_pre_grad)
    head_flat_grad = head_pre_full.reshape(head_pre_full.shape[:3] + (-1,))
    block_grad = conv_input_grad(head_flat_grad, heads_flat, masks)
    heads_grad = conv_weight_grad(block_out, head_flat_grad, masks).reshape(heads_full.shape)
    summed_grad = block_grad * silu_slope(summed)
    third_grad = summed_grad[:, :, :, None, :]
    third_shift, third_scale = grad_sums(pixel_sum(third_grad), pixel_sum(third_grad * third_norm))
    third_pre = normalize_back(
        third_grad, third_norm, third_inv, output_scale[None], third_shift, third_scale, count
    ).astype(jnp.bfloat16)[:, :, :, 0, :]
    expand_grad = jnp.einsum(
        "nhwc,nhwo->co", second_full, third_pre, preferred_element_type=jnp.float32
    )
    second_grad = channel_sum(
        jnp.einsum("nhwo,co->nhwc", third_pre, expand_full, preferred_element_type=jnp.float32)[
            :, :, :, None, :
        ]
    )
    second_grad = second_grad * silu_slope(second_out)
    second_shift, second_scale = grad_sums(
        pixel_sum(second_grad), pixel_sum(second_grad * second_norm)
    )
    second_pre = normalize_back(
        second_grad, second_norm, second_inv, block_scale[1:2], second_shift, second_scale, count
    ).astype(jnp.bfloat16)[:, :, :, 0, :]
    spatial_grad = conv_weight_grad(first_full, second_pre, masks)
    first_grad = channel_sum(conv_input_grad(second_pre, spatial_full, masks)[:, :, :, None, :])
    first_grad = first_grad * silu_slope(first_out)
    first_shift, first_scale = grad_sums(pixel_sum(first_grad), pixel_sum(first_grad * first_norm))
    first_pre = normalize_back(
        first_grad, first_norm, first_inv, block_scale[0:1], first_shift, first_scale, count
    ).astype(jnp.bfloat16)
    first_pre_full = channel_gather(first_pre)[:, :, :, 0, :]
    reduce_grad = jnp.einsum(
        "nhwc,nhwo->co", inputs, first_pre_full, preferred_element_type=jnp.float32
    )
    input_grad = summed_grad + jnp.einsum(
        "nhwo,co->nhwc", first_pre_full, reduce_full, preferred_element_type=jnp.float32
    )
    weight_grads = (reduce_grad, spatial_grad, expand_grad, heads_grad, distil_grad)
    small_grads = (
        jnp.concatenate([first_scale, second_scale], axis=0),
        jnp.concatenate([first_shift, second_shift], axis=0),
        scale_sums,
        shift_sums[:4],
        shift_sums[4:],
        third_scale[0],
        third_shift[0],
    )
    return (outputs[0], outputs[1], input_grad, weight_grads, small_grads)


def gathered_local(
    features,
    image_ids,
    reduce_weight,
    spatial_weight,
    expand_weight,
    head_weights,
    distil_weights,
    block_scale,
    block_shift,
    head_scale,
    head_shift,
    gate_bias,
    output_scale,
    output_shift,
    depth_cotangent,
    segment_cotangent,
):
    batch_count = lax.axis_size("batch")
    small = (
        block_scale,
        block_shift,
        head_scale,
        head_shift,
        gate_bias,
        output_scale,
        output_shift,
    )
    depth_list, segment_list, input_list = ([], [], [])
    weight_total = None
    small_total = None
    for micro_index in range(features.shape[0]):
        gathered = fetch_weights(
            reduce_weight, spatial_weight, expand_weight, head_weights, distil_weights
        )
        canvas_pick = slice(micro_index, micro_index + 1)
        depth_out, segment_out, input_grad, weight_grads, small_grads = micro_step(
            features[canvas_pick],
            image_ids[canvas_pick],
            depth_cotangent[canvas_pick],
            segment_cotangent[canvas_pick],
            gathered,
            small,
            batch_count,
        )
        weight_grads = scatter_weights(weight_grads)
        weight_total = (
            weight_grads
            if weight_total is None
            else jax.tree.map(jnp.add, weight_total, weight_grads)
        )
        small_total = (
            small_grads if small_total is None else jax.tree.map(jnp.add, small_total, small_grads)
        )
        depth_list.append(depth_out)
        segment_list.append(segment_out)
        input_list.append(input_grad)
    reduce_grad, spatial_grad, expand_grad, heads_grad, distil_grad = weight_total
    scale_mid, shift_mid, scale_heads, shift_heads, bias_gates, scale_out, shift_out = small_total
    return (
        jnp.concatenate(depth_list, axis=0),
        jnp.concatenate(segment_list, axis=0),
        jnp.concatenate(input_list, axis=0),
        reduce_grad,
        spatial_grad,
        expand_grad,
        heads_grad,
        distil_grad,
        scale_mid,
        shift_mid,
        scale_heads,
        shift_heads,
        bias_gates,
        scale_out,
        shift_out,
    )


MESH = pl.DeviceIdType.MESH
PIXELS = 256
PAD = 32
LANES = 128


def whereabouts():
    place, lane = lax.axis_index("batch"), lax.axis_index("chan")
    return place, lane, place // 2, place % 2, lane // 2, lane % 2


def ranked(depth, rank):
    high, low = depth // 2, depth % 2
    up, odd = rank // 2, rank % 2
    return (
        (1 - odd) * (1 - up) * depth
        + odd * (1 - up) * (1 + low)
        + (1 - odd) * up * (2 - 2 * low + high)
        + odd * up * (3 - 3 * high)
    )


def middle(depth):
    return (depth // 2 + depth % 2) % 2


def inner(depth):
    return 1 + depth % 2


def outer(depth):
    return 3 * (depth // 2)


def onward(depth, rank):
    second = (1 - rank % 2) * (rank // 2)
    return outer(depth) + second * (3 - depth - outer(depth))


def homeward(depth, rank):
    second = (1 - rank % 2) * (rank // 2) * middle(depth)
    return inner(depth) + second * (outer(depth) - inner(depth))


def staggered(step):
    late = ((step + 1) % 2) * ((step + 14) // 15) + step // 15
    return (1 - late) * ((step + 1) // 2) + late * (step // 2 - 1 + step // 15), late


def push(source, target, send_sem, recv_sem, place, lane):
    return pltpu.make_async_remote_copy(
        src_ref=source,
        dst_ref=target,
        send_sem=send_sem,
        recv_sem=recv_sem,
        device_id=(place, lane),
        device_id_type=MESH,
    )


def announce(peers):
    barrier = pltpu.get_barrier_semaphore()
    for place, lane in peers:
        pl.semaphore_signal(barrier, inc=1, device_id=(place, lane), device_id_type=MESH)


def gathered_peers(peers):
    pl.semaphore_wait(pltpu.get_barrier_semaphore(), len(peers))


def greet(peers):
    announce(peers)
    gathered_peers(peers)


def batch_peers():
    place, lane, _, _, _, _ = whereabouts()
    return [((place + step) % 8, lane) for step in range(1, 8)]


def line_peers():
    place, lane, depth, side, _, _ = whereabouts()
    peers = [(ranked(depth, rank) * 2 + side, lane) for rank in range(1, 4)]
    return peers + [(depth * 2 + 1 - side, lane)]


def chan_peers():
    place, lane, _, _, _, _ = whereabouts()
    return [(place, (lane + step) % 4) for step in range(1, 4)]


class Gather:
    def __init__(self, values, recv, cross, line, parts, direct=False):
        self.values, self.recv, self.cross, self.line = values, recv, cross, line
        self.parts, self.direct = parts, direct

    def view(self, block, part):
        return self.values.at[block] if self.parts == 1 else self.values.at[block, part]

    def copy(self, block, part, sem, depth, side):
        lane = lax.axis_index("chan")
        here = self.view(block, part)
        return push(here, here, sem, self.recv.at[block, part], depth * 2 + side, lane)

    def start(self, part=0):
        place, lane, depth, side, _, _ = whereabouts()
        if self.direct:
            self.copy(place, part, self.cross.at[0, part], depth, 1 - side).start()
            for rank in range(1, 4):
                self.copy(
                    place, part, self.line.at[0, rank, part], ranked(depth, rank), side
                ).start()
            return
        self.copy(place, part, self.line.at[0, 0, part], inner(depth), side).start()

        @pl.when(middle(depth) == 1)
        def _():
            self.copy(place, part, self.line.at[1, 0, part], outer(depth), side).start()

        self.copy(place, part, self.cross.at[0, part], depth, 1 - side).start()

    def near(self, rank, part=0):
        place, lane, depth, side, _, _ = whereabouts()
        block = ranked(depth, rank) * 2 + side
        self.copy(block, part, self.cross.at[rank, part], depth, side).wait_recv()

        if not self.direct:

            @pl.when(middle(depth) == 1)
            def _():
                self.copy(
                    block, part, self.line.at[0, rank, part], onward(depth, rank), side
                ).start()

        self.copy(block, part, self.cross.at[rank, part], depth, 1 - side).start()

    def far(self, rank, part=0):
        place, lane, depth, side, _, _ = whereabouts()
        block = ranked(depth, rank) * 2 + 1 - side
        self.copy(block, part, self.cross.at[rank, part], depth, side).wait_recv()

    def next(self, step):
        place, lane, depth, side, _, _ = whereabouts()
        item, late = staggered(step)
        part, rank = item // 4, item % 4

        @pl.when((late == 0) & (rank > 0))
        def _():
            self.near(rank, part)

        @pl.when(late == 1)
        def _():
            self.far(rank, part)

        return ranked(depth, rank) * 2 + (side + late) % 2, part

    def close(self):
        place, lane, depth, side, _, _ = whereabouts()
        for part in range(self.parts):
            for rank in range(4):
                self.copy(place, part, self.cross.at[rank, part], depth, side).wait_send()
            if self.direct:
                for rank in range(1, 4):
                    self.copy(place, part, self.line.at[0, rank, part], depth, side).wait_send()
                continue
            self.copy(place, part, self.line.at[0, 0, part], depth, side).wait_send()

            @pl.when(middle(depth) == 1)
            def _():
                self.copy(place, part, self.line.at[1, 0, part], depth, side).wait_send()
                for rank in range(1, 4):
                    self.copy(place, part, self.line.at[0, rank, part], depth, side).wait_send()


def gather_sems(parts):
    return [
        pltpu.SemaphoreType.DMA((8, parts)),
        pltpu.SemaphoreType.DMA((4, parts)),
        pltpu.SemaphoreType.DMA((2, 4, parts)),
    ]


def clear_edges(turned):
    edge = jnp.zeros((3, PAD, turned.shape[2]), turned.dtype)
    turned[:, 0:PAD] = edge
    turned[:, PAD + PIXELS :] = edge


def fill_columns(value, mask, turned, columns, row=0, flip=False):
    width = value.shape[1]
    lanes = slice(0, width)
    wide = value.astype(jnp.float32)
    inside = slice(PAD, PAD + PIXELS)
    turned[0, inside, lanes] = pltpu.roll(wide, 1, 0).astype(jnp.bfloat16)
    turned[1, inside, lanes] = value
    turned[2, inside, lanes] = pltpu.roll(wide, PIXELS - 1, 0).astype(jnp.bfloat16)
    for number, (vertical, lateral) in enumerate(OFFSETS):
        start = PAD + 32 * vertical
        slot = 8 - number if flip else number
        columns[row : row + PIXELS, slot * width : (slot + 1) * width] = (
            turned[lateral + 1, start : start + PIXELS, lanes] * mask[:, number : number + 1]
        )


def vmem(count):
    return [pl.BlockSpec(memory_space=pltpu.VMEM)] * count


def kernel_params(number):
    return pltpu.CompilerParams(
        collective_id=number, has_side_effects=True, vmem_limit_bytes=60 * 2**20
    )


class Exchange:
    def __init__(self, values, send, recv, axis):
        self.values, self.send, self.recv, self.axis = values, send, recv, axis

    def steps(self):
        place, lane, _, _, _, _ = whereabouts()
        if self.axis == "batch":
            return [(step - 1, (place + step) % 8, lane, (place + step) % 8) for step in range(1, 8)]
        return [(step - 1, place, (lane + step) % 4, (lane + step) % 4) for step in range(1, 4)]

    def mine(self):
        place, lane, _, _, _, _ = whereabouts()
        return place if self.axis == "batch" else lane

    def start(self):
        here = self.values.at[self.mine()]
        for number, place, lane, _ in self.steps():
            push(here, here, self.send.at[number], self.recv.at[self.mine()], place, lane).start()

    def wait(self):
        for number, place, lane, slot in self.steps():
            there = self.values.at[slot]
            push(there, there, self.send.at[number], self.recv.at[slot], place, lane).wait_recv()

    def close(self):
        here = self.values.at[self.mine()]
        for number, place, lane, _ in self.steps():
            push(here, here, self.send.at[number], self.recv.at[self.mine()], place, lane).wait_send()

    def total(self):
        result = self.values[0]
        for slot in range(1, self.values.shape[0]):
            result = result + self.values[slot]
        return result


class Pieces:
    def __init__(self, stage, got, send, recv):
        self.stage, self.got, self.send, self.recv = stage, got, send, recv

    def start(self, part):
        place, lane, _, _, _, _ = whereabouts()
        for slot in range(4):
            self.stage[slot] = part[:, slot * LANES : (slot + 1) * LANES].astype(jnp.bfloat16)
        for step in (2, 1, 3):
            slot = (lane + step) % 4
            push(
                self.stage.at[slot],
                self.got.at[lane],
                self.send.at[slot],
                self.recv.at[lane],
                place,
                slot,
            ).start()

    def finish(self):
        place, lane, _, _, _, _ = whereabouts()
        self.got[lane] = self.stage[lane]
        for step in range(1, 4):
            slot = (lane + step) % 4
            push(
                self.stage.at[slot],
                self.got.at[slot],
                self.send.at[slot],
                self.recv.at[slot],
                place,
                lane,
            ).wait()
        result = self.got[0].astype(jnp.float32)
        for slot in range(1, 4):
            result = result + self.got[slot].astype(jnp.float32)
        return result


class Local:
    def __init__(self, pairs, sems):
        self.copies = [
            pltpu.make_async_copy(source, target, sems.at[number])
            for number, (source, target) in enumerate(pairs)
        ]

    def start(self, *numbers):
        for number in numbers:
            self.copies[number].start()

    def wait(self, *numbers):
        for number in numbers:
            self.copies[number].wait()


def anywhere(count):
    return [pl.BlockSpec(memory_space=pl.ANY)] * count


def micro_rows(micro):
    return slice(micro * PIXELS, (micro + 1) * PIXELS)


def moments(value, other):
    rows = []
    for micro in range(2):
        part = value[micro_rows(micro)]
        rows.append(jnp.sum(part, axis=0, keepdims=True))
        rows.append(jnp.sum(part * other[micro_rows(micro)], axis=0, keepdims=True))
    return rows


def tile_rows(rows, height):
    width = rows[0].shape[1]
    return jnp.concatenate(rows + [jnp.zeros((height - len(rows), width), jnp.float32)], axis=0)


def normed_part(value, totals, micro, count):
    center = totals[2 * micro : 2 * micro + 1] / count
    inverse = lax.rsqrt(totals[2 * micro + 1 : 2 * micro + 2] / count - center * center + EPSILON)
    return (value[micro_rows(micro)] - center) * inverse, inverse


def dot_last(first, second):
    return lax.dot_general(
        first, second, (((1,), (1,)), ((), ())), preferred_element_type=jnp.float32
    )


def make_masks(ids_ref, mask_all):
    rows = 8 * ids_ref.shape[0]
    ids = ids_ref[...].reshape(rows, PIXELS).T
    pixel = lax.broadcasted_iota(jnp.int32, (PIXELS, rows), 0)
    taps = []
    for vertical, lateral in OFFSETS:
        offset = 32 * vertical + lateral
        beside = ids if offset == 0 else pltpu.roll(ids, (-offset) % PIXELS, 0)
        row, col = (pixel >> 5) + vertical, (pixel & 31) + lateral
        inside = (row >= 0) & (row < 8) & (col >= 0) & (col < 32)
        taps.append(jnp.where(inside & (beside == ids), 1.0, 0.0).astype(jnp.bfloat16))
    taps = jnp.concatenate(taps + [jnp.zeros_like(taps[0])], axis=1)
    item = lax.broadcasted_iota(jnp.int32, (10 * rows, LANES), 0)
    lane = lax.broadcasted_iota(jnp.int32, (10 * rows, LANES), 1)
    for block in range(8):
        for micro in range(2):
            chosen = jnp.where(item == lane * rows + (8 * block + micro), 1.0, 0.0)
            mask_all[block, micro] = jnp.dot(
                taps, chosen.astype(jnp.bfloat16), preferred_element_type=jnp.float32
            ).astype(jnp.bfloat16)


def front_kernel(
    count,
    x_ref,
    ids_ref,
    reduce_ref,
    spatial_ref,
    expand_ref,
    block_scale,
    block_shift,
    output_scale,
    output_shift,
    head_scale,
    head_shift,
    depth_cot,
    segment_cot,
    y_ref,
    norm3_ref,
    inverse3_ref,
    norm12_ref,
    inverse12_ref,
    mine_ref,
    mask_ref,
    act1_out,
    act2_out,
    reduce_out,
    spatial_out,
    expand_out,
    mask_out,
    cot_out,
    raw_out,
    act1_ref,
    act2_ref,
    reduce_all,
    spatial_all,
    expand_all,
    mask_all,
    cot_all,
    packed,
    turned,
    columns,
    stage,
    got,
    sums1,
    sums2,
    sums3,
    head_all,
    ids_all,
    raw1,
    raw2,
    fits1,
    fits2,
    *sems,
):
    place, lane, depth, side, upper, core = whereabouts()
    reduces = Gather(reduce_all, *sems[0:3], 1, True)
    spatials = Gather(spatial_all, *sems[3:6], 1)
    expands = Gather(expand_all, *sems[6:9], 1)
    ids = Exchange(ids_all, sems[9], sems[10], "batch")
    pieces = Pieces(stage, got, sems[11], sems[12])
    first_sums = Exchange(sums1, sems[13], sems[14], "batch")
    second_sums = Exchange(sums2, sems[15], sems[16], "batch")
    third_sums = Exchange(sums3, sems[17], sems[18], "batch")
    heads = Exchange(head_all, sems[19], sems[20], "chan")
    first_raw = Exchange(raw1, sems[21], sems[22], "chan")
    second_raw = Exchange(raw2, sems[23], sems[24], "chan")
    first_fits = Exchange(fits1, sems[28], sems[29], "chan")
    second_fits = Exchange(fits2, sems[30], sems[31], "chan")

    def centered(value, raw):
        rows = moments(value, value)
        for micro in range(2):
            raw[lane, micro_rows(micro)] = (
                value[micro_rows(micro)] - rows[2 * micro] / PIXELS
            ).astype(jnp.bfloat16)
        return rows

    def fit(value, rows, totals, layer, fits):
        inverses, offsets, lines = [], [], []
        for micro in range(2):
            normed, inverse = normed_part(value, totals, micro, count)
            norm12_ref[layer, micro_rows(micro)] = normed
            inverses.append(inverse)
            slope = inverse * block_scale[layer : layer + 1]
            center = totals[2 * micro : 2 * micro + 1] / count
            offset = rows[2 * micro] / PIXELS - center
            offsets.append(offset * inverse)
            lines.append(slope)
            lines.append(offset * slope + block_shift[layer : layer + 1])
        fits[lane] = tile_rows(lines, 8)
        return inverses, offsets

    def activate(raw, fits, act):
        for slot in range(4):
            for micro in range(2):
                out = (
                    raw[slot, micro_rows(micro)].astype(jnp.float32)
                    * fits[slot, 2 * micro : 2 * micro + 1]
                    + fits[slot, 2 * micro + 1 : 2 * micro + 2]
                )
                act[slot, micro_rows(micro)] = (out * jax.nn.sigmoid(out)).astype(jnp.bfloat16)


    local = Local(
        (
            (act1_ref, act1_out),
            (act2_ref, act2_out),
            (reduce_all, reduce_out),
            (spatial_all, spatial_out),
            (expand_all, expand_out),
            (mask_all, mask_out),
            (cot_all, cot_out),
            (raw1, raw_out),
        ),
        sems[27],
    )
    cot_sem, cot_recv = sems[25:27]

    def cot_copy(parity, slot, target):
        return push(
            packed.at[parity], cot_all.at[slot], cot_sem.at[parity], cot_recv.at[slot], target, lane
        )

    announce(batch_peers() + chan_peers())
    reduce_all[place] = reduce_ref[...]
    ids_all[place] = jnp.zeros((8, PIXELS), jnp.float32)
    for micro in range(2):
        for row in range(8):
            ids_all[place, micro : micro + 1, row * 32 : (row + 1) * 32] = ids_ref[
                micro, row : row + 1
            ].astype(jnp.float32)
    spatial_all[place] = spatial_ref[...]
    expand_all[place] = expand_ref[...]
    head_all[lane, 0:4] = head_scale[...]
    head_all[lane, 4:8] = head_shift[...]
    clear_edges(turned)
    gathered_peers(batch_peers() + chan_peers())
    reduces.start()
    ids.start()
    heads.start()
    for rank in range(1, 4):
        reduces.near(rank)
    spatials.start()
    for rank in range(4):
        reduces.far(rank)
    x = x_ref[...].reshape(2 * PIXELS, x_ref.shape[2])
    pieces.start(dot_last(x, reduce_all[...].reshape(512, 512)))
    ids.wait()
    make_masks(ids_all, mask_all)
    mask_ref[...] = mask_all[place]
    local.start(2, 5)
    spatials.near(1)
    first = pieces.finish()
    first_rows = centered(first, raw1)
    sums1[place] = tile_rows(first_rows, 8)
    first_sums.start()
    first_raw.start()
    spatials.near(2)
    expands.start()
    spatials.near(3)
    half_width = LANES // 2
    left = lax.broadcasted_iota(jnp.int32, (PIXELS, LANES), 1) < half_width
    for micro in range(2):
        upper_cot, lower_cot = (ref[micro].astype(jnp.float32) for ref in (depth_cot, segment_cot))
        packed[0, micro] = jnp.where(left, upper_cot, pltpu.roll(lower_cot, half_width, 1)).astype(
            jnp.bfloat16
        )
        packed[1, micro] = jnp.where(left, pltpu.roll(upper_cot, half_width, 1), lower_cot).astype(
            jnp.bfloat16
        )
    first_sums.wait()
    rows, offsets = fit(first, first_rows, first_sums.total(), 0, fits1)
    first_fits.start()
    expands.near(1)
    for rank in range(4):
        spatials.far(rank)
    expands.near(2)
    first_raw.wait()
    first_fits.wait()
    activate(raw1, fits1, act1_ref)
    local.start(0, 3, 7)
    for micro in range(2):
        value = jnp.concatenate([act1_ref[slot, micro_rows(micro)] for slot in range(4)], axis=1)
        fill_columns(value, mask_all[place, micro], turned, columns, micro * PIXELS)
    second = jnp.zeros((2 * PIXELS, LANES), jnp.float32)
    for number in range(9):
        second = second + jnp.dot(
            columns[:, number * 512 : (number + 1) * 512],
            spatial_all[:, number].reshape(512, LANES),
            preferred_element_type=jnp.float32,
        )
    second_rows = centered(second, raw2)
    sums2[place] = tile_rows(second_rows, 8)
    second_sums.start()
    second_raw.start()
    expands.near(3)
    for parity in range(2):
        target = 2 * lane + parity

        @pl.when(target == place)
        def _():
            cot_all[place] = packed[parity]

        @pl.when(target != place)
        def _():
            cot_copy(parity, place, target).start()

    second_sums.wait()
    rows = rows + fit(second, second_rows, second_sums.total(), 1, fits2)[0] + offsets
    second_fits.start()
    inverse12_ref[...] = tile_rows(rows, 8)
    heads.wait()
    low = lax.broadcasted_iota(jnp.int32, (1, LANES), 1) < half_width
    source = place // 2
    even = place % 2 == 0
    for kind in range(2):
        upper_row = head_all[source, pl.ds(4 * kind + 2 * upper, 1)]
        lower_row = head_all[source, pl.ds(4 * kind + 2 * upper + 1, 1)]
        mine_ref[kind : kind + 1] = jnp.where(
            even,
            jnp.where(low, upper_row, pltpu.roll(lower_row, half_width, 1)),
            jnp.where(low, pltpu.roll(upper_row, half_width, 1), lower_row),
        )
    for rank in range(4):
        expands.far(rank)
    second_raw.wait()
    second_fits.wait()
    activate(raw2, fits2, act2_ref)
    local.start(1, 4)
    value = jnp.concatenate([act2_ref[slot] for slot in range(4)], axis=1)
    third = jnp.dot(
        value, expand_all[...].reshape(512, 512), preferred_element_type=jnp.float32
    )
    sums3[place] = tile_rows(moments(third, third), 8)
    third_sums.start()
    third_sums.wait()
    totals = third_sums.total()
    rows = []
    for micro in range(2):
        normed, inverse = normed_part(third, totals, micro, count)
        norm3_ref[micro_rows(micro)] = normed
        rows.append(inverse)
        out = normed * output_scale[...] + output_shift[...] + x_ref[micro].astype(jnp.float32)
        y_ref[micro] = (out * jax.nn.sigmoid(out)).astype(jnp.bfloat16)
    inverse3_ref[...] = tile_rows(rows, 8)
    @pl.when(place // 2 == lane)
    def _():
        for step in range(1, 8):
            cot_copy(0, (place + step) % 8, place).wait_recv()

    local.start(6)
    for parity in range(2):
        @pl.when(2 * lane + parity != place)
        def _():
            cot_copy(parity, place, place).wait_send()

    local.wait(0, 1, 2, 3, 4, 5, 6, 7)
    for item in (reduces, spatials, expands, ids, heads, first_raw, second_raw):
        item.close()
    for item in (first_sums, second_sums, third_sums, first_fits, second_fits):
        item.close()


def exchange_sems(size):
    return [pltpu.SemaphoreType.DMA((size - 1,)), pltpu.SemaphoreType.DMA((size,))]


def run_front(count, *arrays):
    f32, bf16 = jnp.float32, jnp.bfloat16
    kept = (
        (4, 2 * PIXELS, LANES),
        (4, 2 * PIXELS, LANES),
        (8, 64, 512),
        (8, 9, 64, LANES),
        (8, 64, 512),
        (8, 2, PIXELS, LANES),
        (8, 2, PIXELS, LANES),
    )
    return pl.pallas_call(
        functools.partial(front_kernel, count),
        name="front",
        out_shape=(
            jax.ShapeDtypeStruct((2, PIXELS, 512), bf16),
            jax.ShapeDtypeStruct((2 * PIXELS, 512), f32),
            jax.ShapeDtypeStruct((8, 512), f32),
            jax.ShapeDtypeStruct((2, 2 * PIXELS, LANES), f32),
            jax.ShapeDtypeStruct((8, LANES), f32),
            jax.ShapeDtypeStruct((2, LANES), f32),
            jax.ShapeDtypeStruct((2, PIXELS, LANES), bf16),
        )
        + tuple(jax.ShapeDtypeStruct(shape, bf16) for shape in kept + (kept[0],)),
        in_specs=vmem(13),
        out_specs=tuple(vmem(7) + anywhere(8)),
        scratch_shapes=[pltpu.VMEM(shape, bf16) for shape in kept]
        + [
            pltpu.VMEM((2, 2, PIXELS, LANES), bf16),
            pltpu.VMEM((3, 2 * PAD + PIXELS, 512), bf16),
            pltpu.VMEM((2 * PIXELS, 9 * 512), bf16),
            pltpu.VMEM((4, 2 * PIXELS, LANES), bf16),
            pltpu.VMEM((4, 2 * PIXELS, LANES), bf16),
            pltpu.VMEM((8, 8, LANES), f32),
            pltpu.VMEM((8, 8, LANES), f32),
            pltpu.VMEM((8, 8, 512), f32),
            pltpu.VMEM((4, 8, LANES), f32),
            pltpu.VMEM((8, 8, PIXELS), f32),
            pltpu.VMEM((4, 2 * PIXELS, LANES), bf16),
            pltpu.VMEM((4, 2 * PIXELS, LANES), bf16),
            pltpu.VMEM((4, 8, LANES), f32),
            pltpu.VMEM((4, 8, LANES), f32),
        ]
        + gather_sems(1) * 3
        + exchange_sems(8)
        + [pltpu.SemaphoreType.DMA((4,))] * 2
        + exchange_sems(8) * 3
        + exchange_sems(4) * 3
        + [
            pltpu.SemaphoreType.DMA((2,)),
            pltpu.SemaphoreType.DMA((8,)),
            pltpu.SemaphoreType.DMA((8,)),
        ]
        + exchange_sems(4) * 2,
        compiler_params=kernel_params(1),
    )(*arrays)


class Scatter:
    def __init__(self, part, far_buf, far_got, near_buf, near_got, sems):
        self.part, self.far_buf, self.far_got = part, far_buf, far_got
        self.near_buf, self.near_got = near_buf, near_got
        self.far_send, self.far_recv, self.near_send, self.near_recv = sems

    def far_copy(self, level, place):
        return push(
            self.far_buf.at[level],
            self.far_got.at[level],
            self.far_send.at[level],
            self.far_recv.at[level],
            place,
            lax.axis_index("chan"),
        )

    def near_copy(self, rank, level, place):
        return push(
            self.near_buf.at[rank - 1],
            self.near_got.at[level],
            self.near_send.at[rank - 1],
            self.near_recv.at[level],
            place,
            lax.axis_index("chan"),
        )

    def start(self):
        place, lane, depth, side, _, _ = whereabouts()
        for rank in (3, 2, 1, 0):
            level = ranked(depth, rank)
            self.far_buf[level] = self.part[level * 2 + 1 - side].astype(jnp.bfloat16)
            self.far_copy(level, depth * 2 + 1 - side).start()

    def middle(self):
        place, lane, depth, side, _, _ = whereabouts()
        for rank in (3, 2, 1):
            level = ranked(depth, rank)
            self.far_copy(level, place).wait_recv()
            self.near_buf[rank - 1] = (
                self.part[level * 2 + side] + self.far_got[level].astype(jnp.float32)
            ).astype(jnp.bfloat16)
            self.near_copy(rank, depth, level * 2 + side).start()

    def finish(self):
        place, lane, depth, side, _, _ = whereabouts()
        self.far_copy(depth, place).wait_recv()
        result = self.part[place] + self.far_got[depth].astype(jnp.float32)
        for level in range(4):
            self.far_copy(level, place).wait_send()
        for rank in (3, 2, 1):
            level = ranked(depth, rank)
            self.near_copy(rank, level, place).wait()
            result = result + self.near_got[level].astype(jnp.float32)
        return result


def scatter_scratch(width):
    return [
        pltpu.VMEM((8, 64, width), jnp.float32),
        pltpu.VMEM((4, 64, width), jnp.bfloat16),
        pltpu.VMEM((4, 64, width), jnp.bfloat16),
        pltpu.VMEM((3, 64, width), jnp.bfloat16),
        pltpu.VMEM((4, 64, width), jnp.bfloat16),
    ]


def scatter_sems():
    return [
        pltpu.SemaphoreType.DMA((4,)),
        pltpu.SemaphoreType.DMA((4,)),
        pltpu.SemaphoreType.DMA((3,)),
        pltpu.SemaphoreType.DMA((4,)),
    ]


def back_part(value, normed, inverse, scale, shift_sum, scale_sum, count):
    return (scale * inverse * (value - (shift_sum + normed * scale_sum) / count)).astype(
        jnp.bfloat16
    )


def rear_kernel(
    count,
    grad_ref,
    x_ref,
    norm3_ref,
    inverse3_ref,
    norm12_ref,
    inverse12_ref,
    mask_ref,
    block_scale,
    block_shift,
    output_scale,
    output_shift,
    head_ref,
    gate_ref,
    block_hbm,
    back_hbm,
    masks_hbm,
    act1_hbm,
    act2_hbm,
    reduce_hbm,
    spatial_hbm,
    expand_hbm,
    raw_hbm,
    features_ref,
    reduce_out,
    spatial_out,
    expand_out,
    block_scale_out,
    block_shift_out,
    head_scale_out,
    head_shift_out,
    gate_out,
    output_scale_out,
    output_shift_out,
    head_out,
    head_grad,
    block_all,
    head_back,
    mask_all,
    act1_ref,
    act2_ref,
    reduce_all,
    spatial_all,
    expand_all,
    raw_ref,
    fits_all,
    spatial_rows,
    turned_wide,
    columns_wide,
    turned,
    columns,
    stage,
    got,
    stage_next,
    got_next,
    sums_a,
    sums_b,
    sums_c,
    head_all,
    act_all,
    back3,
    *rest,
):
    expand_bufs, spatial_bufs, reduce_bufs, sems = rest[0:5], rest[5:10], rest[10:15], rest[15:]
    place, lane, depth, side, upper, core = whereabouts()
    pieces = Pieces(stage, got, sems[0], sems[1])
    first = Exchange(sums_a, sems[2], sems[3], "batch")
    second = Exchange(sums_b, sems[4], sems[5], "batch")
    third = Exchange(sums_c, sems[6], sems[7], "batch")
    heads = Exchange(head_all, sems[8], sems[9], "chan")
    acts = Exchange(act_all, sems[10], sems[11], "chan")
    fits = Exchange(fits_all, sems[27], sems[28], "chan")
    expands = Scatter(*expand_bufs, sems[12:16])
    spatials = Scatter(*spatial_bufs, sems[16:20])
    reduces = Scatter(*reduce_bufs, sems[20:24])
    pieces_next = Pieces(stage_next, got_next, sems[24], sems[25])

    local = Local(
        (
            (expand_hbm, expand_all),
            (act2_hbm, act2_ref),
            (block_hbm, block_all),
            (back_hbm, head_back),
            (masks_hbm, mask_all),
            (spatial_hbm, spatial_all),
            (act1_hbm, act1_ref),
            (reduce_hbm, reduce_all),
            (head_grad, head_out),
            (raw_hbm, raw_ref),
        ),
        sems[26],
    )
    local.start(0, 1, 2, 3, 4, 5, 6, 7, 9)

    def weigh(block):
        for micro in range(2):
            fill_columns(
                block_all[block, micro],
                mask_all[block, micro],
                turned_wide,
                columns_wide,
                micro * PIXELS,
            )
        value = jnp.concatenate(
            [
                jnp.concatenate([head_back[half, micro, block] for half in range(2)], axis=1)
                for micro in range(2)
            ],
            axis=0,
        ).T

        def tap(number, _):
            product = jnp.dot(
                value,
                columns_wide[:, pl.ds(pl.multiple_of(number * 512, 512), 512)],
                preferred_element_type=jnp.float32,
            )
            if block == 0:
                head_grad[number] = product
            else:
                head_grad[number] += product
            return 0

        lax.fori_loop(0, 9, tap, 0)

    announce(batch_peers() + chan_peers())
    clear_edges(turned_wide)
    half_width = LANES // 2
    even = place % 2 == 0
    mine = lax.broadcasted_iota(jnp.int32, (1, LANES), 1) >> 6 == place % 2
    rows = []
    for kind in range(2):
        own = head_ref[kind : kind + 1]
        turned_own = pltpu.roll(own, half_width, 1)
        first_row = jnp.where(mine, jnp.where(even, own, turned_own), 0.0)
        second_row = jnp.where(mine, jnp.where(even, turned_own, own), 0.0)
        for half in range(2):
            for row in (first_row, second_row):
                rows.append(jnp.where(upper == half, row, 0.0))
    head_all[lane] = jnp.concatenate(rows, axis=0)
    clear_edges(turned)
    wide_rows = []
    for micro in range(2):
        normed = norm3_ref[micro_rows(micro)]
        out = normed * output_scale[...] + output_shift[...] + x_ref[micro].astype(jnp.float32)
        value = grad_ref[micro_rows(micro)] * silu_slope(out)
        features_ref[micro] = value
        wide_rows.append(jnp.sum(value, axis=0, keepdims=True))
        wide_rows.append(jnp.sum(value * normed, axis=0, keepdims=True))
    gathered_peers(batch_peers() + chan_peers())
    sums_a[place] = tile_rows(wide_rows, 8)
    first.start()
    heads.start()
    local.wait(0, 1, 2, 3, 4)
    weigh(0)
    first.wait()
    totals = first.total()
    output_scale_out[...] = totals[1:2] + totals[3:4]
    output_shift_out[...] = totals[0:1] + totals[2:3]
    for micro in range(2):
        back3[micro_rows(micro)] = back_part(
            features_ref[micro],
            norm3_ref[micro_rows(micro)],
            inverse3_ref[micro : micro + 1],
            output_scale[...],
            totals[2 * micro : 2 * micro + 1],
            totals[2 * micro + 1 : 2 * micro + 2],
            count,
        )
    pieces.start(dot_last(back3[...], expand_all[...].reshape(512, 512)))
    value = jnp.concatenate([act2_ref[slot] for slot in range(4)], axis=1)
    expands.part[...] = jnp.dot(
        value.T, back3[...], preferred_element_type=jnp.float32
    ).reshape(8, 64, 512)
    expands.start()
    weigh(1)
    weigh(2)
    grad = pieces.finish()
    normed = norm12_ref[1]
    grad = grad * silu_slope(normed * block_scale[1:2] + block_shift[1:2])
    heads.wait()
    sums_b[place, 0:8] = tile_rows(moments(grad, normed), 8)
    sums_b[place, 4:6] = gate_ref[...]
    sums_b[place, 8:16] = jnp.where(place // 2 == lane, heads.total(), 0.0)
    second.start()
    local.wait(5, 6, 7, 9)
    for number in range(9):
        spatial_rows[number * LANES : (number + 1) * LANES] = (
            spatial_all[:, number].reshape(512, LANES).T
        )
    weigh(3)
    expands.middle()
    second.wait()
    totals = second.total()
    head_scale_out[...] = totals[8:12]
    head_shift_out[...] = totals[12:16]
    gate_out[...] = totals[4:6]
    block_scale_out[1:2] = totals[1:2] + totals[3:4]
    block_shift_out[1:2] = totals[0:1] + totals[2:3]
    for micro in range(2):
        value = back_part(
            grad[micro_rows(micro)],
            normed[micro_rows(micro)],
            inverse12_ref[2 + micro : 3 + micro],
            block_scale[1:2],
            totals[2 * micro : 2 * micro + 1],
            totals[2 * micro + 1 : 2 * micro + 2],
            count,
        )
        fill_columns(value, mask_ref[micro], turned, columns, micro * PIXELS, True)
    part = jnp.dot(columns[...], spatial_rows[...], preferred_element_type=jnp.float32)
    pieces_next.start(part)
    value = jnp.concatenate([act1_ref[slot] for slot in range(4)], axis=1)
    spatials.part[...] = jnp.dot(
        value.T, columns[...], preferred_element_type=jnp.float32
    ).reshape(8, 64, 9 * LANES)
    spatials.start()
    weigh(4)
    weigh(5)
    grad = pieces_next.finish()
    normed = norm12_ref[0]
    grad = grad * silu_slope(normed * block_scale[0:1] + block_shift[0:1])
    rows = moments(grad, normed)
    sums_c[place] = tile_rows(rows, 8)
    third.start()
    for micro in range(2):
        act_all[lane, micro_rows(micro)] = (
            grad[micro_rows(micro)] - rows[2 * micro] / PIXELS
        ).astype(jnp.bfloat16)
    acts.start()
    weigh(6)
    spatials.middle()
    expand_out[...] = expands.finish()
    third.wait()
    totals = third.total()
    block_scale_out[0:1] = totals[1:2] + totals[3:4]
    block_shift_out[0:1] = totals[0:1] + totals[2:3]
    lines = []
    for micro in range(2):
        shift_sum = totals[2 * micro : 2 * micro + 1]
        scale_sum = totals[2 * micro + 1 : 2 * micro + 2]
        inverse = inverse12_ref[micro : micro + 1]
        factor = block_scale[0:1] * inverse
        lines.append(factor)
        lines.append(-factor * scale_sum * inverse / count)
        lines.append(
            factor
            * (
                rows[2 * micro] / PIXELS
                - (shift_sum + inverse12_ref[4 + micro : 5 + micro] * scale_sum) / count
            )
        )
    fits_all[lane] = tile_rows(lines, 8)
    fits.start()
    weigh(7)
    local.start(8)
    acts.wait()
    fits.wait()

    def whole(slot):
        parts = []
        for micro in range(2):
            line = [fits_all[slot, 3 * micro + row : 3 * micro + row + 1] for row in range(3)]
            parts.append(
                act_all[slot, micro_rows(micro)].astype(jnp.float32) * line[0]
                + raw_ref[slot, micro_rows(micro)].astype(jnp.float32) * line[1]
                + line[2]
            )
        return jnp.concatenate(parts, axis=0).astype(jnp.bfloat16)

    value = jnp.concatenate([whole(slot) for slot in range(4)], axis=1)
    x = x_ref[...].reshape(2 * PIXELS, 512)
    reduces.part[...] = jnp.dot(value.T, x, preferred_element_type=jnp.float32).reshape(8, 64, 512)
    reduces.start()
    more = jnp.dot(value, reduce_all[...].reshape(512, 512), preferred_element_type=jnp.float32)
    for micro in range(2):
        features_ref[micro] = features_ref[micro] + more[micro_rows(micro)]
    reduces.middle()
    result = spatials.finish()
    for number in range(9):
        spatial_out[number] = result[:, number * LANES : (number + 1) * LANES]
    reduce_out[...] = reduces.finish()
    for item in (first, second, third, heads, acts, fits):
        item.close()
    local.wait(8)


def run_rear(count, *arrays):
    f32, bf16 = jnp.float32, jnp.bfloat16
    return pl.pallas_call(
        functools.partial(rear_kernel, count),
        name="rear",
        out_shape=(
            jax.ShapeDtypeStruct((2, PIXELS, 512), f32),
            jax.ShapeDtypeStruct((64, 512), f32),
            jax.ShapeDtypeStruct((9, 64, LANES), f32),
            jax.ShapeDtypeStruct((64, 512), f32),
            jax.ShapeDtypeStruct((2, LANES), f32),
            jax.ShapeDtypeStruct((2, LANES), f32),
            jax.ShapeDtypeStruct((4, LANES), f32),
            jax.ShapeDtypeStruct((4, LANES), f32),
            jax.ShapeDtypeStruct((2, LANES), f32),
            jax.ShapeDtypeStruct((1, 512), f32),
            jax.ShapeDtypeStruct((1, 512), f32),
            jax.ShapeDtypeStruct((9, 256, 512), f32),
        ),
        in_specs=vmem(13) + anywhere(9),
        out_specs=tuple(vmem(11) + anywhere(1)),
        scratch_shapes=[
            pltpu.VMEM((9, 256, 512), f32),
            pltpu.VMEM((8, 2, PIXELS, 512), bf16),
            pltpu.VMEM((2, 2, 8, PIXELS, LANES), bf16),
            pltpu.VMEM((8, 2, PIXELS, LANES), bf16),
            pltpu.VMEM((4, 2 * PIXELS, LANES), bf16),
            pltpu.VMEM((4, 2 * PIXELS, LANES), bf16),
            pltpu.VMEM((8, 64, 512), bf16),
            pltpu.VMEM((8, 9, 64, LANES), bf16),
            pltpu.VMEM((8, 64, 512), bf16),
            pltpu.VMEM((4, 2 * PIXELS, LANES), bf16),
            pltpu.VMEM((4, 8, LANES), f32),
            pltpu.VMEM((9 * LANES, 512), bf16),
            pltpu.VMEM((3, 2 * PAD + PIXELS, 512), bf16),
            pltpu.VMEM((2 * PIXELS, 9 * 512), bf16),
            pltpu.VMEM((3, 2 * PAD + PIXELS, LANES), bf16),
            pltpu.VMEM((2 * PIXELS, 9 * LANES), bf16),
            pltpu.VMEM((4, 2 * PIXELS, LANES), bf16),
            pltpu.VMEM((4, 2 * PIXELS, LANES), bf16),
            pltpu.VMEM((4, 2 * PIXELS, LANES), bf16),
            pltpu.VMEM((4, 2 * PIXELS, LANES), bf16),
            pltpu.VMEM((8, 8, 512), f32),
            pltpu.VMEM((8, 16, LANES), f32),
            pltpu.VMEM((8, 8, LANES), f32),
            pltpu.VMEM((4, 8, LANES), f32),
            pltpu.VMEM((4, 2 * PIXELS, LANES), bf16),
            pltpu.VMEM((2 * PIXELS, 512), bf16),
        ]
        + scatter_scratch(512)
        + scatter_scratch(9 * LANES)
        + scatter_scratch(512)
        + [pltpu.SemaphoreType.DMA((4,))] * 2
        + exchange_sems(8) * 3
        + exchange_sems(4) * 2
        + scatter_sems() * 3
        + [pltpu.SemaphoreType.DMA((4,))] * 2
        + [pltpu.SemaphoreType.DMA((10,))]
        + exchange_sems(4),
        compiler_params=kernel_params(5),
    )(*arrays)


class Reduce:
    def __init__(self, part, keep, far_buf, far_got, line_buf, line_got, sems):
        self.part, self.keep, self.far_buf, self.far_got = part, keep, far_buf, far_got
        self.line_buf, self.line_got = line_buf, line_got
        self.far_send, self.far_recv, self.line_send, self.line_recv = sems

    def block(self, step):
        place, lane, depth, side, _, _ = whereabouts()
        item, late = staggered(step)
        return ranked(depth, 3 - item % 4) * 2 + (side + 1 + late) % 2, item // 4

    def far_copy(self, micro, rank, place):
        return push(
            self.far_buf.at[micro, rank],
            self.far_got.at[micro, rank],
            self.far_send.at[micro, rank],
            self.far_recv.at[micro, rank],
            place,
            lax.axis_index("chan"),
        )

    def line_copy(self, micro, rank, slot, place):
        return push(
            self.line_buf.at[micro, rank],
            self.line_got.at[micro, slot],
            self.line_send.at[micro, rank],
            self.line_recv.at[micro, slot],
            place,
            lax.axis_index("chan"),
        )

    def line_value(self, micro, slot):
        self.line_copy(micro, 0, slot, lax.axis_index("batch")).wait_recv()
        return self.line_got[micro, slot].astype(jnp.float32)

    def step(self, step):
        place, lane, depth, side, _, _ = whereabouts()
        item, late = staggered(step)
        micro, rank = item // 4, 3 - item % 4
        owner = ranked(depth, rank)

        @pl.when(late == 0)
        def _():
            self.far_buf[micro, rank] = self.part[...].astype(jnp.bfloat16)
            self.far_copy(micro, rank, depth * 2 + 1 - side).start()

        @pl.when(late == 1)
        def _():
            self.far_copy(micro, rank, place).wait_recv()
            self.keep[micro] = self.part[...] + self.far_got[micro, rank].astype(jnp.float32)

            @pl.when((middle(depth) == 1) & (rank > 0))
            def _():
                self.keep[micro] = self.keep[micro] + self.line_value(micro, owner)

            @pl.when(rank > 0)
            def _():
                first = (rank % 2) * (1 - rank // 2) * (1 - middle(depth))
                slot = owner + first * (4 - owner)
                self.line_buf[micro, rank - 1] = self.keep[micro].astype(jnp.bfloat16)
                self.line_copy(
                    micro, rank - 1, slot, homeward(depth, rank) * 2 + side
                ).start()

    def close(self, micro):
        place, lane, depth, side, _, _ = whereabouts()
        self.keep[micro] = self.keep[micro] + self.line_value(micro, depth)

        @pl.when(middle(depth) == 1)
        def _():
            self.keep[micro] = self.keep[micro] + self.line_value(micro, 4)

        for rank in range(4):
            self.far_copy(micro, rank, place).wait_send()
        for rank in range(3):
            self.line_copy(micro, rank, 0, place).wait_send()


class Channels:
    def __init__(self, stage, got, stage_sem, got_sem, values, out_sem, in_sem):
        self.stage, self.got, self.stage_sem, self.got_sem = stage, got, stage_sem, got_sem
        self.values, self.out_sem, self.in_sem = values, out_sem, in_sem

    def piece(self, slot, target, block, lane):
        return push(
            self.stage.at[slot, block],
            self.got.at[lane, block],
            self.stage_sem.at[slot, block],
            self.got_sem.at[lane, block],
            lax.axis_index("batch"),
            target,
        )

    def send(self, part, block, micro):
        _, lane, _, _, upper, core = whereabouts()
        for half in range(2):
            piece = part[:, half * LANES : (half + 1) * LANES]
            target = half * 2 + micro

            @pl.when(target == lane)
            def _():
                self.got[lane, block] = piece

            @pl.when(target != lane)
            def _():
                self.stage[target, block] = piece
                self.piece(target, target, block, lane).start()

    def collect(self, micro, take):
        _, lane, _, _, _, core = whereabouts()

        @pl.when(core == micro)
        def _():
            def body(block, _):
                for step in range(1, 4):
                    other = (lane + step) % 4
                    self.piece(other, other, block, other).wait_recv()
                take(block)
                return 0

            lax.fori_loop(0, 8, body, 0)

    def value(self, block):
        result = self.got[0, block].astype(jnp.float32)
        for other in range(1, 4):
            result = result + self.got[other, block].astype(jnp.float32)
        return result

    def sent(self):
        _, lane, _, _, _, _ = whereabouts()

        def body(block, _):
            for step in range(1, 4):
                other = (lane + step) % 4
                self.piece(other, other, block, lane).wait_send()
            return 0

        lax.fori_loop(0, 8, body, 0)

    def chunk(self, path, half, micro, chunk, place_lane):
        here = self.values.at[half, micro, pl.ds(2 * chunk, 2)]
        return push(
            here,
            here,
            self.out_sem.at[path, chunk],
            self.in_sem.at[half, micro, chunk],
            lax.axis_index("batch"),
            place_lane,
        )

    def spread(self, chunk):
        _, lane, _, _, upper, core = whereabouts()
        self.chunk(0, upper, core, chunk, 2 - 2 * upper + core).start()
        self.chunk(1, upper, core, chunk, upper * 2 + 1 - core).start()

    def relay(self, micro):
        _, lane, _, _, upper, core = whereabouts()

        @pl.when(core == micro)
        def _():
            for chunk in range(4):
                copy = self.chunk(2, 1 - upper, core, chunk, upper * 2 + 1 - core)
                copy.wait_recv()
                copy.start()

    def finish(self, micro):
        _, lane, _, _, upper, core = whereabouts()

        @pl.when(core != micro)
        def _():
            for chunk in range(4):
                for half in range(2):
                    self.chunk(0, half, micro, chunk, lane).wait_recv()

    def close(self):
        _, lane, _, _, upper, core = whereabouts()
        for chunk in range(4):
            for path in range(3):
                self.chunk(path, upper, core, chunk, lane).wait_send()


def middle_kernel(
    count,
    block_ref,
    bias_ref,
    mine_ref,
    head_hbm,
    distil_hbm,
    mask_hbm,
    depth_hbm,
    segment_hbm,
    cot_hbm,
    depth_out,
    segment_out,
    gate_sums,
    head_sums,
    back_out,
    block_hbm,
    back_hbm,
    distil_out,
    distil_grad,
    block_all,
    head_back,
    head_ref,
    distil_ref,
    mask_ref,
    depth_cot,
    segment_cot,
    cot_all,
    head_weight,
    mixed,
    mixed_back,
    turned,
    columns,
    acts,
    norm_ref,
    slope_ref,
    grads_all,
    own_stage,
    own_got,
    stage,
    got,
    part_ref,
    keep,
    far_buf,
    far_got,
    line_buf,
    line_got,
    stats,
    *sems,
):
    place, lane, depth, side, upper, core = whereabouts()
    half_width = LANES // 2
    source = place // 2 == lane
    low = lax.broadcasted_iota(jnp.int32, (PIXELS, LANES), 1) < half_width
    gather = Gather(block_all, *sems[0:3], 2)
    gather_back = Gather(grads_all, *sems[3:6], 2)
    reduce = Reduce(part_ref, keep, far_buf, far_got, line_buf, line_got, sems[6:10])
    ahead = Channels(stage, got, sems[10], sems[11], acts, sems[12], sems[13])
    behind = Channels(stage, got, sems[10], sems[11], head_back, sems[14], sems[15])
    own_sem, own_recv = sems[16:18]
    local = Local(
        (
            (head_hbm, head_ref),
            (mask_hbm, mask_ref),
            (distil_hbm, distil_ref),
            (depth_hbm, depth_cot),
            (segment_hbm, segment_cot),
            (cot_hbm, cot_all),
            (block_all, block_hbm),
            (head_back, back_hbm),
            (distil_grad, distil_out),
        ),
        sems[18],
    )
    local.start(0, 1, 2, 3, 4, 5)

    greet(batch_peers() + chan_peers())
    block_all[place] = block_ref[...]
    gather.start(0)
    clear_edges(turned)
    local.wait(0)
    for number in range(9):
        head_weight[number * 512 : (number + 1) * 512] = head_ref[number].T
    local.wait(1)

    def forward_step(step, _):
        block, micro = gather.next(step)
        fill_columns(block_all[block, micro], mask_ref[block, micro], turned, columns)
        part = jnp.dot(columns[0:PIXELS], head_weight[...], preferred_element_type=jnp.float32)
        ahead.send(part.astype(jnp.bfloat16), block, micro)

        @pl.when(step == 0)
        def _():
            local.wait(2)
            prepare_mixed()

        @pl.when(step == 1)
        def _():
            gather.start(1)

        @pl.when(step == 4)
        def _():
            for number in range(9):
                mixed_back[number * 512 : (number + 1) * 512] = mixed[
                    number * 256 : (number + 1) * 256
                ].T

        @pl.when(step == 10)
        def _():
            normalize(0)

        @pl.when(step == 13)
        def _():
            ahead.relay(0)

        return 0

    def prepare_mixed():
        width = half_width
        for number in range(9):
            for stream in range(2):
                for head in range(4):
                    index = head - SOURCE_START[stream]
                    rows = slice(number * 256 + head * width, number * 256 + (head + 1) * width)
                    left = slice(2 * stream * LANES, (2 * stream + 1) * LANES)
                    right = slice((2 * stream + 1) * LANES, (2 * stream + 2) * LANES)
                    nothing = jnp.zeros((width, LANES), jnp.bfloat16)
                    mixed[rows, left] = (
                        distil_ref[stream, number, 0] if head == OWN_HEAD[stream] else nothing
                    )
                    mixed[rows, right] = (
                        distil_ref[stream, number, 1 + index] if 0 <= index < 3 else nothing
                    )

    def normalize(micro):
        zero = jnp.zeros((1, LANES), jnp.float32)

        @pl.when(core == micro)
        def _():
            stats[0:2] = jnp.zeros((2, LANES), jnp.float32)

        def take(block):
            value = ahead.value(block)
            norm_ref[block] = value
            stats[0:1] += jnp.sum(value, axis=0, keepdims=True)
            stats[1:2] += jnp.sum(value * value, axis=0, keepdims=True)

        ahead.collect(micro, take)

        @pl.when(core == micro)
        def _():
            center = stats[0:1] / count
            inverse = lax.rsqrt(stats[1:2] / count - center * center + EPSILON)
            stats[2:3] = inverse

            def activate(chunk, _):
                for item in range(2):
                    block = 2 * chunk + item
                    normed = (norm_ref[block] - center) * inverse
                    norm_ref[block] = normed
                    out = normed * mine_ref[0:1] + mine_ref[1:2]
                    acts[upper, core, block] = (out * jax.nn.sigmoid(out)).astype(jnp.bfloat16)
                ahead.spread(chunk)
                return 0

            lax.fori_loop(0, 4, activate, 0)

    def own_copy(block, micro, slot, target):
        return push(
            own_stage.at[block, micro],
            own_got.at[slot, micro],
            own_sem.at[block, micro],
            own_recv.at[slot, micro],
            target,
            lane,
        )

    def send_own(micro):
        @pl.when(source)
        def _():
            own_got[place % 2, micro] = jnp.where(
                low, acts[0, micro, place], acts[1, micro, place]
            )

            def pack(step, _):
                block = (place + step) % 8
                own_stage[block, micro] = jnp.where(
                    low, acts[0, micro, block], acts[1, micro, block]
                )
                own_copy(block, micro, place % 2, block).start()
                return 0

            lax.fori_loop(1, 8, pack, 0)

    def act_value(block, micro):
        return jnp.concatenate([acts[half, micro, block] for half in range(2)], axis=1)

    def gate(micro):
        reduce.close(micro)
        for parity in range(2):
            @pl.when(2 * lane + parity != place)
            def _():
                own_copy(0, micro, parity, place).wait_recv()

        for stream, cot_ref in enumerate((depth_cot, segment_cot)):
            first = own_got[0, micro].astype(jnp.float32)
            second = own_got[1, micro].astype(jnp.float32)
            if stream == 0:
                second = pltpu.roll(second, half_width, 1)
            else:
                first = pltpu.roll(first, half_width, 1)
            own = jnp.where(low, first, second)
            column = 2 * stream * LANES
            gates = jax.nn.sigmoid(
                keep[micro, :, column : column + LANES] + bias_ref[stream : stream + 1]
            )
            message = keep[micro, :, column + LANES : column + 2 * LANES]
            cot = cot_ref[micro].astype(jnp.float32)
            out_ref = (depth_out, segment_out)[stream]
            out_ref[micro] = (own + gates * message).astype(jnp.bfloat16)
            gate_grad = (cot * message * gates * (1.0 - gates)).astype(jnp.bfloat16)
            bias_sum = jnp.sum(gate_grad.astype(jnp.float32), axis=0, keepdims=True)
            if micro == 0:
                gate_sums[stream : stream + 1] = bias_sum
            else:
                gate_sums[stream : stream + 1] += bias_sum
            grads_all[place, micro, :, column : column + LANES] = gate_grad
            grads_all[place, micro, :, column + LANES : column + 2 * LANES] = (cot * gates).astype(
                jnp.bfloat16
            )

    def distil_step(step, _):
        block, micro = reduce.block(step)
        fill_columns(act_value(block, micro), mask_ref[block, micro], turned, columns)
        part_ref[...] = jnp.dot(
            columns[0:PIXELS, 0 : 9 * 256], mixed[...], preferred_element_type=jnp.float32
        )
        reduce.step(step)

        @pl.when(step == 2)
        def _():
            normalize(1)

        @pl.when(step == 5)
        def _():
            ahead.relay(1)

        @pl.when(step == 6)
        def _():
            ahead.finish(1)
            ahead.sent()
            send_own(1)

        @pl.when(step == 11)
        def _():
            local.wait(3, 4)
            gate(0)
            gather_back.start(0)

        return 0

    distil_grad[...] = jnp.zeros_like(distil_grad)

    def back_step(step, _):
        block, micro = gather_back.next(step)
        fill_columns(
            grads_all[block, micro], mask_ref[block, micro], turned, columns, flip=True
        )
        part = jnp.dot(columns[0:PIXELS], mixed_back[...], preferred_element_type=jnp.float32)
        extra = cot_all[block, micro].astype(jnp.float32)
        part = jnp.concatenate(
            [
                part[:, :LANES] + jnp.where(low & source, extra, 0.0),
                part[:, LANES:] + jnp.where(low | ~source, 0.0, extra),
            ],
            axis=1,
        )
        behind.send(part.astype(jnp.bfloat16), block, micro)
        @pl.when(step == 10)
        def _():
            normalize_back(0)

        @pl.when(step == 13)
        def _():
            behind.relay(0)

        return 0

    def normalize_back(micro):
        @pl.when(core == micro)
        def _():
            stats[4:6] = jnp.zeros((2, LANES), jnp.float32)

        def take(block):
            normed = norm_ref[block]
            value = behind.value(block) * silu_slope(normed * mine_ref[0:1] + mine_ref[1:2])
            slope_ref[block] = value
            stats[4:5] += jnp.sum(value, axis=0, keepdims=True)
            stats[5:6] += jnp.sum(value * normed, axis=0, keepdims=True)

        behind.collect(micro, take)

        @pl.when(core == micro)
        def _():
            shift_sum, scale_sum = stats[4:5], stats[5:6]
            head_sums[0:1] = scale_sum
            head_sums[1:2] = shift_sum
            factor = mine_ref[0:1] * stats[2:3]

            def activate(chunk, _):
                for item in range(2):
                    block = 2 * chunk + item
                    value = slope_ref[block]
                    head_back[upper, core, block] = (
                        factor * (value - (shift_sum + norm_ref[block] * scale_sum) / count)
                    ).astype(jnp.bfloat16)
                behind.spread(chunk)
                return 0

            lax.fori_loop(0, 4, activate, 0)

    def head_value(block, micro):
        return jnp.concatenate([head_back[half, micro, block] for half in range(2)], axis=1)

    def weigh(block):
        for micro in range(2):
            fill_columns(
                grads_all[block, micro],
                mask_ref[block, micro],
                turned,
                columns,
                micro * PIXELS,
                True,
            )
        value = jnp.concatenate([act_value(block, micro) for micro in range(2)], axis=0).T
        width = half_width
        for number in range(9):
            product = jnp.dot(
                value,
                columns[:, number * 512 : (number + 1) * 512],
                preferred_element_type=jnp.float32,
            )
            for stream in range(2):
                for index in range(4):
                    head = OWN_HEAD[stream] if index == 0 else SOURCE_START[stream] + index - 1
                    column = (2 * stream + (index > 0)) * LANES
                    distil_grad[stream, number, index] += product[
                        head * width : (head + 1) * width, column : column + LANES
                    ]

    def block_step(step, _):
        block, micro = reduce.block(step)
        fill_columns(
            head_value(block, micro), mask_ref[block, micro], turned, columns, flip=True
        )
        part_ref[...] = jnp.dot(
            columns[0:PIXELS, 0 : 9 * 256],
            head_ref[...].reshape(9 * 256, 512),
            preferred_element_type=jnp.float32,
        )
        item, late = staggered(step)

        reduce.step(step)

        @pl.when(late == 1)
        def _():
            weigh(item)

        @pl.when(step == 2)
        def _():
            normalize_back(1)

        @pl.when(step == 5)
        def _():
            behind.relay(1)

        @pl.when(step == 6)
        def _():
            behind.finish(1)
            local.start(7)

        return 0

    def schedule(turn, _):
        phase, spot = (turn + 2) // 16, (turn + 2) % 16
        seam = (1 - (spot + 12) // 16) * ((phase + 3) // 4)
        odd = spot % 2
        kind = phase - seam * odd
        step = seam * (14 * odd + spot // 2) + (1 - seam) * (spot - 2)

        @pl.when(kind == 0)
        def _():
            forward_step(step, 0)

        @pl.when((kind == 1) & (step == 0))
        def _():
            ahead.finish(0)
            send_own(0)

        @pl.when(kind == 1)
        def _():
            distil_step(step, 0)

        @pl.when((kind == 2) & (step == 0))
        def _():
            local.wait(5)

        @pl.when((kind == 2) & (step == 6))
        def _():
            gate(1)
            gather_back.start(1)
            ahead.close()

        @pl.when(kind == 2)
        def _():
            back_step(step, 0)

        @pl.when((kind == 3) & (step == 0))
        def _():
            behind.finish(0)
            local.start(6)

        @pl.when(kind == 3)
        def _():
            block_step(step, 0)

        return 0

    lax.fori_loop(0, 66, schedule, 0)
    local.start(8)
    for micro in range(2):
        reduce.close(micro)
        back_out[micro_rows(micro)] = keep[micro]
    behind.sent()
    behind.close()
    gather.close()
    gather_back.close()

    @pl.when(source)
    def _():
        for micro in range(2):
            for step in range(1, 8):
                own_copy((place + step) % 8, micro, 0, place).wait_send()

    local.wait(6, 7, 8)


def run_middle(count, *arrays):
    f32, bf16 = jnp.float32, jnp.bfloat16
    block = (PIXELS, 512)
    dma = pltpu.SemaphoreType.DMA
    return pl.pallas_call(
        functools.partial(middle_kernel, count),
        name="middle",
        out_shape=(
            jax.ShapeDtypeStruct((2, PIXELS, LANES), bf16),
            jax.ShapeDtypeStruct((2, PIXELS, LANES), bf16),
            jax.ShapeDtypeStruct((2, LANES), f32),
            jax.ShapeDtypeStruct((2, LANES), f32),
            jax.ShapeDtypeStruct((2 * PIXELS, 512), f32),
            jax.ShapeDtypeStruct((8, 2) + block, bf16),
            jax.ShapeDtypeStruct((2, 2, 8, PIXELS, LANES), bf16),
            jax.ShapeDtypeStruct((2, 9, 4, 64, LANES), f32),
        ),
        in_specs=vmem(3) + anywhere(6),
        out_specs=tuple(vmem(5) + anywhere(3)),
        scratch_shapes=[
            pltpu.VMEM((2, 9, 4, 64, LANES), f32),
            pltpu.VMEM((8, 2) + block, bf16),
            pltpu.VMEM((2, 2, 8, PIXELS, LANES), bf16),
            pltpu.VMEM((9, 256, 512), bf16),
            pltpu.VMEM((2, 9, 4, 64, LANES), bf16),
            pltpu.VMEM((8, 2, PIXELS, LANES), bf16),
            pltpu.VMEM((2, PIXELS, LANES), bf16),
            pltpu.VMEM((2, PIXELS, LANES), bf16),
            pltpu.VMEM((8, 2, PIXELS, LANES), bf16),
            pltpu.VMEM((9 * 512, 256), bf16),
            pltpu.VMEM((9 * 256, 512), bf16),
            pltpu.VMEM((9 * 512, 256), bf16),
            pltpu.VMEM((3, 2 * PAD + PIXELS, 512), bf16),
            pltpu.VMEM((2 * PIXELS, 9 * 512), bf16),
            pltpu.VMEM((2, 2, 8, PIXELS, LANES), bf16),
            pltpu.VMEM((8, PIXELS, LANES), f32),
            pltpu.VMEM((8, PIXELS, LANES), f32),
            pltpu.VMEM((8, 2) + block, bf16),
            pltpu.VMEM((8, 2, PIXELS, LANES), bf16),
            pltpu.VMEM((2, 2, PIXELS, LANES), bf16),
            pltpu.VMEM((4, 8, PIXELS, LANES), bf16),
            pltpu.VMEM((4, 8, PIXELS, LANES), bf16),
            pltpu.VMEM(block, f32),
            pltpu.VMEM((2,) + block, f32),
            pltpu.VMEM((2, 4) + block, bf16),
            pltpu.VMEM((2, 4) + block, bf16),
            pltpu.VMEM((2, 3) + block, bf16),
            pltpu.VMEM((2, 5) + block, bf16),
            pltpu.VMEM((8, LANES), f32),
        ]
        + gather_sems(2) * 2
        + [dma((2, 4)), dma((2, 4)), dma((2, 3)), dma((2, 5))]
        + [dma((4, 8)), dma((4, 8))]
        + [dma((3, 4)), dma((2, 2, 4))] * 2
        + [dma((8, 2)), dma((2, 2)), dma((9,))],
        compiler_params=kernel_params(2),
    )(*arrays)


def finish_kernel(count, *refs):
    sources, targets, held = refs[:count], refs[count : 2 * count], refs[2 * count : 3 * count]
    sem_in, sem_out = refs[3 * count :]

    def parts(ref):
        large = len(ref.shape) > 2
        return [ref.at[number] for number in range(ref.shape[0])] if large else [ref]

    number = 0
    loads, stores = [], []
    for source, target, hold in zip(sources, targets, held):
        for pieces in zip(parts(source), parts(hold), parts(target)):
            loads.append(pltpu.make_async_copy(pieces[0], pieces[1], sem_in.at[number]))
            stores.append(pltpu.make_async_copy(pieces[1], pieces[2], sem_out.at[number]))
            number += 1
    for load in loads:
        load.start()
    for load, store in zip(loads, stores):
        load.wait()
        store.start()
    for store in stores:
        store.wait()


def run_finish(*arrays):
    anywhere = [pl.BlockSpec(memory_space=pltpu.HBM)] * len(arrays)
    copies = sum(item.shape[0] if item.ndim > 2 else 1 for item in arrays)
    return pl.pallas_call(
        functools.partial(finish_kernel, len(arrays)),
        name="finish",
        out_shape=tuple(jax.ShapeDtypeStruct(item.shape, item.dtype) for item in arrays),
        in_specs=anywhere,
        out_specs=tuple(anywhere),
        scratch_shapes=[pltpu.VMEM(item.shape, item.dtype) for item in arrays]
        + [pltpu.SemaphoreType.DMA((copies,))] * 2,
        compiler_params=pltpu.CompilerParams(vmem_limit_bytes=60 * 2**20),
    )(*arrays)


def stationary_local(
    features,
    image_ids,
    reduce_weight,
    spatial_weight,
    expand_weight,
    head_weights,
    distil_weights,
    block_scale,
    block_shift,
    head_scale,
    head_shift,
    gate_bias,
    output_scale,
    output_shift,
    depth_cotangent,
    segment_cotangent,
):
    canvases, row_count, column_count = image_ids.shape
    pixels = row_count * column_count
    count = float(lax.axis_size("batch") * pixels)
    x = features.reshape(canvases, pixels, -1)
    cots = [item.reshape(canvases, pixels, LANES) for item in (depth_cotangent, segment_cotangent)]
    block_params = (block_scale, block_shift)
    output_params = (output_scale[None], output_shift[None])
    (
        block_out,
        norm3,
        inverse3,
        norm12,
        inverse12,
        mine,
        mask,
        act1,
        act2,
        reduce_all,
        spatial_all,
        expand_all,
        mask_all,
        cot_all,
        raw,
    ) = run_front(
        count,
        x,
        image_ids,
        reduce_weight.T,
        spatial_weight,
        expand_weight,
        *block_params,
        *output_params,
        head_scale,
        head_shift,
        *cots,
    )
    depth_out, segment_out, gate_sums, head_sums, block_grad, block_all, back_all, distil_grad = run_middle(
        count,
        block_out,
        gate_bias,
        mine,
        head_weights.transpose(0, 2, 3, 1).reshape(9, -1, head_weights.shape[1]),
        distil_weights,
        mask_all,
        *cots,
        cot_all,
    )
    (
        features_grad,
        reduce_grad,
        spatial_grad,
        expand_grad,
        block_scale_grad,
        block_shift_grad,
        head_scale_grad,
        head_shift_grad,
        gate_grad,
        output_scale_grad,
        output_shift_grad,
        heads_grad,
    ) = run_rear(
        count,
        block_grad,
        x,
        norm3,
        inverse3,
        norm12,
        inverse12,
        mask,
        *block_params,
        *output_params,
        head_sums,
        gate_sums,
        block_all,
        back_all,
        mask_all,
        act1,
        act2,
        reduce_all,
        spatial_all,
        expand_all,
        raw,
    )
    outs = run_finish(
        depth_out,
        segment_out,
        features_grad,
        reduce_grad,
        spatial_grad,
        expand_grad,
        heads_grad,
        distil_grad,
        block_scale_grad,
        block_shift_grad,
        head_scale_grad,
        head_shift_grad,
        gate_grad,
        output_scale_grad,
        output_shift_grad,
    )
    heads_grad = outs[6].reshape(9, 4, -1, head_weights.shape[1]).transpose(0, 3, 1, 2)
    return (
        outs[0].reshape(depth_cotangent.shape),
        outs[1].reshape(depth_cotangent.shape),
        outs[2].reshape(features.shape),
        outs[3].T,
        *outs[4:6],
        heads_grad,
        *outs[7:13],
        outs[13][0],
        outs[14][0],
    )


def solution(mesh):
    fits = dict(mesh.shape) == {"batch": 8, "chan": 4}
    local = stationary_local if fits else gathered_local
    placed = (
        P("batch", None, None, "chan"),
        P("batch", None, None),
        P("chan", "batch"),
        P(None, "batch", "chan"),
        P("batch", "chan"),
        P(None, "chan", None, "batch"),
        P(None, None, None, "batch", "chan"),
        P(None, "chan"),
        P(None, "chan"),
        P(None, "chan"),
        P(None, "chan"),
        P(None, "chan"),
        P("chan"),
        P("chan"),
        P("batch", None, None, "chan"),
        P("batch", None, None, "chan"),
    )
    return jax.shard_map(
        local,
        mesh=mesh,
        in_specs=placed,
        out_specs=(
            P("batch", None, None, "chan"),
            P("batch", None, None, "chan"),
            P("batch", None, None, "chan"),
            P("chan", "batch"),
            P(None, "batch", "chan"),
            P("batch", "chan"),
            P(None, "chan", None, "batch"),
            P(None, None, None, "batch", "chan"),
            P(None, "chan"),
            P(None, "chan"),
            P(None, "chan"),
            P(None, "chan"),
            P(None, "chan"),
            P("chan"),
            P("chan"),
        ),
        check_vma=False,
    )
```
